32 devices in a mesh: dp: 8 (over z, y), tensor: 4 (over x, core).
Axes of the slice: x: 2, y: 2, z: 4, core: 2. Of those that a mesh axis runs over, the one named last changes fastest.
Arguments:
- tokens: bfloat16 [9456, 768], P('dp'), as said below
- gain_attn: bfloat16 [768], replicated, may hold values from 0.5 to 1.5
- w_query: bfloat16 [768, 768], P(None, 'tensor'), may hold values from -0.3125 to 0.3125
- w_key: bfloat16 [768, 768], P(None, 'tensor'), may hold values from -0.3125 to 0.3125
- w_value: bfloat16 [768, 768], P(None, 'tensor'), may hold values from -0.21875 to 0.21875
- w_output: bfloat16 [768, 768], P('tensor'), may hold values from -0.625 to 0.625
- gain_moe: bfloat16 [768], replicated, may hold values from 0.5 to 1.5
- w_router: bfloat16 [768, 8], replicated, may hold values from -0.21875 to 0.21875
- expert_in: bfloat16 [8, 768, 3072], P('dp', None, 'tensor'), may hold values from -0.21875 to 0.21875
- expert_out: bfloat16 [8, 3072, 768], P('dp', 'tensor'), may hold values from -0.21875 to 0.21875
- routes: int32 [9456, 2], P('dp'), may hold values from 0 to 7, as said below
- slot_ids: int32 [9456, 2], P('dp'), may hold values from 0 to 340, as said below
- capacity: int32 [8], replicated, may hold values from 255 to 340, as said below
- threshold: float32 [12], P('tensor'), may hold values from 5 to 16
- cotangent: bfloat16 [9456, 768], P('dp'), may hold values from -6 to 6
Outputs:
- block_out: bfloat16 [9456, 768], P('dp')
- grad_tokens: bfloat16 [9456, 768], P('dp')
- grad_gain_attn: float32 [768], P('dp')
- grad_gain_moe: float32 [768], P('dp')
- grad_w_query: float32 [768, 768], P('dp', 'tensor')
- grad_w_key: float32 [768, 768], P('dp', 'tensor')
- grad_w_value: float32 [768, 768], P('dp', 'tensor')
- grad_w_output: float32 [768, 768], P('tensor', 'dp')
- grad_router: float32 [768, 8], P('dp')
- grad_expert_in: float32 [8, 768, 3072], P('dp', None, 'tensor')
- grad_expert_out: float32 [8, 3072, 768], P('dp', 'tensor')
- clipped_query: float32 [768, 768], P(None, 'tensor')
- clipped_key: float32 [768, 768], P(None, 'tensor')
- head_max: float32 [12], P('tensor')
The draws below stay inside these ranges and needn't reach their ends.
Inputs may be any that keep to these rules, and one draw needn't show every extreme that they name: `routes`: a token's two experts differ; one expert takes the first choices of the first 341 tokens of every block of 1182 tokens. `slot_ids`: among the pairs of the same block of 1182 tokens and the same expert, first choices take slots 0, 1, ... in token order and second choices follow in token order; a pair whose position would be 340 or more gets slot 340, which happens in every block. `capacity`: one expert accepts 340 pairs, and all its slots are filled from every block. The tokens of an image may share a common part that grows from image to image.
All inputs are finite; a program needn't handle non-finite values.
Results may differ from the reference program's by a relative error of at most 0.015.
The reference program's roundings to bfloat16 on the way count: a program that leaves them out, or rounds other values in their place, can miss the bound.
Values may be sent and summed in bfloat16 or wider, within the bound.
A program may use at most 192 MiB of HBM per device.

```python
import math
import jax
import jax.numpy as jnp
from jax import lax

D = 768
HEADS = 12
HD = 64
FF = 3072
SEQ = 197
IMG_DEV = 6
TOK_DEV = 1182
IMAGES = 48
TOKENS = 9456
EXPERTS = 8
SLOTS = 340
N_DP = 8


def draw_tokens(key, part):
    key_base, key_common = jax.random.split(jax.random.fold_in(key, 3))
    base_vals = jax.random.normal(key_base, (IMAGES, SEQ, D), jnp.float32)
    common = jax.random.normal(key_common, (IMAGES, 1, D), jnp.float32)
    level = 0.9 * jnp.arange(IMAGES, dtype=jnp.float32) / max(IMAGES - 1, 1)
    level = level[:, None, None]
    mixed_vals = jnp.sqrt(1.0 - level * level) * base_vals + level * common
    return mixed_vals.reshape(IMAGES * SEQ, D).astype(jnp.bfloat16)


def routing_draw(key):
    key_weight, key_busy, key_pick, key_offset = jax.random.split(jax.random.fold_in(key, 7), 4)
    expert_ids = jnp.arange(EXPERTS, dtype=jnp.int32)
    weights = 1 + jax.random.randint(key_weight, (EXPERTS,), 0, 4)
    busiest = jax.random.randint(key_busy, (), 0, EXPERTS)
    weights = jnp.where(expert_ids == busiest, 6, weights)
    bounds = jnp.cumsum(weights)
    draw_pick = jax.random.randint(key_pick, (TOKENS,), 0, bounds[-1])
    first_ids = jnp.sum((bounds[None, :] <= draw_pick[:, None]).astype(jnp.int32), axis=1)
    position = jnp.arange(TOKENS, dtype=jnp.int32) % TOK_DEV
    first_ids = jnp.where(position <= SLOTS, busiest, first_ids)
    offset = jax.random.randint(key_offset, (TOKENS,), 1, EXPERTS)
    second_ids = (first_ids + offset) % EXPERTS
    return (jnp.stack([first_ids, second_ids], axis=1).astype(jnp.int32), busiest)


def draw_routes(key, part):
    routes, busiest = routing_draw(key)
    return routes


def draw_slot_ids(key, part):
    routes, busiest = routing_draw(key)
    expert_ids = jnp.arange(EXPERTS, dtype=jnp.int32)
    blocks = TOKENS // TOK_DEV
    first_hot = (routes[:, 0:1] == expert_ids[None, :]).astype(jnp.int32).reshape(blocks, TOK_DEV, EXPERTS)
    second_hot = (routes[:, 1:2] == expert_ids[None, :]).astype(jnp.int32).reshape(blocks, TOK_DEV, EXPERTS)
    first_before = jnp.cumsum(first_hot, axis=1) - first_hot
    first_count = jnp.sum(first_hot, axis=1, keepdims=True)
    second_before = jnp.cumsum(second_hot, axis=1) - second_hot + first_count
    first_slot = jnp.sum(first_before * first_hot, axis=-1).reshape(TOKENS)
    second_slot = jnp.sum(second_before * second_hot, axis=-1).reshape(TOKENS)
    slots = jnp.stack([first_slot, second_slot], axis=1)
    return jnp.minimum(slots, SLOTS).astype(jnp.int32)


def draw_capacity(key, part):
    routes, busiest = routing_draw(key)
    expert_ids = jnp.arange(EXPERTS, dtype=jnp.int32)
    limits = jax.random.randint(jax.random.fold_in(key, 11), (EXPERTS,), 3 * SLOTS // 4, SLOTS + 1)
    return jnp.where(expert_ids == busiest, SLOTS, limits).astype(jnp.int32)


def raised(values, key, source, target, shards_of, factor):
    def block_of(dim):
        return (jnp.arange(values.shape[dim]) // (values.shape[dim] // shards_of)).reshape((-1,) + (1,) * (values.ndim - 1 - dim))

    near = jax.random.permutation(key, shards_of)[block_of(target)]
    far = (block_of(target) + shards_of // 2) % shards_of
    return jnp.where((block_of(source) == near) | (block_of(source) == far), factor * values, values)


def block_scale(stream_key, shape, shards, low, largest):
    level, own = 1.0, jax.random.fold_in(stream_key, 6)
    for dim, parts in shards:
        steps = jnp.exp(jax.random.uniform(jax.random.fold_in(own, dim), (parts,), jnp.float32, low / len(shards), largest / len(shards)))
        level = level * jnp.repeat(steps, shape[dim] // parts).reshape([-1 if axis == dim else 1 for axis in range(len(shape))])
    return level


def normal_values(key, dims, scale, bound, pieces=(), kind=jnp.bfloat16):
    values = scale * jax.random.normal(key, dims, jnp.float32)
    if pieces:
        values = values * block_scale(key, dims, pieces, -0.22, 0.18)
    return jnp.clip(values, -bound, bound).astype(kind)


def bell_draw_with(rng, shape, deviation, bound, shards, heavy, kind=jnp.bfloat16):
    drawn = deviation * jax.random.normal(rng, shape, jnp.float32)
    if shards:
        drawn = drawn * block_scale(rng, shape, shards, -0.22, 0.18)
    return jnp.clip(raised(drawn, jax.random.fold_in(rng, 3), *heavy), -bound, bound).astype(kind)


def setup_inputs(seed: int = 0) -> dict:
    seeds = jax.random.split(jax.random.key(seed), 16)
    return {
        "tokens": draw_tokens(jax.random.fold_in(seeds[15], 71), 0),
        "gain_attn": jnp.clip(1.0 + 0.1 * jax.random.normal(seeds[1], (D,), jnp.float32), 0.5, 1.5).astype(jnp.bfloat16),
        "w_query": normal_values(seeds[2], (D, D), (D // 2) ** -0.5, 0.3125, ((1, 4),)),
        "w_key": normal_values(seeds[3], (D, D), (D // 2) ** -0.5, 0.3125, ((1, 4),)),
        "w_value": normal_values(seeds[4], (D, D), D ** -0.5, 0.21875, ((1, 4),)),
        "w_output": normal_values(seeds[5], (D, D), (D // 8) ** -0.5, 0.625, ((0, 4),)),
        "gain_moe": jnp.clip(1.0 + 0.1 * jax.random.normal(seeds[6], (D,), jnp.float32), 0.5, 1.5).astype(jnp.bfloat16),
        "w_router": normal_values(seeds[7], (D, EXPERTS), D ** -0.5, 0.21875),
        "expert_in": normal_values(seeds[8], (EXPERTS, D, FF), D ** -0.5, 0.21875, ((0, 8), (2, 4))),
        "expert_out": normal_values(seeds[9], (EXPERTS, FF, D), (FF // 4) ** -0.5, 0.21875, ((0, 8), (1, 4))),
        "routes": draw_routes(jax.random.fold_in(seeds[15], 71), 0),
        "slot_ids": draw_slot_ids(jax.random.fold_in(seeds[15], 71), 0),
        "capacity": draw_capacity(jax.random.fold_in(seeds[15], 71), 0),
        "threshold": jnp.clip(jnp.exp(math.log(16.0) - 1.1631508 * jax.random.uniform(seeds[13], (HEADS,), jnp.float32) ** block_scale(seeds[13], (HEADS,), ((0, 4),), -0.2, 0.2)), 5.0, 16.0),
        "cotangent": bell_draw_with(seeds[14], (TOKENS, D), 1.0, 6.0, ((0, 8),), (0, 1, 8, 2.0)),
    }


epsilon = 1e-06
highest = lax.Precision.HIGHEST

@jax.custom_vjp
def low(v):
    return lax.optimization_barrier(v.astype(jnp.bfloat16)).astype(jnp.float32)

@jax.custom_vjp
def low_back(v):
    return v

def low_keep(v):
    return (low(v), None)

def low_pass(kept, grad):
    return (grad,)

def back_keep(v):
    return (v, None)

def back_low(kept, grad):
    return (low(grad),)
low.defvjp(low_keep, low_pass)
low_back.defvjp(back_keep, back_low)

def layer_norm(rows, gain):
    centered = rows - lax.optimization_barrier(jnp.mean(rows, axis=-1, keepdims=True))
    factor = lax.rsqrt(lax.optimization_barrier(jnp.mean(centered * centered, axis=-1, keepdims=True)) + epsilon)
    return centered * factor * gain

def attend(block):
    query_heads, key_heads, value_heads = block
    raw_scores = jnp.einsum('ishd,ithd->ihst', query_heads, key_heads, precision=highest) * HD ** (-0.5)
    peak_vals = lax.optimization_barrier(jnp.max(raw_scores, axis=(0, 2, 3)))
    scores = low_back(raw_scores)
    attn_probs = jax.nn.softmax(scores, axis=-1)
    mixed_vals = jnp.einsum('ihst,ithd->ishd', low(attn_probs), value_heads, precision=highest)
    return (mixed_vals, peak_vals)

def expert_apply(block):
    rows_here, first_w, second_w = block
    pre_act = low_back(jnp.dot(rows_here, first_w, precision=highest))
    hidden = low(jax.nn.gelu(pre_act, approximate=False))
    return jnp.dot(hidden, second_w, precision=highest)

def reference(tokens, gain_attn, w_query, w_key, w_value, w_output, gain_moe, w_router, expert_in, expert_out, routes, slot_ids, capacity, threshold, cotangent):
    groups = IMAGES // IMG_DEV
    source = jnp.arange(TOKENS, dtype=jnp.int32) // TOK_DEV
    limits = capacity[routes]
    kept_mask = slot_ids < limits
    keep_vals = kept_mask.astype(jnp.float32)
    buffer_rows = EXPERTS * N_DP * SLOTS
    target = routes * (N_DP * SLOTS) + source[:, None] * SLOTS + slot_ids
    target = jnp.where(kept_mask, target, buffer_rows).astype(jnp.int32)

    def forward(inputs, gain_one, query_w, key_w, value_w, output_w, gain_two, router_w, first_w, second_w):
        normed = low(layer_norm(inputs, gain_one))

        def project(weight):
            made = low_back(low(jnp.dot(normed, weight, precision=highest)))
            return made.reshape(groups, IMG_DEV, SEQ, HEADS, HD)
        mixed_vals, peak_vals = lax.map(jax.checkpoint(attend), (project(query_w), project(key_w), project(value_w)))
        mixed_rows = low_back(low(mixed_vals.reshape(TOKENS, D)))
        attended = low_back(jnp.dot(mixed_rows, output_w, precision=highest))
        residual = inputs + attended
        normed_two = low(layer_norm(residual, gain_two))
        logits = low_back(jnp.dot(normed_two, router_w, precision=highest))
        chosen = jnp.take_along_axis(logits, routes, axis=1)
        gate_vals = jax.nn.softmax(chosen, axis=-1)
        spread = normed_two[:, None, :] * keep_vals[:, :, None]
        buffer = jnp.zeros((buffer_rows + 1, D), jnp.float32).at[target.reshape(-1)].add(spread.reshape(-1, D))
        buffer = low_back(buffer[:buffer_rows]).reshape(EXPERTS, N_DP * SLOTS, D)
        outputs = lax.map(jax.checkpoint(expert_apply), (buffer, first_w, second_w))
        outputs = low_back(low(outputs.reshape(buffer_rows, D)))
        padded = jnp.concatenate([outputs, jnp.zeros((1, D), jnp.float32)], axis=0)
        gathered = padded[target] * keep_vals[:, :, None]
        mixture = lax.optimization_barrier(jnp.sum(gate_vals[:, :, None] * gathered, axis=1))
        return (residual + mixture, lax.optimization_barrier(jnp.max(peak_vals, axis=0)))
    primals = (tokens.astype(jnp.float32), gain_attn.astype(jnp.float32), w_query.astype(jnp.float32), w_key.astype(jnp.float32), w_value.astype(jnp.float32), w_output.astype(jnp.float32), gain_moe.astype(jnp.float32), w_router.astype(jnp.float32), expert_in.astype(jnp.float32), expert_out.astype(jnp.float32))
    result, pullback, head_max = jax.vjp(forward, *primals, has_aux=True)
    grads = pullback(cotangent.astype(jnp.float32))
    factor = jnp.sqrt(jnp.minimum(1.0, threshold / head_max))
    column_factor = jnp.repeat(factor, HD)[None, :]
    clipped_query = primals[2] * column_factor
    clipped_key = primals[3] * column_factor
    return (result.astype(jnp.bfloat16), grads[0].astype(jnp.bfloat16), grads[1], grads[6], grads[2], grads[3], grads[4], grads[5], grads[7], grads[8], grads[9], clipped_query, clipped_key, head_max)
```

```python
import functools
import math

import jax
import jax.numpy as jnp
from jax import lax
from jax.experimental import pallas as pl
from jax.experimental.pallas import tpu as pltpu
from jax.sharding import PartitionSpec as P

HD = 64
SEQ = 197
TOK_DEV = 1182
PIECE = 208
MESH = pl.DeviceIdType.MESH
VMEM_LIMIT = 60 * 2**20


epsilon = 1e-06
contract = (((0,), (0,)), ((), ()))
contract_last = (((1,), (1,)), ((), ()))


def split_up(array, dim, peers):
    before, after = (array.shape[:dim], array.shape[dim + 1 :])
    return jnp.moveaxis(array.reshape(*before, peers, -1, *after), dim, 0)


def sent_and_summed(array, axis, dim):
    blocks = split_up(array, dim, lax.axis_size(axis))
    arrived = lax.all_to_all(blocks, axis, split_axis=0, concat_axis=0, tiled=True)
    return arrived.astype(jnp.float32).sum(axis=0)


def in_one_piece(arrays, axis, dim, along):
    ends, at = ([], 0)
    for a in arrays[:-1]:
        at += a.shape[along]
        ends.append(at)
    both = jnp.concatenate(arrays, axis=along)
    return tuple(jnp.split(sent_and_summed(both, axis, dim), ends, axis=along))


def in_one_piece_2(arrays, axis, dim, along):
    widths = [math.prod(a.shape[along:]) for a in arrays]
    both = jnp.concatenate(
        [a.reshape(*a.shape[:along], w) for a, w in zip(arrays, widths)], axis=along
    )
    whole = sent_and_summed(both, axis, dim)
    blocks = jnp.split(whole, [sum(widths[:k]) for k in range(1, len(widths))], axis=along)
    return tuple(
        (b.reshape(*whole.shape[:along], *a.shape[along:]) for a, b in zip(arrays, blocks))
    )


def norm_rows(rows, gain):
    centered = rows - jnp.mean(rows, axis=-1, keepdims=True)
    factor = lax.rsqrt(jnp.mean(centered * centered, axis=-1, keepdims=True) + epsilon)
    return centered * factor * gain


def exact_gelu(values_in):
    return jax.nn.gelu(values_in, approximate=False)


def dot_plain(a, b):
    return jnp.dot(a, b, preferred_element_type=jnp.float32)


def dot_last(a, b):
    return lax.dot_general(a, b, contract_last, preferred_element_type=jnp.float32)


def dot_first(a, b):
    return lax.dot_general(a, b, contract, preferred_element_type=jnp.float32)


def places():
    dp = lax.axis_index("dp")
    t = lax.axis_index("tensor")
    return dp, t, t % 2, t // 2, t + 1 - 2 * (t % 2), (t + 2) % 4


def remote(src, dst, sends, recvs, device):
    return pltpu.make_async_remote_copy(
        src_ref=src,
        dst_ref=dst,
        send_sem=sends,
        recv_sem=recvs,
        device_id=device,
        device_id_type=MESH,
    )


def signal(sem, device):
    pl.semaphore_signal(sem, inc=1, device_id=device, device_id_type=MESH)


def total_kernel(part_ref, out_ref, pair_in, far_out, far_in, ps, pr, fs, fr, os_, or_):
    dp, t, half, _, mate, far = places()
    barrier = pltpu.get_barrier_semaphore()
    signal(barrier, (dp, mate))
    signal(barrier, (dp, far))
    pl.semaphore_wait(barrier, 2)

    def rows(owner, j):
        return pl.ds(pl.multiple_of((owner * 3 + j) * PIECE, PIECE), PIECE)

    def pair_copy(j):
        return remote(
            part_ref.at[rows(1 - half, j)], pair_in.at[j], ps.at[j], pr.at[j], (dp, mate)
        )

    def far_copy(j):
        return remote(far_out.at[j], far_in.at[j], fs.at[j], fr.at[j], (dp, far))

    def out_copy(j):
        return remote(
            out_ref.at[rows(half, j)], out_ref.at[rows(half, j)], os_.at[j], or_.at[j], (dp, mate)
        )

    def out_arrival(j):
        return remote(
            out_ref.at[rows(1 - half, j)],
            out_ref.at[rows(1 - half, j)],
            os_.at[j],
            or_.at[j],
            (dp, mate),
        )

    for j in range(3):
        pair_copy(j).start()
    for j in range(3):
        pair_copy(j).wait_recv()
        far_out[j] = (part_ref[rows(half, j), :] + pair_in[j]).astype(jnp.bfloat16)
        far_copy(j).start()
    for j in range(3):
        far_copy(j).wait_recv()
        out_ref[rows(half, j), :] = far_out[j].astype(jnp.float32) + far_in[j].astype(jnp.float32)
        out_copy(j).start()
    for j in range(3):
        pair_copy(j).wait_send()
        far_copy(j).wait_send()
        out_copy(j).wait_send()
        out_arrival(j).wait_recv()


def tensor_total(part, collective_id, name):
    rows, width = part.shape
    padded = jnp.pad(part, ((0, 6 * PIECE - rows), (0, 0)))
    dma = pltpu.SemaphoreType.DMA((3,))
    out = pl.pallas_call(
        total_kernel,
        out_shape=jax.ShapeDtypeStruct(padded.shape, jnp.float32),
        in_specs=[pl.BlockSpec(memory_space=pltpu.VMEM)],
        out_specs=pl.BlockSpec(memory_space=pltpu.VMEM),
        scratch_shapes=[
            pltpu.VMEM((3, PIECE, width), jnp.float32),
            pltpu.VMEM((3, PIECE, width), jnp.bfloat16),
            pltpu.VMEM((3, PIECE, width), jnp.bfloat16),
            dma, dma, dma, dma, dma, dma,
        ],
        compiler_params=pltpu.CompilerParams(
            collective_id=collective_id, has_side_effects=True, vmem_limit_bytes=VMEM_LIMIT
        ),
        name=name,
    )(padded)
    return out[:rows]


def columns_kernel(mine_ref, other_ref, fs, fr, ps, pr):
    dp, t, half, _, mate, far = places()
    barrier = pltpu.get_barrier_semaphore()
    signal(barrier, (dp, mate))
    signal(barrier, (dp, far))
    pl.semaphore_wait(barrier, 2)

    def rows(owner, j):
        return pl.ds(pl.multiple_of((owner * 3 + j) * PIECE, PIECE), PIECE)

    def far_copy(j):
        return remote(
            mine_ref.at[rows(half, j)], other_ref.at[rows(half, j)], fs.at[j], fr.at[j], (dp, far)
        )

    def pair_copy(j, owner):
        return remote(
            other_ref.at[rows(owner, j)], other_ref.at[rows(owner, j)], ps.at[j], pr.at[j], (dp, mate)
        )

    for j in range(3):
        far_copy(j).start()
    for j in range(3):
        far_copy(j).wait_recv()
        pair_copy(j, half).start()
    for j in range(3):
        far_copy(j).wait_send()
        pair_copy(j, half).wait_send()
        pair_copy(j, 1 - half).wait_recv()


def other_columns(mine, collective_id, name):
    dma = pltpu.SemaphoreType.DMA((3,))
    return pl.pallas_call(
        columns_kernel,
        out_shape=jax.ShapeDtypeStruct(mine.shape, mine.dtype),
        in_specs=[pl.BlockSpec(memory_space=pltpu.VMEM)],
        out_specs=pl.BlockSpec(memory_space=pltpu.VMEM),
        scratch_shapes=[dma, dma, dma, dma],
        compiler_params=pltpu.CompilerParams(
            collective_id=collective_id, has_side_effects=True, vmem_limit_bytes=VMEM_LIMIT
        ),
        name=name,
    )(mine)


def expert_kernel(
    n,
    hp,
    target_ref,
    gate_ref,
    normed_ref,
    upstream_ref,
    first_ref,
    second_ref,
    peak_ref,
    back_ref,
    grad_first_ref,
    grad_second_ref,
    top_ref,
    outgoing,
    arrived,
    hidden_all,
    pre_grad_all,
    parts,
    pair_in,
    kept,
    far_out,
    far_in,
    final,
    peaks,
    local_sem,
    zs,
    zr,
    xs,
    xr,
    cs,
    cr,
    ps,
    pr,
    fs,
    fr,
    rs,
    rr,
    ms,
    mr,
    ks,
    kr,
):
    dp, t, half, side, mate, far = places()
    row_count, width = normed_ref.shape
    barrier = pltpu.get_barrier_semaphore()

    def greet(k, carry):
        signal(barrier, ((dp + k) % n, t))
        return carry

    lax.fori_loop(1, n, greet, 0)
    signal(barrier, (dp, mate))
    signal(barrier, (dp, far))

    def half_rows(owner):
        return pl.ds(pl.multiple_of(owner * hp, hp), hp)

    def side_columns(owner):
        return pl.ds(pl.multiple_of(owner * width, width), width)

    def quarter(k, row_owner, column_owner):
        return arrived.at[k, :, half_rows(row_owner), side_columns(column_owner)]

    def ahead(k):
        return ((dp + k) % n, t)

    def behind(k):
        return ((dp + n - k) % n, t)

    def own_copy():
        return pltpu.make_async_copy(outgoing.at[0], quarter(0, half, side), local_sem)

    def dispatch_copy(k):
        return remote(
            outgoing.at[k], quarter(k, half, side), zs.at[k], zr.at[k], ahead(k)
        )

    def side_copy(k):
        return remote(quarter(k, half, side), quarter(k, half, side), xs.at[k], xr.at[k], (dp, far))

    def side_arrival(k):
        return remote(
            quarter(k, half, 1 - side), quarter(k, half, 1 - side), xs.at[k], xr.at[k], (dp, far)
        )

    def pair_copy(k, owner):
        rows = arrived.at[k, :, half_rows(owner)]
        return remote(rows, rows, cs.at[k], cr.at[k], (dp, mate))

    def part_copy(k):
        return remote(
            parts.at[k % 3, :, half_rows(1 - half)],
            pair_in.at[k],
            ps.at[k % 3],
            pr.at[k],
            (dp, mate),
        )

    def far_copy(k):
        return remote(far_out.at[k % 3], far_in.at[k], fs.at[k % 3], fr.at[k], (dp, far))

    def back_half(k, owner):
        return back_ref.at[k, :, half_rows(owner)]

    def return_copy(k):
        return remote(final.at[k], back_half(k, half), rs.at[k], rr.at[k], behind(k))

    def own_return():
        return pltpu.make_async_copy(final.at[0], back_half(0, half), local_sem)

    def mate_copy(k, owner):
        return remote(back_half(k, owner), back_half(k, owner), ms.at[k], mr.at[k], (dp, mate))

    def peak_copy(k):
        return remote(peak_ref, peaks.at[k], ks.at[k], kr.at[k], ahead(k))

    pl.semaphore_wait(barrier, n + 1)

    def dispatch(k, carry):
        first_slot = target_ref[0:1, :]
        second_slot = target_ref[1:2, :]
        slots = lax.broadcasted_iota(jnp.int32, (hp, row_count), 0) + k * hp
        is_first = first_slot == slots
        is_second = second_slot == slots
        hot = jnp.where(is_first | is_second, 1.0, 0.0).astype(jnp.bfloat16)
        gate = jnp.sum(
            jnp.where(is_first, gate_ref[0:1, :], 0.0) + jnp.where(is_second, gate_ref[1:2, :], 0.0),
            axis=1,
            keepdims=True,
        )
        outgoing[k, 0] = dot_plain(hot, normed_ref[...]).astype(jnp.bfloat16)
        outgoing[k, 1] = (dot_plain(hot, upstream_ref[...]) * gate).astype(jnp.bfloat16)

        @pl.when(k == 0)
        def _():
            own_copy().start()

        @pl.when(k > 0)
        def _():
            dispatch_copy(k).start()
            peak_copy(k).start()

        return carry

    lax.fori_loop(0, n, dispatch, 0)

    def chunk(k):
        rows_in = arrived[k, 0]
        answer_grad = arrived[k, 1]
        pre = dot_plain(rows_in, first_ref[...])
        share = 0.5 * (1.0 + lax.erf(pre * math.sqrt(0.5)))
        slope = share + pre * (jnp.exp(-0.5 * pre * pre) * (1.0 / math.sqrt(2.0 * math.pi)))
        hidden = (pre * share).astype(jnp.bfloat16)
        pre_grad = (dot_last(answer_grad, second_ref[...]) * slope).astype(jnp.bfloat16)
        hidden_all[k] = hidden
        pre_grad_all[k] = pre_grad
        parts[k % 3, 0] = dot_plain(hidden, second_ref[...]).astype(jnp.bfloat16)
        parts[k % 3, 1] = dot_last(pre_grad, first_ref[...]).astype(jnp.bfloat16)

    def step(i, carry):
        @pl.when(i < n)
        def _():
            @pl.when(i == 0)
            def _():
                own_copy().wait()

            @pl.when(i > 0)
            def _():
                dispatch_copy(i).wait_recv()

            side_copy(i).start()

        @pl.when((i >= 1) & (i < n + 1))
        def _():
            k = i - 1
            side_arrival(k).wait_recv()
            pair_copy(k, half).start()

        @pl.when((i >= 2) & (i < n + 2))
        def _():
            k = i - 2
            pair_copy(k, 1 - half).wait_recv()

            @pl.when(k >= 3)
            def _():
                part_copy(k - 3).wait_send()

            chunk(k)
            part_copy(k).start()

        @pl.when((i >= 3) & (i < n + 3))
        def _():
            k = i - 3
            part_copy(k).wait_recv()

            @pl.when(k >= 3)
            def _():
                far_copy(k - 3).wait_send()

            for j in range(2):
                whole = parts[k % 3, j, half_rows(half), :].astype(jnp.float32) + pair_in[k, j].astype(jnp.float32)
                low, high = whole[:, :width], whole[:, width:]
                kept[k % 3, j] = jnp.where(side == 0, low, high)
                far_out[k % 3, j] = jnp.where(side == 0, high, low).astype(jnp.bfloat16)
            far_copy(k).start()

        @pl.when(i >= 4)
        def _():
            k = i - 4
            far_copy(k).wait_recv()
            final[k] = (kept[k % 3] + far_in[k].astype(jnp.float32)).astype(jnp.bfloat16)

            @pl.when(k == 0)
            def _():
                own_return().start()

            @pl.when(k > 0)
            def _():
                return_copy(k).start()

        return carry

    lax.fori_loop(0, n + 4, step, 0)

    model = 2 * width
    tile = 256
    def grads(m, carry):
        cols = pl.ds(pl.multiple_of(m * tile, tile), tile)
        rows_in = arrived[:, 0, :, cols].reshape(n * 2 * hp, tile)
        pre_grad = pre_grad_all[...].reshape(n * 2 * hp, -1)
        grad_first_ref[cols, :] = dot_first(rows_in, pre_grad)
        hidden = hidden_all[:, :, cols].reshape(n * 2 * hp, tile)
        answer_grad = arrived[:, 1].reshape(n * 2 * hp, model)
        grad_second_ref[cols, :] = dot_first(hidden, answer_grad)
        return carry

    lax.fori_loop(0, model // tile, grads, 0)

    peaks[0] = peak_ref[...]

    def collect(k, carry):
        @pl.when(k == 0)
        def _():
            own_return().wait()

        @pl.when(k > 0)
        def _():
            return_copy(k).wait_recv()
            peak_copy(k).wait_recv()

        mate_copy(k, half).start()
        return carry

    lax.fori_loop(0, n, collect, 0)
    top_ref[...] = jnp.max(peaks[...], axis=0)

    def finish(k, carry):
        mate_copy(k, 1 - half).wait_recv()
        mate_copy(k, half).wait_send()
        side_copy(k).wait_send()
        pair_copy(k, half).wait_send()

        @pl.when(k > 0)
        def _():
            dispatch_copy(k).wait_send()
            return_copy(k).wait_send()
            peak_copy(k).wait_send()

        @pl.when(k >= n - 3)
        def _():
            part_copy(k).wait_send()
            far_copy(k).wait_send()

        return carry

    lax.fori_loop(0, n, finish, 0)


def run_experts(n, hp, target, gates, normed, upstream, first, second, peak):
    width = normed.shape[1]
    model = 2 * width
    hidden = first.shape[1]
    vmem = pl.BlockSpec(memory_space=pltpu.VMEM)
    low, full = jnp.bfloat16, jnp.float32
    many = pltpu.SemaphoreType.DMA((n,))
    few = pltpu.SemaphoreType.DMA((3,))
    return pl.pallas_call(
        functools.partial(expert_kernel, n, hp),
        out_shape=(
            jax.ShapeDtypeStruct((n, 2, 2 * hp, width), low),
            jax.ShapeDtypeStruct((model, hidden), full),
            jax.ShapeDtypeStruct((hidden, model), full),
            jax.ShapeDtypeStruct(peak.shape, full),
        ),
        in_specs=[vmem] * 7,
        out_specs=[vmem] * 4,
        scratch_shapes=[
            pltpu.VMEM((n, 2, hp, width), low),
            pltpu.VMEM((n, 2, 2 * hp, model), low),
            pltpu.VMEM((n, 2 * hp, hidden), low),
            pltpu.VMEM((n, 2 * hp, hidden), low),
            pltpu.VMEM((3, 2, 2 * hp, model), low),
            pltpu.VMEM((n, 2, hp, model), low),
            pltpu.VMEM((3, 2, hp, width), full),
            pltpu.VMEM((3, 2, hp, width), low),
            pltpu.VMEM((n, 2, hp, width), low),
            pltpu.VMEM((n, 2, hp, width), low),
            pltpu.VMEM((n, *peak.shape), full),
            pltpu.SemaphoreType.DMA,
            many, many, many, many, many, many, few, many, few, many,
            many, many, many, many, many, many,
        ],
        compiler_params=pltpu.CompilerParams(
            collective_id=3, has_side_effects=True, vmem_limit_bytes=VMEM_LIMIT
        ),
        name="experts",
    )(target, gates, normed, upstream, first, second, peak)


def body(
    tokens,
    gain_attn,
    w_query,
    w_key,
    w_value,
    w_output,
    gain_moe,
    w_router,
    expert_in,
    expert_out,
    routes,
    slot_ids,
    capacity,
    threshold,
    cotangent,
):
    dp_count = lax.axis_size("dp")
    row_count = tokens.shape[0]
    images = row_count // SEQ
    heads_here = w_query.shape[1] // HD
    experts = expert_in.shape[0] * dp_count
    slot_count = 23 * TOK_DEV // (10 * experts) + 1
    score_scale = HD ** (-0.5)

    def heads_view(rows):
        return rows.reshape(images, SEQ, heads_here, HD)

    def as_rows(heads):
        return heads.reshape(row_count, heads_here * HD)

    inputs = tokens.astype(jnp.float32)
    norm_one, norm_one_back = jax.vjp(norm_rows, inputs, gain_attn.astype(jnp.float32))
    normed_one = norm_one.astype(jnp.bfloat16)
    queries = jnp.dot(normed_one, w_query, preferred_element_type=jnp.float32).astype(jnp.bfloat16)
    key_rows = jnp.dot(normed_one, w_key, preferred_element_type=jnp.float32).astype(jnp.bfloat16)
    value_rows = jnp.dot(normed_one, w_value, preferred_element_type=jnp.float32).astype(
        jnp.bfloat16
    )
    query_heads = heads_view(queries)
    key_heads = heads_view(key_rows)
    value_heads = heads_view(value_rows)
    raw_scores = (
        jnp.einsum("ishd,ithd->ihst", query_heads, key_heads, preferred_element_type=jnp.float32)
        * score_scale
    )
    peak_local = jnp.max(raw_scores, axis=(0, 2, 3))
    top_row = jnp.max(raw_scores, axis=-1, keepdims=True)
    log_total = top_row + jnp.log(jnp.sum(jnp.exp(raw_scores - top_row), axis=-1, keepdims=True))
    attn_probs = jnp.exp(raw_scores - log_total)
    mixed_heads = jnp.einsum(
        "ihst,ithd->ishd",
        attn_probs.astype(jnp.bfloat16),
        value_heads,
        preferred_element_type=jnp.float32,
    )
    mixed_rows = as_rows(mixed_heads).astype(jnp.bfloat16)
    attended = tensor_total(
        jnp.dot(mixed_rows, w_output, preferred_element_type=jnp.float32), 0, "attended"
    )
    residual = inputs + attended
    norm_two, norm_two_back = jax.vjp(norm_rows, residual, gain_moe.astype(jnp.float32))
    normed_two = norm_two.astype(jnp.bfloat16)
    logits = jnp.dot(normed_two, w_router, preferred_element_type=jnp.float32)
    expert_ids = jnp.arange(experts, dtype=jnp.int32)
    route_match = routes[:, :, None] == expert_ids[None, None, :]
    pick_hot = route_match.astype(jnp.float32)
    chosen = jnp.sum(pick_hot * logits[:, None, :], axis=-1)
    gate_vals = jax.nn.softmax(chosen, axis=-1)
    limits = jnp.sum(jnp.where(route_match, capacity[None, None, :], 0), axis=-1)
    kept_mask = slot_ids < limits
    hp = -(-(-(-slot_count // 2)) // 16) * 16
    per_half = -(-slot_count // 2)
    dp_here = lax.axis_index("dp")
    tensor_here = lax.axis_index("tensor")
    half_here = tensor_here % 2
    side_here = tensor_here // 2
    width = tokens.shape[1] // 2
    row_pad = 6 * PIECE - row_count

    def my_columns(array):
        cut = lax.dynamic_slice_in_dim(array, side_here * width, width, 1)
        return jnp.pad(cut, ((0, row_pad), (0, 0)))

    steps_ahead = (routes + dp_count - dp_here) % dp_count
    half_of = slot_ids // per_half
    in_half = slot_ids % per_half
    place = jnp.where(kept_mask & (half_of == half_here), steps_ahead * hp + in_half, -1)
    place = jnp.pad(place.T, ((0, 6), (0, row_pad)), constant_values=-1)
    gate_rows = jnp.pad(gate_vals.T, ((0, 6), (0, row_pad)))
    peak_tile = jnp.pad(
        jnp.broadcast_to(peak_local[:, None], (heads_here, 128)), ((0, 8 - heads_here), (0, 0))
    )
    back, grad_expert_in, grad_expert_out, top_tile = run_experts(
        dp_count,
        hp,
        place,
        gate_rows,
        my_columns(normed_two),
        my_columns(cotangent),
        expert_in[0],
        expert_out[0],
        peak_tile,
    )
    grad_expert_in = grad_expert_in[None]
    grad_expert_out = grad_expert_out[None]
    head_max = top_tile[:heads_here, 0]
    column_factor = jnp.repeat(jnp.sqrt(jnp.minimum(1.0, threshold / head_max)), HD)[None, :]
    clipped_query = w_query.astype(jnp.float32) * column_factor
    clipped_key = w_key.astype(jnp.float32) * column_factor

    upstream = cotangent.astype(jnp.float32)
    target = steps_ahead * (2 * hp) + half_of * hp + in_half
    columns = jnp.arange(dp_count * 2 * hp, dtype=jnp.int32)[None, :]
    hot_first = ((target[:, 0:1] == columns) & kept_mask[:, 0:1]).astype(jnp.bfloat16)
    hot_second = ((target[:, 1:2] == columns) & kept_mask[:, 1:2]).astype(jnp.bfloat16)
    answers = back[:, 0].reshape(-1, width)
    buffer_grads = back[:, 1].reshape(-1, width)
    from_first = jnp.dot(hot_first, answers, preferred_element_type=jnp.float32)
    from_second = jnp.dot(hot_second, answers, preferred_element_type=jnp.float32)
    moe_back_mine = jnp.dot(hot_first + hot_second, buffer_grads, preferred_element_type=jnp.float32)
    upstream_mine = lax.dynamic_slice_in_dim(upstream, side_here * width, width, 1)
    residual_mine = lax.dynamic_slice_in_dim(residual, side_here * width, width, 1)
    mixture = gate_vals[:, 0:1] * from_first + gate_vals[:, 1:2] * from_second
    block_out_mine = (residual_mine + mixture).astype(jnp.bfloat16)
    gate_part = jnp.stack(
        [jnp.sum(upstream_mine * from_first, axis=-1), jnp.sum(upstream_mine * from_second, axis=-1)], axis=1
    )
    both_mine = jnp.concatenate([block_out_mine, moe_back_mine.astype(jnp.bfloat16)], axis=1)
    both_mine = jnp.pad(both_mine, ((0, row_pad), (0, 0)))
    both_other = other_columns(both_mine, 2, "columns")
    gate_mine = jnp.pad(gate_part, ((0, row_pad), (0, 126)))
    gate_other = other_columns(gate_mine, 4, "gate_sums")
    gate_grad = (gate_mine + gate_other)[:row_count, :2]

    def both_sides(mine, other):
        low = jnp.where(side_here == 0, mine, other)
        high = jnp.where(side_here == 0, other, mine)
        return jnp.concatenate([low, high], axis=1)[:row_count]

    block_out = both_sides(both_mine[:, :width], both_other[:, :width])
    moe_back = both_sides(both_mine[:, width:], both_other[:, width:]).astype(jnp.float32)
    chosen_grad = gate_vals * (gate_grad - jnp.sum(gate_vals * gate_grad, axis=-1, keepdims=True))
    logit_grad = jnp.sum(chosen_grad[:, :, None] * pick_hot, axis=1).astype(jnp.bfloat16)
    grad_router = lax.dot_general(
        normed_two, logit_grad, contract, preferred_element_type=jnp.float32
    )
    router_back = lax.dot_general(
        logit_grad, w_router, contract_last, preferred_element_type=jnp.float32
    )
    resid_two_grad, grad_gain_moe = norm_two_back(moe_back + router_back)
    residual_grad = upstream + resid_two_grad
    att_grad = residual_grad.astype(jnp.bfloat16)
    grad_w_output = lax.dot_general(
        mixed_rows, att_grad, contract, preferred_element_type=jnp.float32
    )
    mixed_grad = lax.dot_general(
        att_grad, w_output, contract_last, preferred_element_type=jnp.float32
    ).astype(jnp.bfloat16)
    mixed_grad_heads = heads_view(mixed_grad)
    probs_again = jnp.exp(
        jnp.einsum("ishd,ithd->ihst", query_heads, key_heads, preferred_element_type=jnp.float32)
        * score_scale
        - log_total
    )
    value_grad = jnp.einsum(
        "ihst,ishd->ithd",
        probs_again.astype(jnp.bfloat16),
        mixed_grad_heads,
        preferred_element_type=jnp.float32,
    ).astype(jnp.bfloat16)
    probs_grad = jnp.einsum(
        "ishd,ithd->ihst", mixed_grad_heads, value_heads, preferred_element_type=jnp.float32
    )
    score_grad = probs_again * (
        probs_grad - jnp.sum(probs_again * probs_grad, axis=-1, keepdims=True)
    )
    score_grad = score_grad.astype(jnp.bfloat16)
    query_grad = (
        jnp.einsum("ihst,ithd->ishd", score_grad, key_heads, preferred_element_type=jnp.float32)
        * score_scale
    ).astype(jnp.bfloat16)
    key_grad = (
        jnp.einsum("ihst,ishd->ithd", score_grad, query_heads, preferred_element_type=jnp.float32)
        * score_scale
    ).astype(jnp.bfloat16)
    query_grad = as_rows(query_grad)
    key_grad = as_rows(key_grad)
    value_grad = as_rows(value_grad)
    grad_w_query = lax.dot_general(
        normed_one, query_grad, contract, preferred_element_type=jnp.float32
    )
    grad_w_key = lax.dot_general(normed_one, key_grad, contract, preferred_element_type=jnp.float32)
    grad_w_value = lax.dot_general(
        normed_one, value_grad, contract, preferred_element_type=jnp.float32
    )
    norm_grad_part = lax.dot_general(
        query_grad, w_query, contract_last, preferred_element_type=jnp.float32
    )
    norm_grad_part = norm_grad_part + lax.dot_general(
        key_grad, w_key, contract_last, preferred_element_type=jnp.float32
    )
    norm_grad_part = norm_grad_part + lax.dot_general(
        value_grad, w_value, contract_last, preferred_element_type=jnp.float32
    )
    normed_one_grad = tensor_total(norm_grad_part, 1, "normed_grad")
    input_ln_grad, grad_gain_attn = norm_one_back(normed_one_grad)
    grad_tokens = (residual_grad + input_ln_grad).astype(jnp.bfloat16)
    reduced = (
        *in_one_piece(
            (
                grad_w_query.astype(jnp.bfloat16),
                grad_w_key.astype(jnp.bfloat16),
                grad_w_value.astype(jnp.bfloat16),
            ),
            "dp",
            0,
            1,
        ),
        sent_and_summed(grad_w_output.astype(jnp.bfloat16), "dp", 1),
        sent_and_summed(grad_gain_attn.astype(jnp.bfloat16), "dp", 0),
        *in_one_piece_2(
            (grad_gain_moe.astype(jnp.bfloat16), grad_router.astype(jnp.bfloat16)), "dp", 0, 1
        ),
    )
    return (
        block_out,
        grad_tokens,
        reduced[4],
        reduced[5],
        reduced[0],
        reduced[1],
        reduced[2],
        reduced[3],
        reduced[6],
        grad_expert_in,
        grad_expert_out,
        clipped_query,
        clipped_key,
        head_max,
    )


def solution(mesh):
    in_specs = (
        P("dp", None),
        P(),
        P(None, "tensor"),
        P(None, "tensor"),
        P(None, "tensor"),
        P("tensor", None),
        P(),
        P(),
        P("dp", None, "tensor"),
        P("dp", "tensor", None),
        P("dp", None),
        P("dp", None),
        P(),
        P("tensor"),
        P("dp", None),
    )
    out_specs = (
        P("dp", None),
        P("dp", None),
        P("dp"),
        P("dp"),
        P("dp", "tensor"),
        P("dp", "tensor"),
        P("dp", "tensor"),
        P("tensor", "dp"),
        P("dp", None),
        P("dp", None, "tensor"),
        P("dp", "tensor", None),
        P(None, "tensor"),
        P(None, "tensor"),
        P("tensor"),
    )
    return jax.shard_map(body, mesh=mesh, in_specs=in_specs, out_specs=out_specs, check_vma=False)
```

```python
import functools
import math

import jax
import jax.numpy as jnp
from jax import lax
from jax.experimental import pallas as pl
from jax.experimental.pallas import tpu as pltpu
from jax.sharding import PartitionSpec as P

HD = 64
SEQ = 197
PIECE = 208
TOK_DEV = 1182
EPSILON = 1e-06
MESH = pl.DeviceIdType.MESH
VMEM_LIMIT = 60 * 2**20
VMEM = pltpu.VMEM
LOW, FULL = jnp.bfloat16, jnp.float32


def dot_plain(a, b):
    return jnp.dot(a, b, preferred_element_type=FULL)


def dot_last(a, b):
    return lax.dot_general(a, b, (((1,), (1,)), ((), ())), preferred_element_type=FULL)


def dot_first(a, b):
    return lax.dot_general(a, b, (((0,), (0,)), ((), ())), preferred_element_type=FULL)


def normalized(rows):
    centered = rows - jnp.mean(rows, axis=-1, keepdims=True)
    factor = lax.rsqrt(jnp.mean(centered * centered, axis=-1, keepdims=True) + EPSILON)
    return centered * factor, factor


def normalized_back(u, unit, factor):
    first = jnp.mean(u, axis=-1, keepdims=True)
    second = jnp.mean(u * unit, axis=-1, keepdims=True)
    return factor * (u - first - unit * second)


def same_index(size):
    rows = lax.broadcasted_iota(jnp.int32, (size, size), 0)
    return rows == lax.broadcasted_iota(jnp.int32, (size, size), 1)


def row_to_column(row):
    return jnp.sum(jnp.where(same_index(row.shape[1]), row, 0.0), axis=1, keepdims=True)


def column_to_row(column):
    return jnp.sum(jnp.where(same_index(column.shape[0]), column, 0.0), axis=0, keepdims=True)


def attention_probs(queries, keys):
    scores = dot_last(queries, keys) * HD**-0.5
    real = lax.broadcasted_iota(jnp.int32, scores.shape, 1) < SEQ
    scores = jnp.where(real, scores, -1e30)
    top = jnp.max(scores, axis=1, keepdims=True)
    powers = jnp.exp(scores - top)
    return powers * (1.0 / jnp.sum(powers, axis=1, keepdims=True)), top


def partner(dp, k, n):
    other, weight = 0, 1
    while weight < n:
        other = other + ((dp // weight + k // weight) % 2) * weight
        weight *= 2
    return other


def places():
    dp = lax.axis_index("dp")
    t = lax.axis_index("tensor")
    return dp, t, t % 2, t // 2, t + 1 - 2 * (t % 2), (t + 2) % 4


def remote(src, dst, sends, recvs, device):
    return pltpu.make_async_remote_copy(
        src_ref=src,
        dst_ref=dst,
        send_sem=sends,
        recv_sem=recvs,
        device_id=device,
        device_id_type=MESH,
    )


def signal(sem, device):
    pl.semaphore_signal(sem, inc=1, device_id=device, device_id_type=MESH)


def greet(n, dp, t, others):
    barrier = pltpu.get_barrier_semaphore()

    def one(k, carry):
        signal(barrier, (partner(dp, k, n), t))
        return carry

    lax.fori_loop(1, n, one, 0)
    for other in others:
        signal(barrier, (dp, other))


def await_greetings(n, others):
    pl.semaphore_wait(pltpu.get_barrier_semaphore(), n - 1 + len(others))


def image_rows(image):
    return pl.ds(pl.multiple_of(image * PIECE, PIECE), PIECE)


def dma(*shape):
    return pltpu.SemaphoreType.DMA(shape)


def near_count(n):
    return min(4, n)


class Spread:
    def __init__(self, n, hp, place, near_out, far_out, arrived, zs, zr, xs, xr, cs, cr, own):
        self.n, self.hp, self.near = n, hp, near_count(n)
        self.place, self.near_out, self.far_out, self.arrived = place, near_out, far_out, arrived
        self.zs, self.zr, self.xs, self.xr, self.cs, self.cr, self.own = zs, zr, xs, xr, cs, cr, own
        self.dp, self.t, self.half, self.side, self.mate, self.far = places()
        self.width = far_out.shape[2]

    def rows(self, owner):
        return pl.ds(pl.multiple_of(owner * self.hp, self.hp), self.hp)

    def columns(self, owner):
        return pl.ds(pl.multiple_of(owner * self.width, self.width), self.width)

    def peer(self, k):
        return (partner(self.dp, k, self.n), self.t)

    def own_copy(self):
        return pltpu.make_async_copy(
            self.near_out.at[0], self.arrived.at[0, self.rows(self.half)], self.own
        )

    def near_copy(self, k):
        return remote(
            self.near_out.at[k],
            self.arrived.at[k, self.rows(self.half)],
            self.zs.at[k],
            self.zr.at[k],
            self.peer(k),
        )

    def far_copy(self, k):
        return remote(
            self.far_out.at[k - self.near],
            self.arrived.at[k, self.rows(self.half), self.columns(self.side)],
            self.zs.at[k],
            self.zr.at[k],
            self.peer(k),
        )

    def side_copy(self, k, side):
        part = self.arrived.at[k, self.rows(self.half), self.columns(side)]
        return remote(part, part, self.xs.at[k], self.xr.at[k], (self.dp, self.far))

    def pair_copy(self, k, half):
        part = self.arrived.at[k, self.rows(half)]
        return remote(part, part, self.cs.at[k], self.cr.at[k], (self.dp, self.mate))

    def send(self, k, rows_ref):
        slots = lax.broadcasted_iota(jnp.int32, (self.hp, rows_ref.shape[0]), 0) + k * self.hp
        is_first = self.place[0:1, :] == slots
        is_second = self.place[1:2, :] == slots
        hot = jnp.where(is_first | is_second, 1.0, 0.0).astype(LOW)

        @pl.when(k < self.near)
        def _():
            self.near_out[k] = dot_plain(hot, rows_ref[...]).astype(LOW)

            @pl.when(k == 0)
            def _():
                self.own_copy().start()

            @pl.when(k > 0)
            def _():
                self.near_copy(k).start()

        @pl.when(k >= self.near)
        def _():
            mine = rows_ref[:, self.columns(self.side)]
            self.far_out[k - self.near] = dot_plain(hot, mine).astype(LOW)
            self.far_copy(k).start()

        return is_first, is_second

    def first_hop(self, k):
        @pl.when(k == 0)
        def _():
            self.own_copy().wait()

        @pl.when((k > 0) & (k < self.near))
        def _():
            self.near_copy(k).wait_recv()

        @pl.when(k >= self.near)
        def _():
            self.far_copy(k).wait_recv()
            self.side_copy(k, self.side).start()

    def second_hop(self, k):
        @pl.when(k >= self.near)
        def _():
            self.side_copy(k, 1 - self.side).wait_recv()

        self.pair_copy(k, self.half).start()

    def last_hop(self, k):
        self.pair_copy(k, 1 - self.half).wait_recv()

    def sent(self, k):
        @pl.when((k > 0) & (k < self.near))
        def _():
            self.near_copy(k).wait_send()

        @pl.when(k >= self.near)
        def _():
            self.far_copy(k).wait_send()
            self.side_copy(k, self.side).wait_send()

        self.pair_copy(k, self.half).wait_send()

    @staticmethod
    def scratch(n, hp, width):
        near = near_count(n)
        return [VMEM((near, hp, 2 * width), LOW), VMEM((n - near, hp, width), LOW)]

    @staticmethod
    def semaphores(n):
        return [dma(n), dma(n), dma(n), dma(n), dma(n), dma(n), pltpu.SemaphoreType.DMA]


class Total:
    def __init__(self, part_out, pair_in, far_out, far_in, ps, pr, fs, fr):
        self.part_out, self.pair_in, self.far_out, self.far_in = part_out, pair_in, far_out, far_in
        self.ps, self.pr, self.fs, self.fr = ps, pr, fs, fr
        self.dp, _, _, _, self.mate, self.far = places()

    def pair_copy(self, j):
        return remote(
            self.part_out.at[j], self.pair_in.at[j], self.ps.at[j], self.pr.at[j], (self.dp, self.mate)
        )

    def far_copy(self, j):
        return remote(
            self.far_out.at[j], self.far_in.at[j], self.fs.at[j], self.fr.at[j], (self.dp, self.far)
        )

    def give(self, j, rows):
        self.part_out[j] = rows
        self.pair_copy(j).start()

    def take(self, j, rows):
        self.pair_copy(j).wait_recv()
        self.far_out[j] = (rows + self.pair_in[j]).astype(LOW)
        self.far_copy(j).start()

    def result(self, j):
        self.far_copy(j).wait_recv()
        return self.far_out[j].astype(FULL) + self.far_in[j].astype(FULL)

    def sent(self, j):
        self.pair_copy(j).wait_send()
        self.far_copy(j).wait_send()

    @staticmethod
    def scratch(model):
        wide, slim = VMEM((3, PIECE, model), FULL), VMEM((3, PIECE, model), LOW)
        return [wide, wide, slim, slim, dma(3), dma(3), dma(3), dma(3)]


def front_kernel(
    n,
    hp,
    tokens_ref,
    upstream_ref,
    place_ref,
    gain_one_ref,
    gain_two_ref,
    query_w_ref,
    key_w_ref,
    value_w_ref,
    output_w_ref,
    normed_one_ref,
    query_ref,
    key_ref,
    value_ref,
    mixed_ref,
    residual_ref,
    normed_two_ref,
    peak_ref,
    spread_ref,
    *scratch,
):
    dp, t, half, side, mate, far = places()
    heads = query_w_ref.shape[1] // HD
    spread = Spread(n, hp, place_ref, *scratch[:2], spread_ref, *scratch[2:9])
    total = Total(*scratch[9:17])
    ns, nr = scratch[17:19]
    greet(n, dp, t, (mate, far))
    peak_ref[...] = jnp.full(peak_ref.shape, -1e30, FULL)

    def image_forward(image):
        rows = image_rows(image)
        unit, _ = normalized(tokens_ref[rows, :].astype(FULL))
        normed = (unit * gain_one_ref[...]).astype(LOW)
        normed_one_ref[rows, :] = normed
        queries = dot_plain(normed, query_w_ref[...]).astype(LOW)
        keys = dot_plain(normed, key_w_ref[...]).astype(LOW)
        values = dot_plain(normed, value_w_ref[...]).astype(LOW)
        query_ref[rows, :] = queries
        key_ref[rows, :] = keys
        value_ref[rows, :] = values
        mixed = []
        for h in range(heads):
            cols = slice(h * HD, (h + 1) * HD)
            probs, top = attention_probs(queries[:, cols], keys[:, cols])
            real = lax.broadcasted_iota(jnp.int32, top.shape, 0) < SEQ
            best = jnp.max(jnp.where(real, top, -1e30), axis=0, keepdims=True)
            peak_ref[h : h + 1, :] = jnp.maximum(peak_ref[h : h + 1, :], best)
            mixed.append(dot_plain(probs.astype(LOW), values[:, cols]))
        mixed = jnp.concatenate(mixed, axis=1).astype(LOW)
        mixed_ref[rows, :] = mixed
        return dot_plain(mixed, output_w_ref[...])

    def normed_copy(j, owner):
        rows = normed_two_ref.at[image_rows(2 * j + owner)]
        return remote(rows, rows, ns.at[j], nr.at[j], (dp, mate))

    def finish(j):
        rows = image_rows(2 * j + half)
        residual = tokens_ref[rows, :].astype(FULL) + total.result(j)
        residual_ref[rows, :] = residual
        unit, _ = normalized(residual)
        normed_two_ref[rows, :] = (unit * gain_two_ref[...]).astype(LOW)
        normed_copy(j, half).start()

    per_step = -(-n // 3)

    def step(j, carry):
        given = image_forward(2 * j + 1 - half)

        @pl.when(j == 0)
        def _():
            await_greetings(n, (mate, far))

        total.give(j, given)
        total.take(j, image_forward(2 * j + half))

        def dispatch(i, inner):
            @pl.when(i < n)
            def _():
                spread.send((i + spread.near) % n, upstream_ref)

            return inner

        lax.fori_loop(j * per_step, (j + 1) * per_step, dispatch, 0)

        @pl.when(j >= 1)
        def _():
            finish(j - 1)

        return carry

    lax.fori_loop(0, 3, step, 0)

    def each(body, first=0):
        def one(k, carry):
            body(k)
            return carry

        lax.fori_loop(first, n, one, 0)

    each(spread.first_hop)
    finish(2)
    each(spread.second_hop)
    each(spread.last_hop)
    each(spread.sent)
    for j in range(3):
        total.sent(j)
        normed_copy(j, half).wait_send()
        normed_copy(j, 1 - half).wait_recv()


def run_front(n, hp, tokens, upstream, place, gains, weights):
    rows, model = tokens.shape
    heads_width = weights[0].shape[1]
    vmem = pl.BlockSpec(memory_space=VMEM)
    shape = jax.ShapeDtypeStruct
    slim = shape((rows, heads_width), LOW)
    return pl.pallas_call(
        functools.partial(front_kernel, n, hp),
        out_shape=(
            shape((rows, model), LOW),
            slim,
            slim,
            slim,
            slim,
            shape((rows, model), FULL),
            shape((rows, model), LOW),
            shape((8, 128), FULL),
            shape((n, 2 * hp, model), LOW),
        ),
        in_specs=[vmem] * 9,
        out_specs=[vmem] * 9,
        scratch_shapes=[
            *Spread.scratch(n, hp, model // 2),
            *Spread.semaphores(n),
            *Total.scratch(model),
            dma(3),
            dma(3),
        ],
        compiler_params=pltpu.CompilerParams(
            collective_id=0, has_side_effects=True, vmem_limit_bytes=VMEM_LIMIT
        ),
        name="front",
    )(tokens, upstream, place, *gains, *weights)


def expert_kernel(
    n,
    hp,
    place_ref,
    gate_ref,
    normed_ref,
    first_ref,
    second_ref,
    peak_ref,
    upstream_hbm,
    answer_ref,
    back_ref,
    gate_sum_ref,
    grad_first_ref,
    grad_second_ref,
    top_ref,
    *scratch,
):
    dp, t, half, side, mate, far = places()
    arrived = scratch[2]
    spread = Spread(n, hp, place_ref, *scratch[:10])
    (
        upstream,
        hidden_all,
        pre_grad_all,
        parts,
        pair_in,
        kept,
        far_out,
        far_in,
        final,
        gate_out,
        gate_in,
        sum_out,
        sum_in,
        sums,
        peaks,
        us,
        ps,
        pr,
        fs,
        fr,
        rs,
        rr,
        ms,
        mr,
        gs,
        gr,
        hs,
        hr,
        ks,
        kr,
        qs,
        qr,
        ss,
        sr,
    ) = scratch[10:]
    model = normed_ref.shape[1]
    width = model // 2
    backs = (answer_ref, back_ref)
    greet(n, dp, t, [(t + d) % 4 for d in (1, 2, 3)])
    fetch = pltpu.make_async_copy(upstream_hbm, upstream, us)
    fetch.start()

    def gate_copy(k):
        return remote(gate_out.at[k], gate_in.at[k, half], gs.at[k], gr.at[k], spread.peer(k))

    def gate_pair_copy(k, owner):
        tile = gate_in.at[k, owner]
        return remote(tile, tile, hs.at[k], hr.at[k], (dp, mate))

    def part_copy(k):
        return remote(
            parts.at[k % 3, :, spread.rows(1 - half)],
            pair_in.at[k],
            ps.at[k % 3],
            pr.at[k],
            (dp, mate),
        )

    def far_copy(k):
        return remote(far_out.at[k % 3], far_in.at[k], fs.at[k % 3], fr.at[k], (dp, far))

    def return_copy(k, j):
        return remote(
            final.at[j, k],
            backs[j].at[k, spread.rows(half)],
            rs.at[j, k],
            rr.at[j, k],
            spread.peer(k),
        )

    def mate_copy(k, j, owner):
        rows = backs[j].at[k, spread.rows(owner)]
        return remote(rows, rows, ms.at[j, k], mr.at[j, k], (dp, mate))

    def sum_copy(k):
        return remote(sum_out.at[k], sum_in.at[k], ks.at[k], kr.at[k], spread.peer(k))

    def peak_copy(k):
        return remote(peak_ref, peaks.at[k], qs.at[k], qr.at[k], spread.peer(k))

    def share_copy(d, owner):
        return remote(
            sums.at[owner], sums.at[owner], ss.at[d - 1], sr.at[d - 1], (dp, (t + d) % 4)
        )

    def loop(body, first=0, last=n):
        def one(k, carry):
            body(k)
            return carry

        lax.fori_loop(first, last, one, 0)

    await_greetings(n, (1, 2, 3))

    def dispatch(k):
        is_first, is_second = spread.send(k, normed_ref)
        gate = jnp.sum(
            jnp.where(is_first, gate_ref[0:1, :], 0.0) + jnp.where(is_second, gate_ref[1:2, :], 0.0),
            axis=1,
            keepdims=True,
        )
        tile = jnp.broadcast_to(column_to_row(gate), (8, hp))

        @pl.when(k == 0)
        def _():
            gate_in[0, half] = tile

        @pl.when(k > 0)
        def _():
            gate_out[k] = tile
            gate_copy(k).start()
            peak_copy(k).start()

    loop(dispatch)
    fetch.wait()

    def chunk(k):
        gate = jnp.concatenate(
            [row_to_column(gate_in[k, 0, 0:1, :]), row_to_column(gate_in[k, 1, 0:1, :])], axis=0
        )
        gradient = upstream[k].astype(FULL)
        answer_grad = (gradient * gate).astype(LOW)
        pre = dot_plain(arrived[k], first_ref[...])
        share = 0.5 * (1.0 + lax.erf(pre * math.sqrt(0.5)))
        slope = share + pre * (jnp.exp(-0.5 * pre * pre) * (1.0 / math.sqrt(2.0 * math.pi)))
        hidden = (pre * share).astype(LOW)
        hidden_all[k] = hidden
        answer = dot_plain(hidden, second_ref[...])
        parts[k % 3, 0] = answer.astype(LOW)
        gate_sum = jnp.sum(answer * gradient, axis=1, keepdims=True)
        upstream[k] = answer_grad
        pre_grad = (dot_last(answer_grad, second_ref[...]) * slope).astype(LOW)
        pre_grad_all[k] = pre_grad
        parts[k % 3, 1] = dot_last(pre_grad, first_ref[...]).astype(LOW)
        tile = jnp.broadcast_to(column_to_row(gate_sum), (8, 2 * hp))

        @pl.when(k == 0)
        def _():
            sum_in[0] = tile

        @pl.when(k > 0)
        def _():
            sum_out[k] = tile
            sum_copy(k).start()

    def step(i):
        @pl.when(i < n)
        def _():
            spread.first_hop(i)

        @pl.when((i >= 1) & (i < n + 1))
        def _():
            k = i - 1
            spread.second_hop(k)

            @pl.when(k > 0)
            def _():
                gate_copy(k).wait_recv()

            gate_pair_copy(k, half).start()

        @pl.when((i >= 2) & (i < n + 2))
        def _():
            k = i - 2
            spread.last_hop(k)
            gate_pair_copy(k, 1 - half).wait_recv()

            @pl.when(k >= 3)
            def _():
                part_copy(k - 3).wait_send()

            chunk(k)
            part_copy(k).start()

        @pl.when((i >= 3) & (i < n + 3))
        def _():
            k = i - 3
            part_copy(k).wait_recv()

            @pl.when(k >= 3)
            def _():
                far_copy(k - 3).wait_send()

            for j in range(2):
                whole = parts[k % 3, j, spread.rows(half), :].astype(FULL) + pair_in[k, j].astype(FULL)
                low, high = whole[:, :width], whole[:, width:]
                kept[k % 3, j] = jnp.where(side == 0, low, high)
                far_out[k % 3, j] = jnp.where(side == 0, high, low).astype(LOW)
            far_copy(k).start()

        @pl.when(i >= 4)
        def _():
            k = i - 4
            far_copy(k).wait_recv()
            for j in range(2):
                rows = (kept[k % 3, j] + far_in[k, j].astype(FULL)).astype(LOW)

                @pl.when(k == 0)
                def _():
                    backs[j][0, spread.rows(half), :] = rows

                @pl.when(k > 0)
                def _():
                    final[j, k] = rows
                    return_copy(k, j).start()

    loop(step, 0, n + 4)

    tile = 256

    def grads(m):
        cols = pl.ds(pl.multiple_of(m * tile, tile), tile)
        rows_in = arrived[:, :, cols].reshape(n * 2 * hp, tile)
        grad_first_ref[cols, :] = dot_first(rows_in, pre_grad_all[...].reshape(n * 2 * hp, -1))
        hidden = hidden_all[:, :, cols].reshape(n * 2 * hp, tile)
        grad_second_ref[cols, :] = dot_first(hidden, upstream[...].reshape(n * 2 * hp, model))

    loop(grads, 0, model // tile)

    peaks[0] = peak_ref[...]

    def collect(k):
        for j in (1, 0):

            @pl.when(k > 0)
            def _():
                return_copy(k, j).wait_recv()

            mate_copy(k, j, half).start()

        @pl.when(k > 0)
        def _():
            peak_copy(k).wait_recv()
            sum_copy(k).wait_recv()

        sums[t, pl.ds(k, 1), :] = sum_in[k, 0:1, :]

    loop(collect)
    for d in (1, 2, 3):
        share_copy(d, t).start()
    top_ref[...] = jnp.max(peaks[...], axis=0)
    for d in (1, 2, 3):
        share_copy(d, (t + 4 - d) % 4).wait_recv()
    gate_sum_ref[...] = (sums[0] + sums[1]) + (sums[2] + sums[3])

    def finish(k):
        for j in range(2):
            mate_copy(k, j, 1 - half).wait_recv()
            mate_copy(k, j, half).wait_send()

            @pl.when(k > 0)
            def _():
                return_copy(k, j).wait_send()

        spread.sent(k)
        gate_pair_copy(k, half).wait_send()

        @pl.when(k > 0)
        def _():
            gate_copy(k).wait_send()
            sum_copy(k).wait_send()
            peak_copy(k).wait_send()

        @pl.when(k >= n - 3)
        def _():
            part_copy(k).wait_send()
            far_copy(k).wait_send()

    loop(finish)
    for d in (1, 2, 3):
        share_copy(d, t).wait_send()


def run_experts(n, hp, place, gates, normed, first, second, peak, upstream):
    model = normed.shape[1]
    width = model // 2
    hidden = first.shape[1]
    vmem = pl.BlockSpec(memory_space=VMEM)
    shape = jax.ShapeDtypeStruct
    return pl.pallas_call(
        functools.partial(expert_kernel, n, hp),
        out_shape=(
            shape((n, 2 * hp, width), LOW),
            shape((n, 2 * hp, width), LOW),
            shape((n, 2 * hp), FULL),
            shape((model, hidden), FULL),
            shape((hidden, model), FULL),
            shape(peak.shape, FULL),
        ),
        in_specs=[vmem] * 6 + [pl.BlockSpec(memory_space=pl.ANY)],
        out_specs=[vmem] * 6,
        scratch_shapes=[
            *Spread.scratch(n, hp, width),
            VMEM((n, 2 * hp, model), LOW),
            *Spread.semaphores(n),
            VMEM((n, 2 * hp, model), LOW),
            VMEM((n, 2 * hp, hidden), LOW),
            VMEM((n, 2 * hp, hidden), LOW),
            VMEM((3, 2, 2 * hp, model), LOW),
            VMEM((n, 2, hp, model), LOW),
            VMEM((3, 2, hp, width), FULL),
            VMEM((3, 2, hp, width), LOW),
            VMEM((n, 2, hp, width), LOW),
            VMEM((2, n, hp, width), LOW),
            VMEM((n, 8, hp), FULL),
            VMEM((n, 2, 8, hp), FULL),
            VMEM((n, 8, 2 * hp), FULL),
            VMEM((n, 8, 2 * hp), FULL),
            VMEM((4, n, 2 * hp), FULL),
            VMEM((n, *peak.shape), FULL),
            pltpu.SemaphoreType.DMA,
            dma(3), dma(n), dma(3), dma(n), dma(2, n), dma(2, n), dma(2, n), dma(2, n),
            dma(n), dma(n), dma(n), dma(n), dma(n), dma(n), dma(n), dma(n), dma(3), dma(3),
        ],
        compiler_params=pltpu.CompilerParams(
            collective_id=1, has_side_effects=True, vmem_limit_bytes=VMEM_LIMIT
        ),
        name="experts",
    )(place, gates, normed, first, second, peak, upstream)


def back_kernel(
    n,
    answer_ref,
    back_ref,
    gate_sum_ref,
    index_ref,
    residual_ref,
    upstream_ref,
    normed_one_ref,
    query_ref,
    key_ref,
    value_ref,
    mixed_ref,
    tokens_ref,
    gain_one_ref,
    gain_two_ref,
    query_w_ref,
    key_w_ref,
    value_w_ref,
    output_w_ref,
    router_ref,
    block_ref,
    grad_tokens_ref,
    weights_ref,
    small_ref,
    *scratch,
):
    dp, t, half, side, mate, far = places()
    (
        moe_mine,
        moe_other,
        block_mine,
        block_other,
        attention_grad,
        residual_grad,
        query_grad,
        key_grad,
        value_grad,
        gain_two_sum,
        gain_one_sum,
        gain_one_all,
        router_sum,
        router_in,
        gain_two_in,
        totals,
        pieces,
        pieces_in,
        as_,
        ar,
        bs,
        br,
        ts,
        tr,
        cs,
        cr,
        gs,
        gr,
        ws,
        wr,
        ls,
        lr,
        os_,
        or_,
    ) = scratch[:34]
    total = Total(*scratch[34:])
    heads = query_w_ref.shape[1] // HD
    model = tokens_ref.shape[1]
    width = model // 2
    slots = answer_ref.shape[0]
    piece = pieces.shape[1]
    greet(n, dp, t, [(t + d) % 4 for d in (1, 2, 3)])

    def moe_copy(j):
        return remote(moe_mine.at[j], moe_other.at[j], as_.at[j], ar.at[j], (dp, far))

    def block_copy(j):
        return remote(block_mine.at[j], block_other.at[j], bs.at[j], br.at[j], (dp, far))

    def attention_copy(j, owner):
        rows = attention_grad.at[image_rows(2 * j + owner)]
        return remote(rows, rows, ts.at[j], tr.at[j], (dp, mate))

    def tokens_copy(j, owner):
        rows = grad_tokens_ref.at[image_rows(2 * j + owner)]
        return remote(rows, rows, cs.at[j], cr.at[j], (dp, mate))

    def block_pair_copy(j, owner):
        rows = block_ref.at[image_rows(2 * j + owner)]
        return remote(rows, rows, ls.at[j], lr.at[j], (dp, mate))

    def gain_copy(d, owner):
        return remote(
            gain_one_all.at[owner], gain_one_all.at[owner], gs.at[d - 1], gr.at[d - 1], (dp, (t + d) % 4)
        )

    def router_copy():
        return remote(router_sum, router_in, os_.at[0], or_.at[0], (dp, mate))

    def gain_two_copy():
        return remote(gain_two_sum, gain_two_in, os_.at[1], or_.at[1], (dp, mate))

    def piece_copy(k):
        return remote(
            pieces.at[k], pieces_in.at[k], ws.at[k], wr.at[k], (partner(dp, k, n), t)
        )

    def loop(body, first, last):
        def one(k, carry):
            body(k)
            return carry

        lax.fori_loop(first, last, one, 0)

    def both_sides(mine, other):
        low = jnp.where(side == 0, mine, other)
        high = jnp.where(side == 0, other, mine)
        return jnp.concatenate([low, high], axis=1)

    def hots(rows):
        columns = lax.broadcasted_iota(jnp.int32, (PIECE, slots), 1)
        return index_ref[rows, 0:1] == columns, index_ref[rows, 1:2] == columns

    def as_low(mask):
        return jnp.where(mask, 1.0, 0.0).astype(LOW)

    gain_two_sum[...] = jnp.zeros_like(gain_two_sum)
    gain_one_sum[...] = jnp.zeros_like(gain_one_sum)
    router_sum[...] = jnp.zeros_like(router_sum)
    await_greetings(n, (1, 2, 3))

    def combine(j):
        first, second = hots(image_rows(2 * j + half))
        moe_mine[j] = dot_plain(as_low(first | second), back_ref[...]).astype(LOW)
        moe_copy(j).start()

    loop(combine, 0, 3)

    def gates_of(rows, normed):
        logits = dot_plain(normed, router_ref[...])
        lanes = lax.broadcasted_iota(jnp.int32, logits.shape, 1)
        hot_one = index_ref[rows, 2:3] == lanes
        hot_two = index_ref[rows, 3:4] == lanes
        one = jnp.sum(jnp.where(hot_one, logits, 0.0), axis=1, keepdims=True)
        two = jnp.sum(jnp.where(hot_two, logits, 0.0), axis=1, keepdims=True)
        top = jnp.maximum(one, two)
        one, two = jnp.exp(one - top), jnp.exp(two - top)
        return one / (one + two), two / (one + two), hot_one, hot_two

    def moe_back(j):
        rows = image_rows(2 * j + half)
        unit, factor = normalized(residual_ref[rows, :])
        normed = (unit * gain_two_ref[...]).astype(LOW)
        gate_one, gate_two, hot_one, hot_two = gates_of(rows, normed)
        first, second = hots(rows)
        slot_sums = gate_sum_ref[0:1, :]
        grad_one = jnp.sum(jnp.where(first, slot_sums, 0.0), axis=1, keepdims=True)
        grad_two = jnp.sum(jnp.where(second, slot_sums, 0.0), axis=1, keepdims=True)
        mean = gate_one * grad_one + gate_two * grad_two
        logit_grad = jnp.where(hot_one, gate_one * (grad_one - mean), 0.0)
        logit_grad = logit_grad + jnp.where(hot_two, gate_two * (grad_two - mean), 0.0)
        logit_grad = logit_grad.astype(LOW)
        router_sum[...] += dot_first(normed, logit_grad)
        normed_grad = dot_last(logit_grad, router_ref[...])
        moe_copy(j).wait_recv()
        normed_grad = normed_grad + both_sides(moe_mine[j].astype(FULL), moe_other[j].astype(FULL))
        gain_two_sum[...] += jnp.sum((normed_grad * unit).reshape(PIECE // 8, 8, model), axis=0)
        grad = normalized_back(normed_grad * gain_two_ref[...], unit, factor)
        grad = grad + upstream_ref[rows, :].astype(FULL)
        residual_grad[j] = grad
        attention_grad[rows, :] = grad.astype(LOW)
        attention_copy(j, half).start()

    loop(moe_back, 0, 3)
    router_copy().start()
    gain_two_copy().start()

    def image_back(image):
        rows = image_rows(image)
        mixed_grad = dot_last(attention_grad[rows, :], output_w_ref[...]).astype(LOW)
        queries, keys, values = query_ref[rows, :], key_ref[rows, :], value_ref[rows, :]
        query_parts, key_parts, value_parts = [], [], []
        for h in range(heads):
            cols = slice(h * HD, (h + 1) * HD)
            probs, _ = attention_probs(queries[:, cols], keys[:, cols])
            value_parts.append(dot_first(probs.astype(LOW), mixed_grad[:, cols]))
            probs_grad = dot_last(mixed_grad[:, cols], values[:, cols])
            level = jnp.sum(probs * probs_grad, axis=1, keepdims=True)
            score_grad = (probs * (probs_grad - level)).astype(LOW)
            query_parts.append(dot_plain(score_grad, keys[:, cols]) * HD**-0.5)
            key_parts.append(dot_first(score_grad, queries[:, cols]) * HD**-0.5)
        grads = [jnp.concatenate(p, axis=1).astype(LOW) for p in (query_parts, key_parts, value_parts)]
        query_grad[rows, :], key_grad[rows, :], value_grad[rows, :] = grads
        part = dot_last(grads[0], query_w_ref[...])
        part = part + dot_last(grads[1], key_w_ref[...])
        part = part + dot_last(grads[2], value_w_ref[...])
        unit, _ = normalized(tokens_ref[rows, :].astype(FULL))
        gain_one_sum[...] += jnp.sum((part * unit).reshape(PIECE // 8, 8, model), axis=0)
        return part

    def block_rows(j):
        rows = image_rows(2 * j + half)
        residual = residual_ref[rows, :]
        unit, _ = normalized(residual)
        gate_one, gate_two, _, _ = gates_of(rows, (unit * gain_two_ref[...]).astype(LOW))
        first, second = hots(rows)
        from_first = dot_plain(as_low(first), answer_ref[...])
        from_second = dot_plain(as_low(second), answer_ref[...])
        mine = jnp.where(side == 0, residual[:, :width], residual[:, width:])
        block_mine[j] = (mine + (gate_one * from_first + gate_two * from_second)).astype(LOW)
        block_copy(j).start()

    def attention_back(j):
        attention_copy(j, 1 - half).wait_recv()
        total.give(j, image_back(2 * j + 1 - half))
        total.take(j, image_back(2 * j + half))
        block_rows(j)

    loop(attention_back, 0, 3)

    gain_one_all[t] = gain_one_sum[...]
    for d in (1, 2, 3):
        gain_copy(d, t).start()
    normed_one = normed_one_ref[...]
    totals[:, :model] = jnp.concatenate(
        [
            dot_first(normed_one, query_grad[...]),
            dot_first(normed_one, key_grad[...]),
            dot_first(normed_one, value_grad[...]),
            dot_first(attention_grad[...], mixed_ref[...]),
        ],
        axis=1,
    )
    router_copy().wait_recv()
    gain_two_copy().wait_recv()
    for d in (1, 2, 3):
        gain_copy(d, (t + 4 - d) % 4).wait_recv()
    lanes = lax.broadcasted_iota(jnp.int32, (model, 128), 1)

    def column_of(eight):
        row = jnp.sum(eight, axis=0, keepdims=True)
        return jnp.concatenate(
            [row_to_column(row[:, i : i + 256]) for i in range(0, model, 256)], axis=0
        )

    gain_one_total = (gain_one_all[0] + gain_one_all[1]) + (gain_one_all[2] + gain_one_all[3])
    totals[:, model:] = (
        router_sum[...]
        + router_in[...]
        + jnp.where(lanes == 126, column_of(gain_one_total), 0.0)
        + jnp.where(lanes == 127, column_of(gain_two_sum[...] + gain_two_in[...]), 0.0)
    )

    def send_piece(k):
        at = partner(dp, k, n) * piece
        grain = math.gcd(piece, 8)
        span = -(-(piece + 8 - grain) // 8) * 8
        taken = totals[pl.ds(pl.multiple_of(at // 8 * 8, 8), span), :]
        rows = taken[:piece]
        for shift in range(grain, 8, grain):
            rows = jnp.where(at % 8 == shift, taken[shift : shift + piece], rows)
        pieces[k] = rows.astype(LOW)

        @pl.when(k > 0)
        def _():
            piece_copy(k).start()

    loop(send_piece, 0, n)

    def tokens_back(j):
        rows = image_rows(2 * j + half)
        normed_grad = total.result(j)
        unit, factor = normalized(tokens_ref[rows, :].astype(FULL))
        grad = normalized_back(normed_grad * gain_one_ref[...], unit, factor)
        grad_tokens_ref[rows, :] = (residual_grad[j] + grad).astype(LOW)
        tokens_copy(j, half).start()
        block_copy(j).wait_recv()
        block_ref[rows, :] = both_sides(block_mine[j], block_other[j])
        block_pair_copy(j, half).start()

    loop(tokens_back, 0, 3)
    pieces_in[0] = pieces[0]

    def arrive(k):
        piece_copy(k).wait_recv()

    loop(arrive, 1, n)
    whole = jnp.sum(pieces_in[...].astype(FULL), axis=0)
    weights_ref[...] = whole[:, :model]
    small_ref[...] = whole[:, model:]

    for j in range(3):
        moe_copy(j).wait_send()
        block_copy(j).wait_send()
        attention_copy(j, half).wait_send()
        total.sent(j)
        tokens_copy(j, half).wait_send()
        tokens_copy(j, 1 - half).wait_recv()
        block_pair_copy(j, half).wait_send()
        block_pair_copy(j, 1 - half).wait_recv()
        gain_copy(j + 1, t).wait_send()
    router_copy().wait_send()
    gain_two_copy().wait_send()

    def left(k):
        piece_copy(k).wait_send()

    loop(left, 1, n)


def run_back(n, *operands):
    tokens = operands[11]
    rows, model = tokens.shape
    heads_width = operands[7].shape[1]
    width = model // 2
    piece = model // n
    vmem = pl.BlockSpec(memory_space=VMEM)
    shape = jax.ShapeDtypeStruct
    slim = VMEM((3, PIECE, width), LOW)
    heads = VMEM((rows, heads_width), LOW)
    eight = VMEM((8, model), FULL)
    return pl.pallas_call(
        functools.partial(back_kernel, n),
        out_shape=(
            shape((rows, model), LOW),
            shape((rows, model), LOW),
            shape((piece, model), FULL),
            shape((piece, 128), FULL),
        ),
        in_specs=[vmem] * len(operands),
        out_specs=[vmem] * 4,
        scratch_shapes=[
            slim, slim, slim, slim,
            VMEM((rows, model), LOW),
            VMEM((3, PIECE, model), FULL),
            heads, heads, heads,
            eight, eight,
            VMEM((4, 8, model), FULL),
            VMEM((model, 128), FULL),
            VMEM((model, 128), FULL),
            eight,
            VMEM((model, model + 128), FULL),
            VMEM((n, piece, model + 128), LOW),
            VMEM((n, piece, model + 128), LOW),
            dma(3), dma(3), dma(3), dma(3), dma(3), dma(3), dma(3), dma(3), dma(3), dma(3),
            dma(n), dma(n), dma(3), dma(3), dma(2), dma(2),
            *Total.scratch(model),
        ],
        compiler_params=pltpu.CompilerParams(
            collective_id=2, has_side_effects=True, vmem_limit_bytes=VMEM_LIMIT
        ),
        name="back",
    )(*operands)


def body(
    tokens,
    gain_attn,
    w_query,
    w_key,
    w_value,
    w_output,
    gain_moe,
    w_router,
    expert_in,
    expert_out,
    routes,
    slot_ids,
    capacity,
    threshold,
    cotangent,
):
    n = lax.axis_size("dp")
    row_count, model = tokens.shape
    images = row_count // SEQ
    heads_here = w_query.shape[1] // HD
    slot_count = 23 * TOK_DEV // (10 * n) + 1
    per_half = -(-slot_count // 2)
    hp = -(-per_half // 16) * 16
    dp_here = lax.axis_index("dp")
    half_here = lax.axis_index("tensor") % 2

    def padded(rows, fill=0):
        split = rows.reshape(images, SEQ, -1)
        split = jnp.pad(split, ((0, 0), (0, PIECE - SEQ), (0, 0)), constant_values=fill)
        return split.reshape(images * PIECE, -1)

    def unpadded(rows):
        return rows.reshape(images, PIECE, -1)[:, :SEQ].reshape(row_count, -1)

    expert_ids = jnp.arange(n, dtype=jnp.int32)
    limits = jnp.sum(
        jnp.where(routes[:, :, None] == expert_ids, capacity[None, None, :], 0), axis=-1
    )
    kept = slot_ids < limits
    step = jnp.bitwise_xor(routes, dp_here)
    slot_half = slot_ids // per_half
    in_half = slot_ids % per_half
    place = jnp.where(kept & (slot_half == half_here), step * hp + in_half, -1)
    position = jnp.where(kept, step * (2 * hp) + slot_half * hp + in_half, -1)
    index = padded(jnp.concatenate([position, routes, place], axis=1), -1)
    place_rows = jnp.pad(index[:, 4:6].T, ((0, 6), (0, 0)), constant_values=-1)
    route_rows = index[:, 2:4].T

    tokens_in = padded(tokens)
    upstream = padded(cotangent)
    gain_one = gain_attn.astype(FULL)[None]
    gain_two = gain_moe.astype(FULL)[None]
    weights = (w_query, w_key, w_value, w_output)
    normed_one, query, key, value, mixed, residual, normed_two, peak, spread = run_front(
        n, hp, tokens_in, upstream, place_rows, (gain_one, gain_two), weights
    )
    logit_rows = lax.dot_general(
        w_router, normed_two, (((0,), (1,)), ((), ())), preferred_element_type=FULL
    )
    chosen = jnp.stack(
        [jnp.sum(jnp.where(expert_ids[:, None] == route_rows[k], logit_rows, 0.0), axis=0) for k in (0, 1)]
    )
    gate_rows = jnp.pad(jax.nn.softmax(chosen, axis=0), ((0, 6), (0, 0)))
    answers, back, gate_sums, grad_first, grad_second, top = run_experts(
        n, hp, place_rows, gate_rows, normed_two, expert_in[0], expert_out[0], peak, spread
    )
    router_wide = jnp.pad(w_router, ((0, 0), (0, 128 - n)))
    block_rows, token_rows, weight_grads, small = run_back(
        n,
        answers.reshape(n * 2 * hp, -1),
        back.reshape(n * 2 * hp, -1),
        jnp.broadcast_to(gate_sums.reshape(1, -1), (8, n * 2 * hp)),
        index,
        residual,
        upstream,
        normed_one,
        query,
        key,
        value,
        mixed,
        tokens_in,
        gain_one,
        gain_two,
        *weights,
        router_wide,
    )
    head_max = top[:heads_here, 0]
    column_factor = jnp.repeat(jnp.sqrt(jnp.minimum(1.0, threshold / head_max)), HD)[None, :]
    wide = w_query.shape[1]
    return (
        unpadded(block_rows),
        unpadded(token_rows),
        small[:, 126],
        small[:, 127],
        weight_grads[:, :wide],
        weight_grads[:, wide : 2 * wide],
        weight_grads[:, 2 * wide : 3 * wide],
        weight_grads[:, 3 * wide :].T,
        small[:, :n],
        grad_first[None],
        grad_second[None],
        w_query.astype(FULL) * column_factor,
        w_key.astype(FULL) * column_factor,
        head_max,
    )


def solution(mesh):
    in_specs = (
        P("dp", None),
        P(),
        P(None, "tensor"),
        P(None, "tensor"),
        P(None, "tensor"),
        P("tensor", None),
        P(),
        P(),
        P("dp", None, "tensor"),
        P("dp", "tensor", None),
        P("dp", None),
        P("dp", None),
        P(),
        P("tensor"),
        P("dp", None),
    )
    out_specs = (
        P("dp", None),
        P("dp", None),
        P("dp"),
        P("dp"),
        P("dp", "tensor"),
        P("dp", "tensor"),
        P("dp", "tensor"),
        P("tensor", "dp"),
        P("dp", None),
        P("dp", None, "tensor"),
        P("dp", "tensor", None),
        P(None, "tensor"),
        P(None, "tensor"),
        P("tensor"),
    )
    return jax.shard_map(body, mesh=mesh, in_specs=in_specs, out_specs=out_specs, check_vma=False)
```

```python
import functools
import math

import jax
import jax.numpy as jnp
from jax import lax
from jax.experimental import pallas as pl
from jax.experimental.pallas import tpu as pltpu
from jax.sharding import PartitionSpec as P

HD = 64
SEQ = 197
PIECE = 208
TOK_DEV = 1182
EPSILON = 1e-06
MESH = pl.DeviceIdType.MESH
VMEM_LIMIT = 60 * 2**20
VMEM = pltpu.VMEM
LOW, FULL = jnp.bfloat16, jnp.float32


def dot_plain(a, b):
    return jnp.dot(a, b, preferred_element_type=FULL)


def dot_last(a, b):
    return lax.dot_general(a, b, (((1,), (1,)), ((), ())), preferred_element_type=FULL)


def dot_first(a, b):
    return lax.dot_general(a, b, (((0,), (0,)), ((), ())), preferred_element_type=FULL)


def normalized(rows):
    centered = rows - jnp.mean(rows, axis=-1, keepdims=True)
    factor = lax.rsqrt(jnp.mean(centered * centered, axis=-1, keepdims=True) + EPSILON)
    return centered * factor, factor


def normalized_back(u, unit, factor):
    first = jnp.mean(u, axis=-1, keepdims=True)
    second = jnp.mean(u * unit, axis=-1, keepdims=True)
    return factor * (u - first - unit * second)


def same_index(size):
    rows = lax.broadcasted_iota(jnp.int32, (size, size), 0)
    return rows == lax.broadcasted_iota(jnp.int32, (size, size), 1)


def row_to_column(row):
    return jnp.sum(jnp.where(same_index(row.shape[1]), row, 0.0), axis=1, keepdims=True)


def column_to_row(column):
    return jnp.sum(jnp.where(same_index(column.shape[0]), column, 0.0), axis=0, keepdims=True)


def attention_probs(queries, keys):
    scores = dot_last(queries, keys) * HD**-0.5
    real = lax.broadcasted_iota(jnp.int32, scores.shape, 1) < SEQ
    scores = jnp.where(real, scores, -1e30)
    top = jnp.max(scores, axis=1, keepdims=True)
    powers = jnp.exp(scores - top)
    return powers * (1.0 / jnp.sum(powers, axis=1, keepdims=True)), top


def partner(dp, k, n):
    other, weight = 0, 1
    while weight < n:
        other = other + ((dp // weight + k // weight) % 2) * weight
        weight *= 2
    return other


def places():
    dp = lax.axis_index("dp")
    t = lax.axis_index("tensor")
    return dp, t, t % 2, t // 2, t + 1 - 2 * (t % 2), (t + 2) % 4


def remote(src, dst, sends, recvs, device):
    return pltpu.make_async_remote_copy(
        src_ref=src,
        dst_ref=dst,
        send_sem=sends,
        recv_sem=recvs,
        device_id=device,
        device_id_type=MESH,
    )


def signal(sem, device):
    pl.semaphore_signal(sem, inc=1, device_id=device, device_id_type=MESH)


def greet(n, dp, t, others):
    barrier = pltpu.get_barrier_semaphore()

    def one(k, carry):
        signal(barrier, (partner(dp, k, n), t))
        return carry

    lax.fori_loop(1, n, one, 0)
    for other in others:
        signal(barrier, (dp, other))


def await_greetings(n, others):
    pl.semaphore_wait(pltpu.get_barrier_semaphore(), n - 1 + len(others))


def image_rows(image):
    return pl.ds(pl.multiple_of(image * PIECE, PIECE), PIECE)


def dma(*shape):
    return pltpu.SemaphoreType.DMA(shape)


def near_count(n):
    return min(4, n)


class Spread:
    def __init__(self, n, hp, place, near_out, far_out, arrived, zs, zr, xs, xr, cs, cr, own):
        self.n, self.hp, self.near = n, hp, near_count(n)
        self.place, self.near_out, self.far_out, self.arrived = place, near_out, far_out, arrived
        self.zs, self.zr, self.xs, self.xr, self.cs, self.cr, self.own = zs, zr, xs, xr, cs, cr, own
        self.dp, self.t, self.half, self.side, self.mate, self.far = places()
        self.width = far_out.shape[2]

    def rows(self, owner):
        return pl.ds(pl.multiple_of(owner * self.hp, self.hp), self.hp)

    def columns(self, owner):
        return pl.ds(pl.multiple_of(owner * self.width, self.width), self.width)

    def peer(self, k):
        return (partner(self.dp, k, self.n), self.t)

    def own_copy(self):
        return pltpu.make_async_copy(
            self.near_out.at[0], self.arrived.at[0, self.rows(self.half)], self.own
        )

    def near_copy(self, k):
        return remote(
            self.near_out.at[k],
            self.arrived.at[k, self.rows(self.half)],
            self.zs.at[k],
            self.zr.at[k],
            self.peer(k),
        )

    def far_copy(self, k):
        return remote(
            self.far_out.at[k - self.near],
            self.arrived.at[k, self.rows(self.half), self.columns(self.side)],
            self.zs.at[k],
            self.zr.at[k],
            self.peer(k),
        )

    def side_copy(self, k, side):
        part = self.arrived.at[k, self.rows(self.half), self.columns(side)]
        return remote(part, part, self.xs.at[k], self.xr.at[k], (self.dp, self.far))

    def pair_copy(self, k, half):
        part = self.arrived.at[k, self.rows(half)]
        return remote(part, part, self.cs.at[k], self.cr.at[k], (self.dp, self.mate))

    def send(self, k, rows_ref):
        slots = lax.broadcasted_iota(jnp.int32, (self.hp, rows_ref.shape[0]), 0) + k * self.hp
        is_first = self.place[0:1, :] == slots
        is_second = self.place[1:2, :] == slots
        hot = jnp.where(is_first | is_second, 1.0, 0.0).astype(LOW)

        @pl.when(k < self.near)
        def _():
            self.near_out[k] = dot_plain(hot, rows_ref[...]).astype(LOW)

            @pl.when(k == 0)
            def _():
                self.own_copy().start()

            @pl.when(k > 0)
            def _():
                self.near_copy(k).start()

        @pl.when(k >= self.near)
        def _():
            mine = rows_ref[:, self.columns(self.side)]
            self.far_out[k - self.near] = dot_plain(hot, mine).astype(LOW)
            self.far_copy(k).start()

        return is_first, is_second

    def first_hop(self, k):
        @pl.when(k == 0)
        def _():
            self.own_copy().wait()

        @pl.when((k > 0) & (k < self.near))
        def _():
            self.near_copy(k).wait_recv()

        @pl.when(k >= self.near)
        def _():
            self.far_copy(k).wait_recv()
            self.side_copy(k, self.side).start()

    def second_hop(self, k):
        @pl.when(k >= self.near)
        def _():
            self.side_copy(k, 1 - self.side).wait_recv()

        self.pair_copy(k, self.half).start()

    def last_hop(self, k):
        self.pair_copy(k, 1 - self.half).wait_recv()

    def sent(self, k):
        @pl.when((k > 0) & (k < self.near))
        def _():
            self.near_copy(k).wait_send()

        @pl.when(k >= self.near)
        def _():
            self.far_copy(k).wait_send()
            self.side_copy(k, self.side).wait_send()

        self.pair_copy(k, self.half).wait_send()

    @staticmethod
    def scratch(n, hp, width):
        near = near_count(n)
        return [VMEM((near, hp, 2 * width), LOW), VMEM((n - near, hp, width), LOW)]

    @staticmethod
    def semaphores(n):
        return [dma(n), dma(n), dma(n), dma(n), dma(n), dma(n), pltpu.SemaphoreType.DMA]


class Total:
    def __init__(self, part_out, pair_in, far_out, far_in, ps, pr, fs, fr):
        self.part_out, self.pair_in, self.far_out, self.far_in = part_out, pair_in, far_out, far_in
        self.ps, self.pr, self.fs, self.fr = ps, pr, fs, fr
        self.dp, _, _, _, self.mate, self.far = places()

    def pair_copy(self, j):
        return remote(
            self.part_out.at[j], self.pair_in.at[j], self.ps.at[j], self.pr.at[j], (self.dp, self.mate)
        )

    def far_copy(self, j):
        return remote(
            self.far_out.at[j], self.far_in.at[j], self.fs.at[j], self.fr.at[j], (self.dp, self.far)
        )

    def give(self, j, rows):
        self.part_out[j] = rows
        self.pair_copy(j).start()

    def take(self, j, rows):
        self.pair_copy(j).wait_recv()
        self.far_out[j] = (rows + self.pair_in[j]).astype(LOW)
        self.far_copy(j).start()

    def result(self, j):
        self.far_copy(j).wait_recv()
        return self.far_out[j].astype(FULL) + self.far_in[j].astype(FULL)

    def sent(self, j):
        self.pair_copy(j).wait_send()
        self.far_copy(j).wait_send()

    @staticmethod
    def scratch(model):
        wide, slim = VMEM((3, PIECE, model), FULL), VMEM((3, PIECE, model), LOW)
        return [wide, wide, slim, slim, dma(3), dma(3), dma(3), dma(3)]


def front_kernel(
    n,
    hp,
    tokens_ref,
    upstream_ref,
    place_ref,
    gain_one_ref,
    gain_two_ref,
    query_w_ref,
    key_w_ref,
    value_w_ref,
    output_w_ref,
    normed_one_ref,
    query_ref,
    key_ref,
    value_ref,
    mixed_ref,
    residual_ref,
    normed_two_ref,
    peak_ref,
    spread_ref,
    *scratch,
):
    dp, t, half, side, mate, far = places()
    heads = query_w_ref.shape[1] // HD
    spread = Spread(n, hp, place_ref, *scratch[:2], spread_ref, *scratch[2:9])
    total = Total(*scratch[9:17])
    ns, nr = scratch[17:19]
    greet(n, dp, t, (mate, far))
    peak_ref[...] = jnp.full(peak_ref.shape, -1e30, FULL)

    def image_forward(image):
        rows = image_rows(image)
        unit, _ = normalized(tokens_ref[rows, :].astype(FULL))
        normed = (unit * gain_one_ref[...]).astype(LOW)
        normed_one_ref[rows, :] = normed
        queries = dot_plain(normed, query_w_ref[...]).astype(LOW)
        keys = dot_plain(normed, key_w_ref[...]).astype(LOW)
        values = dot_plain(normed, value_w_ref[...]).astype(LOW)
        query_ref[rows, :] = queries
        key_ref[rows, :] = keys
        value_ref[rows, :] = values
        mixed = []
        for h in range(heads):
            cols = slice(h * HD, (h + 1) * HD)
            probs, top = attention_probs(queries[:, cols], keys[:, cols])
            real = lax.broadcasted_iota(jnp.int32, top.shape, 0) < SEQ
            best = jnp.max(jnp.where(real, top, -1e30), axis=0, keepdims=True)
            peak_ref[h : h + 1, :] = jnp.maximum(peak_ref[h : h + 1, :], best)
            mixed.append(dot_plain(probs.astype(LOW), values[:, cols]))
        mixed = jnp.concatenate(mixed, axis=1).astype(LOW)
        mixed_ref[rows, :] = mixed
        return dot_plain(mixed, output_w_ref[...])

    def normed_copy(j, owner):
        rows = normed_two_ref.at[image_rows(2 * j + owner)]
        return remote(rows, rows, ns.at[j], nr.at[j], (dp, mate))

    def finish(j):
        rows = image_rows(2 * j + half)
        residual = tokens_ref[rows, :].astype(FULL) + total.result(j)
        residual_ref[rows, :] = residual
        unit, _ = normalized(residual)
        normed_two_ref[rows, :] = (unit * gain_two_ref[...]).astype(LOW)
        normed_copy(j, half).start()

    per_step = -(-n // 3)

    def step(j, carry):
        given = image_forward(2 * j + 1 - half)

        @pl.when(j == 0)
        def _():
            await_greetings(n, (mate, far))

        total.give(j, given)
        total.take(j, image_forward(2 * j + half))

        def dispatch(i, inner):
            @pl.when(i < n)
            def _():
                spread.send((i + spread.near) % n, upstream_ref)

            return inner

        lax.fori_loop(j * per_step, (j + 1) * per_step, dispatch, 0)

        @pl.when(j >= 1)
        def _():
            finish(j - 1)

        return carry

    lax.fori_loop(0, 3, step, 0)

    def each(body, first=0):
        def one(k, carry):
            body(k)
            return carry

        lax.fori_loop(first, n, one, 0)

    each(spread.first_hop)
    finish(2)
    each(spread.second_hop)
    each(spread.last_hop)
    each(spread.sent)
    for j in range(3):
        total.sent(j)
        normed_copy(j, half).wait_send()
        normed_copy(j, 1 - half).wait_recv()


def run_front(n, hp, tokens, upstream, place, gains, weights):
    rows, model = tokens.shape
    heads_width = weights[0].shape[1]
    vmem = pl.BlockSpec(memory_space=VMEM)
    shape = jax.ShapeDtypeStruct
    slim = shape((rows, heads_width), LOW)
    return pl.pallas_call(
        functools.partial(front_kernel, n, hp),
        out_shape=(
            shape((rows, model), LOW),
            slim,
            slim,
            slim,
            slim,
            shape((rows, model), FULL),
            shape((rows, model), LOW),
            shape((8, 128), FULL),
            shape((n, 2 * hp, model), LOW),
        ),
        in_specs=[vmem] * 9,
        out_specs=[vmem] * 9,
        scratch_shapes=[
            *Spread.scratch(n, hp, model // 2),
            *Spread.semaphores(n),
            *Total.scratch(model),
            dma(3),
            dma(3),
        ],
        compiler_params=pltpu.CompilerParams(
            collective_id=0, has_side_effects=True, vmem_limit_bytes=VMEM_LIMIT
        ),
        name="front",
    )(tokens, upstream, place, *gains, *weights)


def in_turn(i, near):
    return jnp.where(i < 2 * near, i // 2 + (i % 2) * near, i)


def expert_kernel(
    n,
    hp,
    place_ref,
    gate_ref,
    normed_ref,
    first_ref,
    second_ref,
    peak_ref,
    upstream_hbm,
    answer_out,
    answer_kept,
    back_ref,
    gate_sum_ref,
    grad_first_ref,
    grad_second_ref,
    top_ref,
    *scratch,
):
    dp, t, half, side, mate, far = places()
    arrived = scratch[2]
    spread = Spread(n, hp, place_ref, *scratch[:10])
    (
        upstream,
        hidden_all,
        pre_grad_all,
        parts,
        pair_in,
        kept,
        far_out,
        far_in,
        final,
        gate_out,
        gate_in,
        sum_out,
        sum_in,
        sums,
        peaks,
        us,
        ps,
        pr,
        fs,
        fr,
        rs,
        rr,
        ms,
        mr,
        gs,
        gr,
        hs,
        hr,
        ks,
        kr,
        qs,
        qr,
        ss,
        sr,
    ) = scratch[10:]
    model = normed_ref.shape[1]
    width = model // 2
    near = spread.near
    greet(n, dp, t, [(t + d) % 4 for d in (1, 2, 3)])
    fetch = pltpu.make_async_copy(upstream_hbm, upstream, us)
    fetch.start()

    def gate_copy(k):
        return remote(gate_out.at[k], gate_in.at[k, half], gs.at[k], gr.at[k], spread.peer(k))

    def gate_pair_copy(k, owner):
        tile = gate_in.at[k, owner]
        return remote(tile, tile, hs.at[k], hr.at[k], (dp, mate))

    def part_copy(i, k):
        return remote(
            parts.at[i % 3, :, spread.rows(1 - half)],
            pair_in.at[k],
            ps.at[i % 3],
            pr.at[k],
            (dp, mate),
        )

    def far_copy(i, k):
        return remote(far_out.at[i % 3], far_in.at[k], fs.at[i % 3], fr.at[k], (dp, far))

    def return_copy(k):
        return remote(
            final.at[k], back_ref.at[k, spread.rows(half)], rs.at[k], rr.at[k], spread.peer(k)
        )

    def mate_copy(k, owner):
        rows = back_ref.at[k, spread.rows(owner)]
        return remote(rows, rows, ms.at[k], mr.at[k], (dp, mate))

    def sum_copy(k):
        return remote(sum_out.at[k], sum_in.at[k], ks.at[k], kr.at[k], spread.peer(k))

    def peak_copy(k):
        return remote(peak_ref, peaks.at[k], qs.at[k], qr.at[k], spread.peer(k))

    def share_copy(d, owner):
        return remote(
            sums.at[owner], sums.at[owner], ss.at[d - 1], sr.at[d - 1], (dp, (t + d) % 4)
        )

    def loop(body, first=0, last=n):
        def one(k, carry):
            body(k)
            return carry

        lax.fori_loop(first, last, one, 0)

    await_greetings(n, (1, 2, 3))

    def dispatch(i):
        k = (i + near) % n
        is_first, is_second = spread.send(k, normed_ref)
        gate = jnp.sum(
            jnp.where(is_first, gate_ref[0:1, :], 0.0) + jnp.where(is_second, gate_ref[1:2, :], 0.0),
            axis=1,
            keepdims=True,
        )
        tile = jnp.broadcast_to(column_to_row(gate), (8, hp))

        @pl.when(k == 0)
        def _():
            gate_in[0, half] = tile

        @pl.when(k > 0)
        def _():
            gate_out[k] = tile
            gate_copy(k).start()

    loop(dispatch)
    fetch.wait()

    def chunk(i, k):
        gate = jnp.concatenate(
            [row_to_column(gate_in[k, 0, 0:1, :]), row_to_column(gate_in[k, 1, 0:1, :])], axis=0
        )
        gradient = upstream[k].astype(FULL)
        answer_grad = (gradient * gate).astype(LOW)
        pre = dot_plain(arrived[k], first_ref[...])
        share = 0.5 * (1.0 + lax.erf(pre * math.sqrt(0.5)))
        slope = share + pre * (jnp.exp(-0.5 * pre * pre) * (1.0 / math.sqrt(2.0 * math.pi)))
        hidden = (pre * share).astype(LOW)
        hidden_all[k] = hidden
        answer = dot_plain(hidden, second_ref[...])
        parts[i % 3, 0] = answer.astype(LOW)
        gate_sum = jnp.sum(answer * gradient, axis=1, keepdims=True)
        upstream[k] = answer_grad
        pre_grad = (dot_last(answer_grad, second_ref[...]) * slope).astype(LOW)
        pre_grad_all[k] = pre_grad
        parts[i % 3, 1] = dot_last(pre_grad, first_ref[...]).astype(LOW)
        tile = jnp.broadcast_to(column_to_row(gate_sum), (8, 2 * hp))

        @pl.when(k == 0)
        def _():
            sum_in[0] = tile

        @pl.when(k > 0)
        def _():
            sum_out[k] = tile
            sum_copy(k).start()
            peak_copy(k).start()

    def step(i):
        @pl.when(i < n)
        def _():
            spread.first_hop(in_turn(i, near))

        @pl.when((i >= 1) & (i < n + 1))
        def _():
            k = in_turn(i - 1, near)
            spread.second_hop(k)

            @pl.when(k > 0)
            def _():
                gate_copy(k).wait_recv()

            gate_pair_copy(k, half).start()

        @pl.when((i >= 2) & (i < n + 2))
        def _():
            k = in_turn(i - 2, near)
            spread.last_hop(k)
            gate_pair_copy(k, 1 - half).wait_recv()

            @pl.when(i >= 5)
            def _():
                part_copy(i - 5, in_turn(i - 5, near)).wait_send()

            chunk(i - 2, k)
            part_copy(i - 2, k).start()

        @pl.when((i >= 3) & (i < n + 3))
        def _():
            k = in_turn(i - 3, near)
            part_copy(i - 3, k).wait_recv()

            @pl.when(i >= 6)
            def _():
                far_copy(i - 6, in_turn(i - 6, near)).wait_send()

            for j in (1, 0):
                whole = parts[i % 3, j, spread.rows(half), :].astype(FULL) + pair_in[k, j].astype(FULL)
                low, high = whole[:, :width], whole[:, width:]
                stays = jnp.where(side == 0, low, high)
                goes = jnp.where(side == 0, high, low).astype(LOW)
                if j:
                    kept[i % 3] = stays
                    far_out[i % 3] = goes
                    far_copy(i - 3, k).start()
                else:
                    answer_kept[k] = stays
                    answer_out[k] = goes

        @pl.when(i >= 4)
        def _():
            k = in_turn(i - 4, near)
            far_copy(i - 4, k).wait_recv()
            rows = (kept[(i - 4) % 3] + far_in[k].astype(FULL)).astype(LOW)

            @pl.when(k == 0)
            def _():
                back_ref[0, spread.rows(half), :] = rows

            @pl.when(k > 0)
            def _():
                final[k] = rows
                return_copy(k).start()

    loop(step, 0, n + 4)

    tile = 256

    def grads(m):
        cols = pl.ds(pl.multiple_of(m * tile, tile), tile)
        rows_in = arrived[:, :, cols].reshape(n * 2 * hp, tile)
        grad_first_ref[cols, :] = dot_first(rows_in, pre_grad_all[...].reshape(n * 2 * hp, -1))
        hidden = hidden_all[:, :, cols].reshape(n * 2 * hp, tile)
        grad_second_ref[cols, :] = dot_first(hidden, upstream[...].reshape(n * 2 * hp, model))

    loop(grads, 0, model // tile)

    peaks[0] = peak_ref[...]

    def collect_sums(k):
        @pl.when(k > 0)
        def _():
            peak_copy(k).wait_recv()
            sum_copy(k).wait_recv()

        sums[t, pl.ds(k, 1), :] = sum_in[k, 0:1, :]

    loop(collect_sums)
    for d in (1, 2, 3):
        share_copy(d, t).start()
    top_ref[...] = jnp.max(peaks[...], axis=0)

    def collect(i):
        k = in_turn(i, near)

        @pl.when(k > 0)
        def _():
            return_copy(k).wait_recv()

        mate_copy(k, half).start()

    loop(collect)
    for d in (1, 2, 3):
        share_copy(d, (t + 4 - d) % 4).wait_recv()
    gate_sum_ref[...] = (sums[0] + sums[1]) + (sums[2] + sums[3])

    def finish(i):
        k = in_turn(i, near)
        mate_copy(k, 1 - half).wait_recv()
        mate_copy(k, half).wait_send()
        spread.sent(k)
        gate_pair_copy(k, half).wait_send()

        @pl.when(k > 0)
        def _():
            return_copy(k).wait_send()
            gate_copy(k).wait_send()
            sum_copy(k).wait_send()
            peak_copy(k).wait_send()

        @pl.when(i >= n - 3)
        def _():
            part_copy(i, k).wait_send()
            far_copy(i, k).wait_send()

    loop(finish)
    for d in (1, 2, 3):
        share_copy(d, t).wait_send()


def run_experts(n, hp, place, gates, normed, first, second, peak, upstream):
    model = normed.shape[1]
    width = model // 2
    hidden = first.shape[1]
    vmem = pl.BlockSpec(memory_space=VMEM)
    shape = jax.ShapeDtypeStruct
    return pl.pallas_call(
        functools.partial(expert_kernel, n, hp),
        out_shape=(
            shape((n, hp, width), LOW),
            shape((n, hp, width), FULL),
            shape((n, 2 * hp, width), LOW),
            shape((n, 2 * hp), FULL),
            shape((model, hidden), FULL),
            shape((hidden, model), FULL),
            shape(peak.shape, FULL),
        ),
        in_specs=[vmem] * 6 + [pl.BlockSpec(memory_space=pl.ANY)],
        out_specs=[vmem] * 7,
        scratch_shapes=[
            *Spread.scratch(n, hp, width),
            VMEM((n, 2 * hp, model), LOW),
            *Spread.semaphores(n),
            VMEM((n, 2 * hp, model), LOW),
            VMEM((n, 2 * hp, hidden), LOW),
            VMEM((n, 2 * hp, hidden), LOW),
            VMEM((3, 2, 2 * hp, model), LOW),
            VMEM((n, 2, hp, model), LOW),
            VMEM((3, hp, width), FULL),
            VMEM((3, hp, width), LOW),
            VMEM((n, hp, width), LOW),
            VMEM((n, hp, width), LOW),
            VMEM((n, 8, hp), FULL),
            VMEM((n, 2, 8, hp), FULL),
            VMEM((n, 8, 2 * hp), FULL),
            VMEM((n, 8, 2 * hp), FULL),
            VMEM((4, n, 2 * hp), FULL),
            VMEM((n, *peak.shape), FULL),
            pltpu.SemaphoreType.DMA,
            dma(3), dma(n), dma(3), dma(n), dma(n), dma(n), dma(n), dma(n),
            dma(n), dma(n), dma(n), dma(n), dma(n), dma(n), dma(n), dma(n), dma(3), dma(3),
        ],
        compiler_params=pltpu.CompilerParams(
            collective_id=1, has_side_effects=True, vmem_limit_bytes=VMEM_LIMIT
        ),
        name="experts",
    )(place, gates, normed, first, second, peak, upstream)


def back_kernel(
    n,
    hp,
    back_ref,
    gate_sum_ref,
    index_ref,
    residual_ref,
    upstream_ref,
    gain_one_ref,
    gain_two_ref,
    output_w_ref,
    router_ref,
    answer_out,
    *refs,
):
    later, outs, scratch = refs[:10], refs[10:15], refs[15:]
    block_ref, grad_tokens_ref, weights_ref, small_ref, gain_ref = outs
    held, scratch = scratch[:10], scratch[10:]
    (
        answer_kept,
        normed_one_ref,
        query_ref,
        key_ref,
        value_ref,
        mixed_ref,
        tokens_ref,
        query_w_ref,
        key_w_ref,
        value_w_ref,
    ) = held
    dp, t, half, side, mate, far = places()
    (
        moe_mine,
        moe_other,
        block_mine,
        block_other,
        attention_grad,
        residual_grad,
        query_grad,
        key_grad,
        value_grad,
        gain_two_sum,
        gain_two_in,
        gain_one_sum,
        gain_one_all,
        gain_rows,
        router_sum,
        router_in,
        totals,
        totals_two,
        pieces,
        pieces_in,
        small_pieces,
        small_in,
        answer_far,
        answer_final,
        answers,
        hs,
        as_,
        ar,
        bs,
        br,
        ts,
        tr,
        cs,
        cr,
        gs,
        gr,
        ws,
        wr,
        ls,
        lr,
        os_,
        or_,
        vs,
        vr,
        ds,
        dr,
        es,
        er,
        fs,
        fr,
        ks,
        kr,
    ) = scratch[:52]
    total = Total(*scratch[52:])
    heads = query_w_ref.shape[1] // HD
    model = upstream_ref.shape[1]
    width = model // 2
    slots = back_ref.shape[0]
    piece = pieces.shape[1]
    near = near_count(n)
    greet(n, dp, t, [(t + d) % 4 for d in (1, 2, 3)])
    fetches = [pltpu.make_async_copy(a, b, hs.at[i]) for i, (a, b) in enumerate(zip(later, held))]
    for fetch in fetches:
        fetch.start()

    def peer(k):
        return (partner(dp, k, n), t)

    def moe_copy(j):
        return remote(moe_mine.at[j], moe_other.at[j], as_.at[j], ar.at[j], (dp, far))

    def block_copy(j):
        return remote(block_mine.at[j], block_other.at[j], bs.at[j], br.at[j], (dp, far))

    def attention_copy(j, owner):
        rows = attention_grad.at[image_rows(2 * j + owner)]
        return remote(rows, rows, ts.at[j], tr.at[j], (dp, mate))

    def tokens_copy(j, owner):
        rows = grad_tokens_ref.at[image_rows(2 * j + owner)]
        return remote(rows, rows, cs.at[j], cr.at[j], (dp, mate))

    def block_pair_copy(j, owner):
        rows = block_ref.at[image_rows(2 * j + owner)]
        return remote(rows, rows, ls.at[j], lr.at[j], (dp, mate))

    def gain_copy(d, owner):
        return remote(
            gain_one_all.at[owner], gain_one_all.at[owner], gs.at[d - 1], gr.at[d - 1], (dp, (t + d) % 4)
        )

    def gain_row_copy(k):
        return remote(gain_rows.at[0], gain_rows.at[k], ks.at[k], kr.at[k], peer(k))

    def router_copy():
        return remote(router_sum, router_in, os_.at[0], or_.at[0], (dp, mate))

    def gain_two_copy():
        return remote(gain_two_sum, gain_two_in, os_.at[1], or_.at[1], (dp, mate))

    def piece_copy(k):
        return remote(pieces.at[k], pieces_in.at[k], ws.at[k], wr.at[k], peer(k))

    def small_copy(k):
        return remote(small_pieces.at[k], small_in.at[k], vs.at[k], vr.at[k], peer(k))

    def answer_rows(k, owner):
        return answers.at[pl.ds(pl.multiple_of((2 * k + owner) * hp, hp), hp)]

    def answer_side_copy(k):
        return remote(answer_out.at[k], answer_far.at[k], ds.at[k], dr.at[k], (dp, far))

    def answer_copy(k):
        return remote(answer_final.at[k], answer_rows(k, half), es.at[k], er.at[k], peer(k))

    def answer_pair_copy(k, owner):
        return remote(answer_rows(k, owner), answer_rows(k, owner), fs.at[k], fr.at[k], (dp, mate))

    def loop(body, first=0, last=n):
        def one(k, carry):
            body(k)
            return carry

        lax.fori_loop(first, last, one, 0)

    def both_sides(mine, other):
        low = jnp.where(side == 0, mine, other)
        high = jnp.where(side == 0, other, mine)
        return jnp.concatenate([low, high], axis=1)

    def hots(rows):
        columns = lax.broadcasted_iota(jnp.int32, (PIECE, slots), 1)
        return index_ref[rows, 0:1] == columns, index_ref[rows, 1:2] == columns

    def as_low(mask):
        return jnp.where(mask, 1.0, 0.0).astype(LOW)

    gain_two_sum[...] = jnp.zeros_like(gain_two_sum)
    gain_one_sum[...] = jnp.zeros_like(gain_one_sum)
    router_sum[...] = jnp.zeros_like(router_sum)

    def combine(j):
        first, second = hots(image_rows(2 * j + half))
        moe_mine[j] = dot_plain(as_low(first | second), back_ref[...]).astype(LOW)

        @pl.when(j == 0)
        def _():
            await_greetings(n, (1, 2, 3))

        moe_copy(j).start()

    loop(combine, 0, 3)
    loop(lambda k: answer_side_copy((k + near) % n).start())

    def gates_of(rows, normed):
        logits = dot_plain(normed, router_ref[...])
        lanes = lax.broadcasted_iota(jnp.int32, logits.shape, 1)
        hot_one = index_ref[rows, 2:3] == lanes
        hot_two = index_ref[rows, 3:4] == lanes
        one = jnp.sum(jnp.where(hot_one, logits, 0.0), axis=1, keepdims=True)
        two = jnp.sum(jnp.where(hot_two, logits, 0.0), axis=1, keepdims=True)
        top = jnp.maximum(one, two)
        one, two = jnp.exp(one - top), jnp.exp(two - top)
        return one / (one + two), two / (one + two), hot_one, hot_two

    def moe_back(j):
        rows = image_rows(2 * j + half)
        unit, factor = normalized(residual_ref[rows, :])
        normed = (unit * gain_two_ref[...]).astype(LOW)
        gate_one, gate_two, hot_one, hot_two = gates_of(rows, normed)
        first, second = hots(rows)
        slot_sums = gate_sum_ref[0:1, :]
        grad_one = jnp.sum(jnp.where(first, slot_sums, 0.0), axis=1, keepdims=True)
        grad_two = jnp.sum(jnp.where(second, slot_sums, 0.0), axis=1, keepdims=True)
        mean = gate_one * grad_one + gate_two * grad_two
        logit_grad = jnp.where(hot_one, gate_one * (grad_one - mean), 0.0)
        logit_grad = logit_grad + jnp.where(hot_two, gate_two * (grad_two - mean), 0.0)
        logit_grad = logit_grad.astype(LOW)
        router_sum[...] += dot_first(normed, logit_grad)
        normed_grad = dot_last(logit_grad, router_ref[...])
        moe_copy(j).wait_recv()
        normed_grad = normed_grad + both_sides(moe_mine[j].astype(FULL), moe_other[j].astype(FULL))
        gain_two_sum[...] += jnp.sum((normed_grad * unit).reshape(PIECE // 8, 8, model), axis=0)
        grad = normalized_back(normed_grad * gain_two_ref[...], unit, factor)
        grad = grad + upstream_ref[rows, :].astype(FULL)
        residual_grad[j] = grad
        attention_grad[rows, :] = grad.astype(LOW)
        attention_copy(j, half).start()

    loop(moe_back, 0, 3)
    router_copy().start()
    gain_two_copy().start()
    for fetch in fetches:
        fetch.wait()

    def image_back(image):
        rows = image_rows(image)
        mixed_grad = dot_last(attention_grad[rows, :], output_w_ref[...]).astype(LOW)
        queries, keys, values = query_ref[rows, :], key_ref[rows, :], value_ref[rows, :]
        query_parts, key_parts, value_parts = [], [], []
        for h in range(heads):
            cols = slice(h * HD, (h + 1) * HD)
            probs, _ = attention_probs(queries[:, cols], keys[:, cols])
            value_parts.append(dot_first(probs.astype(LOW), mixed_grad[:, cols]))
            probs_grad = dot_last(mixed_grad[:, cols], values[:, cols])
            level = jnp.sum(probs * probs_grad, axis=1, keepdims=True)
            score_grad = (probs * (probs_grad - level)).astype(LOW)
            query_parts.append(dot_plain(score_grad, keys[:, cols]) * HD**-0.5)
            key_parts.append(dot_first(score_grad, queries[:, cols]) * HD**-0.5)
        grads = [jnp.concatenate(p, axis=1).astype(LOW) for p in (query_parts, key_parts, value_parts)]
        query_grad[rows, :], key_grad[rows, :], value_grad[rows, :] = grads

    def answer_turn(k):
        answer_side_copy(k).wait_recv()
        rows = (answer_kept[k] + answer_far[k].astype(FULL)).astype(LOW)

        @pl.when(k == 0)
        def _():
            answer_rows(0, half)[...] = rows

        @pl.when(k > 0)
        def _():
            answer_final[k] = rows
            answer_copy(k).start()

    per_image = -(-n // 4)

    def attention_back(i):
        j = i % 3

        @pl.when(i >= 3)
        def _():
            attention_copy(j, 1 - half).wait_recv()

        image_back(2 * j + jnp.where(i < 3, half, 1 - half))

        def turn(m):
            @pl.when(m < n)
            def _():
                answer_turn((m + near) % n)

        @pl.when(i >= 2)
        def _():
            loop(turn, (i - 2) * per_image, (i - 1) * per_image)

    loop(attention_back, 0, 6)

    normed_one = normed_one_ref[...]
    totals[:, : 3 * query_grad.shape[1]] = jnp.concatenate(
        [
            dot_first(normed_one, query_grad[...]),
            dot_first(normed_one, key_grad[...]),
            dot_first(normed_one, value_grad[...]),
        ],
        axis=1,
    )

    def my_piece(source, k):
        at = partner(dp, k, n) * piece
        grain = math.gcd(piece, 8)
        span = -(-(piece + 8 - grain) // 8) * 8
        taken = source[pl.ds(pl.multiple_of(at // 8 * 8, 8), span), :]
        rows = taken[:piece]
        for shift in range(grain, 8, grain):
            rows = jnp.where(at % 8 == shift, taken[shift : shift + piece], rows)
        return rows.astype(LOW)

    def send_piece(i):
        k = (i + near) % n
        pieces[k] = my_piece(totals, k)

        @pl.when(k > 0)
        def _():
            piece_copy(k).start()

    loop(send_piece)

    def grad_part(image):
        rows = image_rows(image)
        part = dot_last(query_grad[rows, :], query_w_ref[...])
        part = part + dot_last(key_grad[rows, :], key_w_ref[...])
        part = part + dot_last(value_grad[rows, :], value_w_ref[...])
        unit, _ = normalized(tokens_ref[rows, :].astype(FULL))
        gain_one_sum[...] += jnp.sum((part * unit).reshape(PIECE // 8, 8, model), axis=0)
        return part

    def sum_images(j):
        total.give(j, grad_part(2 * j + 1 - half))
        total.take(j, grad_part(2 * j + half))

    loop(sum_images, 0, 3)
    gain_one_all[t] = gain_one_sum[...]
    for d in (1, 2, 3):
        gain_copy(d, t).start()

    router_copy().wait_recv()
    gain_two_copy().wait_recv()
    lanes = lax.broadcasted_iota(jnp.int32, (model, 128), 1)
    row = jnp.sum(gain_two_sum[...] + gain_two_in[...], axis=0, keepdims=True)
    column = jnp.concatenate(
        [row_to_column(row[:, i : i + 256]) for i in range(0, model, 256)], axis=0
    )
    totals_two[...] = jnp.concatenate(
        [
            router_sum[...] + router_in[...] + jnp.where(lanes == 127, column, 0.0),
            dot_first(attention_grad[...], mixed_ref[...]),
        ],
        axis=1,
    )

    def send_small(i):
        k = (i + near) % n
        small_pieces[k] = my_piece(totals_two, k)

        @pl.when(k > 0)
        def _():
            small_copy(k).start()

    loop(send_small)

    def answers_here(i):
        k = in_turn(i, near)

        @pl.when(k > 0)
        def _():
            answer_copy(k).wait_recv()

        answer_pair_copy(k, half).start()

    loop(answers_here)
    for d in (1, 2, 3):
        gain_copy(d, (t + 4 - d) % 4).wait_recv()
    gain_rows[0] = (gain_one_all[0] + gain_one_all[1]) + (gain_one_all[2] + gain_one_all[3])

    def send_gain(k):
        gain_row_copy(k).start()

    loop(send_gain, 1)
    loop(lambda k: answer_pair_copy(k, 1 - half).wait_recv())

    def block_rows(j):
        rows = image_rows(2 * j + half)
        residual = residual_ref[rows, :]
        unit, _ = normalized(residual)
        gate_one, gate_two, _, _ = gates_of(rows, (unit * gain_two_ref[...]).astype(LOW))
        first, second = hots(rows)
        from_first = dot_plain(as_low(first), answers[...])
        from_second = dot_plain(as_low(second), answers[...])
        mine = jnp.where(side == 0, residual[:, :width], residual[:, width:])
        block_mine[j] = (mine + (gate_one * from_first + gate_two * from_second)).astype(LOW)
        block_copy(j).start()

    loop(block_rows, 0, 3)

    def tokens_back(j):
        rows = image_rows(2 * j + half)
        normed_grad = total.result(j)
        unit, factor = normalized(tokens_ref[rows, :].astype(FULL))
        grad = normalized_back(normed_grad * gain_one_ref[...], unit, factor)
        grad_tokens_ref[rows, :] = (residual_grad[j] + grad).astype(LOW)
        tokens_copy(j, half).start()

    loop(tokens_back, 0, 3)

    def block_back(j):
        block_copy(j).wait_recv()
        block_ref[image_rows(2 * j + half), :] = both_sides(block_mine[j], block_other[j])
        block_pair_copy(j, half).start()

    loop(block_back, 0, 3)
    pieces_in[0] = pieces[0]
    small_in[0] = small_pieces[0]

    def arrive(k):
        piece_copy(k).wait_recv()
        small_copy(k).wait_recv()
        gain_row_copy(k).wait_recv()

    loop(arrive, 1)
    weights_ref[...] = jnp.sum(pieces_in[...].astype(FULL), axis=0)
    small_ref[...] = jnp.sum(small_in[...].astype(FULL), axis=0)
    gain_ref[...] = jnp.sum(gain_rows[...], axis=0)

    for j in range(3):
        moe_copy(j).wait_send()
        block_copy(j).wait_send()
        attention_copy(j, half).wait_send()
        total.sent(j)
        tokens_copy(j, half).wait_send()
        tokens_copy(j, 1 - half).wait_recv()
        block_pair_copy(j, half).wait_send()
        block_pair_copy(j, 1 - half).wait_recv()
        gain_copy(j + 1, t).wait_send()
    router_copy().wait_send()
    gain_two_copy().wait_send()

    def left(k):
        answer_side_copy(k).wait_send()
        answer_pair_copy(k, half).wait_send()

        @pl.when(k > 0)
        def _():
            piece_copy(k).wait_send()
            small_copy(k).wait_send()
            gain_row_copy(k).wait_send()
            answer_copy(k).wait_send()

    loop(left)


def run_back(n, hp, first, later):
    upstream = first[4]
    rows, model = upstream.shape
    heads_width = later[2].shape[1]
    width = model // 2
    piece = model // n
    vmem = pl.BlockSpec(memory_space=VMEM)
    shape = jax.ShapeDtypeStruct
    slim = VMEM((3, PIECE, width), LOW)
    heads = VMEM((rows, heads_width), LOW)
    eight = VMEM((8, model), FULL)
    wide, narrow = 3 * heads_width, heads_width + 128
    quarter = VMEM((n, hp, width), LOW)
    three, many = dma(3), dma(n)
    return pl.pallas_call(
        functools.partial(back_kernel, n, hp),
        out_shape=(
            shape((rows, model), LOW),
            shape((rows, model), LOW),
            shape((piece, wide), FULL),
            shape((piece, narrow), FULL),
            shape((8, model), FULL),
        ),
        in_specs=[vmem] * len(first) + [pl.BlockSpec(memory_space=pl.ANY)] * len(later),
        out_specs=[vmem] * 5,
        scratch_shapes=[
            *[VMEM(a.shape, a.dtype) for a in later],
            slim, slim, slim, slim,
            VMEM((rows, model), LOW),
            VMEM((3, PIECE, model), FULL),
            heads, heads, heads,
            eight, eight, eight,
            VMEM((4, 8, model), FULL),
            VMEM((n, 8, model), FULL),
            VMEM((model, 128), FULL),
            VMEM((model, 128), FULL),
            VMEM((model, wide), FULL),
            VMEM((model, narrow), FULL),
            VMEM((n, piece, wide), LOW),
            VMEM((n, piece, wide), LOW),
            VMEM((n, piece, narrow), LOW),
            VMEM((n, piece, narrow), LOW),
            quarter, quarter,
            VMEM((n * 2 * hp, width), LOW),
            dma(len(later)),
            three, three, three, three, three, three, three, three, three, three,
            many, many, three, three, dma(2), dma(2),
            many, many, many, many, many, many, many, many, many, many,
            *Total.scratch(model),
        ],
        compiler_params=pltpu.CompilerParams(
            collective_id=2, has_side_effects=True, vmem_limit_bytes=VMEM_LIMIT
        ),
        name="back",
    )(*first, *later)


def body(
    tokens,
    gain_attn,
    w_query,
    w_key,
    w_value,
    w_output,
    gain_moe,
    w_router,
    expert_in,
    expert_out,
    routes,
    slot_ids,
    capacity,
    threshold,
    cotangent,
):
    n = lax.axis_size("dp")
    row_count, model = tokens.shape
    images = row_count // SEQ
    heads_here = w_query.shape[1] // HD
    slot_count = 23 * TOK_DEV // (10 * n) + 1
    per_half = -(-slot_count // 2)
    hp = -(-per_half // 16) * 16
    dp_here = lax.axis_index("dp")
    half_here = lax.axis_index("tensor") % 2

    def padded(rows, fill=0):
        split = rows.reshape(images, SEQ, -1)
        split = jnp.pad(split, ((0, 0), (0, PIECE - SEQ), (0, 0)), constant_values=fill)
        return split.reshape(images * PIECE, -1)

    def unpadded(rows):
        return rows.reshape(images, PIECE, -1)[:, :SEQ].reshape(row_count, -1)

    expert_ids = jnp.arange(n, dtype=jnp.int32)
    limits = jnp.sum(
        jnp.where(routes[:, :, None] == expert_ids, capacity[None, None, :], 0), axis=-1
    )
    kept = slot_ids < limits
    step = jnp.bitwise_xor(routes, dp_here)
    slot_half = slot_ids // per_half
    in_half = slot_ids % per_half
    place = jnp.where(kept & (slot_half == half_here), step * hp + in_half, -1)
    position = jnp.where(kept, step * (2 * hp) + slot_half * hp + in_half, -1)
    index = padded(jnp.concatenate([position, routes, place], axis=1), -1)
    place_rows = jnp.pad(index[:, 4:6].T, ((0, 6), (0, 0)), constant_values=-1)
    route_rows = index[:, 2:4].T

    tokens_in = padded(tokens)
    upstream = padded(cotangent)
    gain_one = gain_attn.astype(FULL)[None]
    gain_two = gain_moe.astype(FULL)[None]
    weights = (w_query, w_key, w_value, w_output)
    normed_one, query, key, value, mixed, residual, normed_two, peak, spread = run_front(
        n, hp, tokens_in, upstream, place_rows, (gain_one, gain_two), weights
    )
    logit_rows = lax.dot_general(
        w_router, normed_two, (((0,), (1,)), ((), ())), preferred_element_type=FULL
    )
    chosen = jnp.stack(
        [jnp.sum(jnp.where(expert_ids[:, None] == route_rows[k], logit_rows, 0.0), axis=0) for k in (0, 1)]
    )
    gate_rows = jnp.pad(jax.nn.softmax(chosen, axis=0), ((0, 6), (0, 0)))
    answer_out, answer_kept, back, gate_sums, grad_first, grad_second, top = run_experts(
        n, hp, place_rows, gate_rows, normed_two, expert_in[0], expert_out[0], peak, spread
    )
    router_wide = jnp.pad(w_router, ((0, 0), (0, 128 - n)))
    block_rows, token_rows, weight_grads, small, gain_rows = run_back(
        n,
        hp,
        (
            back.reshape(n * 2 * hp, -1),
            jnp.broadcast_to(gate_sums.reshape(1, -1), (8, n * 2 * hp)),
            index,
            residual,
            upstream,
            gain_one,
            gain_two,
            w_output,
            router_wide,
            answer_out,
        ),
        (
            answer_kept,
            normed_one,
            query,
            key,
            value,
            mixed,
            tokens_in,
            w_query,
            w_key,
            w_value,
        ),
    )
    head_max = top[:heads_here, 0]
    column_factor = jnp.repeat(jnp.sqrt(jnp.minimum(1.0, threshold / head_max)), HD)[None, :]
    wide = w_query.shape[1]
    piece = model // n
    return (
        unpadded(block_rows),
        unpadded(token_rows),
        lax.dynamic_slice_in_dim(gain_rows.sum(axis=0), dp_here * piece, piece),
        small[:, 127],
        weight_grads[:, :wide],
        weight_grads[:, wide : 2 * wide],
        weight_grads[:, 2 * wide :],
        small[:, 128:].T,
        small[:, :n],
        grad_first[None],
        grad_second[None],
        w_query.astype(FULL) * column_factor,
        w_key.astype(FULL) * column_factor,
        head_max,
    )


def solution(mesh):
    in_specs = (
        P("dp", None),
        P(),
        P(None, "tensor"),
        P(None, "tensor"),
        P(None, "tensor"),
        P("tensor", None),
        P(),
        P(),
        P("dp", None, "tensor"),
        P("dp", "tensor", None),
        P("dp", None),
        P("dp", None),
        P(),
        P("tensor"),
        P("dp", None),
    )
    out_specs = (
        P("dp", None),
        P("dp", None),
        P("dp"),
        P("dp"),
        P("dp", "tensor"),
        P("dp", "tensor"),
        P("dp", "tensor"),
        P("tensor", "dp"),
        P("dp", None),
        P("dp", None, "tensor"),
        P("dp", "tensor", None),
        P(None, "tensor"),
        P(None, "tensor"),
        P("tensor"),
    )
    return jax.shard_map(body, mesh=mesh, in_specs=in_specs, out_specs=out_specs, check_vma=False)
```

```python
import functools
import math

import jax
import jax.numpy as jnp
from jax import lax
from jax.experimental import pallas as pl
from jax.experimental.pallas import tpu as pltpu
from jax.sharding import PartitionSpec as P

HD = 64
SEQ = 197
PIECE = 208
TOK_DEV = 1182
EPSILON = 1e-06
MESH = pl.DeviceIdType.MESH
VMEM_LIMIT = 60 * 2**20
VMEM = pltpu.VMEM
LOW, FULL = jnp.bfloat16, jnp.float32


def dot_plain(a, b):
    return jnp.dot(a, b, preferred_element_type=FULL)


def dot_last(a, b):
    return lax.dot_general(a, b, (((1,), (1,)), ((), ())), preferred_element_type=FULL)


def dot_first(a, b):
    return lax.dot_general(a, b, (((0,), (0,)), ((), ())), preferred_element_type=FULL)


def normalized(rows):
    centered = rows - jnp.mean(rows, axis=-1, keepdims=True)
    factor = lax.rsqrt(jnp.mean(centered * centered, axis=-1, keepdims=True) + EPSILON)
    return centered * factor, factor


def normalized_back(u, unit, factor):
    first = jnp.mean(u, axis=-1, keepdims=True)
    second = jnp.mean(u * unit, axis=-1, keepdims=True)
    return factor * (u - first - unit * second)


def same_index(size):
    rows = lax.broadcasted_iota(jnp.int32, (size, size), 0)
    return rows == lax.broadcasted_iota(jnp.int32, (size, size), 1)


def row_to_column(row):
    return jnp.sum(jnp.where(same_index(row.shape[1]), row, 0.0), axis=1, keepdims=True)


def column_to_row(column):
    return jnp.sum(jnp.where(same_index(column.shape[0]), column, 0.0), axis=0, keepdims=True)


def attention_probs(queries, keys):
    scores = dot_last(queries, keys) * HD**-0.5
    real = lax.broadcasted_iota(jnp.int32, scores.shape, 1) < SEQ
    scores = jnp.where(real, scores, -1e30)
    top = jnp.max(scores, axis=1, keepdims=True)
    powers = jnp.exp(scores - top)
    return powers * (1.0 / jnp.sum(powers, axis=1, keepdims=True)), top


def partner(dp, k, n):
    other, weight = 0, 1
    while weight < n:
        other = other + ((dp // weight + k // weight) % 2) * weight
        weight *= 2
    return other


def places():
    dp = lax.axis_index("dp")
    t = lax.axis_index("tensor")
    return dp, t, t % 2, t // 2, t + 1 - 2 * (t % 2), (t + 2) % 4


def remote(src, dst, sends, recvs, device):
    return pltpu.make_async_remote_copy(
        src_ref=src,
        dst_ref=dst,
        send_sem=sends,
        recv_sem=recvs,
        device_id=device,
        device_id_type=MESH,
    )


def signal(sem, device):
    pl.semaphore_signal(sem, inc=1, device_id=device, device_id_type=MESH)


def greet(n, dp, t, others):
    barrier = pltpu.get_barrier_semaphore()

    def one(k, carry):
        signal(barrier, (partner(dp, k, n), t))
        return carry

    lax.fori_loop(1, n, one, 0)
    for other in others:
        signal(barrier, (dp, other))


def await_greetings(n, others):
    pl.semaphore_wait(pltpu.get_barrier_semaphore(), n - 1 + len(others))


def image_rows(image):
    return pl.ds(pl.multiple_of(image * PIECE, PIECE), PIECE)


def dma(*shape):
    return pltpu.SemaphoreType.DMA(shape)


def near_count(n):
    return min(4, n)


class Spread:
    def __init__(self, n, hp, place, near_out, far_out, arrived, zs, zr, xs, xr, cs, cr, own):
        self.n, self.hp, self.near = n, hp, near_count(n)
        self.place, self.near_out, self.far_out, self.arrived = place, near_out, far_out, arrived
        self.zs, self.zr, self.xs, self.xr, self.cs, self.cr, self.own = zs, zr, xs, xr, cs, cr, own
        self.dp, self.t, self.half, self.side, self.mate, self.far = places()
        self.width = far_out.shape[2]

    def rows(self, owner):
        return pl.ds(pl.multiple_of(owner * self.hp, self.hp), self.hp)

    def columns(self, owner):
        return pl.ds(pl.multiple_of(owner * self.width, self.width), self.width)

    def peer(self, k):
        return (partner(self.dp, k, self.n), self.t)

    def own_copy(self):
        return pltpu.make_async_copy(
            self.near_out.at[0], self.arrived.at[0, self.rows(self.half)], self.own
        )

    def near_copy(self, k):
        return remote(
            self.near_out.at[k],
            self.arrived.at[k, self.rows(self.half)],
            self.zs.at[k],
            self.zr.at[k],
            self.peer(k),
        )

    def far_copy(self, k):
        return remote(
            self.far_out.at[k - self.near],
            self.arrived.at[k, self.rows(self.half), self.columns(self.side)],
            self.zs.at[k],
            self.zr.at[k],
            self.peer(k),
        )

    def side_copy(self, k, side):
        part = self.arrived.at[k, self.rows(self.half), self.columns(side)]
        return remote(part, part, self.xs.at[k], self.xr.at[k], (self.dp, self.far))

    def pair_copy(self, k, half):
        part = self.arrived.at[k, self.rows(half)]
        return remote(part, part, self.cs.at[k], self.cr.at[k], (self.dp, self.mate))

    def hot(self, k, row_count):
        slots = lax.broadcasted_iota(jnp.int32, (self.hp, row_count), 0) + k * self.hp
        is_first = self.place[0:1, :] == slots
        is_second = self.place[1:2, :] == slots
        return is_first, is_second

    def send(self, k, rows_ref):
        is_first, is_second = self.hot(k, rows_ref.shape[0])
        hot = jnp.where(is_first | is_second, 1.0, 0.0).astype(LOW)

        @pl.when(k < self.near)
        def _():
            self.near_out[k] = dot_plain(hot, rows_ref[...]).astype(LOW)

            @pl.when(k == 0)
            def _():
                self.own_copy().start()

            @pl.when(k > 0)
            def _():
                self.near_copy(k).start()

        @pl.when(k >= self.near)
        def _():
            mine = rows_ref[:, self.columns(self.side)]
            self.far_out[k - self.near] = dot_plain(hot, mine).astype(LOW)
            self.far_copy(k).start()

        return is_first, is_second

    def first_hop(self, k):
        @pl.when(k == 0)
        def _():
            self.own_copy().wait()

        @pl.when((k > 0) & (k < self.near))
        def _():
            self.near_copy(k).wait_recv()

        @pl.when(k >= self.near)
        def _():
            self.far_copy(k).wait_recv()
            self.side_copy(k, self.side).start()

    def second_hop(self, k):
        @pl.when(k >= self.near)
        def _():
            self.side_copy(k, 1 - self.side).wait_recv()

        self.pair_copy(k, self.half).start()

    def last_hop(self, k):
        self.pair_copy(k, 1 - self.half).wait_recv()

    def sent(self, k):
        @pl.when((k > 0) & (k < self.near))
        def _():
            self.near_copy(k).wait_send()

        @pl.when(k >= self.near)
        def _():
            self.far_copy(k).wait_send()
            self.side_copy(k, self.side).wait_send()

        self.pair_copy(k, self.half).wait_send()

    @staticmethod
    def scratch(n, hp, width):
        near = near_count(n)
        return [VMEM((near, hp, 2 * width), LOW), VMEM((n - near, hp, width), LOW)]

    @staticmethod
    def semaphores(n):
        return [dma(n), dma(n), dma(n), dma(n), dma(n), dma(n), pltpu.SemaphoreType.DMA]


class Total:
    def __init__(self, part_out, pair_in, far_out, far_in, ps, pr, fs, fr):
        self.part_out, self.pair_in, self.far_out, self.far_in = part_out, pair_in, far_out, far_in
        self.ps, self.pr, self.fs, self.fr = ps, pr, fs, fr
        self.dp, _, _, _, self.mate, self.far = places()

    def pair_copy(self, j):
        return remote(
            self.part_out.at[j], self.pair_in.at[j], self.ps.at[j], self.pr.at[j], (self.dp, self.mate)
        )

    def far_copy(self, j):
        return remote(
            self.far_out.at[j], self.far_in.at[j], self.fs.at[j], self.fr.at[j], (self.dp, self.far)
        )

    def give(self, j, rows):
        self.part_out[j] = rows
        self.pair_copy(j).start()

    def take(self, j, rows):
        self.pair_copy(j).wait_recv()
        self.far_out[j] = (rows + self.pair_in[j]).astype(LOW)
        self.far_copy(j).start()

    def result(self, j):
        self.far_copy(j).wait_recv()
        return self.far_out[j].astype(FULL) + self.far_in[j].astype(FULL)

    def sent(self, j):
        self.pair_copy(j).wait_send()
        self.far_copy(j).wait_send()

    @staticmethod
    def scratch(model):
        wide, slim = VMEM((3, PIECE, model), FULL), VMEM((3, PIECE, model), LOW)
        return [wide, wide, slim, slim, dma(3), dma(3), dma(3), dma(3)]


def padded_image(rows_ref, image):
    start = image * SEQ // 8 * 8
    length = min(PIECE, rows_ref.shape[0] - start)
    rows = lax.broadcasted_iota(jnp.int32, (PIECE, length), 0)
    columns = lax.broadcasted_iota(jnp.int32, (PIECE, length), 1)
    pick = (columns == rows + (image * SEQ - start)) & (rows < SEQ)
    return dot_plain(jnp.where(pick, 1.0, 0.0).astype(LOW), rows_ref[start : start + length, :])


def front_kernel(
    n,
    hp,
    per_half,
    capacity_ref,
    routes_ref,
    slot_ids_ref,
    tokens_ref,
    upstream_ref,
    gains_ref,
    query_w_ref,
    key_w_ref,
    value_w_ref,
    output_w_ref,
    place_ref,
    index_ref,
    peak_ref,
    *refs,
):
    outs, spread_hbm, scratch = refs[:9], refs[9], refs[10:]
    held, scratch = scratch[:9], scratch[9:]
    (
        tokens,
        upstream,
        normed_one,
        query,
        key,
        value,
        mixed_rows,
        residual_rows,
        normed_two,
    ) = held
    near_out, far_out, zs, zr, own, ns, nr, hs = scratch[:8]
    total = Total(*scratch[8:])
    dp, t, half, side, mate, far = places()
    heads = query_w_ref.shape[0] // HD
    near = near_count(n)
    width = far_out.shape[2]
    row_count = tokens.shape[0]
    greet(n, dp, t, (mate, far))
    peak_ref[...] = jnp.full(peak_ref.shape, -1e30, FULL)
    for image in range(row_count // PIECE):
        tokens[image * PIECE : (image + 1) * PIECE, :] = padded_image(tokens_ref, image).astype(LOW)

    def image_forward(image):
        rows = image_rows(image)
        unit, _ = normalized(tokens[rows, :].astype(FULL))
        normed = (unit * gains_ref[0:1, :]).astype(LOW)
        normed_one[rows, :] = normed
        queries = dot_last(normed, query_w_ref[...]).astype(LOW)
        keys = dot_last(normed, key_w_ref[...]).astype(LOW)
        values = dot_last(normed, value_w_ref[...]).astype(LOW)
        query[rows, :] = queries
        key[rows, :] = keys
        value[rows, :] = values
        mixed = []
        for h in range(heads):
            cols = slice(h * HD, (h + 1) * HD)
            probs, top = attention_probs(queries[:, cols], keys[:, cols])
            real = lax.broadcasted_iota(jnp.int32, top.shape, 0) < SEQ
            best = jnp.max(jnp.where(real, top, -1e30), axis=0, keepdims=True)
            peak_ref[h : h + 1, :] = jnp.maximum(peak_ref[h : h + 1, :], best)
            mixed.append(dot_plain(probs.astype(LOW), values[:, cols]))
        mixed = jnp.concatenate(mixed, axis=1).astype(LOW)
        mixed_rows[rows, :] = mixed
        return dot_plain(mixed, output_w_ref[...])

    def normed_copy(j, owner):
        rows = normed_two.at[image_rows(2 * j + owner)]
        return remote(rows, rows, ns.at[j], nr.at[j], (dp, mate))

    def keep(i):
        return pltpu.make_async_copy(held[i], outs[i], hs.at[i])

    def finish(j):
        rows = image_rows(2 * j + half)
        residual = tokens[rows, :].astype(FULL) + total.result(j)
        residual_rows[j] = residual
        unit, _ = normalized(residual)
        normed_two[rows, :] = (unit * gains_ref[1:2, :]).astype(LOW)
        normed_copy(j, half).start()

    def peer(k):
        return (partner(dp, k, n), t)

    def half_rows():
        return pl.ds(pl.multiple_of(half * hp, hp), hp)

    def side_columns():
        return pl.ds(pl.multiple_of(side * width, width), width)

    def own_copy():
        return pltpu.make_async_copy(near_out.at[0], spread_hbm.at[0, half_rows()], own)

    def near_copy(k):
        return remote(near_out.at[k], spread_hbm.at[k, half_rows()], zs.at[k], zr.at[k], peer(k))

    def far_copy(k):
        return remote(
            far_out.at[k - near],
            spread_hbm.at[k, half_rows(), side_columns()],
            zs.at[k],
            zr.at[k],
            peer(k),
        )

    def dispatch(k):
        slots = lax.broadcasted_iota(jnp.int32, (hp, row_count), 0) + k * hp
        hot = (place_ref[0:1, :] == slots) | (place_ref[1:2, :] == slots)
        hot = jnp.where(hot, 1.0, 0.0).astype(LOW)

        @pl.when(k < near)
        def _():
            near_out[k] = dot_plain(hot, upstream[...]).astype(LOW)

            @pl.when(k == 0)
            def _():
                own_copy().start()

            @pl.when(k > 0)
            def _():
                near_copy(k).start()

        @pl.when(k >= near)
        def _():
            far_out[k - near] = dot_plain(hot, upstream[:, side_columns()]).astype(LOW)
            far_copy(k).start()

    def places_of_pairs():
        routes, slot_ids = routes_ref[...], slot_ids_ref[...]
        limits = jnp.zeros_like(routes)
        for e in range(n):
            limits = jnp.where(routes == e, capacity_ref[e], limits)
        kept = slot_ids < limits
        step = jnp.zeros_like(routes)
        weight = 1
        while weight < n:
            step = step + (routes // weight + dp // weight) % 2 * weight
            weight *= 2
        upper = slot_ids >= per_half
        in_half = slot_ids - jnp.where(upper, per_half, 0)
        in_block = in_half + jnp.where(upper, hp, 0)
        mine = kept & (upper == (half == 1))
        place = jnp.where(mine, step * hp + in_half, -1)
        position = jnp.where(kept, step * (2 * hp) + in_block, -1)
        both = jnp.concatenate([place, position, routes, jnp.full_like(routes, -1)], axis=0)
        fill = jnp.full((8, PIECE - SEQ), -1, jnp.int32)
        spaced = []
        for image in range(row_count // PIECE):
            spaced += [both[:, image * SEQ : (image + 1) * SEQ], fill]
        return jnp.concatenate(spaced, axis=1)

    pairs = places_of_pairs()
    place_ref[...] = pairs
    index_ref[...] = pairs.T
    per_step = -(-n // 3)

    def step(j, carry):
        given = image_forward(2 * j + 1 - half)

        @pl.when(j == 0)
        def _():
            await_greetings(n, (mate, far))

        total.give(j, given)
        total.take(j, image_forward(2 * j + half))

        @pl.when(j == 0)
        def _():
            for image in range(row_count // PIECE):
                upstream[image * PIECE : (image + 1) * PIECE, :] = padded_image(
                    upstream_ref, image
                ).astype(LOW)

        def turn(i, inner):
            @pl.when(i < n)
            def _():
                dispatch((i + near) % n)

            return inner

        lax.fori_loop(j * per_step, (j + 1) * per_step, turn, 0)

        @pl.when(j >= 1)
        def _():
            finish(j - 1)

        return carry

    lax.fori_loop(0, 3, step, 0)
    for i in range(7):
        keep(i).start()
    finish(2)
    keep(7).start()
    own_copy().wait()

    def arrive(k, carry):
        @pl.when(k < near)
        def _():
            near_copy(k).wait()

        @pl.when(k >= near)
        def _():
            far_copy(k).wait()

        return carry

    for j in range(3):
        normed_copy(j, 1 - half).wait_recv()
    keep(8).start()
    lax.fori_loop(1, n, arrive, 0)
    for j in range(3):
        total.sent(j)
        normed_copy(j, half).wait_send()
    for i in range(9):
        keep(i).wait()


def run_front(n, hp, per_half, capacity, routes, slot_ids, tokens, upstream, gains, weights):
    model = tokens.shape[1]
    rows = tokens.shape[0] // SEQ * PIECE
    heads_width = weights[0].shape[0]
    near = near_count(n)
    width = model // 2
    vmem = pl.BlockSpec(memory_space=VMEM)
    hbm = pl.BlockSpec(memory_space=pl.ANY)
    shape = jax.ShapeDtypeStruct
    slim, wide = shape((rows, heads_width), LOW), shape((rows, model), LOW)
    held = (wide, wide, wide, slim, slim, slim, slim, shape((3, PIECE, model), FULL), wide)
    return pl.pallas_call(
        functools.partial(front_kernel, n, hp, per_half),
        out_shape=(
            shape((8, rows), jnp.int32),
            shape((rows, 8), jnp.int32),
            shape((8, 128), FULL),
            *held,
            shape((n, 2 * hp, model), LOW),
        ),
        in_specs=[pl.BlockSpec(memory_space=pltpu.SMEM)] + [vmem] * 9,
        out_specs=[vmem] * 3 + [hbm] * 10,
        scratch_shapes=[
            *[VMEM(a.shape, a.dtype) for a in held],
            VMEM((near, hp, model), LOW),
            VMEM((n - near, hp, width), LOW),
            dma(n),
            dma(n),
            pltpu.SemaphoreType.DMA,
            dma(3),
            dma(3),
            dma(9),
            *Total.scratch(model),
        ],
        compiler_params=pltpu.CompilerParams(
            collective_id=0, has_side_effects=True, vmem_limit_bytes=VMEM_LIMIT
        ),
        name="front",
    )(capacity, routes, slot_ids, tokens, upstream, gains, *weights)


def in_turn(i, near):
    return jnp.where(i < 2 * near, i // 2 + (i % 2) * near, i)


def expert_kernel(
    n,
    hp,
    place_ref,
    router_ref,
    peak_ref,
    normed_hbm,
    first_hbm,
    second_hbm,
    upstream_hbm,
    back_ref,
    gate_sum_ref,
    top_ref,
    answer_out_hbm,
    answer_kept_hbm,
    grad_first_hbm,
    grad_second_hbm,
    *scratch,
):
    dp, t, half, side, mate, far = places()
    arrived = scratch[2]
    spread = Spread(n, hp, place_ref, *scratch[:10])
    (
        normed_ref,
        first_ref,
        second_ref,
        answer_out,
        answer_kept,
        grad_first_ref,
        grad_second_ref,
        os_,
        ws,
        xs,
        xr,
        cs,
        cr,
    ) = scratch[44:]
    (
        upstream,
        hidden_all,
        pre_grad_all,
        parts,
        pair_in,
        kept,
        far_out,
        far_in,
        final,
        gate_out,
        gate_in,
        sum_out,
        sum_in,
        sums,
        peaks,
        us,
        ps,
        pr,
        fs,
        fr,
        rs,
        rr,
        ms,
        mr,
        gs,
        gr,
        hs,
        hr,
        ks,
        kr,
        qs,
        qr,
        ss,
        sr,
    ) = scratch[10:44]
    model = normed_ref.shape[1]
    width = model // 2
    near = spread.near
    greet(n, dp, t, [(t + d) % 4 for d in (1, 2, 3)])
    fetches = [
        pltpu.make_async_copy(a, b, ws.at[i])
        for i, (a, b) in enumerate(
            ((normed_hbm, normed_ref), (first_hbm, first_ref), (second_hbm, second_ref))
        )
    ]
    mine = (slice(0, near), spread.rows(half))
    fetches.append(pltpu.make_async_copy(upstream_hbm.at[mine], upstream.at[mine], us.at[0]))
    mine = (slice(near, n), spread.rows(half), spread.columns(side))
    fetches.append(pltpu.make_async_copy(upstream_hbm.at[mine], upstream.at[mine], us.at[1]))
    for fetch in fetches:
        fetch.start()

    def upstream_side_copy(k, owner):
        part = upstream.at[k, spread.rows(half), spread.columns(owner)]
        return remote(part, part, xs.at[k], xr.at[k], (dp, far))

    def upstream_pair_copy(k, owner):
        part = upstream.at[k, spread.rows(owner)]
        return remote(part, part, cs.at[k], cr.at[k], (dp, mate))

    def keep(i):
        pairs = (
            (answer_out, answer_out_hbm),
            (answer_kept, answer_kept_hbm),
        )
        return pltpu.make_async_copy(*pairs[i], os_.at[i])

    def gate_copy(k):
        return remote(gate_out.at[k], gate_in.at[k, half], gs.at[k], gr.at[k], spread.peer(k))

    def gate_pair_copy(k, owner):
        tile = gate_in.at[k, owner]
        return remote(tile, tile, hs.at[k], hr.at[k], (dp, mate))

    def part_copy(i, k):
        return remote(
            parts.at[i % 3, :, spread.rows(1 - half)],
            pair_in.at[k],
            ps.at[i % 3],
            pr.at[k],
            (dp, mate),
        )

    def far_copy(i, k):
        return remote(far_out.at[i % 3], far_in.at[k], fs.at[i % 3], fr.at[k], (dp, far))

    def return_copy(k):
        return remote(
            final.at[k], back_ref.at[k, spread.rows(half)], rs.at[k], rr.at[k], spread.peer(k)
        )

    def mate_copy(k, owner):
        rows = back_ref.at[k, spread.rows(owner)]
        return remote(rows, rows, ms.at[k], mr.at[k], (dp, mate))

    def sum_copy(k):
        return remote(sum_out.at[k], sum_in.at[k], ks.at[k], kr.at[k], spread.peer(k))

    def peak_copy(k):
        return remote(peak_ref, peaks.at[k], qs.at[k], qr.at[k], spread.peer(k))

    def share_copy(d, owner):
        return remote(
            sums.at[owner], sums.at[owner], ss.at[d - 1], sr.at[d - 1], (dp, (t + d) % 4)
        )

    def loop(body, first=0, last=n):
        def one(k, carry):
            body(k)
            return carry

        lax.fori_loop(first, last, one, 0)

    fetches[0].wait()
    logits = dot_last(router_ref[...], normed_ref[...])
    rows_of = lax.broadcasted_iota(jnp.int32, logits.shape, 0)
    one, two = (
        jnp.sum(jnp.where(rows_of == place_ref[r : r + 1, :], logits, 0.0), axis=0, keepdims=True)
        for r in (4, 5)
    )
    best = jnp.maximum(one, two)
    one, two = jnp.exp(one - best), jnp.exp(two - best)
    gate_one, gate_two = one / (one + two), two / (one + two)
    await_greetings(n, (1, 2, 3))

    def dispatch(i):
        k = (i + near) % n
        is_first, is_second = spread.send(k, normed_ref)
        gate = jnp.sum(
            jnp.where(is_first, gate_one, 0.0) + jnp.where(is_second, gate_two, 0.0),
            axis=1,
            keepdims=True,
        )
        tile = jnp.broadcast_to(column_to_row(gate), (8, hp))

        @pl.when(k == 0)
        def _():
            gate_in[0, half] = tile

        @pl.when(k > 0)
        def _():
            gate_out[k] = tile
            gate_copy(k).start()

    loop(dispatch)
    for fetch in fetches[1:]:
        fetch.wait()
    loop(lambda k: upstream_side_copy(k, side).start(), near)
    loop(lambda k: upstream_pair_copy(k, half).start(), 0, near)

    def chunk(i, k):
        gate = jnp.concatenate(
            [row_to_column(gate_in[k, 0, 0:1, :]), row_to_column(gate_in[k, 1, 0:1, :])], axis=0
        )
        gradient = upstream[k].astype(FULL)
        answer_grad = (gradient * gate).astype(LOW)
        pre = dot_plain(arrived[k], first_ref[...])
        share = 0.5 * (1.0 + lax.erf(pre * math.sqrt(0.5)))
        slope = share + pre * (jnp.exp(-0.5 * pre * pre) * (1.0 / math.sqrt(2.0 * math.pi)))
        hidden = (pre * share).astype(LOW)
        hidden_all[k] = hidden
        answer = dot_plain(hidden, second_ref[...])
        parts[i % 3, 0] = answer.astype(LOW)
        gate_sum = jnp.sum(answer * gradient, axis=1, keepdims=True)
        upstream[k] = answer_grad
        pre_grad = (dot_last(answer_grad, second_ref[...]) * slope).astype(LOW)
        pre_grad_all[k] = pre_grad
        parts[i % 3, 1] = dot_last(pre_grad, first_ref[...]).astype(LOW)
        tile = jnp.broadcast_to(column_to_row(gate_sum), (8, 2 * hp))

        @pl.when(k == 0)
        def _():
            sum_in[0] = tile

        @pl.when(k > 0)
        def _():
            sum_out[k] = tile
            sum_copy(k).start()
            peak_copy(k).start()

    tile = 256
    tiles = model // tile

    def grad_copy(m, j):
        cols = pl.ds(pl.multiple_of(m * tile, tile), tile)
        ref, hbm = ((grad_first_ref, grad_first_hbm), (grad_second_ref, grad_second_hbm))[j]
        return pltpu.make_async_copy(ref.at[cols], hbm.at[cols], os_.at[2 + 2 * m + j])

    def grads(m):
        cols = pl.ds(pl.multiple_of(m * tile, tile), tile)
        rows_in = arrived[:, :, cols].reshape(n * 2 * hp, tile)
        grad_first_ref[cols, :] = dot_first(rows_in, pre_grad_all[...].reshape(n * 2 * hp, -1))
        grad_copy(m, 0).start()
        hidden = hidden_all[:, :, cols].reshape(n * 2 * hp, tile)
        grad_second_ref[cols, :] = dot_first(hidden, upstream[...].reshape(n * 2 * hp, model))
        grad_copy(m, 1).start()

    def step(i):
        @pl.when(i < n)
        def _():
            spread.first_hop(in_turn(i, near))

        @pl.when(i < n - near)
        def _():
            upstream_side_copy(i + near, 1 - side).wait_recv()
            upstream_pair_copy(i + near, half).start()

        @pl.when((i >= 1) & (i < n + 1))
        def _():
            k = in_turn(i - 1, near)
            spread.second_hop(k)

            @pl.when(k > 0)
            def _():
                gate_copy(k).wait_recv()

            gate_pair_copy(k, half).start()

        @pl.when((i >= 2) & (i < n + 2))
        def _():
            k = in_turn(i - 2, near)
            spread.last_hop(k)
            gate_pair_copy(k, 1 - half).wait_recv()
            upstream_pair_copy(k, 1 - half).wait_recv()
            upstream_pair_copy(k, half).wait_send()

            @pl.when(k >= near)
            def _():
                upstream_side_copy(k, side).wait_send()

            @pl.when(i >= 5)
            def _():
                part_copy(i - 5, in_turn(i - 5, near)).wait_send()

            chunk(i - 2, k)
            part_copy(i - 2, k).start()

        @pl.when((i >= n + 2) & (i < n + 2 + tiles))
        def _():
            grads(i - (n + 2))

        @pl.when((i >= 3) & (i < n + 3))
        def _():
            k = in_turn(i - 3, near)
            part_copy(i - 3, k).wait_recv()

            @pl.when(i >= 6)
            def _():
                far_copy(i - 6, in_turn(i - 6, near)).wait_send()

            for j in (1, 0):
                whole = parts[i % 3, j, spread.rows(half), :].astype(FULL) + pair_in[k, j].astype(FULL)
                low, high = whole[:, :width], whole[:, width:]
                stays = jnp.where(side == 0, low, high)
                goes = jnp.where(side == 0, high, low).astype(LOW)
                if j:
                    kept[i % 3] = stays
                    far_out[i % 3] = goes
                    far_copy(i - 3, k).start()
                else:
                    answer_kept[k] = stays
                    answer_out[k] = goes

        @pl.when((i >= 4) & (i < n + 4))
        def _():
            k = in_turn(i - 4, near)
            far_copy(i - 4, k).wait_recv()
            rows = (kept[(i - 4) % 3] + far_in[k].astype(FULL)).astype(LOW)

            @pl.when(k == 0)
            def _():
                back_ref[0, spread.rows(half), :] = rows

            @pl.when(k > 0)
            def _():
                final[k] = rows
                return_copy(k).start()

    loop(step, 0, n + 2 + tiles)
    keep(0).start()
    keep(1).start()
    peaks[0] = peak_ref[...]

    def collect_sums(k):
        @pl.when(k > 0)
        def _():
            peak_copy(k).wait_recv()
            sum_copy(k).wait_recv()

        sums[t, pl.ds(k, 1), :] = sum_in[k, 0:1, :]

    loop(collect_sums)
    for d in (1, 2, 3):
        share_copy(d, t).start()
    top_ref[...] = jnp.max(peaks[...], axis=0)

    def collect(i):
        k = in_turn(i, near)

        @pl.when(k > 0)
        def _():
            return_copy(k).wait_recv()

        mate_copy(k, half).start()

    loop(collect)
    for d in (1, 2, 3):
        share_copy(d, (t + 4 - d) % 4).wait_recv()
    whole = (sums[0] + sums[1]) + (sums[2] + sums[3])
    whole = jnp.concatenate([whole[k : k + 1] for k in range(n)], axis=1)
    gate_sum_ref[...] = jnp.broadcast_to(whole, gate_sum_ref.shape)

    def finish(i):
        k = in_turn(i, near)
        mate_copy(k, 1 - half).wait_recv()
        mate_copy(k, half).wait_send()
        spread.sent(k)
        gate_pair_copy(k, half).wait_send()

        @pl.when(k > 0)
        def _():
            return_copy(k).wait_send()
            gate_copy(k).wait_send()
            sum_copy(k).wait_send()
            peak_copy(k).wait_send()

        @pl.when(i >= n - 3)
        def _():
            part_copy(i, k).wait_send()
            far_copy(i, k).wait_send()

    loop(finish)
    for d in (1, 2, 3):
        share_copy(d, t).wait_send()
    keep(0).wait()
    keep(1).wait()
    for m in range(tiles):
        grad_copy(m, 0).wait()
        grad_copy(m, 1).wait()


def run_experts(n, hp, place, router, peak, normed, first, second, upstream):
    model = normed.shape[1]
    width = model // 2
    hidden = first.shape[1]
    vmem = pl.BlockSpec(memory_space=VMEM)
    hbm = pl.BlockSpec(memory_space=pl.ANY)
    shape = jax.ShapeDtypeStruct
    return pl.pallas_call(
        functools.partial(expert_kernel, n, hp),
        out_shape=(
            shape((n, 2 * hp, width), LOW),
            shape((8, n * 2 * hp), FULL),
            shape(peak.shape, FULL),
            shape((n, hp, width), LOW),
            shape((n, hp, width), FULL),
            shape((model, hidden), FULL),
            shape((hidden, model), FULL),
        ),
        in_specs=[vmem] * 3 + [hbm] * 4,
        out_specs=[vmem] * 3 + [hbm] * 4,
        scratch_shapes=[
            *Spread.scratch(n, hp, width),
            VMEM((n, 2 * hp, model), LOW),
            *Spread.semaphores(n),
            VMEM((n, 2 * hp, model), LOW),
            VMEM((n, 2 * hp, hidden), LOW),
            VMEM((n, 2 * hp, hidden), LOW),
            VMEM((3, 2, 2 * hp, model), LOW),
            VMEM((n, 2, hp, model), LOW),
            VMEM((3, hp, width), FULL),
            VMEM((3, hp, width), LOW),
            VMEM((n, hp, width), LOW),
            VMEM((n, hp, width), LOW),
            VMEM((n, 8, hp), FULL),
            VMEM((n, 2, 8, hp), FULL),
            VMEM((n, 8, 2 * hp), FULL),
            VMEM((n, 8, 2 * hp), FULL),
            VMEM((4, n, 2 * hp), FULL),
            VMEM((n, *peak.shape), FULL),
            dma(2),
            dma(3), dma(n), dma(3), dma(n), dma(n), dma(n), dma(n), dma(n),
            dma(n), dma(n), dma(n), dma(n), dma(n), dma(n), dma(n), dma(n), dma(3), dma(3),
            VMEM(normed.shape, LOW),
            VMEM(first.shape, LOW),
            VMEM(second.shape, LOW),
            VMEM((n, hp, width), LOW),
            VMEM((n, hp, width), FULL),
            VMEM((model, hidden), FULL),
            VMEM((hidden, model), FULL),
            dma(2 + 2 * (model // 256)),
            dma(3), dma(n), dma(n), dma(n), dma(n),
        ],
        compiler_params=pltpu.CompilerParams(
            collective_id=1, has_side_effects=True, vmem_limit_bytes=VMEM_LIMIT
        ),
        name="experts",
    )(place, router, peak, normed, first, second, upstream)


def unpad(rows_ref, out_ref):
    for image in range(rows_ref.shape[0] // PIECE):
        start = image * SEQ // 8 * 8
        length = min(PIECE, out_ref.shape[0] - start)
        shift = image * SEQ - start
        rows = lax.broadcasted_iota(jnp.int32, (length, PIECE), 0)
        columns = lax.broadcasted_iota(jnp.int32, (length, PIECE), 1)
        pick = (rows == columns + shift) & (columns < SEQ)
        image_part = rows_ref[image * PIECE : (image + 1) * PIECE, :]
        moved = dot_plain(jnp.where(pick, 1.0, 0.0).astype(LOW), image_part).astype(LOW)
        if shift:
            before = lax.broadcasted_iota(jnp.int32, (8, moved.shape[1]), 0) < shift
            first = jnp.where(before, out_ref[start : start + 8, :].astype(FULL), moved[:8].astype(FULL))
            out_ref[start : start + 8, :] = first.astype(LOW)
            out_ref[start + 8 : start + length, :] = moved[8:]
        else:
            out_ref[start : start + length, :] = moved


def back_kernel(
    n,
    hp,
    back_ref,
    gate_sum_ref,
    index_ref,
    gains_ref,
    output_w_ref,
    router_ref,
    *refs,
):
    later, outs, scratch = refs[:13], refs[13:18], refs[18:]
    block_out_ref, tokens_out_ref, weights_ref, small_ref, gain_ref = outs
    held, scratch = scratch[:13], scratch[13:]
    (
        residual_ref,
        upstream_ref,
        answer_out,
        answer_kept,
        normed_one_ref,
        query_ref,
        key_ref,
        value_ref,
        mixed_ref,
        tokens_ref,
        query_w_ref,
        key_w_ref,
        value_w_ref,
    ) = held
    dp, t, half, side, mate, far = places()
    (
        moe_mine,
        moe_other,
        block_mine,
        block_other,
        attention_grad,
        residual_grad,
        query_grad,
        key_grad,
        value_grad,
        gain_two_sum,
        gain_two_in,
        gain_one_sum,
        gain_one_all,
        gain_rows,
        router_sum,
        router_in,
        totals,
        totals_two,
        pieces,
        pieces_in,
        small_pieces,
        small_in,
        answer_far,
        answer_final,
        answers,
        block_ref,
        grad_tokens_ref,
        hs,
        as_,
        ar,
        bs,
        br,
        ts,
        tr,
        cs,
        cr,
        gs,
        gr,
        ws,
        wr,
        ls,
        lr,
        os_,
        or_,
        vs,
        vr,
        ds,
        dr,
        es,
        er,
        fs,
        fr,
        ks,
        kr,
    ) = scratch[:54]
    total = Total(*scratch[54:])
    heads = query_w_ref.shape[0] // HD
    model = upstream_ref.shape[1]
    width = model // 2
    slots = back_ref.shape[0]
    piece = pieces.shape[1]
    near = near_count(n)
    greet(n, dp, t, [(t + d) % 4 for d in (1, 2, 3)])
    fetches = [pltpu.make_async_copy(a, b, hs.at[i]) for i, (a, b) in enumerate(zip(later, held))]
    for fetch in fetches:
        fetch.start()

    def peer(k):
        return (partner(dp, k, n), t)

    def moe_copy(j):
        return remote(moe_mine.at[j], moe_other.at[j], as_.at[j], ar.at[j], (dp, far))

    def block_copy(j):
        return remote(block_mine.at[j], block_other.at[j], bs.at[j], br.at[j], (dp, far))

    def attention_copy(j, owner):
        rows = attention_grad.at[image_rows(2 * j + owner)]
        return remote(rows, rows, ts.at[j], tr.at[j], (dp, mate))

    def tokens_copy(j, owner):
        rows = grad_tokens_ref.at[image_rows(2 * j + owner)]
        return remote(rows, rows, cs.at[j], cr.at[j], (dp, mate))

    def block_pair_copy(j, owner):
        rows = block_ref.at[image_rows(2 * j + owner)]
        return remote(rows, rows, ls.at[j], lr.at[j], (dp, mate))

    def gain_copy(d, owner):
        return remote(
            gain_one_all.at[owner], gain_one_all.at[owner], gs.at[d - 1], gr.at[d - 1], (dp, (t + d) % 4)
        )

    def gain_row_copy(k):
        return remote(gain_rows.at[0], gain_rows.at[k], ks.at[k], kr.at[k], peer(k))

    def router_copy():
        return remote(router_sum, router_in, os_.at[0], or_.at[0], (dp, mate))

    def gain_two_copy():
        return remote(gain_two_sum, gain_two_in, os_.at[1], or_.at[1], (dp, mate))

    def piece_copy(k):
        return remote(pieces.at[k], pieces_in.at[k], ws.at[k], wr.at[k], peer(k))

    def small_copy(k):
        return remote(small_pieces.at[k], small_in.at[k], vs.at[k], vr.at[k], peer(k))

    def answer_rows(k, owner):
        return answers.at[pl.ds(pl.multiple_of((2 * k + owner) * hp, hp), hp)]

    def answer_side_copy(k):
        return remote(answer_out.at[k], answer_far.at[k], ds.at[k], dr.at[k], (dp, far))

    def answer_copy(k):
        return remote(answer_final.at[k], answer_rows(k, half), es.at[k], er.at[k], peer(k))

    def answer_pair_copy(k, owner):
        return remote(answer_rows(k, owner), answer_rows(k, owner), fs.at[k], fr.at[k], (dp, mate))

    def loop(body, first=0, last=n):
        def one(k, carry):
            body(k)
            return carry

        lax.fori_loop(first, last, one, 0)

    def both_sides(mine, other):
        low = jnp.where(side == 0, mine, other)
        high = jnp.where(side == 0, other, mine)
        return jnp.concatenate([low, high], axis=1)

    def hots(rows):
        columns = lax.broadcasted_iota(jnp.int32, (PIECE, slots), 1)
        return index_ref[rows, 2:3] == columns, index_ref[rows, 3:4] == columns

    def as_low(mask):
        return jnp.where(mask, 1.0, 0.0).astype(LOW)

    gain_two_sum[...] = jnp.zeros_like(gain_two_sum)
    gain_one_sum[...] = jnp.zeros_like(gain_one_sum)
    router_sum[...] = jnp.zeros_like(router_sum)

    def combine(j):
        first, second = hots(image_rows(2 * j + half))
        moe_mine[j] = dot_plain(as_low(first | second), back_ref[...]).astype(LOW)

        @pl.when(j == 0)
        def _():
            await_greetings(n, (1, 2, 3))

        moe_copy(j).start()

    loop(combine, 0, 3)
    for fetch in fetches[:3]:
        fetch.wait()
    loop(lambda k: answer_side_copy((k + near) % n).start())

    def gates_of(rows, normed):
        logits = dot_last(normed, router_ref[...])
        lanes = lax.broadcasted_iota(jnp.int32, logits.shape, 1)
        hot_one = index_ref[rows, 4:5] == lanes
        hot_two = index_ref[rows, 5:6] == lanes
        one = jnp.sum(jnp.where(hot_one, logits, 0.0), axis=1, keepdims=True)
        two = jnp.sum(jnp.where(hot_two, logits, 0.0), axis=1, keepdims=True)
        top = jnp.maximum(one, two)
        one, two = jnp.exp(one - top), jnp.exp(two - top)
        return one / (one + two), two / (one + two), hot_one, hot_two

    def moe_back(j):
        rows = image_rows(2 * j + half)
        unit, factor = normalized(residual_ref[j])
        normed = (unit * gains_ref[1:2, :]).astype(LOW)
        gate_one, gate_two, hot_one, hot_two = gates_of(rows, normed)
        first, second = hots(rows)
        slot_sums = gate_sum_ref[0:1, :]
        grad_one = jnp.sum(jnp.where(first, slot_sums, 0.0), axis=1, keepdims=True)
        grad_two = jnp.sum(jnp.where(second, slot_sums, 0.0), axis=1, keepdims=True)
        mean = gate_one * grad_one + gate_two * grad_two
        logit_grad = jnp.where(hot_one, gate_one * (grad_one - mean), 0.0)
        logit_grad = logit_grad + jnp.where(hot_two, gate_two * (grad_two - mean), 0.0)
        logit_grad = logit_grad.astype(LOW)
        router_sum[...] += dot_first(normed, logit_grad)
        normed_grad = dot_plain(logit_grad, router_ref[...])
        moe_copy(j).wait_recv()
        normed_grad = normed_grad + both_sides(moe_mine[j].astype(FULL), moe_other[j].astype(FULL))
        gain_two_sum[...] += jnp.sum((normed_grad * unit).reshape(PIECE // 8, 8, model), axis=0)
        grad = normalized_back(normed_grad * gains_ref[1:2, :], unit, factor)
        grad = grad + upstream_ref[rows, :].astype(FULL)
        residual_grad[j] = grad
        attention_grad[rows, :] = grad.astype(LOW)
        attention_copy(j, half).start()

    loop(moe_back, 0, 3)
    router_copy().start()
    gain_two_copy().start()
    for fetch in fetches[3:]:
        fetch.wait()

    def image_back(image):
        rows = image_rows(image)
        mixed_grad = dot_last(attention_grad[rows, :], output_w_ref[...]).astype(LOW)
        queries, keys, values = query_ref[rows, :], key_ref[rows, :], value_ref[rows, :]
        query_parts, key_parts, value_parts = [], [], []
        for h in range(heads):
            cols = slice(h * HD, (h + 1) * HD)
            probs, _ = attention_probs(queries[:, cols], keys[:, cols])
            value_parts.append(dot_first(probs.astype(LOW), mixed_grad[:, cols]))
            probs_grad = dot_last(mixed_grad[:, cols], values[:, cols])
            level = jnp.sum(probs * probs_grad, axis=1, keepdims=True)
            score_grad = (probs * (probs_grad - level)).astype(LOW)
            query_parts.append(dot_plain(score_grad, keys[:, cols]) * HD**-0.5)
            key_parts.append(dot_first(score_grad, queries[:, cols]) * HD**-0.5)
        grads = [jnp.concatenate(p, axis=1).astype(LOW) for p in (query_parts, key_parts, value_parts)]
        query_grad[rows, :], key_grad[rows, :], value_grad[rows, :] = grads

    def answer_turn(k):
        answer_side_copy(k).wait_recv()
        rows = (answer_kept[k] + answer_far[k].astype(FULL)).astype(LOW)

        @pl.when(k == 0)
        def _():
            answer_rows(0, half)[...] = rows

        @pl.when(k > 0)
        def _():
            answer_final[k] = rows
            answer_copy(k).start()

    per_image = -(-n // 4)

    def attention_back(i):
        j = i % 3

        @pl.when(i >= 3)
        def _():
            attention_copy(j, 1 - half).wait_recv()

        image_back(2 * j + jnp.where(i < 3, half, 1 - half))

        def turn(m):
            @pl.when(m < n)
            def _():
                answer_turn((m + near) % n)

        @pl.when(i >= 2)
        def _():
            loop(turn, (i - 2) * per_image, (i - 1) * per_image)

    loop(attention_back, 0, 6)

    normed_one = normed_one_ref[...]
    totals[:, : 3 * query_grad.shape[1]] = jnp.concatenate(
        [
            dot_first(normed_one, query_grad[...]),
            dot_first(normed_one, key_grad[...]),
            dot_first(normed_one, value_grad[...]),
        ],
        axis=1,
    )

    def my_piece(source, k):
        at = partner(dp, k, n) * piece
        grain = math.gcd(piece, 8)
        span = -(-(piece + 8 - grain) // 8) * 8
        taken = source[pl.ds(pl.multiple_of(at // 8 * 8, 8), span), :]
        rows = taken[:piece]
        for shift in range(grain, 8, grain):
            rows = jnp.where(at % 8 == shift, taken[shift : shift + piece], rows)
        return rows.astype(LOW)

    def send_piece(i):
        k = (i + near) % n
        pieces[k] = my_piece(totals, k)

        @pl.when(k > 0)
        def _():
            piece_copy(k).start()

    loop(send_piece)

    def grad_part(image):
        rows = image_rows(image)
        part = dot_plain(query_grad[rows, :], query_w_ref[...])
        part = part + dot_plain(key_grad[rows, :], key_w_ref[...])
        part = part + dot_plain(value_grad[rows, :], value_w_ref[...])
        unit, _ = normalized(tokens_ref[rows, :].astype(FULL))
        gain_one_sum[...] += jnp.sum((part * unit).reshape(PIECE // 8, 8, model), axis=0)
        return part

    def sum_images(j):
        total.give(j, grad_part(2 * j + 1 - half))
        total.take(j, grad_part(2 * j + half))

    loop(sum_images, 0, 3)
    gain_one_all[t] = gain_one_sum[...]
    for d in (1, 2, 3):
        gain_copy(d, t).start()

    router_copy().wait_recv()
    gain_two_copy().wait_recv()
    row = jnp.sum(gain_two_sum[...] + gain_two_in[...], axis=0, keepdims=True)
    column = jnp.concatenate(
        [row_to_column(row[:, i : i + 256]) for i in range(0, model, 256)], axis=0
    )
    totals_two[...] = jnp.concatenate(
        [
            dot_first(attention_grad[...], mixed_ref[...]),
            router_sum[...] + router_in[...],
            column,
        ],
        axis=1,
    )

    def send_small(i):
        k = (i + near) % n
        small_pieces[k] = my_piece(totals_two, k)

        @pl.when(k > 0)
        def _():
            small_copy(k).start()

    loop(send_small)

    def answers_here(i):
        k = in_turn(i, near)

        @pl.when(k > 0)
        def _():
            answer_copy(k).wait_recv()

        answer_pair_copy(k, half).start()

    loop(answers_here)
    for d in (1, 2, 3):
        gain_copy(d, (t + 4 - d) % 4).wait_recv()
    gain_rows[0] = (gain_one_all[0] + gain_one_all[1]) + (gain_one_all[2] + gain_one_all[3])

    def send_gain(k):
        gain_row_copy(k).start()

    loop(send_gain, 1)
    loop(lambda k: answer_pair_copy(k, 1 - half).wait_recv())

    def block_rows(j):
        rows = image_rows(2 * j + half)
        residual = residual_ref[j]
        unit, _ = normalized(residual)
        gate_one, gate_two, _, _ = gates_of(rows, (unit * gains_ref[1:2, :]).astype(LOW))
        first, second = hots(rows)
        from_first = dot_plain(as_low(first), answers[...])
        from_second = dot_plain(as_low(second), answers[...])
        mine = jnp.where(side == 0, residual[:, :width], residual[:, width:])
        block_mine[j] = (mine + (gate_one * from_first + gate_two * from_second)).astype(LOW)
        block_copy(j).start()

    loop(block_rows, 0, 3)

    def tokens_back(j):
        rows = image_rows(2 * j + half)
        normed_grad = total.result(j)
        unit, factor = normalized(tokens_ref[rows, :].astype(FULL))
        grad = normalized_back(normed_grad * gains_ref[0:1, :], unit, factor)
        grad_tokens_ref[rows, :] = (residual_grad[j] + grad).astype(LOW)
        tokens_copy(j, half).start()

    loop(tokens_back, 0, 3)

    def block_back(j):
        block_copy(j).wait_recv()
        block_ref[image_rows(2 * j + half), :] = both_sides(block_mine[j], block_other[j])
        block_pair_copy(j, half).start()

    loop(block_back, 0, 3)
    pieces_in[0] = pieces[0]
    small_in[0] = small_pieces[0]

    def arrive(k):
        piece_copy(k).wait_recv()
        small_copy(k).wait_recv()
        gain_row_copy(k).wait_recv()

    loop(arrive, 1)
    weights_ref[...] = jnp.sum(pieces_in[...].astype(FULL), axis=0)
    small_ref[...] = jnp.sum(small_in[...].astype(FULL), axis=0)
    gain_ref[...] = jnp.sum(gain_rows[...], axis=0)
    for j in range(3):
        tokens_copy(j, 1 - half).wait_recv()
        block_pair_copy(j, 1 - half).wait_recv()
    unpad(grad_tokens_ref, tokens_out_ref)
    unpad(block_ref, block_out_ref)

    for j in range(3):
        moe_copy(j).wait_send()
        block_copy(j).wait_send()
        attention_copy(j, half).wait_send()
        total.sent(j)
        tokens_copy(j, half).wait_send()
        block_pair_copy(j, half).wait_send()
        gain_copy(j + 1, t).wait_send()
    router_copy().wait_send()
    gain_two_copy().wait_send()

    def left(k):
        answer_side_copy(k).wait_send()
        answer_pair_copy(k, half).wait_send()

        @pl.when(k > 0)
        def _():
            piece_copy(k).wait_send()
            small_copy(k).wait_send()
            gain_row_copy(k).wait_send()
            answer_copy(k).wait_send()

    loop(left)


def run_back(n, hp, row_count, first, later):
    upstream = later[1]
    rows, model = upstream.shape
    heads_width = later[8].shape[1]
    width = model // 2
    piece = model // n
    vmem = pl.BlockSpec(memory_space=VMEM)
    shape = jax.ShapeDtypeStruct
    slim = VMEM((3, PIECE, width), LOW)
    heads = VMEM((rows, heads_width), LOW)
    eight = VMEM((8, model), FULL)
    wide, narrow = 3 * heads_width, heads_width + n + 1
    quarter = VMEM((n, hp, width), LOW)
    three, many = dma(3), dma(n)
    return pl.pallas_call(
        functools.partial(back_kernel, n, hp),
        out_shape=(
            shape((row_count, model), LOW),
            shape((row_count, model), LOW),
            shape((piece, wide), FULL),
            shape((piece, narrow), FULL),
            shape((8, model), FULL),
        ),
        in_specs=[vmem] * len(first) + [pl.BlockSpec(memory_space=pl.ANY)] * len(later),
        out_specs=[vmem] * 5,
        scratch_shapes=[
            *[VMEM(a.shape, a.dtype) for a in later],
            slim, slim, slim, slim,
            VMEM((rows, model), LOW),
            VMEM((3, PIECE, model), FULL),
            heads, heads, heads,
            eight, eight, eight,
            VMEM((4, 8, model), FULL),
            VMEM((n, 8, model), FULL),
            VMEM((model, n), FULL),
            VMEM((model, n), FULL),
            VMEM((model, wide), FULL),
            VMEM((model, narrow), FULL),
            VMEM((n, piece, wide), LOW),
            VMEM((n, piece, wide), LOW),
            VMEM((n, piece, narrow), LOW),
            VMEM((n, piece, narrow), LOW),
            quarter, quarter,
            VMEM((n * 2 * hp, width), LOW),
            VMEM((rows, model), LOW),
            VMEM((rows, model), LOW),
            dma(len(later)),
            three, three, three, three, three, three, three, three, three, three,
            many, many, three, three, dma(2), dma(2),
            many, many, many, many, many, many, many, many, many, many,
            *Total.scratch(model),
        ],
        compiler_params=pltpu.CompilerParams(
            collective_id=2, has_side_effects=True, vmem_limit_bytes=VMEM_LIMIT
        ),
        name="back",
    )(*first, *later)


def body(
    tokens,
    gain_attn,
    w_query,
    w_key,
    w_value,
    w_output,
    gain_moe,
    w_router,
    expert_in,
    expert_out,
    routes,
    slot_ids,
    capacity,
    threshold,
    cotangent,
):
    n = lax.axis_size("dp")
    row_count, model = tokens.shape
    heads_here = w_query.shape[1] // HD
    slot_count = 23 * TOK_DEV // (10 * n) + 1
    per_half = -(-slot_count // 2)
    hp = -(-per_half // 16) * 16
    dp_here = lax.axis_index("dp")
    gains = jnp.stack([gain_attn, gain_moe]).astype(FULL)
    across = (w_query.T, w_key.T, w_value.T)
    (
        place,
        index,
        peak,
        tokens_in,
        upstream,
        normed_one,
        query,
        key,
        value,
        mixed,
        residual,
        normed_two,
        spread,
    ) = run_front(
        n,
        hp,
        per_half,
        capacity,
        routes.T,
        slot_ids.T,
        tokens,
        cotangent,
        gains,
        (*across, w_output),
    )
    router = w_router.T
    back, gate_sums, top, answer_out, answer_kept, grad_first, grad_second = run_experts(
        n, hp, place, router, peak, normed_two, expert_in[0], expert_out[0], spread
    )
    block_out, grad_tokens, weight_grads, small, gain_rows = run_back(
        n,
        hp,
        row_count,
        (back.reshape(n * 2 * hp, -1), gate_sums, index, gains, w_output, router),
        (
            residual,
            upstream,
            answer_out,
            answer_kept,
            normed_one,
            query,
            key,
            value,
            mixed,
            tokens_in,
            *across,
        ),
    )
    head_max = top[:heads_here, 0]
    column_factor = jnp.repeat(jnp.sqrt(jnp.minimum(1.0, threshold / head_max)), HD)[None, :]
    wide = w_query.shape[1]
    piece = model // n
    return (
        block_out,
        grad_tokens,
        lax.dynamic_slice_in_dim(gain_rows.sum(axis=0), dp_here * piece, piece),
        small[:, wide + n],
        weight_grads[:, :wide],
        weight_grads[:, wide : 2 * wide],
        weight_grads[:, 2 * wide :],
        small[:, :wide].T,
        small[:, wide : wide + n],
        grad_first[None],
        grad_second[None],
        w_query.astype(FULL) * column_factor,
        w_key.astype(FULL) * column_factor,
        head_max,
    )


def solution(mesh):
    in_specs = (
        P("dp", None),
        P(),
        P(None, "tensor"),
        P(None, "tensor"),
        P(None, "tensor"),
        P("tensor", None),
        P(),
        P(),
        P("dp", None, "tensor"),
        P("dp", "tensor", None),
        P("dp", None),
        P("dp", None),
        P(),
        P("tensor"),
        P("dp", None),
    )
    out_specs = (
        P("dp", None),
        P("dp", None),
        P("dp"),
        P("dp"),
        P("dp", "tensor"),
        P("dp", "tensor"),
        P("dp", "tensor"),
        P("tensor", "dp"),
        P("dp", None),
        P("dp", None, "tensor"),
        P("dp", "tensor", None),
        P(None, "tensor"),
        P(None, "tensor"),
        P("tensor"),
    )
    return jax.shard_map(body, mesh=mesh, in_specs=in_specs, out_specs=out_specs, check_vma=False)
```

```python
import functools
import math

import jax
import jax.numpy as jnp
from jax import lax
from jax.experimental import pallas as pl
from jax.experimental.pallas import tpu as pltpu
from jax.sharding import PartitionSpec as P

HD = 64
SEQ = 197
PIECE = 208
TOK_DEV = 1182
EPSILON = 1e-06
MESH = pl.DeviceIdType.MESH
VMEM_LIMIT = 60 * 2**20
SLOTS = 3
LAG = 4
VMEM = pltpu.VMEM
LOW, FULL = jnp.bfloat16, jnp.float32


def dot_plain(a, b):
    return jnp.dot(a, b, preferred_element_type=FULL)


def dot_last(a, b):
    return lax.dot_general(a, b, (((1,), (1,)), ((), ())), preferred_element_type=FULL)


def dot_first(a, b):
    return lax.dot_general(a, b, (((0,), (0,)), ((), ())), preferred_element_type=FULL)


def normalized(rows):
    centered = rows - jnp.mean(rows, axis=-1, keepdims=True)
    factor = lax.rsqrt(jnp.mean(centered * centered, axis=-1, keepdims=True) + EPSILON)
    return centered * factor, factor


def normalized_back(u, unit, factor):
    first = jnp.mean(u, axis=-1, keepdims=True)
    second = jnp.mean(u * unit, axis=-1, keepdims=True)
    return factor * (u - first - unit * second)


def same_index(size):
    rows = lax.broadcasted_iota(jnp.int32, (size, size), 0)
    return rows == lax.broadcasted_iota(jnp.int32, (size, size), 1)


def row_to_column(row):
    return jnp.sum(jnp.where(same_index(row.shape[1]), row, 0.0), axis=1, keepdims=True)


def column_to_row(column):
    return jnp.sum(jnp.where(same_index(column.shape[0]), column, 0.0), axis=0, keepdims=True)


def attention_probs(queries, keys):
    scores = dot_last(queries, keys) * HD**-0.5
    real = lax.broadcasted_iota(jnp.int32, scores.shape, 1) < SEQ
    scores = jnp.where(real, scores, -1e30)
    top = jnp.max(scores, axis=1, keepdims=True)
    powers = jnp.exp(scores - top)
    return powers * (1.0 / jnp.sum(powers, axis=1, keepdims=True)), top


def partner(dp, k, n):
    other, weight = 0, 1
    while weight < n:
        other = other + ((dp // weight + k // weight) % 2) * weight
        weight *= 2
    return other


def places():
    dp = lax.axis_index("dp")
    t = lax.axis_index("tensor")
    return dp, t, t % 2, t // 2, t + 1 - 2 * (t % 2), (t + 2) % 4


def remote(src, dst, sends, recvs, device):
    return pltpu.make_async_remote_copy(
        src_ref=src,
        dst_ref=dst,
        send_sem=sends,
        recv_sem=recvs,
        device_id=device,
        device_id_type=MESH,
    )


def signal(sem, device):
    pl.semaphore_signal(sem, inc=1, device_id=device, device_id_type=MESH)


def greet(n, dp, t, others):
    barrier = pltpu.get_barrier_semaphore()

    def one(k, carry):
        signal(barrier, (partner(dp, k, n), t))
        return carry

    lax.fori_loop(1, n, one, 0)
    for other in others:
        signal(barrier, (dp, other))


def await_greetings(n, others):
    pl.semaphore_wait(pltpu.get_barrier_semaphore(), n - 1 + len(others))


def image_rows(image):
    return pl.ds(pl.multiple_of(image * PIECE, PIECE), PIECE)


def dma(*shape):
    return pltpu.SemaphoreType.DMA(shape)


def near_count(n):
    return min(4, n)


class Spread:
    def __init__(self, n, hp, place, near_out, far_out, arrived, zs, zr, xs, xr, cs, cr, own):
        self.n, self.hp, self.near = n, hp, near_count(n)
        self.place, self.near_out, self.far_out, self.arrived = place, near_out, far_out, arrived
        self.zs, self.zr, self.xs, self.xr, self.cs, self.cr, self.own = zs, zr, xs, xr, cs, cr, own
        self.dp, self.t, self.half, self.side, self.mate, self.far = places()
        self.width = far_out.shape[2]

    def rows(self, owner):
        return pl.ds(pl.multiple_of(owner * self.hp, self.hp), self.hp)

    def columns(self, owner):
        return pl.ds(pl.multiple_of(owner * self.width, self.width), self.width)

    def peer(self, k):
        return (partner(self.dp, k, self.n), self.t)

    def own_copy(self):
        return pltpu.make_async_copy(
            self.near_out.at[0], self.arrived.at[0, self.rows(self.half)], self.own
        )

    def near_copy(self, k):
        return remote(
            self.near_out.at[k],
            self.arrived.at[k, self.rows(self.half)],
            self.zs.at[k],
            self.zr.at[k],
            self.peer(k),
        )

    def far_copy(self, k):
        return remote(
            self.far_out.at[k - self.near],
            self.arrived.at[k, self.rows(self.half), self.columns(self.side)],
            self.zs.at[k],
            self.zr.at[k],
            self.peer(k),
        )

    def side_copy(self, k, side):
        part = self.arrived.at[k, self.rows(self.half), self.columns(side)]
        return remote(part, part, self.xs.at[k], self.xr.at[k], (self.dp, self.far))

    def pair_copy(self, k, half):
        part = self.arrived.at[k, self.rows(half)]
        return remote(part, part, self.cs.at[k], self.cr.at[k], (self.dp, self.mate))

    def hot(self, k, row_count):
        slots = lax.broadcasted_iota(jnp.int32, (self.hp, row_count), 0) + k * self.hp
        is_first = self.place[0:1, :] == slots
        is_second = self.place[1:2, :] == slots
        return is_first, is_second

    def send(self, k, rows_ref):
        is_first, is_second = self.hot(k, rows_ref.shape[0])
        hot = jnp.where(is_first | is_second, 1.0, 0.0).astype(LOW)

        @pl.when(k < self.near)
        def _():
            self.near_out[k] = dot_plain(hot, rows_ref[...]).astype(LOW)

            @pl.when(k == 0)
            def _():
                self.own_copy().start()

            @pl.when(k > 0)
            def _():
                self.near_copy(k).start()

        @pl.when(k >= self.near)
        def _():
            mine = rows_ref[:, self.columns(self.side)]
            self.far_out[k - self.near] = dot_plain(hot, mine).astype(LOW)
            self.far_copy(k).start()

        return is_first, is_second

    def first_hop(self, k):
        @pl.when(k == 0)
        def _():
            self.own_copy().wait()

        @pl.when((k > 0) & (k < self.near))
        def _():
            self.near_copy(k).wait_recv()

        @pl.when(k >= self.near)
        def _():
            self.far_copy(k).wait_recv()
            self.side_copy(k, self.side).start()

    def second_hop(self, k):
        @pl.when(k >= self.near)
        def _():
            self.side_copy(k, 1 - self.side).wait_recv()

        self.pair_copy(k, self.half).start()

    def last_hop(self, k):
        self.pair_copy(k, 1 - self.half).wait_recv()

    def sent(self, k):
        @pl.when((k > 0) & (k < self.near))
        def _():
            self.near_copy(k).wait_send()

        @pl.when(k >= self.near)
        def _():
            self.far_copy(k).wait_send()
            self.side_copy(k, self.side).wait_send()

        self.pair_copy(k, self.half).wait_send()

    @staticmethod
    def scratch(n, hp, width):
        near = near_count(n)
        return [VMEM((near, hp, 2 * width), LOW), VMEM((n - near, hp, width), LOW)]

    @staticmethod
    def semaphores(n):
        return [dma(n), dma(n), dma(n), dma(n), dma(n), dma(n), pltpu.SemaphoreType.DMA]


class Total:
    def __init__(self, part_out, pair_in, far_out, far_in, ps, pr, fs, fr):
        self.part_out, self.pair_in, self.far_out, self.far_in = part_out, pair_in, far_out, far_in
        self.ps, self.pr, self.fs, self.fr = ps, pr, fs, fr
        self.dp, _, _, _, self.mate, self.far = places()

    def pair_copy(self, j):
        return remote(
            self.part_out.at[j], self.pair_in.at[j], self.ps.at[j], self.pr.at[j], (self.dp, self.mate)
        )

    def far_copy(self, j):
        return remote(
            self.far_out.at[j], self.far_in.at[j], self.fs.at[j], self.fr.at[j], (self.dp, self.far)
        )

    def give(self, j, rows):
        self.part_out[j] = rows
        self.pair_copy(j).start()

    def take(self, j, rows):
        self.pair_copy(j).wait_recv()
        self.far_out[j] = (rows + self.pair_in[j]).astype(LOW)
        self.far_copy(j).start()

    def result(self, j):
        self.far_copy(j).wait_recv()
        return self.far_out[j].astype(FULL) + self.far_in[j].astype(FULL)

    def sent(self, j):
        self.pair_copy(j).wait_send()
        self.far_copy(j).wait_send()

    @staticmethod
    def scratch(model):
        wide, slim = VMEM((3, PIECE, model), FULL), VMEM((3, PIECE, model), LOW)
        return [wide, wide, slim, slim, dma(3), dma(3), dma(3), dma(3)]


def padded_image(rows_ref, image):
    start = image * SEQ // 8 * 8
    length = min(PIECE, rows_ref.shape[0] - start)
    rows = lax.broadcasted_iota(jnp.int32, (PIECE, length), 0)
    columns = lax.broadcasted_iota(jnp.int32, (PIECE, length), 1)
    pick = (columns == rows + (image * SEQ - start)) & (rows < SEQ)
    return dot_plain(jnp.where(pick, 1.0, 0.0).astype(LOW), rows_ref[start : start + length, :])


def front_kernel(
    n,
    hp,
    per_half,
    capacity_ref,
    routes_ref,
    slot_ids_ref,
    tokens_ref,
    upstream_ref,
    gains_ref,
    query_w_ref,
    key_w_ref,
    value_w_ref,
    output_w_ref,
    place_ref,
    index_ref,
    peak_ref,
    *refs,
):
    outs, spread_hbm, scratch = refs[:9], refs[9], refs[10:]
    held, scratch = scratch[:9], scratch[9:]
    (
        tokens,
        upstream,
        normed_one,
        query,
        key,
        value,
        mixed_rows,
        residual_rows,
        normed_two,
    ) = held
    near_out, far_out, zs, zr, own, ns, nr, hs, xs, xr = scratch[:10]
    total = Total(*scratch[10:])
    dp, t, half, side, mate, far = places()
    heads = query_w_ref.shape[0] // HD
    near = near_count(n)
    width = far_out.shape[2]
    row_count = tokens.shape[0]
    greet(n, dp, t, (mate, far))
    peak_ref[...] = jnp.full(peak_ref.shape, -1e30, FULL)
    for image in range(row_count // PIECE):
        tokens[image * PIECE : (image + 1) * PIECE, :] = padded_image(tokens_ref, image).astype(LOW)

    def image_forward(image):
        rows = image_rows(image)
        unit, _ = normalized(tokens[rows, :].astype(FULL))
        normed = (unit * gains_ref[0:1, :]).astype(LOW)
        normed_one[rows, :] = normed
        queries = dot_last(normed, query_w_ref[...]).astype(LOW)
        keys = dot_last(normed, key_w_ref[...]).astype(LOW)
        values = dot_last(normed, value_w_ref[...]).astype(LOW)
        query[rows, :] = queries
        key[rows, :] = keys
        value[rows, :] = values
        mixed = []
        for h in range(heads):
            cols = slice(h * HD, (h + 1) * HD)
            probs, top = attention_probs(queries[:, cols], keys[:, cols])
            real = lax.broadcasted_iota(jnp.int32, top.shape, 0) < SEQ
            best = jnp.max(jnp.where(real, top, -1e30), axis=0, keepdims=True)
            peak_ref[h : h + 1, :] = jnp.maximum(peak_ref[h : h + 1, :], best)
            mixed.append(dot_plain(probs.astype(LOW), values[:, cols]))
        mixed = jnp.concatenate(mixed, axis=1).astype(LOW)
        mixed_rows[rows, :] = mixed
        return dot_plain(mixed, output_w_ref[...])

    def normed_copy(j, owner):
        rows = normed_two.at[image_rows(2 * j + owner)]
        return remote(rows, rows, ns.at[j], nr.at[j], (dp, mate))

    def keep(i):
        return pltpu.make_async_copy(held[i], outs[i], hs.at[i])

    def finish(j):
        rows = image_rows(2 * j + half)
        residual = tokens[rows, :].astype(FULL) + total.result(j)
        residual_rows[j] = residual
        unit, _ = normalized(residual)
        normed_two[rows, :] = (unit * gains_ref[1:2, :]).astype(LOW)
        normed_copy(j, half).start()

    def peer(k):
        return (partner(dp, k, n), t)

    def half_rows():
        return pl.ds(pl.multiple_of(half * hp, hp), hp)

    def side_columns():
        return pl.ds(pl.multiple_of(side * width, width), width)

    def own_copy():
        return pltpu.make_async_copy(near_out.at[0], spread_hbm.at[0, half_rows()], own)

    def near_copy(k):
        return remote(near_out.at[k], spread_hbm.at[k, half_rows()], zs.at[k], zr.at[k], peer(k))

    def far_copy(k):
        return remote(
            far_out.at[k - near],
            spread_hbm.at[k, half_rows(), side_columns()],
            zs.at[k],
            zr.at[k],
            peer(k),
        )

    def side_copy(k, owner):
        columns = pl.ds(pl.multiple_of(owner * width, width), width)
        part = spread_hbm.at[k, half_rows(), columns]
        return remote(part, part, xs.at[k], xr.at[k], (dp, far))

    def forward(k, carry):
        far_copy(k).wait_recv()
        side_copy(k, side).start()
        return carry

    def dispatch(k):
        slots = lax.broadcasted_iota(jnp.int32, (hp, row_count), 0) + k * hp
        hot = (place_ref[0:1, :] == slots) | (place_ref[1:2, :] == slots)
        hot = jnp.where(hot, 1.0, 0.0).astype(LOW)

        @pl.when(k < near)
        def _():
            near_out[k] = dot_plain(hot, upstream[...]).astype(LOW)

            @pl.when(k == 0)
            def _():
                own_copy().start()

            @pl.when(k > 0)
            def _():
                near_copy(k).start()

        @pl.when(k >= near)
        def _():
            far_out[k - near] = dot_plain(hot, upstream[:, side_columns()]).astype(LOW)
            far_copy(k).start()

    def places_of_pairs():
        routes, slot_ids = routes_ref[...], slot_ids_ref[...]
        limits = jnp.zeros_like(routes)
        for e in range(n):
            limits = jnp.where(routes == e, capacity_ref[e], limits)
        kept = slot_ids < limits
        step = jnp.zeros_like(routes)
        weight = 1
        while weight < n:
            step = step + (routes // weight + dp // weight) % 2 * weight
            weight *= 2
        upper = slot_ids >= per_half
        in_half = slot_ids - jnp.where(upper, per_half, 0)
        in_block = in_half + jnp.where(upper, hp, 0)
        mine = kept & (upper == (half == 1))
        place = jnp.where(mine, step * hp + in_half, -1)
        position = jnp.where(kept, step * (2 * hp) + in_block, -1)
        both = jnp.concatenate([place, position, routes, jnp.full_like(routes, -1)], axis=0)
        fill = jnp.full((8, PIECE - SEQ), -1, jnp.int32)
        spaced = []
        for image in range(row_count // PIECE):
            spaced += [both[:, image * SEQ : (image + 1) * SEQ], fill]
        return jnp.concatenate(spaced, axis=1)

    pairs = places_of_pairs()
    place_ref[...] = pairs
    index_ref[...] = pairs.T
    def step(j, carry):
        given = image_forward(2 * j + 1 - half)

        @pl.when(j == 0)
        def _():
            await_greetings(n, (mate, far))

        total.give(j, given)
        total.take(j, image_forward(2 * j + half))

        @pl.when(j == 0)
        def _():
            for image in range(row_count // PIECE):
                upstream[image * PIECE : (image + 1) * PIECE, :] = padded_image(
                    upstream_ref, image
                ).astype(LOW)

        def turn(k, inner):
            dispatch(k)
            return inner

        @pl.when(j == 0)
        def _():
            lax.fori_loop(near, n, turn, 0)

        @pl.when(j == 1)
        def _():
            lax.fori_loop(0, near, turn, 0)

        @pl.when(j >= 1)
        def _():
            finish(j - 1)

        return carry

    lax.fori_loop(0, 3, step, 0)
    for i in range(7):
        keep(i).start()
    early = n - (n - near) // 4
    lax.fori_loop(near, early, forward, 0)
    finish(2)
    lax.fori_loop(early, n, forward, 0)
    keep(7).start()
    own_copy().wait()

    def arrive(k, carry):
        near_copy(k).wait()
        return carry

    def far_arrive(k, carry):
        far_copy(k).wait_send()
        side_copy(k, side).wait_send()
        side_copy(k, 1 - side).wait_recv()
        return carry

    for j in range(3):
        normed_copy(j, 1 - half).wait_recv()
    keep(8).start()
    lax.fori_loop(1, near, arrive, 0)
    lax.fori_loop(near, n, far_arrive, 0)
    for j in range(3):
        total.sent(j)
        normed_copy(j, half).wait_send()
    for i in range(9):
        keep(i).wait()


def run_front(n, hp, per_half, capacity, routes, slot_ids, tokens, upstream, gains, weights):
    model = tokens.shape[1]
    rows = tokens.shape[0] // SEQ * PIECE
    heads_width = weights[0].shape[0]
    near = near_count(n)
    width = model // 2
    vmem = pl.BlockSpec(memory_space=VMEM)
    hbm = pl.BlockSpec(memory_space=pl.ANY)
    shape = jax.ShapeDtypeStruct
    slim, wide = shape((rows, heads_width), LOW), shape((rows, model), LOW)
    held = (wide, wide, wide, slim, slim, slim, slim, shape((3, PIECE, model), FULL), wide)
    return pl.pallas_call(
        functools.partial(front_kernel, n, hp, per_half),
        out_shape=(
            shape((8, rows), jnp.int32),
            shape((rows, 8), jnp.int32),
            shape((8, 128), FULL),
            *held,
            shape((n, 2 * hp, model), LOW),
        ),
        in_specs=[pl.BlockSpec(memory_space=pltpu.SMEM)] + [vmem] * 9,
        out_specs=[vmem] * 3 + [hbm] * 10,
        scratch_shapes=[
            *[VMEM(a.shape, a.dtype) for a in held],
            VMEM((near, hp, model), LOW),
            VMEM((n - near, hp, width), LOW),
            dma(n),
            dma(n),
            pltpu.SemaphoreType.DMA,
            dma(3),
            dma(3),
            dma(9),
            dma(n),
            dma(n),
            *Total.scratch(model),
        ],
        compiler_params=pltpu.CompilerParams(
            collective_id=0, has_side_effects=True, vmem_limit_bytes=VMEM_LIMIT
        ),
        name="front",
    )(capacity, routes, slot_ids, tokens, upstream, gains, *weights)


def in_turn(i, near):
    return jnp.where(i < 2 * near, i // 2 + (i % 2) * near, i)


def expert_kernel(
    n,
    hp,
    place_ref,
    router_ref,
    peak_ref,
    normed_hbm,
    first_hbm,
    second_hbm,
    upstream_hbm,
    back_ref,
    gate_sum_ref,
    top_ref,
    answer_out_hbm,
    answer_kept_hbm,
    answer_ready_hbm,
    grad_first_hbm,
    grad_second_hbm,
    *scratch,
):
    dp, t, half, side, mate, far = places()
    arrived = scratch[2]
    spread = Spread(n, hp, place_ref, *scratch[:10])
    (
        normed_ref,
        first_ref,
        second_ref,
        answer_out,
        answer_kept,
        grad_first_ref,
        grad_second_ref,
        os_,
        ws,
        cs,
        cr,
        answer_far,
        answer_ready,
        xs,
        xr,
    ) = scratch[44:]
    (
        upstream,
        hidden_all,
        pre_grad_all,
        parts,
        pair_in,
        kept,
        far_out,
        far_in,
        final,
        gate_out,
        gate_in,
        sum_out,
        sum_in,
        sums,
        peaks,
        us,
        ps,
        pr,
        fs,
        fr,
        rs,
        rr,
        ms,
        mr,
        gs,
        gr,
        hs,
        hr,
        ks,
        kr,
        qs,
        qr,
        ss,
        sr,
    ) = scratch[10:44]
    model = normed_ref.shape[1]
    width = model // 2
    near = spread.near
    greet(n, dp, t, [(t + d) % 4 for d in (1, 2, 3)])
    fetches = [
        pltpu.make_async_copy(a, b, ws.at[i])
        for i, (a, b) in enumerate(
            ((normed_hbm, normed_ref), (first_hbm, first_ref), (second_hbm, second_ref))
        )
    ]
    mine = (slice(0, n), spread.rows(half))
    fetches.append(pltpu.make_async_copy(upstream_hbm.at[mine], upstream.at[mine], us.at[0]))
    for fetch in fetches:
        fetch.start()

    def upstream_pair_copy(k, owner):
        part = upstream.at[k, spread.rows(owner)]
        return remote(part, part, cs.at[k], cr.at[k], (dp, mate))

    def answer_side_copy(k):
        return remote(
            answer_out.at[k], answer_far.at[k - near], xs.at[k], xr.at[k], (dp, far)
        )

    def keep(i):
        pairs = (
            (answer_out.at[slice(0, near)], answer_out_hbm),
            (answer_kept.at[slice(0, near)], answer_kept_hbm),
            (answer_ready, answer_ready_hbm),
        )
        return pltpu.make_async_copy(*pairs[i], os_.at[i])

    def gate_copy(k):
        return remote(gate_out.at[k], gate_in.at[k, half], gs.at[k], gr.at[k], spread.peer(k))

    def gate_pair_copy(k, owner):
        tile = gate_in.at[k, owner]
        return remote(tile, tile, hs.at[k], hr.at[k], (dp, mate))

    def part_copy(i, k):
        return remote(
            parts.at[i % 3, :, spread.rows(1 - half)],
            pair_in.at[k],
            ps.at[i % 3],
            pr.at[k],
            (dp, mate),
        )

    def far_copy(i, k):
        return remote(far_out.at[i % SLOTS], far_in.at[k], fs.at[i % SLOTS], fr.at[k], (dp, far))

    def return_copy(k):
        return remote(
            final.at[k], back_ref.at[k, spread.rows(half)], rs.at[k], rr.at[k], spread.peer(k)
        )

    def mate_copy(k, owner):
        rows = back_ref.at[k, spread.rows(owner)]
        return remote(rows, rows, ms.at[k], mr.at[k], (dp, mate))

    def sum_copy(k):
        return remote(sum_out.at[k], sum_in.at[k], ks.at[k], kr.at[k], spread.peer(k))

    def peak_copy(k):
        return remote(peak_ref, peaks.at[k], qs.at[k], qr.at[k], spread.peer(k))

    def share_copy(d, owner):
        return remote(
            sums.at[owner], sums.at[owner], ss.at[d - 1], sr.at[d - 1], (dp, (t + d) % 4)
        )

    def loop(body, first=0, last=n):
        def one(k, carry):
            body(k)
            return carry

        lax.fori_loop(first, last, one, 0)

    fetches[0].wait()
    logits = dot_last(router_ref[...], normed_ref[...])
    rows_of = lax.broadcasted_iota(jnp.int32, logits.shape, 0)
    one, two = (
        jnp.sum(jnp.where(rows_of == place_ref[r : r + 1, :], logits, 0.0), axis=0, keepdims=True)
        for r in (4, 5)
    )
    best = jnp.maximum(one, two)
    one, two = jnp.exp(one - best), jnp.exp(two - best)
    gate_one, gate_two = one / (one + two), two / (one + two)
    await_greetings(n, (1, 2, 3))

    def dispatch(i):
        k = (i + near) % n
        is_first, is_second = spread.send(k, normed_ref)
        gate = jnp.sum(
            jnp.where(is_first, gate_one, 0.0) + jnp.where(is_second, gate_two, 0.0),
            axis=1,
            keepdims=True,
        )
        tile = jnp.broadcast_to(column_to_row(gate), (8, hp))

        @pl.when(k == 0)
        def _():
            gate_in[0, half] = tile

        @pl.when(k > 0)
        def _():
            gate_out[k] = tile
            gate_copy(k).start()

    loop(dispatch)
    for fetch in fetches[1:]:
        fetch.wait()
    loop(lambda i: upstream_pair_copy(in_turn(i, near), half).start())

    def chunk(i, k):
        gate = jnp.concatenate(
            [row_to_column(gate_in[k, 0, 0:1, :]), row_to_column(gate_in[k, 1, 0:1, :])], axis=0
        )
        gradient = upstream[k].astype(FULL)
        answer_grad = (gradient * gate).astype(LOW)
        pre = dot_plain(arrived[k], first_ref[...])
        share = 0.5 * (1.0 + lax.erf(pre * math.sqrt(0.5)))
        slope = share + pre * (jnp.exp(-0.5 * pre * pre) * (1.0 / math.sqrt(2.0 * math.pi)))
        hidden = (pre * share).astype(LOW)
        hidden_all[k] = hidden
        answer = dot_plain(hidden, second_ref[...])
        parts[i % 3, 0] = answer.astype(LOW)
        gate_sum = jnp.sum(answer * gradient, axis=1, keepdims=True)
        upstream[k] = answer_grad
        pre_grad = (dot_last(answer_grad, second_ref[...]) * slope).astype(LOW)
        pre_grad_all[k] = pre_grad
        parts[i % 3, 1] = dot_last(pre_grad, first_ref[...]).astype(LOW)
        tile = jnp.broadcast_to(column_to_row(gate_sum), (8, 2 * hp))

        @pl.when(k == 0)
        def _():
            sum_in[0] = tile

        @pl.when(k > 0)
        def _():
            sum_out[k] = tile
            sum_copy(k).start()
            peak_copy(k).start()

    tile = 256
    tiles = model // tile

    def grad_copy(m, j):
        cols = pl.ds(pl.multiple_of(m * tile, tile), tile)
        ref, hbm = ((grad_first_ref, grad_first_hbm), (grad_second_ref, grad_second_hbm))[j]
        return pltpu.make_async_copy(ref.at[cols], hbm.at[cols], os_.at[3 + 2 * m + j])

    def grads(m):
        cols = pl.ds(pl.multiple_of(m * tile, tile), tile)
        rows_in = arrived[:, :, cols].reshape(n * 2 * hp, tile)
        grad_first_ref[cols, :] = dot_first(rows_in, pre_grad_all[...].reshape(n * 2 * hp, -1))
        grad_copy(m, 0).start()
        hidden = hidden_all[:, :, cols].reshape(n * 2 * hp, tile)
        grad_second_ref[cols, :] = dot_first(hidden, upstream[...].reshape(n * 2 * hp, model))
        grad_copy(m, 1).start()

    def step(i):
        @pl.when(i < n)
        def _():
            spread.first_hop(in_turn(i, near))

        @pl.when((i >= 1) & (i < n + 1))
        def _():
            k = in_turn(i - 1, near)
            spread.second_hop(k)

            @pl.when(k > 0)
            def _():
                gate_copy(k).wait_recv()

            gate_pair_copy(k, half).start()

        @pl.when((i >= 2) & (i < n + 2))
        def _():
            k = in_turn(i - 2, near)
            spread.last_hop(k)
            gate_pair_copy(k, 1 - half).wait_recv()
            upstream_pair_copy(k, 1 - half).wait_recv()
            upstream_pair_copy(k, half).wait_send()

            @pl.when(i >= 5)
            def _():
                part_copy(i - 5, in_turn(i - 5, near)).wait_send()

            chunk(i - 2, k)
            part_copy(i - 2, k).start()

        @pl.when((i >= 3) & (i < n + 3))
        def _():
            k = in_turn(i - 3, near)
            part_copy(i - 3, k).wait_recv()

            @pl.when(i >= 3 + SLOTS)
            def _():
                far_copy(i - 3 - SLOTS, in_turn(i - 3 - SLOTS, near)).wait_send()

            for j in (1, 0):
                whole = parts[(i - 3) % 3, j, spread.rows(half), :].astype(FULL) + pair_in[k, j].astype(FULL)
                low, high = whole[:, :width], whole[:, width:]
                stays = jnp.where(side == 0, low, high)
                goes = jnp.where(side == 0, high, low).astype(LOW)
                if j:
                    kept[(i - 3) % SLOTS] = stays
                    far_out[(i - 3) % SLOTS] = goes
                    far_copy(i - 3, k).start()
                else:
                    answer_kept[k] = stays
                    answer_out[k] = goes

        @pl.when((i >= LAG) & (i < n + LAG))
        def _():
            k = in_turn(i - LAG, near)
            far_copy(i - LAG, k).wait_recv()
            rows = (kept[(i - LAG) % SLOTS] + far_in[k].astype(FULL)).astype(LOW)

            @pl.when(k == 0)
            def _():
                back_ref[0, spread.rows(half), :] = rows

            @pl.when(k > 0)
            def _():
                final[k] = rows
                return_copy(k).start()

        @pl.when(i == n + 2)
        def _():
            loop(lambda k: answer_side_copy(k).start(), near)

        @pl.when((i >= n + 2) & (i < n + 2 + tiles))
        def _():
            grads(i - (n + 2))

    loop(step, 0, n + max(LAG, 2 + tiles))
    keep(0).start()
    keep(1).start()
    peaks[0] = peak_ref[...]

    def collect_sums(k):
        @pl.when(k > 0)
        def _():
            peak_copy(k).wait_recv()
            sum_copy(k).wait_recv()

        sums[t, pl.ds(k, 1), :] = sum_in[k, 0:1, :]

    loop(collect_sums)
    for d in (1, 2, 3):
        share_copy(d, t).start()
    top_ref[...] = jnp.max(peaks[...], axis=0)

    def collect(i):
        k = in_turn(i, near)

        @pl.when(k > 0)
        def _():
            return_copy(k).wait_recv()

        mate_copy(k, half).start()

    loop(collect)

    def answers_whole(k):
        answer_side_copy(k).wait_recv()
        answer_ready[k - near] = (answer_kept[k] + answer_far[k - near].astype(FULL)).astype(LOW)

    loop(answers_whole, near)
    keep(2).start()
    for d in (1, 2, 3):
        share_copy(d, (t + 4 - d) % 4).wait_recv()
    whole = (sums[0] + sums[1]) + (sums[2] + sums[3])
    whole = jnp.concatenate([whole[k : k + 1] for k in range(n)], axis=1)
    gate_sum_ref[...] = jnp.broadcast_to(whole, gate_sum_ref.shape)

    def finish(i):
        k = in_turn(i, near)
        mate_copy(k, 1 - half).wait_recv()
        mate_copy(k, half).wait_send()
        spread.sent(k)
        gate_pair_copy(k, half).wait_send()

        @pl.when(k > 0)
        def _():
            return_copy(k).wait_send()
            gate_copy(k).wait_send()
            sum_copy(k).wait_send()
            peak_copy(k).wait_send()

        @pl.when(i >= n - 3)
        def _():
            part_copy(i, k).wait_send()

        @pl.when(i >= n - SLOTS)
        def _():
            far_copy(i, k).wait_send()

    loop(finish)
    for d in (1, 2, 3):
        share_copy(d, t).wait_send()
    loop(lambda k: answer_side_copy(k).wait_send(), near)
    for i in range(3):
        keep(i).wait()
    for m in range(tiles):
        grad_copy(m, 0).wait()
        grad_copy(m, 1).wait()


def run_experts(n, hp, place, router, peak, normed, first, second, upstream):
    model = normed.shape[1]
    width = model // 2
    hidden = first.shape[1]
    near = near_count(n)
    vmem = pl.BlockSpec(memory_space=VMEM)
    hbm = pl.BlockSpec(memory_space=pl.ANY)
    shape = jax.ShapeDtypeStruct
    return pl.pallas_call(
        functools.partial(expert_kernel, n, hp),
        out_shape=(
            shape((n, 2 * hp, width), LOW),
            shape((8, n * 2 * hp), FULL),
            shape(peak.shape, FULL),
            shape((near, hp, width), LOW),
            shape((near, hp, width), FULL),
            shape((n - near, hp, width), LOW),
            shape((model, hidden), FULL),
            shape((hidden, model), FULL),
        ),
        in_specs=[vmem] * 3 + [hbm] * 4,
        out_specs=[vmem] * 3 + [hbm] * 5,
        scratch_shapes=[
            *Spread.scratch(n, hp, width),
            VMEM((n, 2 * hp, model), LOW),
            *Spread.semaphores(n),
            VMEM((n, 2 * hp, model), LOW),
            VMEM((n, 2 * hp, hidden), LOW),
            VMEM((n, 2 * hp, hidden), LOW),
            VMEM((3, 2, 2 * hp, model), LOW),
            VMEM((n, 2, hp, model), LOW),
            VMEM((SLOTS, hp, width), FULL),
            VMEM((SLOTS, hp, width), LOW),
            VMEM((n, hp, width), LOW),
            VMEM((n, hp, width), LOW),
            VMEM((n, 8, hp), FULL),
            VMEM((n, 2, 8, hp), FULL),
            VMEM((n, 8, 2 * hp), FULL),
            VMEM((n, 8, 2 * hp), FULL),
            VMEM((4, n, 2 * hp), FULL),
            VMEM((n, *peak.shape), FULL),
            dma(1),
            dma(3), dma(n), dma(SLOTS), dma(n), dma(n), dma(n), dma(n), dma(n),
            dma(n), dma(n), dma(n), dma(n), dma(n), dma(n), dma(n), dma(n), dma(3), dma(3),
            VMEM(normed.shape, LOW),
            VMEM(first.shape, LOW),
            VMEM(second.shape, LOW),
            VMEM((n, hp, width), LOW),
            VMEM((n, hp, width), FULL),
            VMEM((model, hidden), FULL),
            VMEM((hidden, model), FULL),
            dma(3 + 2 * (model // 256)),
            dma(3), dma(n), dma(n),
            VMEM((n - near, hp, width), LOW),
            VMEM((n - near, hp, width), LOW),
            dma(n), dma(n),
        ],
        compiler_params=pltpu.CompilerParams(
            collective_id=1, has_side_effects=True, vmem_limit_bytes=VMEM_LIMIT
        ),
        name="experts",
    )(place, router, peak, normed, first, second, upstream)


def unpad(rows_ref, out_ref):
    for image in range(rows_ref.shape[0] // PIECE):
        start = image * SEQ // 8 * 8
        length = min(PIECE, out_ref.shape[0] - start)
        shift = image * SEQ - start
        rows = lax.broadcasted_iota(jnp.int32, (length, PIECE), 0)
        columns = lax.broadcasted_iota(jnp.int32, (length, PIECE), 1)
        pick = (rows == columns + shift) & (columns < SEQ)
        image_part = rows_ref[image * PIECE : (image + 1) * PIECE, :]
        moved = dot_plain(jnp.where(pick, 1.0, 0.0).astype(LOW), image_part).astype(LOW)
        if shift:
            before = lax.broadcasted_iota(jnp.int32, (8, moved.shape[1]), 0) < shift
            first = jnp.where(before, out_ref[start : start + 8, :].astype(FULL), moved[:8].astype(FULL))
            out_ref[start : start + 8, :] = first.astype(LOW)
            out_ref[start + 8 : start + length, :] = moved[8:]
        else:
            out_ref[start : start + length, :] = moved


def back_kernel(
    n,
    hp,
    back_ref,
    gate_sum_ref,
    index_ref,
    gains_ref,
    output_w_ref,
    router_ref,
    answer_ready,
    *refs,
):
    later, outs, scratch = refs[:13], refs[13:18], refs[18:]
    block_out_ref, tokens_out_ref, weights_ref, small_ref, gain_ref = outs
    held, scratch = scratch[:13], scratch[13:]
    (
        residual_ref,
        upstream_ref,
        answer_out,
        answer_kept,
        normed_one_ref,
        query_ref,
        key_ref,
        value_ref,
        mixed_ref,
        tokens_ref,
        query_w_ref,
        key_w_ref,
        value_w_ref,
    ) = held
    dp, t, half, side, mate, far = places()
    (
        moe_mine,
        moe_other,
        block_mine,
        block_other,
        attention_grad,
        residual_grad,
        query_grad,
        key_grad,
        value_grad,
        gain_two_sum,
        gain_two_in,
        gain_one_sum,
        gain_one_all,
        gain_rows,
        router_sum,
        router_in,
        totals,
        totals_two,
        pieces,
        pieces_in,
        small_pieces,
        small_in,
        answer_far,
        answer_final,
        answers,
        block_ref,
        grad_tokens_ref,
        hs,
        as_,
        ar,
        bs,
        br,
        ts,
        tr,
        cs,
        cr,
        gs,
        gr,
        ws,
        wr,
        ls,
        lr,
        os_,
        or_,
        vs,
        vr,
        ds,
        dr,
        es,
        er,
        fs,
        fr,
        ks,
        kr,
    ) = scratch[:54]
    total = Total(*scratch[54:])
    heads = query_w_ref.shape[0] // HD
    model = upstream_ref.shape[1]
    width = model // 2
    slots = back_ref.shape[0]
    piece = pieces.shape[1]
    near = near_count(n)
    greet(n, dp, t, [(t + d) % 4 for d in (1, 2, 3)])
    fetches = [pltpu.make_async_copy(a, b, hs.at[i]) for i, (a, b) in enumerate(zip(later, held))]
    for fetch in fetches:
        fetch.start()

    def peer(k):
        return (partner(dp, k, n), t)

    def moe_copy(j):
        return remote(moe_mine.at[j], moe_other.at[j], as_.at[j], ar.at[j], (dp, far))

    def block_copy(j):
        return remote(block_mine.at[j], block_other.at[j], bs.at[j], br.at[j], (dp, far))

    def attention_copy(j, owner):
        rows = attention_grad.at[image_rows(2 * j + owner)]
        return remote(rows, rows, ts.at[j], tr.at[j], (dp, mate))

    def tokens_copy(j, owner):
        rows = grad_tokens_ref.at[image_rows(2 * j + owner)]
        return remote(rows, rows, cs.at[j], cr.at[j], (dp, mate))

    def block_pair_copy(j, owner):
        rows = block_ref.at[image_rows(2 * j + owner)]
        return remote(rows, rows, ls.at[j], lr.at[j], (dp, mate))

    def gain_copy(d, owner):
        return remote(
            gain_one_all.at[owner], gain_one_all.at[owner], gs.at[d - 1], gr.at[d - 1], (dp, (t + d) % 4)
        )

    def gain_row_copy(k):
        return remote(gain_rows.at[0], gain_rows.at[k], ks.at[k], kr.at[k], peer(k))

    def router_copy():
        return remote(router_sum, router_in, os_.at[0], or_.at[0], (dp, mate))

    def gain_two_copy():
        return remote(gain_two_sum, gain_two_in, os_.at[1], or_.at[1], (dp, mate))

    def piece_copy(k):
        return remote(pieces.at[k], pieces_in.at[k], ws.at[k], wr.at[k], peer(k))

    def small_copy(k):
        return remote(small_pieces.at[k], small_in.at[k], vs.at[k], vr.at[k], peer(k))

    def answer_rows(k, owner):
        return answers.at[pl.ds(pl.multiple_of((2 * k + owner) * hp, hp), hp)]

    def answer_side_copy(k):
        return remote(answer_out.at[k], answer_far.at[k], ds.at[k], dr.at[k], (dp, far))

    def answer_copy(k):
        return remote(answer_final.at[k], answer_rows(k, half), es.at[k], er.at[k], peer(k))

    def far_answer_copy(k):
        return remote(answer_ready.at[k - near], answer_rows(k, half), es.at[k], er.at[k], peer(k))

    def answer_pair_copy(k, owner):
        return remote(answer_rows(k, owner), answer_rows(k, owner), fs.at[k], fr.at[k], (dp, mate))

    def loop(body, first=0, last=n):
        def one(k, carry):
            body(k)
            return carry

        lax.fori_loop(first, last, one, 0)

    def both_sides(mine, other):
        low = jnp.where(side == 0, mine, other)
        high = jnp.where(side == 0, other, mine)
        return jnp.concatenate([low, high], axis=1)

    def hots(rows):
        columns = lax.broadcasted_iota(jnp.int32, (PIECE, slots), 1)
        return index_ref[rows, 2:3] == columns, index_ref[rows, 3:4] == columns

    def as_low(mask):
        return jnp.where(mask, 1.0, 0.0).astype(LOW)

    gain_two_sum[...] = jnp.zeros_like(gain_two_sum)
    gain_one_sum[...] = jnp.zeros_like(gain_one_sum)
    router_sum[...] = jnp.zeros_like(router_sum)

    def combine(j):
        first, second = hots(image_rows(2 * j + half))
        moe_mine[j] = dot_plain(as_low(first | second), back_ref[...]).astype(LOW)

        @pl.when(j == 0)
        def _():
            await_greetings(n, (1, 2, 3))
            loop(lambda k: far_answer_copy(k).start(), near)

        moe_copy(j).start()

    loop(combine, 0, 3)
    for fetch in fetches[:3]:
        fetch.wait()
    loop(lambda k: answer_side_copy((k + 1) % near).start(), 0, near)

    def gates_of(rows, normed):
        logits = dot_last(normed, router_ref[...])
        lanes = lax.broadcasted_iota(jnp.int32, logits.shape, 1)
        hot_one = index_ref[rows, 4:5] == lanes
        hot_two = index_ref[rows, 5:6] == lanes
        one = jnp.sum(jnp.where(hot_one, logits, 0.0), axis=1, keepdims=True)
        two = jnp.sum(jnp.where(hot_two, logits, 0.0), axis=1, keepdims=True)
        top = jnp.maximum(one, two)
        one, two = jnp.exp(one - top), jnp.exp(two - top)
        return one / (one + two), two / (one + two), hot_one, hot_two

    def moe_back(j):
        rows = image_rows(2 * j + half)
        unit, factor = normalized(residual_ref[j])
        normed = (unit * gains_ref[1:2, :]).astype(LOW)
        gate_one, gate_two, hot_one, hot_two = gates_of(rows, normed)
        first, second = hots(rows)
        slot_sums = gate_sum_ref[0:1, :]
        grad_one = jnp.sum(jnp.where(first, slot_sums, 0.0), axis=1, keepdims=True)
        grad_two = jnp.sum(jnp.where(second, slot_sums, 0.0), axis=1, keepdims=True)
        mean = gate_one * grad_one + gate_two * grad_two
        logit_grad = jnp.where(hot_one, gate_one * (grad_one - mean), 0.0)
        logit_grad = logit_grad + jnp.where(hot_two, gate_two * (grad_two - mean), 0.0)
        logit_grad = logit_grad.astype(LOW)
        router_sum[...] += dot_first(normed, logit_grad)
        normed_grad = dot_plain(logit_grad, router_ref[...])
        moe_copy(j).wait_recv()
        normed_grad = normed_grad + both_sides(moe_mine[j].astype(FULL), moe_other[j].astype(FULL))
        gain_two_sum[...] += jnp.sum((normed_grad * unit).reshape(PIECE // 8, 8, model), axis=0)
        grad = normalized_back(normed_grad * gains_ref[1:2, :], unit, factor)
        grad = grad + upstream_ref[rows, :].astype(FULL)
        residual_grad[j] = grad
        attention_grad[rows, :] = grad.astype(LOW)
        attention_copy(j, half).start()

    loop(moe_back, 0, 3)
    router_copy().start()
    gain_two_copy().start()
    for fetch in fetches[3:]:
        fetch.wait()

    def image_back(image):
        rows = image_rows(image)
        mixed_grad = dot_last(attention_grad[rows, :], output_w_ref[...]).astype(LOW)
        queries, keys, values = query_ref[rows, :], key_ref[rows, :], value_ref[rows, :]
        query_parts, key_parts, value_parts = [], [], []
        for h in range(heads):
            cols = slice(h * HD, (h + 1) * HD)
            probs, _ = attention_probs(queries[:, cols], keys[:, cols])
            value_parts.append(dot_first(probs.astype(LOW), mixed_grad[:, cols]))
            probs_grad = dot_last(mixed_grad[:, cols], values[:, cols])
            level = jnp.sum(probs * probs_grad, axis=1, keepdims=True)
            score_grad = (probs * (probs_grad - level)).astype(LOW)
            query_parts.append(dot_plain(score_grad, keys[:, cols]) * HD**-0.5)
            key_parts.append(dot_first(score_grad, queries[:, cols]) * HD**-0.5)
        grads = [jnp.concatenate(p, axis=1).astype(LOW) for p in (query_parts, key_parts, value_parts)]
        query_grad[rows, :], key_grad[rows, :], value_grad[rows, :] = grads

    def answer_turn(k):
        answer_side_copy(k).wait_recv()
        rows = (answer_kept[k] + answer_far[k].astype(FULL)).astype(LOW)

        @pl.when(k == 0)
        def _():
            answer_rows(0, half)[...] = rows

        @pl.when(k > 0)
        def _():
            answer_final[k] = rows
            answer_copy(k).start()

    def grad_part(image):
        rows = image_rows(image)
        part = dot_plain(query_grad[rows, :], query_w_ref[...])
        part = part + dot_plain(key_grad[rows, :], key_w_ref[...])
        part = part + dot_plain(value_grad[rows, :], value_w_ref[...])
        unit, _ = normalized(tokens_ref[rows, :].astype(FULL))
        gain_one_sum[...] += jnp.sum((part * unit).reshape(PIECE // 8, 8, model), axis=0)
        return part

    def my_piece(source, k):
        at = partner(dp, k, n) * piece
        grain = math.gcd(piece, 8)
        span = -(-(piece + 8 - grain) // 8) * 8
        taken = source[pl.ds(pl.multiple_of(at // 8 * 8, 8), span), :]
        rows = taken[:piece]
        for shift in range(grain, 8, grain):
            rows = jnp.where(at % 8 == shift, taken[shift : shift + piece], rows)
        return rows.astype(LOW)

    def small_grads():
        router_copy().wait_recv()
        gain_two_copy().wait_recv()
        row = jnp.sum(gain_two_sum[...] + gain_two_in[...], axis=0, keepdims=True)
        column = jnp.concatenate(
            [row_to_column(row[:, i : i + 256]) for i in range(0, model, 256)], axis=0
        )
        totals_two[...] = jnp.concatenate(
            [
                dot_first(attention_grad[...], mixed_ref[...]),
                router_sum[...] + router_in[...],
                column,
            ],
            axis=1,
        )

        def send_small(i):
            k = (i + near) % n
            small_pieces[k] = my_piece(totals_two, k)

            @pl.when(k > 0)
            def _():
                small_copy(k).start()

        loop(send_small)

    for j in range(3):
        attention_copy(j, 1 - half).wait_recv()

    def attention_back(j):
        for owner in (1 - half, half):
            image_back(2 * j + owner)
        total.give(j, grad_part(2 * j + 1 - half))
        total.take(j, grad_part(2 * j + half))
        answer_turn((j + 1) % near)

        @pl.when(j == 1)
        def _():
            small_grads()

        @pl.when(j == 2)
        def _():
            answer_turn(0)

    loop(attention_back, 0, 3)

    gain_one_all[t] = jnp.sum(gain_one_sum[...], axis=0, keepdims=True)
    for d in (1, 2, 3):
        gain_copy(d, t).start()
    normed_one = normed_one_ref[...]
    totals[:, : 3 * query_grad.shape[1]] = jnp.concatenate(
        [
            dot_first(normed_one, query_grad[...]),
            dot_first(normed_one, key_grad[...]),
            dot_first(normed_one, value_grad[...]),
        ],
        axis=1,
    )

    def send_piece(i):
        k = (i + near) % n
        pieces[k] = my_piece(totals, k)

        @pl.when(k > 0)
        def _():
            piece_copy(k).start()

    loop(send_piece)


    def answers_here(i):
        k = in_turn(i, near)

        @pl.when((k > 0) & (k < near))
        def _():
            answer_copy(k).wait_recv()

        @pl.when(k >= near)
        def _():
            far_answer_copy(k).wait_recv()

        answer_pair_copy(k, half).start()

    loop(answers_here)
    loop(lambda k: answer_pair_copy(k, 1 - half).wait_recv())

    def block_rows(j):
        rows = image_rows(2 * j + half)
        residual = residual_ref[j]
        unit, _ = normalized(residual)
        gate_one, gate_two, _, _ = gates_of(rows, (unit * gains_ref[1:2, :]).astype(LOW))
        first, second = hots(rows)
        from_first = dot_plain(as_low(first), answers[...])
        from_second = dot_plain(as_low(second), answers[...])
        mine = jnp.where(side == 0, residual[:, :width], residual[:, width:])
        block_mine[j] = (mine + (gate_one * from_first + gate_two * from_second)).astype(LOW)
        block_copy(j).start()

    loop(block_rows, 0, 3)

    def tokens_back(j):
        rows = image_rows(2 * j + half)
        normed_grad = total.result(j)
        unit, factor = normalized(tokens_ref[rows, :].astype(FULL))
        grad = normalized_back(normed_grad * gains_ref[0:1, :], unit, factor)
        grad_tokens_ref[rows, :] = (residual_grad[j] + grad).astype(LOW)
        tokens_copy(j, half).start()

    loop(tokens_back, 0, 3)
    for d in (1, 2, 3):
        gain_copy(d, (t + 4 - d) % 4).wait_recv()
    gain_rows[0] = (gain_one_all[0] + gain_one_all[1]) + (gain_one_all[2] + gain_one_all[3])

    def send_gain(k):
        gain_row_copy(k).start()

    loop(send_gain, 1)

    def block_back(j):
        block_copy(j).wait_recv()
        block_ref[image_rows(2 * j + half), :] = both_sides(block_mine[j], block_other[j])
        block_pair_copy(j, half).start()

    for j in range(3):
        tokens_copy(j, 1 - half).wait_recv()
    unpad(grad_tokens_ref, tokens_out_ref)
    loop(block_back, 0, 3)
    for j in range(3):
        block_pair_copy(j, 1 - half).wait_recv()
    unpad(block_ref, block_out_ref)
    pieces_in[0] = pieces[0]
    small_in[0] = small_pieces[0]

    def arrive(k):
        piece_copy(k).wait_recv()
        small_copy(k).wait_recv()
        gain_row_copy(k).wait_recv()

    loop(arrive, 1)
    weights_ref[...] = jnp.sum(pieces_in[...].astype(FULL), axis=0)
    small_ref[...] = jnp.sum(small_in[...].astype(FULL), axis=0)
    gain_ref[...] = jnp.sum(gain_rows[...], axis=0)

    for j in range(3):
        moe_copy(j).wait_send()
        block_copy(j).wait_send()
        attention_copy(j, half).wait_send()
        total.sent(j)
        tokens_copy(j, half).wait_send()
        block_pair_copy(j, half).wait_send()
        gain_copy(j + 1, t).wait_send()
    router_copy().wait_send()
    gain_two_copy().wait_send()

    def left(k):
        @pl.when(k < near)
        def _():
            answer_side_copy(k).wait_send()

        @pl.when((k > 0) & (k < near))
        def _():
            answer_copy(k).wait_send()

        @pl.when(k >= near)
        def _():
            far_answer_copy(k).wait_send()

        answer_pair_copy(k, half).wait_send()

        @pl.when(k > 0)
        def _():
            piece_copy(k).wait_send()
            small_copy(k).wait_send()
            gain_row_copy(k).wait_send()

    loop(left)


def run_back(n, hp, row_count, first, later):
    upstream = later[1]
    rows, model = upstream.shape
    heads_width = later[8].shape[1]
    width = model // 2
    piece = model // n
    vmem = pl.BlockSpec(memory_space=VMEM)
    shape = jax.ShapeDtypeStruct
    slim = VMEM((3, PIECE, width), LOW)
    heads = VMEM((rows, heads_width), LOW)
    eight = VMEM((8, model), FULL)
    wide, narrow = 3 * heads_width, heads_width + n + 1
    quarter = VMEM((near_count(n), hp, width), LOW)
    three, many = dma(3), dma(n)
    return pl.pallas_call(
        functools.partial(back_kernel, n, hp),
        out_shape=(
            shape((row_count, model), LOW),
            shape((row_count, model), LOW),
            shape((piece, wide), FULL),
            shape((piece, narrow), FULL),
            shape((1, model), FULL),
        ),
        in_specs=[vmem] * (len(first) - 1) + [pl.BlockSpec(memory_space=pl.ANY)] * (1 + len(later)),
        out_specs=[vmem] * 5,
        scratch_shapes=[
            *[VMEM(a.shape, a.dtype) for a in later],
            slim, slim, slim, slim,
            VMEM((rows, model), LOW),
            VMEM((3, PIECE, model), FULL),
            heads, heads, heads,
            eight, eight, eight,
            VMEM((4, 1, model), FULL),
            VMEM((n, 1, model), FULL),
            VMEM((model, n), FULL),
            VMEM((model, n), FULL),
            VMEM((model, wide), FULL),
            VMEM((model, narrow), FULL),
            VMEM((n, piece, wide), LOW),
            VMEM((n, piece, wide), LOW),
            VMEM((n, piece, narrow), LOW),
            VMEM((n, piece, narrow), LOW),
            quarter, quarter,
            VMEM((n * 2 * hp, width), LOW),
            VMEM((rows, model), LOW),
            VMEM((rows, model), LOW),
            dma(len(later)),
            three, three, three, three, three, three, three, three, three, three,
            many, many, three, three, dma(2), dma(2),
            many, many, many, many, many, many, many, many, many, many,
            *Total.scratch(model),
        ],
        compiler_params=pltpu.CompilerParams(
            collective_id=2, has_side_effects=True, vmem_limit_bytes=VMEM_LIMIT
        ),
        name="back",
    )(*first, *later)


def body(
    tokens,
    gain_attn,
    w_query,
    w_key,
    w_value,
    w_output,
    gain_moe,
    w_router,
    expert_in,
    expert_out,
    routes,
    slot_ids,
    capacity,
    threshold,
    cotangent,
):
    n = lax.axis_size("dp")
    row_count, model = tokens.shape
    heads_here = w_query.shape[1] // HD
    slot_count = 23 * TOK_DEV // (10 * n) + 1
    per_half = -(-slot_count // 2)
    hp = -(-per_half // 16) * 16
    dp_here = lax.axis_index("dp")
    gains = jnp.stack([gain_attn, gain_moe]).astype(FULL)
    across = (w_query.T, w_key.T, w_value.T)
    (
        place,
        index,
        peak,
        tokens_in,
        upstream,
        normed_one,
        query,
        key,
        value,
        mixed,
        residual,
        normed_two,
        spread,
    ) = run_front(
        n,
        hp,
        per_half,
        capacity,
        routes.T,
        slot_ids.T,
        tokens,
        cotangent,
        gains,
        (*across, w_output),
    )
    router = w_router.T
    back, gate_sums, top, answer_out, answer_kept, answer_ready, grad_first, grad_second = run_experts(
        n, hp, place, router, peak, normed_two, expert_in[0], expert_out[0], spread
    )
    block_out, grad_tokens, weight_grads, small, gain_rows = run_back(
        n,
        hp,
        row_count,
        (back.reshape(n * 2 * hp, -1), gate_sums, index, gains, w_output, router, answer_ready),
        (
            residual,
            upstream,
            answer_out,
            answer_kept,
            normed_one,
            query,
            key,
            value,
            mixed,
            tokens_in,
            *across,
        ),
    )
    head_max = top[:heads_here, 0]
    column_factor = jnp.repeat(jnp.sqrt(jnp.minimum(1.0, threshold / head_max)), HD)[None, :]
    wide = w_query.shape[1]
    piece = model // n
    return (
        block_out,
        grad_tokens,
        lax.dynamic_slice_in_dim(gain_rows[0], dp_here * piece, piece),
        small[:, wide + n],
        weight_grads[:, :wide],
        weight_grads[:, wide : 2 * wide],
        weight_grads[:, 2 * wide :],
        small[:, :wide].T,
        small[:, wide : wide + n],
        grad_first[None],
        grad_second[None],
        w_query.astype(FULL) * column_factor,
        w_key.astype(FULL) * column_factor,
        head_max,
    )


def solution(mesh):
    in_specs = (
        P("dp", None),
        P(),
        P(None, "tensor"),
        P(None, "tensor"),
        P(None, "tensor"),
        P("tensor", None),
        P(),
        P(),
        P("dp", None, "tensor"),
        P("dp", "tensor", None),
        P("dp", None),
        P("dp", None),
        P(),
        P("tensor"),
        P("dp", None),
    )
    out_specs = (
        P("dp", None),
        P("dp", None),
        P("dp"),
        P("dp"),
        P("dp", "tensor"),
        P("dp", "tensor"),
        P("dp", "tensor"),
        P("tensor", "dp"),
        P("dp", None),
        P("dp", None, "tensor"),
        P("dp", "tensor", None),
        P(None, "tensor"),
        P(None, "tensor"),
        P("tensor"),
    )
    return jax.shard_map(body, mesh=mesh, in_specs=in_specs, out_specs=out_specs, check_vma=False)
```

```python
import functools
import math

import jax
import jax.numpy as jnp
from jax import lax
from jax.experimental import pallas as pl
from jax.experimental.pallas import tpu as pltpu
from jax.sharding import PartitionSpec as P

HD = 64
SEQ = 197
PIECE = 208
TOK_DEV = 1182
EPSILON = 1e-06
MESH = pl.DeviceIdType.MESH
VMEM_LIMIT = 60 * 2**20
SLOTS = 3
LAG = 4
VMEM = pltpu.VMEM
LOW, FULL = jnp.bfloat16, jnp.float32


def dot_plain(a, b):
    return jnp.dot(a, b, preferred_element_type=FULL)


def dot_last(a, b):
    return lax.dot_general(a, b, (((1,), (1,)), ((), ())), preferred_element_type=FULL)


def dot_first(a, b):
    return lax.dot_general(a, b, (((0,), (0,)), ((), ())), preferred_element_type=FULL)


def normalized(rows):
    centered = rows - jnp.mean(rows, axis=-1, keepdims=True)
    factor = lax.rsqrt(jnp.mean(centered * centered, axis=-1, keepdims=True) + EPSILON)
    return centered * factor, factor


def normalized_back(u, unit, factor):
    first = jnp.mean(u, axis=-1, keepdims=True)
    second = jnp.mean(u * unit, axis=-1, keepdims=True)
    return factor * (u - first - unit * second)


def same_index(size):
    rows = lax.broadcasted_iota(jnp.int32, (size, size), 0)
    return rows == lax.broadcasted_iota(jnp.int32, (size, size), 1)


def row_to_column(row):
    return jnp.sum(jnp.where(same_index(row.shape[1]), row, 0.0), axis=1, keepdims=True)


def column_to_row(column):
    return jnp.sum(jnp.where(same_index(column.shape[0]), column, 0.0), axis=0, keepdims=True)


def attention_probs(queries, keys):
    scores = dot_last(queries, keys) * HD**-0.5
    real = lax.broadcasted_iota(jnp.int32, scores.shape, 1) < SEQ
    scores = jnp.where(real, scores, -1e30)
    top = jnp.max(scores, axis=1, keepdims=True)
    powers = jnp.exp(scores - top)
    return powers * (1.0 / jnp.sum(powers, axis=1, keepdims=True)), top


def partner(dp, k, n):
    other, weight = 0, 1
    while weight < n:
        other = other + ((dp // weight + k // weight) % 2) * weight
        weight *= 2
    return other


def places():
    dp = lax.axis_index("dp")
    t = lax.axis_index("tensor")
    return dp, t, t % 2, t // 2, t + 1 - 2 * (t % 2), (t + 2) % 4


def remote(src, dst, sends, recvs, device):
    return pltpu.make_async_remote_copy(
        src_ref=src,
        dst_ref=dst,
        send_sem=sends,
        recv_sem=recvs,
        device_id=device,
        device_id_type=MESH,
    )


def signal(sem, device):
    pl.semaphore_signal(sem, inc=1, device_id=device, device_id_type=MESH)


def greet(n, dp, t, others):
    barrier = pltpu.get_barrier_semaphore()

    def one(k, carry):
        signal(barrier, (partner(dp, k, n), t))
        return carry

    lax.fori_loop(1, n, one, 0)
    for other in others:
        signal(barrier, (dp, other))


def await_greetings(n, others):
    pl.semaphore_wait(pltpu.get_barrier_semaphore(), n - 1 + len(others))


def image_rows(image):
    return pl.ds(pl.multiple_of(image * PIECE, PIECE), PIECE)


def dma(*shape):
    return pltpu.SemaphoreType.DMA(shape)


def near_count(n):
    return min(4, n)


class Spread:
    def __init__(self, n, hp, place, near_out, far_out, arrived, zs, zr, xs, xr, cs, cr, own):
        self.n, self.hp, self.near = n, hp, near_count(n)
        self.place, self.near_out, self.far_out, self.arrived = place, near_out, far_out, arrived
        self.zs, self.zr, self.xs, self.xr, self.cs, self.cr, self.own = zs, zr, xs, xr, cs, cr, own
        self.dp, self.t, self.half, self.side, self.mate, self.far = places()
        self.width = far_out.shape[2]

    def rows(self, owner):
        return pl.ds(pl.multiple_of(owner * self.hp, self.hp), self.hp)

    def columns(self, owner):
        return pl.ds(pl.multiple_of(owner * self.width, self.width), self.width)

    def peer(self, k):
        return (partner(self.dp, k, self.n), self.t)

    def own_copy(self):
        return pltpu.make_async_copy(
            self.near_out.at[0], self.arrived.at[0, self.rows(self.half)], self.own
        )

    def near_copy(self, k):
        return remote(
            self.near_out.at[k],
            self.arrived.at[k, self.rows(self.half)],
            self.zs.at[k],
            self.zr.at[k],
            self.peer(k),
        )

    def far_copy(self, k):
        return remote(
            self.far_out.at[k - self.near],
            self.arrived.at[k, self.rows(self.half), self.columns(self.side)],
            self.zs.at[k],
            self.zr.at[k],
            self.peer(k),
        )

    def side_copy(self, k, side):
        part = self.arrived.at[k, self.rows(self.half), self.columns(side)]
        return remote(part, part, self.xs.at[k], self.xr.at[k], (self.dp, self.far))

    def pair_copy(self, k, half):
        part = self.arrived.at[k, self.rows(half)]
        return remote(part, part, self.cs.at[k], self.cr.at[k], (self.dp, self.mate))

    def hot(self, k, row_count):
        slots = lax.broadcasted_iota(jnp.int32, (self.hp, row_count), 0) + k * self.hp
        is_first = self.place[0:1, :] == slots
        is_second = self.place[1:2, :] == slots
        return is_first, is_second

    def send(self, k, rows_ref):
        is_first, is_second = self.hot(k, rows_ref.shape[0])
        hot = jnp.where(is_first | is_second, 1.0, 0.0).astype(LOW)

        @pl.when(k < self.near)
        def _():
            self.near_out[k] = dot_plain(hot, rows_ref[...]).astype(LOW)

            @pl.when(k == 0)
            def _():
                self.own_copy().start()

            @pl.when(k > 0)
            def _():
                self.near_copy(k).start()

        @pl.when(k >= self.near)
        def _():
            mine = rows_ref[:, self.columns(self.side)]
            self.far_out[k - self.near] = dot_plain(hot, mine).astype(LOW)
            self.far_copy(k).start()

        return is_first, is_second

    def first_hop(self, k):
        @pl.when(k == 0)
        def _():
            self.own_copy().wait()

        @pl.when((k > 0) & (k < self.near))
        def _():
            self.near_copy(k).wait_recv()

        @pl.when(k >= self.near)
        def _():
            self.far_copy(k).wait_recv()
            self.side_copy(k, self.side).start()

    def second_hop(self, k):
        @pl.when(k >= self.near)
        def _():
            self.side_copy(k, 1 - self.side).wait_recv()

        self.pair_copy(k, self.half).start()

    def last_hop(self, k):
        self.pair_copy(k, 1 - self.half).wait_recv()

    def sent(self, k):
        @pl.when((k > 0) & (k < self.near))
        def _():
            self.near_copy(k).wait_send()

        @pl.when(k >= self.near)
        def _():
            self.far_copy(k).wait_send()
            self.side_copy(k, self.side).wait_send()

        self.pair_copy(k, self.half).wait_send()

    @staticmethod
    def scratch(n, hp, width):
        near = near_count(n)
        return [VMEM((near, hp, 2 * width), LOW), VMEM((n - near, hp, width), LOW)]

    @staticmethod
    def semaphores(n):
        return [dma(n), dma(n), dma(n), dma(n), dma(n), dma(n), pltpu.SemaphoreType.DMA]


class Total:
    def __init__(self, part_out, pair_in, far_out, far_in, ps, pr, fs, fr):
        self.part_out, self.pair_in, self.far_out, self.far_in = part_out, pair_in, far_out, far_in
        self.ps, self.pr, self.fs, self.fr = ps, pr, fs, fr
        self.dp, _, _, _, self.mate, self.far = places()

    def pair_copy(self, j):
        return remote(
            self.part_out.at[j], self.pair_in.at[j], self.ps.at[j], self.pr.at[j], (self.dp, self.mate)
        )

    def far_copy(self, j):
        return remote(
            self.far_out.at[j], self.far_in.at[j], self.fs.at[j], self.fr.at[j], (self.dp, self.far)
        )

    def give(self, j, rows):
        self.part_out[j] = rows
        self.pair_copy(j).start()

    def take(self, j, rows):
        self.pair_copy(j).wait_recv()
        self.far_out[j] = (rows + self.pair_in[j]).astype(LOW)
        self.far_copy(j).start()

    def result(self, j):
        self.far_copy(j).wait_recv()
        return self.far_out[j].astype(FULL) + self.far_in[j].astype(FULL)

    def sent(self, j):
        self.pair_copy(j).wait_send()
        self.far_copy(j).wait_send()

    @staticmethod
    def scratch(model):
        wide, slim = VMEM((3, PIECE, model), FULL), VMEM((3, PIECE, model), LOW)
        return [wide, wide, slim, slim, dma(3), dma(3), dma(3), dma(3)]


def padded_image(rows_ref, image):
    start = image * SEQ // 8 * 8
    length = min(PIECE, rows_ref.shape[0] - start)
    rows = lax.broadcasted_iota(jnp.int32, (PIECE, length), 0)
    columns = lax.broadcasted_iota(jnp.int32, (PIECE, length), 1)
    pick = (columns == rows + (image * SEQ - start)) & (rows < SEQ)
    return dot_plain(jnp.where(pick, 1.0, 0.0).astype(LOW), rows_ref[start : start + length, :])


def front_kernel(
    n,
    hp,
    per_half,
    capacity_ref,
    routes_ref,
    slot_ids_ref,
    tokens_ref,
    upstream_ref,
    gains_ref,
    query_w_ref,
    key_w_ref,
    value_w_ref,
    output_w_ref,
    place_ref,
    index_ref,
    peak_ref,
    *refs,
):
    outs, spread_hbm, scratch = refs[:9], refs[9], refs[10:]
    held, scratch = scratch[:9], scratch[9:]
    (
        tokens,
        upstream,
        normed_one,
        query,
        key,
        value,
        mixed_rows,
        residual_rows,
        normed_two,
    ) = held
    near_out, far_out, zs, zr, own, ns, nr, hs, xs, xr = scratch[:10]
    total = Total(*scratch[10:])
    dp, t, half, side, mate, far = places()
    heads = query_w_ref.shape[0] // HD
    near = near_count(n)
    width = far_out.shape[2]
    row_count = tokens.shape[0]
    greet(n, dp, t, (mate, far))
    peak_ref[...] = jnp.full(peak_ref.shape, -1e30, FULL)
    for image in range(row_count // PIECE):
        tokens[image * PIECE : (image + 1) * PIECE, :] = padded_image(tokens_ref, image).astype(LOW)

    def image_forward(image):
        rows = image_rows(image)
        unit, _ = normalized(tokens[rows, :].astype(FULL))
        normed = (unit * gains_ref[0:1, :]).astype(LOW)
        normed_one[rows, :] = normed
        queries = dot_last(normed, query_w_ref[...]).astype(LOW)
        keys = dot_last(normed, key_w_ref[...]).astype(LOW)
        values = dot_last(normed, value_w_ref[...]).astype(LOW)
        query[rows, :] = queries
        key[rows, :] = keys
        value[rows, :] = values
        mixed = []
        for h in range(heads):
            cols = slice(h * HD, (h + 1) * HD)
            probs, top = attention_probs(queries[:, cols], keys[:, cols])
            real = lax.broadcasted_iota(jnp.int32, top.shape, 0) < SEQ
            best = jnp.max(jnp.where(real, top, -1e30), axis=0, keepdims=True)
            peak_ref[h : h + 1, :] = jnp.maximum(peak_ref[h : h + 1, :], best)
            mixed.append(dot_plain(probs.astype(LOW), values[:, cols]))
        mixed = jnp.concatenate(mixed, axis=1).astype(LOW)
        mixed_rows[rows, :] = mixed
        return dot_plain(mixed, output_w_ref[...])

    def normed_copy(j, owner):
        rows = normed_two.at[image_rows(2 * j + owner)]
        return remote(rows, rows, ns.at[j], nr.at[j], (dp, mate))

    def keep(i):
        return pltpu.make_async_copy(held[i], outs[i], hs.at[i])

    def finish(j):
        rows = image_rows(2 * j + half)
        residual = tokens[rows, :].astype(FULL) + total.result(j)
        residual_rows[j] = residual
        unit, _ = normalized(residual)
        normed_two[rows, :] = (unit * gains_ref[1:2, :]).astype(LOW)
        normed_copy(j, half).start()

    def peer(k):
        return (partner(dp, k, n), t)

    def half_rows():
        return pl.ds(pl.multiple_of(half * hp, hp), hp)

    def side_columns():
        return pl.ds(pl.multiple_of(side * width, width), width)

    def own_copy():
        return pltpu.make_async_copy(near_out.at[0], spread_hbm.at[0, half_rows()], own)

    def near_copy(k):
        return remote(near_out.at[k], spread_hbm.at[k, half_rows()], zs.at[k], zr.at[k], peer(k))

    def far_copy(k):
        return remote(
            far_out.at[k - near],
            spread_hbm.at[k, half_rows(), side_columns()],
            zs.at[k],
            zr.at[k],
            peer(k),
        )

    def side_copy(k, owner):
        columns = pl.ds(pl.multiple_of(owner * width, width), width)
        part = spread_hbm.at[k, half_rows(), columns]
        return remote(part, part, xs.at[k], xr.at[k], (dp, far))

    def forward(k, carry):
        far_copy(k).wait_recv()
        side_copy(k, side).start()
        return carry

    def dispatch(k):
        slots = lax.broadcasted_iota(jnp.int32, (hp, row_count), 0) + k * hp
        hot = (place_ref[0:1, :] == slots) | (place_ref[1:2, :] == slots)
        hot = jnp.where(hot, 1.0, 0.0).astype(LOW)

        @pl.when(k < near)
        def _():
            near_out[k] = dot_plain(hot, upstream[...]).astype(LOW)

            @pl.when(k == 0)
            def _():
                own_copy().start()

            @pl.when(k > 0)
            def _():
                near_copy(k).start()

        @pl.when(k >= near)
        def _():
            far_out[k - near] = dot_plain(hot, upstream[:, side_columns()]).astype(LOW)
            far_copy(k).start()

    def places_of_pairs():
        routes, slot_ids = routes_ref[...], slot_ids_ref[...]
        limits = jnp.zeros_like(routes)
        for e in range(n):
            limits = jnp.where(routes == e, capacity_ref[e], limits)
        kept = slot_ids < limits
        step = jnp.zeros_like(routes)
        weight = 1
        while weight < n:
            step = step + (routes // weight + dp // weight) % 2 * weight
            weight *= 2
        upper = slot_ids >= per_half
        in_half = slot_ids - jnp.where(upper, per_half, 0)
        in_block = in_half + jnp.where(upper, hp, 0)
        mine = kept & (upper == (half == 1))
        place = jnp.where(mine, step * hp + in_half, -1)
        position = jnp.where(kept, step * (2 * hp) + in_block, -1)
        both = jnp.concatenate([place, position, routes, jnp.full_like(routes, -1)], axis=0)
        fill = jnp.full((8, PIECE - SEQ), -1, jnp.int32)
        spaced = []
        for image in range(row_count // PIECE):
            spaced += [both[:, image * SEQ : (image + 1) * SEQ], fill]
        return jnp.concatenate(spaced, axis=1)

    pairs = places_of_pairs()
    place_ref[...] = pairs
    index_ref[...] = pairs.T
    def step(j, carry):
        given = image_forward(2 * j + 1 - half)

        @pl.when(j == 0)
        def _():
            await_greetings(n, (mate, far))

        total.give(j, given)
        total.take(j, image_forward(2 * j + half))

        @pl.when(j == 0)
        def _():
            for image in range(row_count // PIECE):
                upstream[image * PIECE : (image + 1) * PIECE, :] = padded_image(
                    upstream_ref, image
                ).astype(LOW)

        def turn(k, inner):
            dispatch(k)
            return inner

        @pl.when(j == 0)
        def _():
            lax.fori_loop(near, n, turn, 0)

        @pl.when(j == 1)
        def _():
            lax.fori_loop(0, near, turn, 0)

        @pl.when(j >= 1)
        def _():
            finish(j - 1)

        return carry

    lax.fori_loop(0, 3, step, 0)
    for i in range(7):
        keep(i).start()
    early = n - (n - near) // 4
    lax.fori_loop(near, early, forward, 0)
    finish(2)
    lax.fori_loop(early, n, forward, 0)
    keep(7).start()
    own_copy().wait()

    def arrive(k, carry):
        near_copy(k).wait()
        return carry

    def far_arrive(k, carry):
        far_copy(k).wait_send()
        side_copy(k, side).wait_send()
        side_copy(k, 1 - side).wait_recv()
        return carry

    for j in range(3):
        normed_copy(j, 1 - half).wait_recv()
    keep(8).start()
    lax.fori_loop(1, near, arrive, 0)
    lax.fori_loop(near, n, far_arrive, 0)
    for j in range(3):
        total.sent(j)
        normed_copy(j, half).wait_send()
    for i in range(9):
        keep(i).wait()


def run_front(n, hp, per_half, capacity, routes, slot_ids, tokens, upstream, gains, weights):
    model = tokens.shape[1]
    rows = tokens.shape[0] // SEQ * PIECE
    heads_width = weights[0].shape[0]
    near = near_count(n)
    width = model // 2
    vmem = pl.BlockSpec(memory_space=VMEM)
    hbm = pl.BlockSpec(memory_space=pl.ANY)
    shape = jax.ShapeDtypeStruct
    slim, wide = shape((rows, heads_width), LOW), shape((rows, model), LOW)
    held = (wide, wide, wide, slim, slim, slim, slim, shape((3, PIECE, model), FULL), wide)
    return pl.pallas_call(
        functools.partial(front_kernel, n, hp, per_half),
        out_shape=(
            shape((8, rows), jnp.int32),
            shape((rows, 8), jnp.int32),
            shape((8, 128), FULL),
            *held,
            shape((n, 2 * hp, model), LOW),
        ),
        in_specs=[pl.BlockSpec(memory_space=pltpu.SMEM)] + [vmem] * 9,
        out_specs=[vmem] * 3 + [hbm] * 10,
        scratch_shapes=[
            *[VMEM(a.shape, a.dtype) for a in held],
            VMEM((near, hp, model), LOW),
            VMEM((n - near, hp, width), LOW),
            dma(n),
            dma(n),
            pltpu.SemaphoreType.DMA,
            dma(3),
            dma(3),
            dma(9),
            dma(n),
            dma(n),
            *Total.scratch(model),
        ],
        compiler_params=pltpu.CompilerParams(
            collective_id=0, has_side_effects=True, vmem_limit_bytes=VMEM_LIMIT
        ),
        name="front",
    )(capacity, routes, slot_ids, tokens, upstream, gains, *weights)


def in_turn(i, near):
    return jnp.where(i < 2 * near, i // 2 + (i % 2) * near, i)


def expert_kernel(
    n,
    hp,
    place_ref,
    router_ref,
    peak_ref,
    normed_hbm,
    first_hbm,
    second_hbm,
    upstream_hbm,
    back_ref,
    gate_sum_ref,
    top_ref,
    answer_out_hbm,
    answer_kept_hbm,
    answer_ready_hbm,
    grad_first_hbm,
    grad_second_hbm,
    *scratch,
):
    dp, t, half, side, mate, far = places()
    arrived = scratch[2]
    spread = Spread(n, hp, place_ref, *scratch[:10])
    (
        normed_ref,
        first_ref,
        second_ref,
        answer_out,
        answer_kept,
        grad_first_ref,
        grad_second_ref,
        os_,
        ws,
        cs,
        cr,
        answer_far,
        answer_ready,
        xs,
        xr,
    ) = scratch[44:]
    (
        upstream,
        hidden_all,
        pre_grad_all,
        parts,
        pair_in,
        kept,
        far_out,
        far_in,
        final,
        gate_out,
        gate_in,
        sum_out,
        sum_in,
        sums,
        peaks,
        us,
        ps,
        pr,
        fs,
        fr,
        rs,
        rr,
        ms,
        mr,
        gs,
        gr,
        hs,
        hr,
        ks,
        kr,
        qs,
        qr,
        ss,
        sr,
    ) = scratch[10:44]
    model = normed_ref.shape[1]
    width = model // 2
    near = spread.near
    greet(n, dp, t, [(t + d) % 4 for d in (1, 2, 3)])
    fetches = [
        pltpu.make_async_copy(a, b, ws.at[i])
        for i, (a, b) in enumerate(
            ((normed_hbm, normed_ref), (first_hbm, first_ref), (second_hbm, second_ref))
        )
    ]
    mine = (slice(0, n), spread.rows(half))
    fetches.append(pltpu.make_async_copy(upstream_hbm.at[mine], upstream.at[mine], us.at[0]))
    for fetch in fetches:
        fetch.start()

    def upstream_pair_copy(k, owner):
        part = upstream.at[k, spread.rows(owner)]
        return remote(part, part, cs.at[k], cr.at[k], (dp, mate))

    def answer_side_copy(k):
        return remote(
            answer_out.at[k], answer_far.at[k - near], xs.at[k], xr.at[k], (dp, far)
        )

    def keep(i):
        pairs = (
            (answer_out.at[slice(0, near)], answer_out_hbm),
            (answer_kept.at[slice(0, near)], answer_kept_hbm),
            (answer_ready, answer_ready_hbm),
        )
        return pltpu.make_async_copy(*pairs[i], os_.at[i])

    def gate_copy(k):
        return remote(gate_out.at[k], gate_in.at[k, half], gs.at[k], gr.at[k], spread.peer(k))

    def gate_pair_copy(k, owner):
        tile = gate_in.at[k, owner]
        return remote(tile, tile, hs.at[k], hr.at[k], (dp, mate))

    def part_copy(i, k):
        return remote(
            parts.at[i % 3, :, spread.rows(1 - half)],
            pair_in.at[k],
            ps.at[i % 3],
            pr.at[k],
            (dp, mate),
        )

    def far_copy(i, k):
        return remote(far_out.at[i % SLOTS], far_in.at[k], fs.at[i % SLOTS], fr.at[k], (dp, far))

    def return_copy(k):
        return remote(
            final.at[k], back_ref.at[k, spread.rows(half)], rs.at[k], rr.at[k], spread.peer(k)
        )

    def mate_copy(k, owner):
        rows = back_ref.at[k, spread.rows(owner)]
        return remote(rows, rows, ms.at[k], mr.at[k], (dp, mate))

    def sum_copy(k):
        return remote(sum_out.at[k], sum_in.at[k], ks.at[k], kr.at[k], spread.peer(k))

    def peak_copy(k):
        return remote(peak_ref, peaks.at[k], qs.at[k], qr.at[k], spread.peer(k))

    def share_copy(d, owner):
        return remote(
            sums.at[owner], sums.at[owner], ss.at[d - 1], sr.at[d - 1], (dp, (t + d) % 4)
        )

    def loop(body, first=0, last=n):
        def one(k, carry):
            body(k)
            return carry

        lax.fori_loop(first, last, one, 0)

    fetches[0].wait()
    logits = dot_last(router_ref[...], normed_ref[...])
    rows_of = lax.broadcasted_iota(jnp.int32, logits.shape, 0)
    one, two = (
        jnp.sum(jnp.where(rows_of == place_ref[r : r + 1, :], logits, 0.0), axis=0, keepdims=True)
        for r in (4, 5)
    )
    best = jnp.maximum(one, two)
    one, two = jnp.exp(one - best), jnp.exp(two - best)
    gate_one, gate_two = one / (one + two), two / (one + two)
    await_greetings(n, (1, 2, 3))

    def dispatch(i):
        k = (i + near) % n
        is_first, is_second = spread.send(k, normed_ref)
        gate = jnp.sum(
            jnp.where(is_first, gate_one, 0.0) + jnp.where(is_second, gate_two, 0.0),
            axis=1,
            keepdims=True,
        )
        tile = jnp.broadcast_to(column_to_row(gate), (8, hp))

        @pl.when(k == 0)
        def _():
            gate_in[0, half] = tile

        @pl.when(k > 0)
        def _():
            gate_out[k] = tile
            gate_copy(k).start()

    loop(dispatch)
    for fetch in fetches[1:]:
        fetch.wait()
    loop(lambda i: upstream_pair_copy(in_turn(i, near), half).start())

    def chunk(i, k):
        gate = jnp.concatenate(
            [row_to_column(gate_in[k, 0, 0:1, :]), row_to_column(gate_in[k, 1, 0:1, :])], axis=0
        )
        gradient = upstream[k].astype(FULL)
        answer_grad = (gradient * gate).astype(LOW)
        pre = dot_plain(arrived[k], first_ref[...])
        share = 0.5 * (1.0 + lax.erf(pre * math.sqrt(0.5)))
        slope = share + pre * (jnp.exp(-0.5 * pre * pre) * (1.0 / math.sqrt(2.0 * math.pi)))
        hidden = (pre * share).astype(LOW)
        hidden_all[k] = hidden
        answer = dot_plain(hidden, second_ref[...])
        parts[i % 3, 0] = answer.astype(LOW)
        gate_sum = jnp.sum(answer * gradient, axis=1, keepdims=True)
        upstream[k] = answer_grad
        pre_grad = (dot_last(answer_grad, second_ref[...]) * slope).astype(LOW)
        pre_grad_all[k] = pre_grad
        parts[i % 3, 1] = dot_last(pre_grad, first_ref[...]).astype(LOW)
        tile = jnp.broadcast_to(column_to_row(gate_sum), (8, 2 * hp))

        @pl.when(k == 0)
        def _():
            sum_in[0] = tile

        @pl.when(k > 0)
        def _():
            sum_out[k] = tile
            sum_copy(k).start()
            peak_copy(k).start()

    tile = 256
    tiles = model // tile

    def grad_copy(m, j):
        cols = pl.ds(pl.multiple_of(m * tile, tile), tile)
        ref, hbm = ((grad_first_ref, grad_first_hbm), (grad_second_ref, grad_second_hbm))[j]
        return pltpu.make_async_copy(ref.at[cols], hbm.at[cols], os_.at[3 + 2 * m + j])

    def grads(m):
        cols = pl.ds(pl.multiple_of(m * tile, tile), tile)
        rows_in = arrived[:, :, cols].reshape(n * 2 * hp, tile)
        grad_first_ref[cols, :] = dot_first(rows_in, pre_grad_all[...].reshape(n * 2 * hp, -1))
        grad_copy(m, 0).start()
        hidden = hidden_all[:, :, cols].reshape(n * 2 * hp, tile)
        grad_second_ref[cols, :] = dot_first(hidden, upstream[...].reshape(n * 2 * hp, model))
        grad_copy(m, 1).start()

    def step(i):
        @pl.when(i < n)
        def _():
            spread.first_hop(in_turn(i, near))

        @pl.when((i >= 1) & (i < n + 1))
        def _():
            k = in_turn(i - 1, near)
            spread.second_hop(k)

            @pl.when(k > 0)
            def _():
                gate_copy(k).wait_recv()

            gate_pair_copy(k, half).start()

        @pl.when((i >= 2) & (i < n + 2))
        def _():
            k = in_turn(i - 2, near)
            spread.last_hop(k)
            gate_pair_copy(k, 1 - half).wait_recv()
            upstream_pair_copy(k, 1 - half).wait_recv()
            upstream_pair_copy(k, half).wait_send()

            @pl.when(i >= 5)
            def _():
                part_copy(i - 5, in_turn(i - 5, near)).wait_send()

            chunk(i - 2, k)
            part_copy(i - 2, k).start()

        @pl.when((i >= 3) & (i < n + 3))
        def _():
            k = in_turn(i - 3, near)
            part_copy(i - 3, k).wait_recv()

            @pl.when(i >= 3 + SLOTS)
            def _():
                far_copy(i - 3 - SLOTS, in_turn(i - 3 - SLOTS, near)).wait_send()

            for j in (1, 0):
                whole = parts[(i - 3) % 3, j, spread.rows(half), :].astype(FULL) + pair_in[k, j].astype(FULL)
                low, high = whole[:, :width], whole[:, width:]
                stays = jnp.where(side == 0, low, high)
                goes = jnp.where(side == 0, high, low).astype(LOW)
                if j:
                    kept[(i - 3) % SLOTS] = stays
                    far_out[(i - 3) % SLOTS] = goes
                    far_copy(i - 3, k).start()
                else:
                    answer_kept[k] = stays
                    answer_out[k] = goes

        @pl.when((i >= LAG) & (i < n + LAG))
        def _():
            k = in_turn(i - LAG, near)
            far_copy(i - LAG, k).wait_recv()
            rows = (kept[(i - LAG) % SLOTS] + far_in[k].astype(FULL)).astype(LOW)

            @pl.when(k == 0)
            def _():
                back_ref[0, spread.rows(half), :] = rows

            @pl.when(k > 0)
            def _():
                final[k] = rows
                return_copy(k).start()

        @pl.when(i == n + 2)
        def _():
            loop(lambda k: answer_side_copy(k).start(), near)

        @pl.when((i >= n + 2) & (i < n + 2 + tiles))
        def _():
            grads(i - (n + 2))

    loop(step, 0, n + max(LAG, 2 + tiles))
    keep(0).start()
    keep(1).start()
    peaks[0] = peak_ref[...]

    def collect_sums(k):
        @pl.when(k > 0)
        def _():
            peak_copy(k).wait_recv()
            sum_copy(k).wait_recv()

        sums[t, pl.ds(k, 1), :] = sum_in[k, 0:1, :]

    loop(collect_sums)
    for d in (1, 2, 3):
        share_copy(d, t).start()
    top_ref[...] = jnp.max(peaks[...], axis=0)

    def collect(i):
        k = in_turn(i, near)

        @pl.when(k > 0)
        def _():
            return_copy(k).wait_recv()

        mate_copy(k, half).start()

    loop(collect)

    def answers_whole(k):
        answer_side_copy(k).wait_recv()
        answer_ready[k - near] = (answer_kept[k] + answer_far[k - near].astype(FULL)).astype(LOW)

    loop(answers_whole, near)
    keep(2).start()
    for d in (1, 2, 3):
        share_copy(d, (t + 4 - d) % 4).wait_recv()
    whole = (sums[0] + sums[1]) + (sums[2] + sums[3])
    whole = jnp.concatenate([whole[k : k + 1] for k in range(n)], axis=1)
    gate_sum_ref[...] = jnp.broadcast_to(whole, gate_sum_ref.shape)

    def finish(i):
        k = in_turn(i, near)
        mate_copy(k, 1 - half).wait_recv()
        mate_copy(k, half).wait_send()
        spread.sent(k)
        gate_pair_copy(k, half).wait_send()

        @pl.when(k > 0)
        def _():
            return_copy(k).wait_send()
            gate_copy(k).wait_send()
            sum_copy(k).wait_send()
            peak_copy(k).wait_send()

        @pl.when(i >= n - 3)
        def _():
            part_copy(i, k).wait_send()

        @pl.when(i >= n - SLOTS)
        def _():
            far_copy(i, k).wait_send()

    loop(finish)
    for d in (1, 2, 3):
        share_copy(d, t).wait_send()
    loop(lambda k: answer_side_copy(k).wait_send(), near)
    for i in range(3):
        keep(i).wait()
    for m in range(tiles):
        grad_copy(m, 0).wait()
        grad_copy(m, 1).wait()


def run_experts(n, hp, place, router, peak, normed, first, second, upstream):
    model = normed.shape[1]
    width = model // 2
    hidden = first.shape[1]
    near = near_count(n)
    vmem = pl.BlockSpec(memory_space=VMEM)
    hbm = pl.BlockSpec(memory_space=pl.ANY)
    shape = jax.ShapeDtypeStruct
    return pl.pallas_call(
        functools.partial(expert_kernel, n, hp),
        out_shape=(
            shape((n, 2 * hp, width), LOW),
            shape((8, n * 2 * hp), FULL),
            shape(peak.shape, FULL),
            shape((near, hp, width), LOW),
            shape((near, hp, width), FULL),
            shape((n - near, hp, width), LOW),
            shape((model, hidden), FULL),
            shape((hidden, model), FULL),
        ),
        in_specs=[vmem] * 3 + [hbm] * 4,
        out_specs=[vmem] * 3 + [hbm] * 5,
        scratch_shapes=[
            *Spread.scratch(n, hp, width),
            VMEM((n, 2 * hp, model), LOW),
            *Spread.semaphores(n),
            VMEM((n, 2 * hp, model), LOW),
            VMEM((n, 2 * hp, hidden), LOW),
            VMEM((n, 2 * hp, hidden), LOW),
            VMEM((3, 2, 2 * hp, model), LOW),
            VMEM((n, 2, hp, model), LOW),
            VMEM((SLOTS, hp, width), FULL),
            VMEM((SLOTS, hp, width), LOW),
            VMEM((n, hp, width), LOW),
            VMEM((n, hp, width), LOW),
            VMEM((n, 8, hp), FULL),
            VMEM((n, 2, 8, hp), FULL),
            VMEM((n, 8, 2 * hp), FULL),
            VMEM((n, 8, 2 * hp), FULL),
            VMEM((4, n, 2 * hp), FULL),
            VMEM((n, *peak.shape), FULL),
            dma(1),
            dma(3), dma(n), dma(SLOTS), dma(n), dma(n), dma(n), dma(n), dma(n),
            dma(n), dma(n), dma(n), dma(n), dma(n), dma(n), dma(n), dma(n), dma(3), dma(3),
            VMEM(normed.shape, LOW),
            VMEM(first.shape, LOW),
            VMEM(second.shape, LOW),
            VMEM((n, hp, width), LOW),
            VMEM((n, hp, width), FULL),
            VMEM((model, hidden), FULL),
            VMEM((hidden, model), FULL),
            dma(3 + 2 * (model // 256)),
            dma(3), dma(n), dma(n),
            VMEM((n - near, hp, width), LOW),
            VMEM((n - near, hp, width), LOW),
            dma(n), dma(n),
        ],
        compiler_params=pltpu.CompilerParams(
            collective_id=1, has_side_effects=True, vmem_limit_bytes=VMEM_LIMIT
        ),
        name="experts",
    )(place, router, peak, normed, first, second, upstream)


def unpad(rows_ref, out_ref):
    for image in range(rows_ref.shape[0] // PIECE):
        start = image * SEQ // 8 * 8
        length = min(PIECE, out_ref.shape[0] - start)
        shift = image * SEQ - start
        rows = lax.broadcasted_iota(jnp.int32, (length, PIECE), 0)
        columns = lax.broadcasted_iota(jnp.int32, (length, PIECE), 1)
        pick = (rows == columns + shift) & (columns < SEQ)
        image_part = rows_ref[image * PIECE : (image + 1) * PIECE, :]
        moved = dot_plain(jnp.where(pick, 1.0, 0.0).astype(LOW), image_part).astype(LOW)
        if shift:
            before = lax.broadcasted_iota(jnp.int32, (8, moved.shape[1]), 0) < shift
            first = jnp.where(before, out_ref[start : start + 8, :].astype(FULL), moved[:8].astype(FULL))
            out_ref[start : start + 8, :] = first.astype(LOW)
            out_ref[start + 8 : start + length, :] = moved[8:]
        else:
            out_ref[start : start + length, :] = moved


def back_kernel(
    n,
    hp,
    back_ref,
    gate_sum_ref,
    index_ref,
    gains_ref,
    output_w_ref,
    router_ref,
    answer_ready,
    *refs,
):
    later, outs, scratch = refs[:13], refs[13:18], refs[18:]
    block_out_ref, tokens_out_ref, weights_ref, small_ref, gain_ref = outs
    held, scratch = scratch[:13], scratch[13:]
    (
        residual_ref,
        upstream_ref,
        answer_out,
        answer_kept,
        normed_one_ref,
        query_ref,
        key_ref,
        value_ref,
        mixed_ref,
        tokens_ref,
        query_w_ref,
        key_w_ref,
        value_w_ref,
    ) = held
    dp, t, half, side, mate, far = places()
    (
        moe_mine,
        moe_other,
        block_mine,
        block_other,
        attention_grad,
        residual_grad,
        query_grad,
        key_grad,
        value_grad,
        gain_two_sum,
        gain_two_in,
        gain_one_sum,
        gain_one_all,
        gain_rows,
        router_sum,
        router_in,
        totals,
        totals_two,
        pieces,
        pieces_in,
        small_pieces,
        small_in,
        answer_far,
        answer_final,
        answers,
        block_ref,
        grad_tokens_ref,
        hs,
        as_,
        ar,
        bs,
        br,
        ts,
        tr,
        cs,
        cr,
        gs,
        gr,
        ws,
        wr,
        ls,
        lr,
        os_,
        or_,
        vs,
        vr,
        ds,
        dr,
        es,
        er,
        fs,
        fr,
        ks,
        kr,
    ) = scratch[:54]
    total = Total(*scratch[54:])
    heads = query_w_ref.shape[0] // HD
    model = upstream_ref.shape[1]
    width = model // 2
    slots = back_ref.shape[0]
    piece = pieces.shape[1]
    near = near_count(n)
    greet(n, dp, t, [(t + d) % 4 for d in (1, 2, 3)])
    fetches = [pltpu.make_async_copy(a, b, hs.at[i]) for i, (a, b) in enumerate(zip(later, held))]
    for fetch in fetches:
        fetch.start()

    def peer(k):
        return (partner(dp, k, n), t)

    def moe_copy(j):
        return remote(moe_mine.at[j], moe_other.at[j], as_.at[j], ar.at[j], (dp, far))

    def block_copy(j):
        return remote(block_mine.at[j], block_other.at[j], bs.at[j], br.at[j], (dp, far))

    def attention_copy(j, owner):
        rows = attention_grad.at[image_rows(2 * j + owner)]
        return remote(rows, rows, ts.at[j], tr.at[j], (dp, mate))

    def tokens_copy(j, owner):
        rows = grad_tokens_ref.at[image_rows(2 * j + owner)]
        return remote(rows, rows, cs.at[j], cr.at[j], (dp, mate))

    def block_pair_copy(j, owner):
        rows = block_ref.at[image_rows(2 * j + owner)]
        return remote(rows, rows, ls.at[j], lr.at[j], (dp, mate))

    def gain_copy(d, owner):
        return remote(
            gain_one_all.at[owner], gain_one_all.at[owner], gs.at[d - 1], gr.at[d - 1], (dp, (t + d) % 4)
        )

    def gain_row_copy(k):
        return remote(gain_rows.at[0], gain_rows.at[k], ks.at[k], kr.at[k], peer(k))

    def router_copy():
        return remote(router_sum, router_in, os_.at[0], or_.at[0], (dp, mate))

    def gain_two_copy():
        return remote(gain_two_sum, gain_two_in, os_.at[1], or_.at[1], (dp, mate))

    def piece_copy(k):
        return remote(pieces.at[k], pieces_in.at[k], ws.at[k], wr.at[k], peer(k))

    def small_copy(k):
        return remote(small_pieces.at[k], small_in.at[k], vs.at[k], vr.at[k], peer(k))

    def answer_rows(k, owner):
        return answers.at[pl.ds(pl.multiple_of((2 * k + owner) * hp, hp), hp)]

    def answer_side_copy(k):
        return remote(answer_out.at[k], answer_far.at[k], ds.at[k], dr.at[k], (dp, far))

    def answer_copy(k):
        return remote(answer_final.at[k], answer_rows(k, half), es.at[k], er.at[k], peer(k))

    def far_answer_copy(k):
        return remote(answer_ready.at[k - near], answer_rows(k, half), es.at[k], er.at[k], peer(k))

    def answer_pair_copy(k, owner):
        return remote(answer_rows(k, owner), answer_rows(k, owner), fs.at[k], fr.at[k], (dp, mate))

    def loop(body, first=0, last=n):
        def one(k, carry):
            body(k)
            return carry

        lax.fori_loop(first, last, one, 0)

    def both_sides(mine, other):
        low = jnp.where(side == 0, mine, other)
        high = jnp.where(side == 0, other, mine)
        return jnp.concatenate([low, high], axis=1)

    def hots(rows):
        columns = lax.broadcasted_iota(jnp.int32, (PIECE, slots), 1)
        return index_ref[rows, 2:3] == columns, index_ref[rows, 3:4] == columns

    def as_low(mask):
        return jnp.where(mask, 1.0, 0.0).astype(LOW)

    gain_two_sum[...] = jnp.zeros_like(gain_two_sum)
    gain_one_sum[...] = jnp.zeros_like(gain_one_sum)
    router_sum[...] = jnp.zeros_like(router_sum)

    def combine(j):
        first, second = hots(image_rows(2 * j + half))
        moe_mine[j] = dot_plain(as_low(first | second), back_ref[...]).astype(LOW)

        @pl.when(j == 0)
        def _():
            await_greetings(n, (1, 2, 3))
            loop(lambda k: far_answer_copy(k).start(), near)

        moe_copy(j).start()

    loop(combine, 0, 3)
    for fetch in fetches[:3]:
        fetch.wait()
    loop(lambda k: answer_side_copy((k + 1) % near).start(), 0, near)

    def gates_of(rows, normed):
        logits = dot_last(normed, router_ref[...])
        lanes = lax.broadcasted_iota(jnp.int32, logits.shape, 1)
        hot_one = index_ref[rows, 4:5] == lanes
        hot_two = index_ref[rows, 5:6] == lanes
        one = jnp.sum(jnp.where(hot_one, logits, 0.0), axis=1, keepdims=True)
        two = jnp.sum(jnp.where(hot_two, logits, 0.0), axis=1, keepdims=True)
        top = jnp.maximum(one, two)
        one, two = jnp.exp(one - top), jnp.exp(two - top)
        return one / (one + two), two / (one + two), hot_one, hot_two

    def moe_back(j):
        rows = image_rows(2 * j + half)
        unit, factor = normalized(residual_ref[j])
        normed = (unit * gains_ref[1:2, :]).astype(LOW)
        gate_one, gate_two, hot_one, hot_two = gates_of(rows, normed)
        first, second = hots(rows)
        slot_sums = gate_sum_ref[0:1, :]
        grad_one = jnp.sum(jnp.where(first, slot_sums, 0.0), axis=1, keepdims=True)
        grad_two = jnp.sum(jnp.where(second, slot_sums, 0.0), axis=1, keepdims=True)
        mean = gate_one * grad_one + gate_two * grad_two
        logit_grad = jnp.where(hot_one, gate_one * (grad_one - mean), 0.0)
        logit_grad = logit_grad + jnp.where(hot_two, gate_two * (grad_two - mean), 0.0)
        logit_grad = logit_grad.astype(LOW)
        router_sum[...] += dot_first(normed, logit_grad)
        normed_grad = dot_plain(logit_grad, router_ref[...])
        moe_copy(j).wait_recv()
        normed_grad = normed_grad + both_sides(moe_mine[j].astype(FULL), moe_other[j].astype(FULL))
        gain_two_sum[...] += jnp.sum((normed_grad * unit).reshape(PIECE // 8, 8, model), axis=0)
        grad = normalized_back(normed_grad * gains_ref[1:2, :], unit, factor)
        grad = grad + upstream_ref[rows, :].astype(FULL)
        residual_grad[j] = grad
        attention_grad[rows, :] = grad.astype(LOW)
        attention_copy(j, half).start()

    loop(moe_back, 0, 3)
    router_copy().start()
    gain_two_copy().start()
    for fetch in fetches[3:]:
        fetch.wait()

    def image_back(image):
        rows = image_rows(image)
        mixed_grad = dot_last(attention_grad[rows, :], output_w_ref[...]).astype(LOW)
        queries, keys, values = query_ref[rows, :], key_ref[rows, :], value_ref[rows, :]
        query_parts, key_parts, value_parts = [], [], []
        for h in range(heads):
            cols = slice(h * HD, (h + 1) * HD)
            probs, _ = attention_probs(queries[:, cols], keys[:, cols])
            value_parts.append(dot_first(probs.astype(LOW), mixed_grad[:, cols]))
            probs_grad = dot_last(mixed_grad[:, cols], values[:, cols])
            level = jnp.sum(probs * probs_grad, axis=1, keepdims=True)
            score_grad = (probs * (probs_grad - level)).astype(LOW)
            query_parts.append(dot_plain(score_grad, keys[:, cols]) * HD**-0.5)
            key_parts.append(dot_first(score_grad, queries[:, cols]) * HD**-0.5)
        grads = [jnp.concatenate(p, axis=1).astype(LOW) for p in (query_parts, key_parts, value_parts)]
        query_grad[rows, :], key_grad[rows, :], value_grad[rows, :] = grads

    def answer_turn(k):
        answer_side_copy(k).wait_recv()
        rows = (answer_kept[k] + answer_far[k].astype(FULL)).astype(LOW)

        @pl.when(k == 0)
        def _():
            answer_rows(0, half)[...] = rows

        @pl.when(k > 0)
        def _():
            answer_final[k] = rows
            answer_copy(k).start()

    def grad_part(image):
        rows = image_rows(image)
        part = dot_plain(query_grad[rows, :], query_w_ref[...])
        part = part + dot_plain(key_grad[rows, :], key_w_ref[...])
        part = part + dot_plain(value_grad[rows, :], value_w_ref[...])
        unit, _ = normalized(tokens_ref[rows, :].astype(FULL))
        gain_one_sum[...] += jnp.sum((part * unit).reshape(PIECE // 8, 8, model), axis=0)
        return part

    def my_piece(source, k):
        at = partner(dp, k, n) * piece
        grain = math.gcd(piece, 8)
        span = -(-(piece + 8 - grain) // 8) * 8
        taken = source[pl.ds(pl.multiple_of(at // 8 * 8, 8), span), :]
        rows = taken[:piece]
        for shift in range(grain, 8, grain):
            rows = jnp.where(at % 8 == shift, taken[shift : shift + piece], rows)
        return rows.astype(LOW)

    def small_grads():
        router_copy().wait_recv()
        gain_two_copy().wait_recv()
        row = jnp.sum(gain_two_sum[...] + gain_two_in[...], axis=0, keepdims=True)
        column = jnp.concatenate(
            [row_to_column(row[:, i : i + 256]) for i in range(0, model, 256)], axis=0
        )
        totals_two[...] = jnp.concatenate(
            [
                dot_first(attention_grad[...], mixed_ref[...]),
                router_sum[...] + router_in[...],
                column,
            ],
            axis=1,
        )

        def send_small(i):
            k = (i + near) % n
            small_pieces[k] = my_piece(totals_two, k)

            @pl.when(k > 0)
            def _():
                small_copy(k).start()

        loop(send_small)

    for j in range(3):
        attention_copy(j, 1 - half).wait_recv()

    def attention_back(j):
        for owner in (1 - half, half):
            image_back(2 * j + owner)
        total.give(j, grad_part(2 * j + 1 - half))
        total.take(j, grad_part(2 * j + half))
        answer_turn((j + 1) % near)

        @pl.when(j == 1)
        def _():
            small_grads()

        @pl.when(j == 2)
        def _():
            answer_turn(0)

    loop(attention_back, 0, 3)

    gain_one_all[t] = jnp.sum(gain_one_sum[...], axis=0, keepdims=True)
    for d in (1, 2, 3):
        gain_copy(d, t).start()
    normed_one = normed_one_ref[...]
    totals[:, : 3 * query_grad.shape[1]] = jnp.concatenate(
        [
            dot_first(normed_one, query_grad[...]),
            dot_first(normed_one, key_grad[...]),
            dot_first(normed_one, value_grad[...]),
        ],
        axis=1,
    )

    def send_piece(i):
        k = (i + near) % n
        pieces[k] = my_piece(totals, k)

        @pl.when(k > 0)
        def _():
            piece_copy(k).start()

    loop(send_piece)


    def answers_here(i):
        k = in_turn(i, near)

        @pl.when((k > 0) & (k < near))
        def _():
            answer_copy(k).wait_recv()

        @pl.when(k >= near)
        def _():
            far_answer_copy(k).wait_recv()

        answer_pair_copy(k, half).start()

    loop(answers_here)
    loop(lambda k: answer_pair_copy(k, 1 - half).wait_recv())

    def block_rows(j):
        rows = image_rows(2 * j + half)
        residual = residual_ref[j]
        unit, _ = normalized(residual)
        gate_one, gate_two, _, _ = gates_of(rows, (unit * gains_ref[1:2, :]).astype(LOW))
        first, second = hots(rows)
        from_first = dot_plain(as_low(first), answers[...])
        from_second = dot_plain(as_low(second), answers[...])
        mine = jnp.where(side == 0, residual[:, :width], residual[:, width:])
        block_mine[j] = (mine + (gate_one * from_first + gate_two * from_second)).astype(LOW)
        block_copy(j).start()

    loop(block_rows, 0, 3)

    def tokens_back(j):
        rows = image_rows(2 * j + half)
        normed_grad = total.result(j)
        unit, factor = normalized(tokens_ref[rows, :].astype(FULL))
        grad = normalized_back(normed_grad * gains_ref[0:1, :], unit, factor)
        grad_tokens_ref[rows, :] = (residual_grad[j] + grad).astype(LOW)
        tokens_copy(j, half).start()

    loop(tokens_back, 0, 3)
    for d in (1, 2, 3):
        gain_copy(d, (t + 4 - d) % 4).wait_recv()
    gain_rows[0] = (gain_one_all[0] + gain_one_all[1]) + (gain_one_all[2] + gain_one_all[3])

    def send_gain(k):
        gain_row_copy(k).start()

    loop(send_gain, 1)

    def block_back(j):
        block_copy(j).wait_recv()
        block_ref[image_rows(2 * j + half), :] = both_sides(block_mine[j], block_other[j])
        block_pair_copy(j, half).start()

    for j in range(3):
        tokens_copy(j, 1 - half).wait_recv()
    unpad(grad_tokens_ref, tokens_out_ref)
    loop(block_back, 0, 3)
    for j in range(3):
        block_pair_copy(j, 1 - half).wait_recv()
    unpad(block_ref, block_out_ref)
    pieces_in[0] = pieces[0]
    small_in[0] = small_pieces[0]

    def arrive(k):
        piece_copy(k).wait_recv()
        small_copy(k).wait_recv()
        gain_row_copy(k).wait_recv()

    loop(arrive, 1)
    weights_ref[...] = jnp.sum(pieces_in[...].astype(FULL), axis=0)
    small_ref[...] = jnp.sum(small_in[...].astype(FULL), axis=0)
    gain_ref[...] = jnp.sum(gain_rows[...], axis=0)

    for j in range(3):
        moe_copy(j).wait_send()
        block_copy(j).wait_send()
        attention_copy(j, half).wait_send()
        total.sent(j)
        tokens_copy(j, half).wait_send()
        block_pair_copy(j, half).wait_send()
        gain_copy(j + 1, t).wait_send()
    router_copy().wait_send()
    gain_two_copy().wait_send()

    def left(k):
        @pl.when(k < near)
        def _():
            answer_side_copy(k).wait_send()

        @pl.when((k > 0) & (k < near))
        def _():
            answer_copy(k).wait_send()

        @pl.when(k >= near)
        def _():
            far_answer_copy(k).wait_send()

        answer_pair_copy(k, half).wait_send()

        @pl.when(k > 0)
        def _():
            piece_copy(k).wait_send()
            small_copy(k).wait_send()
            gain_row_copy(k).wait_send()

    loop(left)


def run_back(n, hp, row_count, first, later):
    upstream = later[1]
    rows, model = upstream.shape
    heads_width = later[8].shape[1]
    width = model // 2
    piece = model // n
    vmem = pl.BlockSpec(memory_space=VMEM)
    shape = jax.ShapeDtypeStruct
    slim = VMEM((3, PIECE, width), LOW)
    heads = VMEM((rows, heads_width), LOW)
    eight = VMEM((8, model), FULL)
    wide, narrow = 3 * heads_width, heads_width + n + 1
    quarter = VMEM((near_count(n), hp, width), LOW)
    three, many = dma(3), dma(n)
    return pl.pallas_call(
        functools.partial(back_kernel, n, hp),
        out_shape=(
            shape((row_count, model), LOW),
            shape((row_count, model), LOW),
            shape((piece, wide), FULL),
            shape((piece, narrow), FULL),
            shape((1, model), FULL),
        ),
        in_specs=[vmem] * (len(first) - 1) + [pl.BlockSpec(memory_space=pl.ANY)] * (1 + len(later)),
        out_specs=[vmem] * 5,
        scratch_shapes=[
            *[VMEM(a.shape, a.dtype) for a in later],
            slim, slim, slim, slim,
            VMEM((rows, model), LOW),
            VMEM((3, PIECE, model), FULL),
            heads, heads, heads,
            eight, eight, eight,
            VMEM((4, 1, model), FULL),
            VMEM((n, 1, model), FULL),
            VMEM((model, n), FULL),
            VMEM((model, n), FULL),
            VMEM((model, wide), FULL),
            VMEM((model, narrow), FULL),
            VMEM((n, piece, wide), LOW),
            VMEM((n, piece, wide), LOW),
            VMEM((n, piece, narrow), LOW),
            VMEM((n, piece, narrow), LOW),
            quarter, quarter,
            VMEM((n * 2 * hp, width), LOW),
            VMEM((rows, model), LOW),
            VMEM((rows, model), LOW),
            dma(len(later)),
            three, three, three, three, three, three, three, three, three, three,
            many, many, three, three, dma(2), dma(2),
            many, many, many, many, many, many, many, many, many, many,
            *Total.scratch(model),
        ],
        compiler_params=pltpu.CompilerParams(
            collective_id=2, has_side_effects=True, vmem_limit_bytes=VMEM_LIMIT
        ),
        name="back",
    )(*first, *later)


def results_kernel(
    threshold_ref,
    weights_ref,
    small_ref,
    gain_row_ref,
    top_ref,
    query_w_ref,
    key_w_ref,
    *refs,
):
    moved_in, moved_out = refs[:4], refs[4:8]
    (
        gain_one_ref,
        gain_two_ref,
        query_ref,
        key_ref,
        value_ref,
        output_ref,
        router_ref,
        clipped_query_ref,
        clipped_key_ref,
        head_max_ref,
        *held,
        sems,
    ) = refs[8:]
    fetches, copies = [], []
    for i, (source, target) in enumerate(zip(moved_in, moved_out)):
        rows = source.shape[0]
        cut = rows // 16 * 8
        for part, at in enumerate((slice(0, cut), slice(cut, rows))):
            sem = sems.at[2 * i + part]
            fetches.append(pltpu.make_async_copy(source.at[at], held[i].at[at], sem))
            sem = sems.at[8 + 2 * i + part]
            copies.append(pltpu.make_async_copy(held[i].at[at], target.at[at], sem))
    for fetch in fetches:
        fetch.start()
    for fetch, copy in zip(fetches, copies):
        fetch.wait()
        copy.start()
    piece, wide = query_ref.shape
    heads = head_max_ref.shape[0]
    query_ref[...] = weights_ref[:, :wide]
    key_ref[...] = weights_ref[:, wide : 2 * wide]
    value_ref[...] = weights_ref[:, 2 * wide :]
    small = small_ref[...]
    output_ref[...] = small[:, :wide].T
    n = router_ref.shape[0]
    router_ref[...] = small[:, wide : wide + n].T
    gain_two_ref[...] = column_to_row(small[:, wide + n :])[0]
    model = gain_row_ref.shape[1]
    lanes = lax.broadcasted_iota(jnp.int32, (piece, model), 1)
    mine = lax.broadcasted_iota(jnp.int32, (piece, model), 0) + lax.axis_index("dp") * piece
    column = jnp.sum(jnp.where(lanes == mine, gain_row_ref[...], 0.0), axis=1, keepdims=True)
    gain_one_ref[...] = column_to_row(column)[0]
    head_max_ref[...] = column_to_row(top_ref[:, 0:1])[0, :heads]
    for h in range(heads):
        rows = slice(h * HD, (h + 1) * HD)
        factor = jnp.sqrt(jnp.minimum(1.0, threshold_ref[h] / top_ref[h : h + 1, 0:1]))
        clipped_query_ref[rows, :] = query_w_ref[rows, :].astype(FULL) * factor
        clipped_key_ref[rows, :] = key_w_ref[rows, :].astype(FULL) * factor
    for copy in copies:
        copy.wait()


def run_results(n, threshold, weights, small, gain_row, top, query_w, key_w, moved):
    wide, model = query_w.shape
    piece = weights.shape[0]
    shape = jax.ShapeDtypeStruct
    vmem = pl.BlockSpec(memory_space=VMEM)
    hbm = pl.BlockSpec(memory_space=pl.ANY)
    grad, clipped = shape((piece, wide), FULL), shape((wide, model), FULL)
    return pl.pallas_call(
        results_kernel,
        out_shape=(
            *[shape(a.shape, a.dtype) for a in moved],
            shape((piece,), FULL),
            shape((piece,), FULL),
            grad,
            grad,
            grad,
            shape((wide, piece), FULL),
            shape((n, piece), FULL),
            clipped,
            clipped,
            shape(threshold.shape, FULL),
        ),
        in_specs=[pl.BlockSpec(memory_space=pltpu.SMEM)] + [vmem] * 6 + [hbm] * 4,
        out_specs=[hbm] * 4 + [vmem] * 10,
        scratch_shapes=[*[VMEM(a.shape, a.dtype) for a in moved], dma(16)],
        compiler_params=pltpu.CompilerParams(vmem_limit_bytes=VMEM_LIMIT),
        name="results",
    )(threshold, weights, small, gain_row, top, query_w, key_w, *moved)


def body(
    tokens,
    gain_attn,
    w_query,
    w_key,
    w_value,
    w_output,
    gain_moe,
    w_router,
    expert_in,
    expert_out,
    routes,
    slot_ids,
    capacity,
    threshold,
    cotangent,
):
    n = lax.axis_size("dp")
    row_count, model = tokens.shape
    slot_count = 23 * TOK_DEV // (10 * n) + 1
    per_half = -(-slot_count // 2)
    hp = -(-per_half // 16) * 16
    gains = jnp.stack([gain_attn, gain_moe]).astype(FULL)
    across = (w_query.T, w_key.T, w_value.T)
    (
        place,
        index,
        peak,
        tokens_in,
        upstream,
        normed_one,
        query,
        key,
        value,
        mixed,
        residual,
        normed_two,
        spread,
    ) = run_front(
        n,
        hp,
        per_half,
        capacity,
        routes.T,
        slot_ids.T,
        tokens,
        cotangent,
        gains,
        (*across, w_output),
    )
    router = w_router.T
    back, gate_sums, top, answer_out, answer_kept, answer_ready, grad_first, grad_second = run_experts(
        n, hp, place, router, peak, normed_two, expert_in[0], expert_out[0], spread
    )
    block_out, grad_tokens, weight_grads, small, gain_rows = run_back(
        n,
        hp,
        row_count,
        (back.reshape(n * 2 * hp, -1), gate_sums, index, gains, w_output, router, answer_ready),
        (
            residual,
            upstream,
            answer_out,
            answer_kept,
            normed_one,
            query,
            key,
            value,
            mixed,
            tokens_in,
            *across,
        ),
    )
    (
        block_out,
        grad_tokens,
        grad_first,
        grad_second,
        gain_one,
        gain_two,
        grad_query,
        grad_key,
        grad_value,
        grad_output,
        grad_router,
        clipped_query,
        clipped_key,
        head_max,
    ) = run_results(
        n,
        threshold,
        weight_grads,
        small,
        gain_rows,
        top,
        *across[:2],
        (block_out, grad_tokens, grad_first, grad_second),
    )
    return (
        block_out,
        grad_tokens,
        gain_one,
        gain_two,
        grad_query,
        grad_key,
        grad_value,
        grad_output,
        grad_router.T,
        grad_first[None],
        grad_second[None],
        clipped_query.T,
        clipped_key.T,
        head_max,
    )


def solution(mesh):
    in_specs = (
        P("dp", None),
        P(),
        P(None, "tensor"),
        P(None, "tensor"),
        P(None, "tensor"),
        P("tensor", None),
        P(),
        P(),
        P("dp", None, "tensor"),
        P("dp", "tensor", None),
        P("dp", None),
        P("dp", None),
        P(),
        P("tensor"),
        P("dp", None),
    )
    out_specs = (
        P("dp", None),
        P("dp", None),
        P("dp"),
        P("dp"),
        P("dp", "tensor"),
        P("dp", "tensor"),
        P("dp", "tensor"),
        P("tensor", "dp"),
        P("dp", None),
        P("dp", None, "tensor"),
        P("dp", "tensor", None),
        P(None, "tensor"),
        P(None, "tensor"),
        P("tensor"),
    )
    return jax.shard_map(body, mesh=mesh, in_specs=in_specs, out_specs=out_specs, check_vma=False)
```

```python
import functools
import math

import jax
import jax.numpy as jnp
from jax import lax
from jax.experimental import pallas as pl
from jax.experimental.pallas import tpu as pltpu
from jax.sharding import PartitionSpec as P

HD = 64
SEQ = 197
PIECE = 208
SENT = slice(0, 200)
TOK_DEV = 1182
EPSILON = 1e-06
MESH = pl.DeviceIdType.MESH
VMEM_LIMIT = 60 * 2**20
SLOTS = 3
LAG = 4
VMEM = pltpu.VMEM
LOW, FULL = jnp.bfloat16, jnp.float32


def dot_plain(a, b):
    return jnp.dot(a, b, preferred_element_type=FULL)


def dot_last(a, b):
    return lax.dot_general(a, b, (((1,), (1,)), ((), ())), preferred_element_type=FULL)


def dot_first(a, b):
    return lax.dot_general(a, b, (((0,), (0,)), ((), ())), preferred_element_type=FULL)


def normalized(rows):
    centered = rows - jnp.mean(rows, axis=-1, keepdims=True)
    factor = lax.rsqrt(jnp.mean(centered * centered, axis=-1, keepdims=True) + EPSILON)
    return centered * factor, factor


def normalized_back(u, unit, factor):
    first = jnp.mean(u, axis=-1, keepdims=True)
    second = jnp.mean(u * unit, axis=-1, keepdims=True)
    return factor * (u - first - unit * second)


def same_index(size):
    rows = lax.broadcasted_iota(jnp.int32, (size, size), 0)
    return rows == lax.broadcasted_iota(jnp.int32, (size, size), 1)


def row_to_column(row):
    return jnp.sum(jnp.where(same_index(row.shape[1]), row, 0.0), axis=1, keepdims=True)


def column_to_row(column):
    return jnp.sum(jnp.where(same_index(column.shape[0]), column, 0.0), axis=0, keepdims=True)


def attention_probs(queries, keys):
    scores = dot_last(queries, keys) * HD**-0.5
    real = lax.broadcasted_iota(jnp.int32, scores.shape, 1) < SEQ
    scores = jnp.where(real, scores, -1e30)
    top = jnp.max(scores, axis=1, keepdims=True)
    powers = jnp.exp(scores - top)
    return powers * (1.0 / jnp.sum(powers, axis=1, keepdims=True)), top


def partner(dp, k, n):
    other, weight = 0, 1
    while weight < n:
        other = other + ((dp // weight + k // weight) % 2) * weight
        weight *= 2
    return other


def places():
    dp = lax.axis_index("dp")
    t = lax.axis_index("tensor")
    return dp, t, t % 2, t // 2, t + 1 - 2 * (t % 2), (t + 2) % 4


def remote(src, dst, sends, recvs, device):
    return pltpu.make_async_remote_copy(
        src_ref=src,
        dst_ref=dst,
        send_sem=sends,
        recv_sem=recvs,
        device_id=device,
        device_id_type=MESH,
    )


def signal(sem, device):
    pl.semaphore_signal(sem, inc=1, device_id=device, device_id_type=MESH)


def greet(n, dp, t, others):
    barrier = pltpu.get_barrier_semaphore()

    def one(k, carry):
        signal(barrier, (partner(dp, k, n), t))
        return carry

    lax.fori_loop(1, n, one, 0)
    for other in others:
        signal(barrier, (dp, other))


def await_greetings(n, others):
    pl.semaphore_wait(pltpu.get_barrier_semaphore(), n - 1 + len(others))


def image_rows(image):
    return pl.ds(pl.multiple_of(image * PIECE, PIECE), PIECE)


def dma(*shape):
    return pltpu.SemaphoreType.DMA(shape)


def near_count(n):
    return min(4, n)


class Spread:
    def __init__(self, n, hp, place, near_out, far_out, arrived, zs, zr, xs, xr, cs, cr, own):
        self.n, self.hp, self.near = n, hp, near_count(n)
        self.place, self.near_out, self.far_out, self.arrived = place, near_out, far_out, arrived
        self.zs, self.zr, self.xs, self.xr, self.cs, self.cr, self.own = zs, zr, xs, xr, cs, cr, own
        self.dp, self.t, self.half, self.side, self.mate, self.far = places()
        self.width = far_out.shape[2]

    def rows(self, owner):
        return pl.ds(pl.multiple_of(owner * self.hp, self.hp), self.hp)

    def columns(self, owner):
        return pl.ds(pl.multiple_of(owner * self.width, self.width), self.width)

    def peer(self, k):
        return (partner(self.dp, k, self.n), self.t)

    def own_copy(self):
        return pltpu.make_async_copy(
            self.near_out.at[0], self.arrived.at[0, self.rows(self.half)], self.own
        )

    def near_copy(self, k):
        return remote(
            self.near_out.at[k],
            self.arrived.at[k, self.rows(self.half)],
            self.zs.at[k],
            self.zr.at[k],
            self.peer(k),
        )

    def far_copy(self, k):
        return remote(
            self.far_out.at[k - self.near],
            self.arrived.at[k, self.rows(self.half), self.columns(self.side)],
            self.zs.at[k],
            self.zr.at[k],
            self.peer(k),
        )

    def side_copy(self, k, side):
        part = self.arrived.at[k, self.rows(self.half), self.columns(side)]
        return remote(part, part, self.xs.at[k], self.xr.at[k], (self.dp, self.far))

    def pair_copy(self, k, half):
        part = self.arrived.at[k, self.rows(half)]
        return remote(part, part, self.cs.at[k], self.cr.at[k], (self.dp, self.mate))

    def hot(self, k, row_count):
        slots = lax.broadcasted_iota(jnp.int32, (self.hp, row_count), 0) + k * self.hp
        is_first = self.place[0:1, :] == slots
        is_second = self.place[1:2, :] == slots
        return is_first, is_second

    def send(self, k, rows_ref):
        is_first, is_second = self.hot(k, rows_ref.shape[0])
        hot = jnp.where(is_first | is_second, 1.0, 0.0).astype(LOW)

        @pl.when(k < self.near)
        def _():
            self.near_out[k] = dot_plain(hot, rows_ref[...]).astype(LOW)

            @pl.when(k == 0)
            def _():
                self.own_copy().start()

            @pl.when(k > 0)
            def _():
                self.near_copy(k).start()

        @pl.when(k >= self.near)
        def _():
            mine = rows_ref[:, self.columns(self.side)]
            self.far_out[k - self.near] = dot_plain(hot, mine).astype(LOW)
            self.far_copy(k).start()

        return is_first, is_second

    def first_hop(self, k):
        @pl.when(k == 0)
        def _():
            self.own_copy().wait()

        @pl.when((k > 0) & (k < self.near))
        def _():
            self.near_copy(k).wait_recv()

        @pl.when(k >= self.near)
        def _():
            self.far_copy(k).wait_recv()
            self.side_copy(k, self.side).start()

    def second_hop(self, k):
        @pl.when(k >= self.near)
        def _():
            self.side_copy(k, 1 - self.side).wait_recv()

        self.pair_copy(k, self.half).start()

    def last_hop(self, k):
        self.pair_copy(k, 1 - self.half).wait_recv()

    def sent(self, k):
        @pl.when((k > 0) & (k < self.near))
        def _():
            self.near_copy(k).wait_send()

        @pl.when(k >= self.near)
        def _():
            self.far_copy(k).wait_send()
            self.side_copy(k, self.side).wait_send()

        self.pair_copy(k, self.half).wait_send()

    @staticmethod
    def scratch(n, hp, width):
        near = near_count(n)
        return [VMEM((near, hp, 2 * width), LOW), VMEM((n - near, hp, width), LOW)]

    @staticmethod
    def semaphores(n):
        return [dma(n), dma(n), dma(n), dma(n), dma(n), dma(n), pltpu.SemaphoreType.DMA]


def clear_unsent(rows_in):
    count, rows, width = rows_in.shape
    rows_in[:, SENT.stop :, :] = jnp.zeros((count, rows - SENT.stop, width), rows_in.dtype)


class Total:
    def __init__(self, part_out, pair_in, far_out, far_in, ps, pr, fs, fr):
        self.part_out, self.pair_in, self.far_out, self.far_in = part_out, pair_in, far_out, far_in
        self.ps, self.pr, self.fs, self.fr = ps, pr, fs, fr
        self.dp, _, _, _, self.mate, self.far = places()
        clear_unsent(far_in)

    def pair_copy(self, j):
        return remote(
            self.part_out.at[j], self.pair_in.at[j], self.ps.at[j], self.pr.at[j], (self.dp, self.mate)
        )

    def far_copy(self, j):
        return remote(
            self.far_out.at[j, SENT],
            self.far_in.at[j, SENT],
            self.fs.at[j],
            self.fr.at[j],
            (self.dp, self.far),
        )

    def give(self, j, rows):
        self.part_out[j] = rows
        self.pair_copy(j).start()

    def take(self, j, rows):
        self.pair_copy(j).wait_recv()
        self.far_out[j] = (rows + self.pair_in[j]).astype(LOW)
        self.far_copy(j).start()

    def result(self, j):
        self.far_copy(j).wait_recv()
        return self.far_out[j].astype(FULL) + self.far_in[j].astype(FULL)

    def sent(self, j):
        self.pair_copy(j).wait_send()
        self.far_copy(j).wait_send()

    @staticmethod
    def scratch(model):
        wide, slim = VMEM((3, PIECE, model), FULL), VMEM((3, PIECE, model), LOW)
        return [wide, wide, slim, slim, dma(3), dma(3), dma(3), dma(3)]


def padded_image(rows_ref, image):
    start = image * SEQ // 8 * 8
    length = min(PIECE, rows_ref.shape[0] - start)
    rows = lax.broadcasted_iota(jnp.int32, (PIECE, length), 0)
    columns = lax.broadcasted_iota(jnp.int32, (PIECE, length), 1)
    pick = (columns == rows + (image * SEQ - start)) & (rows < SEQ)
    return dot_plain(jnp.where(pick, 1.0, 0.0).astype(LOW), rows_ref[start : start + length, :])


def front_kernel(
    n,
    hp,
    per_half,
    capacity_ref,
    routes_ref,
    slot_ids_ref,
    tokens_ref,
    upstream_ref,
    gains_ref,
    query_w_ref,
    key_w_ref,
    value_w_ref,
    output_w_ref,
    place_ref,
    index_ref,
    peak_ref,
    *refs,
):
    outs, spread_hbm, scratch = refs[:9], refs[9], refs[10:]
    held, scratch = scratch[:9], scratch[9:]
    (
        tokens,
        upstream,
        normed_one,
        query,
        key,
        value,
        mixed_rows,
        residual_rows,
        normed_two,
    ) = held
    near_out, far_out, zs, zr, own, ns, nr, hs, xs, xr = scratch[:10]
    total = Total(*scratch[10:])
    dp, t, half, side, mate, far = places()
    heads = query_w_ref.shape[0] // HD
    near = near_count(n)
    width = far_out.shape[2]
    row_count = tokens.shape[0]
    greet(n, dp, t, (mate, far))
    peak_ref[...] = jnp.full(peak_ref.shape, -1e30, FULL)
    for image in range(row_count // PIECE):
        tokens[image * PIECE : (image + 1) * PIECE, :] = padded_image(tokens_ref, image).astype(LOW)

    def image_forward(image):
        rows = image_rows(image)
        unit, _ = normalized(tokens[rows, :].astype(FULL))
        normed = (unit * gains_ref[0:1, :]).astype(LOW)
        normed_one[rows, :] = normed
        queries = dot_last(normed, query_w_ref[...]).astype(LOW)
        keys = dot_last(normed, key_w_ref[...]).astype(LOW)
        values = dot_last(normed, value_w_ref[...]).astype(LOW)
        query[rows, :] = queries
        key[rows, :] = keys
        value[rows, :] = values
        mixed = []
        for h in range(heads):
            cols = slice(h * HD, (h + 1) * HD)
            probs, top = attention_probs(queries[:, cols], keys[:, cols])
            real = lax.broadcasted_iota(jnp.int32, top.shape, 0) < SEQ
            best = jnp.max(jnp.where(real, top, -1e30), axis=0, keepdims=True)
            peak_ref[h : h + 1, :] = jnp.maximum(peak_ref[h : h + 1, :], best)
            mixed.append(dot_plain(probs.astype(LOW), values[:, cols]))
        mixed = jnp.concatenate(mixed, axis=1).astype(LOW)
        mixed_rows[rows, :] = mixed
        return dot_plain(mixed, output_w_ref[...])

    def normed_copy(j, owner):
        rows = normed_two.at[image_rows(2 * j + owner)]
        return remote(rows, rows, ns.at[j], nr.at[j], (dp, mate))

    def keep(i):
        return pltpu.make_async_copy(held[i], outs[i], hs.at[i])

    def finish(j):
        rows = image_rows(2 * j + half)
        residual = tokens[rows, :].astype(FULL) + total.result(j)
        residual_rows[j] = residual
        unit, _ = normalized(residual)
        normed_two[rows, :] = (unit * gains_ref[1:2, :]).astype(LOW)
        normed_copy(j, half).start()

    def peer(k):
        return (partner(dp, k, n), t)

    def half_rows():
        return pl.ds(pl.multiple_of(half * hp, hp), hp)

    def side_columns():
        return pl.ds(pl.multiple_of(side * width, width), width)

    def own_copy():
        return pltpu.make_async_copy(near_out.at[0], spread_hbm.at[0, half_rows()], own)

    def near_copy(k):
        return remote(near_out.at[k], spread_hbm.at[k, half_rows()], zs.at[k], zr.at[k], peer(k))

    def far_copy(k):
        return remote(
            far_out.at[k - near],
            spread_hbm.at[k, half_rows(), side_columns()],
            zs.at[k],
            zr.at[k],
            peer(k),
        )

    def side_copy(k, owner):
        columns = pl.ds(pl.multiple_of(owner * width, width), width)
        part = spread_hbm.at[k, half_rows(), columns]
        return remote(part, part, xs.at[k], xr.at[k], (dp, far))

    def forward(k, carry):
        far_copy(k).wait_recv()
        side_copy(k, side).start()
        return carry

    def dispatch(k):
        slots = lax.broadcasted_iota(jnp.int32, (hp, row_count), 0) + k * hp
        hot = (place_ref[0:1, :] == slots) | (place_ref[1:2, :] == slots)
        hot = jnp.where(hot, 1.0, 0.0).astype(LOW)

        @pl.when(k < near)
        def _():
            near_out[k] = dot_plain(hot, upstream[...]).astype(LOW)

            @pl.when(k == 0)
            def _():
                own_copy().start()

            @pl.when(k > 0)
            def _():
                near_copy(k).start()

        @pl.when(k >= near)
        def _():
            far_out[k - near] = dot_plain(hot, upstream[:, side_columns()]).astype(LOW)
            far_copy(k).start()

    def places_of_pairs():
        routes, slot_ids = routes_ref[...], slot_ids_ref[...]
        limits = jnp.zeros_like(routes)
        for e in range(n):
            limits = jnp.where(routes == e, capacity_ref[e], limits)
        kept = slot_ids < limits
        step = jnp.zeros_like(routes)
        weight = 1
        while weight < n:
            step = step + (routes // weight + dp // weight) % 2 * weight
            weight *= 2
        upper = slot_ids >= per_half
        in_half = slot_ids - jnp.where(upper, per_half, 0)
        in_block = in_half + jnp.where(upper, hp, 0)
        mine = kept & (upper == (half == 1))
        place = jnp.where(mine, step * hp + in_half, -1)
        position = jnp.where(kept, step * (2 * hp) + in_block, -1)
        both = jnp.concatenate([place, position, routes, jnp.full_like(routes, -1)], axis=0)
        fill = jnp.full((8, PIECE - SEQ), -1, jnp.int32)
        spaced = []
        for image in range(row_count // PIECE):
            spaced += [both[:, image * SEQ : (image + 1) * SEQ], fill]
        return jnp.concatenate(spaced, axis=1)

    pairs = places_of_pairs()
    place_ref[...] = pairs
    index_ref[...] = pairs.T
    def step(j, carry):
        given = image_forward(2 * j + 1 - half)

        @pl.when(j == 0)
        def _():
            await_greetings(n, (mate, far))

        total.give(j, given)
        total.take(j, image_forward(2 * j + half))

        @pl.when(j == 0)
        def _():
            for image in range(row_count // PIECE):
                upstream[image * PIECE : (image + 1) * PIECE, :] = padded_image(
                    upstream_ref, image
                ).astype(LOW)

        def turn(k, inner):
            dispatch(k)
            return inner

        @pl.when(j == 0)
        def _():
            lax.fori_loop(near, n, turn, 0)

        @pl.when(j == 1)
        def _():
            lax.fori_loop(0, near, turn, 0)

        @pl.when(j >= 1)
        def _():
            finish(j - 1)

        return carry

    lax.fori_loop(0, 3, step, 0)
    for i in range(7):
        keep(i).start()
    early = n - (n - near) // 4
    lax.fori_loop(near, early, forward, 0)
    finish(2)
    lax.fori_loop(early, n, forward, 0)
    keep(7).start()
    own_copy().wait()

    def arrive(k, carry):
        near_copy(k).wait()
        return carry

    def far_arrive(k, carry):
        far_copy(k).wait_send()
        side_copy(k, side).wait_send()
        side_copy(k, 1 - side).wait_recv()
        return carry

    for j in range(3):
        normed_copy(j, 1 - half).wait_recv()
    keep(8).start()
    lax.fori_loop(1, near, arrive, 0)
    lax.fori_loop(near, n, far_arrive, 0)
    for j in range(3):
        total.sent(j)
        normed_copy(j, half).wait_send()
    for i in range(9):
        keep(i).wait()


def run_front(n, hp, per_half, capacity, routes, slot_ids, tokens, upstream, gains, weights):
    model = tokens.shape[1]
    rows = tokens.shape[0] // SEQ * PIECE
    heads_width = weights[0].shape[0]
    near = near_count(n)
    width = model // 2
    vmem = pl.BlockSpec(memory_space=VMEM)
    hbm = pl.BlockSpec(memory_space=pl.ANY)
    shape = jax.ShapeDtypeStruct
    slim, wide = shape((rows, heads_width), LOW), shape((rows, model), LOW)
    held = (wide, wide, wide, slim, slim, slim, slim, shape((3, PIECE, model), FULL), wide)
    return pl.pallas_call(
        functools.partial(front_kernel, n, hp, per_half),
        out_shape=(
            shape((8, rows), jnp.int32),
            shape((rows, 8), jnp.int32),
            shape((8, 128), FULL),
            *held,
            shape((n, 2 * hp, model), LOW),
        ),
        in_specs=[pl.BlockSpec(memory_space=pltpu.SMEM)] + [vmem] * 9,
        out_specs=[vmem] * 3 + [hbm] * 10,
        scratch_shapes=[
            *[VMEM(a.shape, a.dtype) for a in held],
            VMEM((near, hp, model), LOW),
            VMEM((n - near, hp, width), LOW),
            dma(n),
            dma(n),
            pltpu.SemaphoreType.DMA,
            dma(3),
            dma(3),
            dma(9),
            dma(n),
            dma(n),
            *Total.scratch(model),
        ],
        compiler_params=pltpu.CompilerParams(
            collective_id=0, has_side_effects=True, vmem_limit_bytes=VMEM_LIMIT
        ),
        name="front",
    )(capacity, routes, slot_ids, tokens, upstream, gains, *weights)


def in_turn(i, near):
    return jnp.where(i < 2 * near, i // 2 + (i % 2) * near, i)


def expert_kernel(
    n,
    hp,
    place_ref,
    router_ref,
    peak_ref,
    normed_hbm,
    first_hbm,
    second_hbm,
    upstream_hbm,
    back_ref,
    gate_sum_ref,
    top_ref,
    answer_out_hbm,
    answer_kept_hbm,
    answer_ready_hbm,
    grad_first_hbm,
    grad_second_hbm,
    *scratch,
):
    dp, t, half, side, mate, far = places()
    arrived = scratch[2]
    spread = Spread(n, hp, place_ref, *scratch[:10])
    (
        normed_ref,
        first_ref,
        second_ref,
        answer_out,
        answer_kept,
        grad_first_ref,
        grad_second_ref,
        os_,
        ws,
        cs,
        cr,
        answer_far,
        answer_ready,
        xs,
        xr,
    ) = scratch[44:]
    (
        upstream,
        hidden_all,
        pre_grad_all,
        parts,
        pair_in,
        kept,
        far_out,
        far_in,
        final,
        gate_out,
        gate_in,
        sum_out,
        sum_in,
        sums,
        peaks,
        us,
        ps,
        pr,
        fs,
        fr,
        rs,
        rr,
        ms,
        mr,
        gs,
        gr,
        hs,
        hr,
        ks,
        kr,
        qs,
        qr,
        ss,
        sr,
    ) = scratch[10:44]
    model = normed_ref.shape[1]
    width = model // 2
    near = spread.near
    greet(n, dp, t, [(t + d) % 4 for d in (1, 2, 3)])
    fetches = [
        pltpu.make_async_copy(a, b, ws.at[i])
        for i, (a, b) in enumerate(
            ((normed_hbm, normed_ref), (first_hbm, first_ref), (second_hbm, second_ref))
        )
    ]
    mine = (slice(0, n), spread.rows(half))
    fetches.append(pltpu.make_async_copy(upstream_hbm.at[mine], upstream.at[mine], us.at[0]))
    for fetch in fetches:
        fetch.start()

    def upstream_pair_copy(k, owner):
        part = upstream.at[k, spread.rows(owner)]
        return remote(part, part, cs.at[k], cr.at[k], (dp, mate))

    def answer_side_copy(k):
        return remote(
            answer_out.at[k], answer_far.at[k - near], xs.at[k], xr.at[k], (dp, far)
        )

    def keep(i):
        pairs = (
            (answer_out.at[slice(0, near)], answer_out_hbm),
            (answer_kept.at[slice(0, near)], answer_kept_hbm),
            (answer_ready, answer_ready_hbm),
        )
        return pltpu.make_async_copy(*pairs[i], os_.at[i])

    def gate_copy(k):
        return remote(gate_out.at[k], gate_in.at[k, half], gs.at[k], gr.at[k], spread.peer(k))

    def gate_pair_copy(k, owner):
        tile = gate_in.at[k, owner]
        return remote(tile, tile, hs.at[k], hr.at[k], (dp, mate))

    def part_copy(i, k):
        return remote(
            parts.at[i % 3, :, spread.rows(1 - half)],
            pair_in.at[k],
            ps.at[i % 3],
            pr.at[k],
            (dp, mate),
        )

    def far_copy(i, k):
        return remote(far_out.at[i % SLOTS], far_in.at[k], fs.at[i % SLOTS], fr.at[k], (dp, far))

    def return_copy(k):
        return remote(
            final.at[k], back_ref.at[k, spread.rows(half)], rs.at[k], rr.at[k], spread.peer(k)
        )

    def mate_copy(k, owner):
        rows = back_ref.at[k, spread.rows(owner)]
        return remote(rows, rows, ms.at[k], mr.at[k], (dp, mate))

    def sum_copy(k):
        return remote(sum_out.at[k], sum_in.at[k], ks.at[k], kr.at[k], spread.peer(k))

    def peak_copy(k):
        return remote(peak_ref, peaks.at[k], qs.at[k], qr.at[k], spread.peer(k))

    def share_copy(d, owner):
        return remote(
            sums.at[owner], sums.at[owner], ss.at[d - 1], sr.at[d - 1], (dp, (t + d) % 4)
        )

    def loop(body, first=0, last=n):
        def one(k, carry):
            body(k)
            return carry

        lax.fori_loop(first, last, one, 0)

    fetches[0].wait()
    logits = dot_last(router_ref[...], normed_ref[...])
    rows_of = lax.broadcasted_iota(jnp.int32, logits.shape, 0)
    one, two = (
        jnp.sum(jnp.where(rows_of == place_ref[r : r + 1, :], logits, 0.0), axis=0, keepdims=True)
        for r in (4, 5)
    )
    best = jnp.maximum(one, two)
    one, two = jnp.exp(one - best), jnp.exp(two - best)
    gate_one, gate_two = one / (one + two), two / (one + two)
    await_greetings(n, (1, 2, 3))

    def dispatch(i):
        k = in_turn((i + 1) % n, near)
        is_first, is_second = spread.send(k, normed_ref)
        gate = jnp.sum(
            jnp.where(is_first, gate_one, 0.0) + jnp.where(is_second, gate_two, 0.0),
            axis=1,
            keepdims=True,
        )
        tile = jnp.broadcast_to(column_to_row(gate), (8, hp))

        @pl.when(k == 0)
        def _():
            gate_in[0, half] = tile

        @pl.when(k > 0)
        def _():
            gate_out[k] = tile
            gate_copy(k).start()

    loop(dispatch)
    for fetch in fetches[1:]:
        fetch.wait()
    loop(lambda i: upstream_pair_copy(in_turn(i, near), half).start())

    def chunk(i, k):
        gate = jnp.concatenate(
            [row_to_column(gate_in[k, 0, 0:1, :]), row_to_column(gate_in[k, 1, 0:1, :])], axis=0
        )
        gradient = upstream[k].astype(FULL)
        answer_grad = (gradient * gate).astype(LOW)
        pre = dot_plain(arrived[k], first_ref[...])
        share = 0.5 * (1.0 + lax.erf(pre * math.sqrt(0.5)))
        slope = share + pre * (jnp.exp(-0.5 * pre * pre) * (1.0 / math.sqrt(2.0 * math.pi)))
        hidden = (pre * share).astype(LOW)
        hidden_all[k] = hidden
        answer = dot_plain(hidden, second_ref[...])
        parts[i % 3, 0] = answer.astype(LOW)
        gate_sum = jnp.sum(answer * gradient, axis=1, keepdims=True)
        upstream[k] = answer_grad
        pre_grad = (dot_last(answer_grad, second_ref[...]) * slope).astype(LOW)
        pre_grad_all[k] = pre_grad
        parts[i % 3, 1] = dot_last(pre_grad, first_ref[...]).astype(LOW)
        tile = jnp.broadcast_to(column_to_row(gate_sum), (8, 2 * hp))

        @pl.when(k == 0)
        def _():
            sum_in[0] = tile

        @pl.when(k > 0)
        def _():
            sum_out[k] = tile
            sum_copy(k).start()
            peak_copy(k).start()

    tile = 256
    tiles = model // tile

    def grad_copy(m, j):
        cols = pl.ds(pl.multiple_of(m * tile, tile), tile)
        ref, hbm = ((grad_first_ref, grad_first_hbm), (grad_second_ref, grad_second_hbm))[j]
        return pltpu.make_async_copy(ref.at[cols], hbm.at[cols], os_.at[3 + 2 * m + j])

    def grads(m):
        cols = pl.ds(pl.multiple_of(m * tile, tile), tile)
        rows_in = arrived[:, :, cols].reshape(n * 2 * hp, tile)
        grad_first_ref[cols, :] = dot_first(rows_in, pre_grad_all[...].reshape(n * 2 * hp, -1))
        grad_copy(m, 0).start()
        hidden = hidden_all[:, :, cols].reshape(n * 2 * hp, tile)
        grad_second_ref[cols, :] = dot_first(hidden, upstream[...].reshape(n * 2 * hp, model))
        grad_copy(m, 1).start()

    def step(i):
        @pl.when(i < n)
        def _():
            spread.first_hop(in_turn(i, near))

        @pl.when((i >= 1) & (i < n + 1))
        def _():
            k = in_turn(i - 1, near)
            spread.second_hop(k)

            @pl.when(k > 0)
            def _():
                gate_copy(k).wait_recv()

            gate_pair_copy(k, half).start()

        @pl.when((i >= 2) & (i < n + 2))
        def _():
            k = in_turn(i - 2, near)
            spread.last_hop(k)
            gate_pair_copy(k, 1 - half).wait_recv()
            upstream_pair_copy(k, 1 - half).wait_recv()
            upstream_pair_copy(k, half).wait_send()

            @pl.when(i >= 5)
            def _():
                part_copy(i - 5, in_turn(i - 5, near)).wait_send()

            chunk(i - 2, k)
            part_copy(i - 2, k).start()

        @pl.when((i >= 3) & (i < n + 3))
        def _():
            k = in_turn(i - 3, near)
            part_copy(i - 3, k).wait_recv()

            @pl.when(i >= 3 + SLOTS)
            def _():
                far_copy(i - 3 - SLOTS, in_turn(i - 3 - SLOTS, near)).wait_send()

            for j in (1, 0):
                whole = parts[(i - 3) % 3, j, spread.rows(half), :].astype(FULL) + pair_in[k, j].astype(FULL)
                low, high = whole[:, :width], whole[:, width:]
                stays = jnp.where(side == 0, low, high)
                goes = jnp.where(side == 0, high, low).astype(LOW)
                if j:
                    kept[(i - 3) % SLOTS] = stays
                    far_out[(i - 3) % SLOTS] = goes
                    far_copy(i - 3, k).start()
                else:
                    answer_kept[k] = stays
                    answer_out[k] = goes

        @pl.when((i >= LAG) & (i < n + LAG))
        def _():
            k = in_turn(i - LAG, near)
            far_copy(i - LAG, k).wait_recv()
            rows = (kept[(i - LAG) % SLOTS] + far_in[k].astype(FULL)).astype(LOW)

            @pl.when(k == 0)
            def _():
                back_ref[0, spread.rows(half), :] = rows

            @pl.when(k > 0)
            def _():
                final[k] = rows
                return_copy(k).start()

        @pl.when(i == n + 2)
        def _():
            loop(lambda k: answer_side_copy(k).start(), near)

        @pl.when((i >= n + 2) & (i < n + 2 + tiles))
        def _():
            grads(i - (n + 2))

    loop(step, 0, n + max(LAG, 2 + tiles))
    keep(0).start()
    keep(1).start()
    peaks[0] = peak_ref[...]

    def collect_sums(k):
        @pl.when(k > 0)
        def _():
            peak_copy(k).wait_recv()
            sum_copy(k).wait_recv()

        sums[t, pl.ds(k, 1), :] = sum_in[k, 0:1, :]

    loop(collect_sums)
    for d in (1, 2, 3):
        share_copy(d, t).start()
    top_ref[...] = jnp.max(peaks[...], axis=0)

    def collect(i):
        k = in_turn(i, near)

        @pl.when(k > 0)
        def _():
            return_copy(k).wait_recv()

        mate_copy(k, half).start()

    loop(collect)

    def answers_whole(k):
        answer_side_copy(k).wait_recv()
        answer_ready[k - near] = (answer_kept[k] + answer_far[k - near].astype(FULL)).astype(LOW)

    loop(answers_whole, near)
    keep(2).start()
    for d in (1, 2, 3):
        share_copy(d, (t + 4 - d) % 4).wait_recv()
    whole = (sums[0] + sums[1]) + (sums[2] + sums[3])
    whole = jnp.concatenate([whole[k : k + 1] for k in range(n)], axis=1)
    gate_sum_ref[...] = jnp.broadcast_to(whole, gate_sum_ref.shape)

    def finish(i):
        k = in_turn(i, near)
        mate_copy(k, 1 - half).wait_recv()
        mate_copy(k, half).wait_send()
        spread.sent(k)
        gate_pair_copy(k, half).wait_send()

        @pl.when(k > 0)
        def _():
            return_copy(k).wait_send()
            gate_copy(k).wait_send()
            sum_copy(k).wait_send()
            peak_copy(k).wait_send()

        @pl.when(i >= n - 3)
        def _():
            part_copy(i, k).wait_send()

        @pl.when(i >= n - SLOTS)
        def _():
            far_copy(i, k).wait_send()

    loop(finish)
    for d in (1, 2, 3):
        share_copy(d, t).wait_send()
    loop(lambda k: answer_side_copy(k).wait_send(), near)
    for i in range(3):
        keep(i).wait()
    for m in range(tiles):
        grad_copy(m, 0).wait()
        grad_copy(m, 1).wait()


def run_experts(n, hp, place, router, peak, normed, first, second, upstream):
    model = normed.shape[1]
    width = model // 2
    hidden = first.shape[1]
    near = near_count(n)
    vmem = pl.BlockSpec(memory_space=VMEM)
    hbm = pl.BlockSpec(memory_space=pl.ANY)
    shape = jax.ShapeDtypeStruct
    return pl.pallas_call(
        functools.partial(expert_kernel, n, hp),
        out_shape=(
            shape((n, 2 * hp, width), LOW),
            shape((8, n * 2 * hp), FULL),
            shape(peak.shape, FULL),
            shape((near, hp, width), LOW),
            shape((near, hp, width), FULL),
            shape((n - near, hp, width), LOW),
            shape((model, hidden), FULL),
            shape((hidden, model), FULL),
        ),
        in_specs=[vmem] * 3 + [hbm] * 4,
        out_specs=[vmem] * 3 + [hbm] * 5,
        scratch_shapes=[
            *Spread.scratch(n, hp, width),
            VMEM((n, 2 * hp, model), LOW),
            *Spread.semaphores(n),
            VMEM((n, 2 * hp, model), LOW),
            VMEM((n, 2 * hp, hidden), LOW),
            VMEM((n, 2 * hp, hidden), LOW),
            VMEM((3, 2, 2 * hp, model), LOW),
            VMEM((n, 2, hp, model), LOW),
            VMEM((SLOTS, hp, width), FULL),
            VMEM((SLOTS, hp, width), LOW),
            VMEM((n, hp, width), LOW),
            VMEM((n, hp, width), LOW),
            VMEM((n, 8, hp), FULL),
            VMEM((n, 2, 8, hp), FULL),
            VMEM((n, 8, 2 * hp), FULL),
            VMEM((n, 8, 2 * hp), FULL),
            VMEM((4, n, 2 * hp), FULL),
            VMEM((n, *peak.shape), FULL),
            dma(1),
            dma(3), dma(n), dma(SLOTS), dma(n), dma(n), dma(n), dma(n), dma(n),
            dma(n), dma(n), dma(n), dma(n), dma(n), dma(n), dma(n), dma(n), dma(3), dma(3),
            VMEM(normed.shape, LOW),
            VMEM(first.shape, LOW),
            VMEM(second.shape, LOW),
            VMEM((n, hp, width), LOW),
            VMEM((n, hp, width), FULL),
            VMEM((model, hidden), FULL),
            VMEM((hidden, model), FULL),
            dma(3 + 2 * (model // 256)),
            dma(3), dma(n), dma(n),
            VMEM((n - near, hp, width), LOW),
            VMEM((n - near, hp, width), LOW),
            dma(n), dma(n),
        ],
        compiler_params=pltpu.CompilerParams(
            collective_id=1, has_side_effects=True, vmem_limit_bytes=VMEM_LIMIT
        ),
        name="experts",
    )(place, router, peak, normed, first, second, upstream)


def unpad(rows_ref, out_ref):
    for image in range(rows_ref.shape[0] // PIECE):
        start = image * SEQ // 8 * 8
        length = min(PIECE, out_ref.shape[0] - start)
        shift = image * SEQ - start
        rows = lax.broadcasted_iota(jnp.int32, (length, PIECE), 0)
        columns = lax.broadcasted_iota(jnp.int32, (length, PIECE), 1)
        pick = (rows == columns + shift) & (columns < SEQ)
        image_part = rows_ref[image * PIECE : (image + 1) * PIECE, :]
        moved = dot_plain(jnp.where(pick, 1.0, 0.0).astype(LOW), image_part).astype(LOW)
        if shift:
            before = lax.broadcasted_iota(jnp.int32, (8, moved.shape[1]), 0) < shift
            first = jnp.where(before, out_ref[start : start + 8, :].astype(FULL), moved[:8].astype(FULL))
            out_ref[start : start + 8, :] = first.astype(LOW)
            out_ref[start + 8 : start + length, :] = moved[8:]
        else:
            out_ref[start : start + length, :] = moved


def back_kernel(
    n,
    hp,
    back_ref,
    gate_sum_ref,
    index_ref,
    gains_ref,
    output_w_ref,
    router_ref,
    answer_ready,
    *refs,
):
    later, outs, scratch = refs[:13], refs[13:18], refs[18:]
    block_out_ref, tokens_out_ref, weights_ref, small_ref, gain_ref = outs
    held, scratch = scratch[:13], scratch[13:]
    (
        residual_ref,
        upstream_ref,
        answer_out,
        answer_kept,
        normed_one_ref,
        query_ref,
        key_ref,
        value_ref,
        mixed_ref,
        tokens_ref,
        query_w_ref,
        key_w_ref,
        value_w_ref,
    ) = held
    dp, t, half, side, mate, far = places()
    (
        moe_mine,
        moe_other,
        block_mine,
        block_other,
        attention_grad,
        residual_grad,
        query_grad,
        key_grad,
        value_grad,
        gain_two_sum,
        gain_two_in,
        gain_one_sum,
        gain_one_all,
        gain_rows,
        router_sum,
        router_in,
        totals,
        totals_two,
        pieces,
        pieces_in,
        small_pieces,
        small_in,
        answer_far,
        answer_final,
        answers,
        block_ref,
        grad_tokens_ref,
        hs,
        as_,
        ar,
        bs,
        br,
        ts,
        tr,
        cs,
        cr,
        gs,
        gr,
        ws,
        wr,
        ls,
        lr,
        os_,
        or_,
        vs,
        vr,
        ds,
        dr,
        es,
        er,
        fs,
        fr,
        ks,
        kr,
    ) = scratch[:54]
    total = Total(*scratch[54:])
    heads = query_w_ref.shape[0] // HD
    model = upstream_ref.shape[1]
    width = model // 2
    slots = back_ref.shape[0]
    piece = pieces.shape[1]
    near = near_count(n)
    greet(n, dp, t, [(t + d) % 4 for d in (1, 2, 3)])
    fetches = [pltpu.make_async_copy(a, b, hs.at[i]) for i, (a, b) in enumerate(zip(later, held))]
    for fetch in fetches:
        fetch.start()

    def peer(k):
        return (partner(dp, k, n), t)

    def moe_copy(j):
        return remote(moe_mine.at[j, SENT], moe_other.at[j, SENT], as_.at[j], ar.at[j], (dp, far))

    def block_copy(j):
        return remote(block_mine.at[j, SENT], block_other.at[j, SENT], bs.at[j], br.at[j], (dp, far))

    def attention_copy(j, owner):
        rows = attention_grad.at[image_rows(2 * j + owner)]
        return remote(rows, rows, ts.at[j], tr.at[j], (dp, mate))

    def tokens_copy(j, owner):
        rows = grad_tokens_ref.at[image_rows(2 * j + owner)]
        return remote(rows, rows, cs.at[j], cr.at[j], (dp, mate))

    def block_pair_copy(j, owner):
        rows = block_ref.at[image_rows(2 * j + owner)]
        return remote(rows, rows, ls.at[j], lr.at[j], (dp, mate))

    def gain_copy(d, owner):
        return remote(
            gain_one_all.at[owner], gain_one_all.at[owner], gs.at[d - 1], gr.at[d - 1], (dp, (t + d) % 4)
        )

    def gain_row_copy(k):
        return remote(gain_rows.at[0], gain_rows.at[k], ks.at[k], kr.at[k], peer(k))

    def router_copy():
        return remote(router_sum, router_in, os_.at[0], or_.at[0], (dp, mate))

    def gain_two_copy():
        return remote(gain_two_sum, gain_two_in, os_.at[1], or_.at[1], (dp, mate))

    def piece_copy(k):
        return remote(pieces.at[k], pieces_in.at[k], ws.at[k], wr.at[k], peer(k))

    def small_copy(k):
        return remote(small_pieces.at[k], small_in.at[k], vs.at[k], vr.at[k], peer(k))

    def answer_rows(k, owner):
        return answers.at[pl.ds(pl.multiple_of((2 * k + owner) * hp, hp), hp)]

    def answer_side_copy(k):
        return remote(answer_out.at[k], answer_far.at[k], ds.at[k], dr.at[k], (dp, far))

    def answer_copy(k):
        return remote(answer_final.at[k], answer_rows(k, half), es.at[k], er.at[k], peer(k))

    def far_answer_copy(k):
        return remote(answer_ready.at[k - near], answer_rows(k, half), es.at[k], er.at[k], peer(k))

    def answer_pair_copy(k, owner):
        return remote(answer_rows(k, owner), answer_rows(k, owner), fs.at[k], fr.at[k], (dp, mate))

    def loop(body, first=0, last=n):
        def one(k, carry):
            body(k)
            return carry

        lax.fori_loop(first, last, one, 0)

    def both_sides(mine, other):
        low = jnp.where(side == 0, mine, other)
        high = jnp.where(side == 0, other, mine)
        return jnp.concatenate([low, high], axis=1)

    def hots(rows):
        columns = lax.broadcasted_iota(jnp.int32, (PIECE, slots), 1)
        return index_ref[rows, 2:3] == columns, index_ref[rows, 3:4] == columns

    def as_low(mask):
        return jnp.where(mask, 1.0, 0.0).astype(LOW)

    clear_unsent(moe_other)
    clear_unsent(block_other)
    gain_two_sum[...] = jnp.zeros_like(gain_two_sum)
    gain_one_sum[...] = jnp.zeros_like(gain_one_sum)
    router_sum[...] = jnp.zeros_like(router_sum)

    def combine(j):
        first, second = hots(image_rows(2 * j + half))
        moe_mine[j] = dot_plain(as_low(first | second), back_ref[...]).astype(LOW)

        @pl.when(j == 0)
        def _():
            await_greetings(n, (1, 2, 3))
            loop(lambda k: far_answer_copy(k).start(), near)

        moe_copy(j).start()

    loop(combine, 0, 3)
    for fetch in fetches[:3]:
        fetch.wait()
    loop(lambda k: answer_side_copy((k + 1) % near).start(), 0, near)

    def gates_of(rows, normed):
        logits = dot_last(normed, router_ref[...])
        lanes = lax.broadcasted_iota(jnp.int32, logits.shape, 1)
        hot_one = index_ref[rows, 4:5] == lanes
        hot_two = index_ref[rows, 5:6] == lanes
        one = jnp.sum(jnp.where(hot_one, logits, 0.0), axis=1, keepdims=True)
        two = jnp.sum(jnp.where(hot_two, logits, 0.0), axis=1, keepdims=True)
        top = jnp.maximum(one, two)
        one, two = jnp.exp(one - top), jnp.exp(two - top)
        return one / (one + two), two / (one + two), hot_one, hot_two

    def moe_back(j):
        rows = image_rows(2 * j + half)
        unit, factor = normalized(residual_ref[j])
        normed = (unit * gains_ref[1:2, :]).astype(LOW)
        gate_one, gate_two, hot_one, hot_two = gates_of(rows, normed)
        first, second = hots(rows)
        slot_sums = gate_sum_ref[0:1, :]
        grad_one = jnp.sum(jnp.where(first, slot_sums, 0.0), axis=1, keepdims=True)
        grad_two = jnp.sum(jnp.where(second, slot_sums, 0.0), axis=1, keepdims=True)
        mean = gate_one * grad_one + gate_two * grad_two
        logit_grad = jnp.where(hot_one, gate_one * (grad_one - mean), 0.0)
        logit_grad = logit_grad + jnp.where(hot_two, gate_two * (grad_two - mean), 0.0)
        logit_grad = logit_grad.astype(LOW)
        router_sum[...] += dot_first(normed, logit_grad)
        normed_grad = dot_plain(logit_grad, router_ref[...])
        moe_copy(j).wait_recv()
        normed_grad = normed_grad + both_sides(moe_mine[j].astype(FULL), moe_other[j].astype(FULL))
        gain_two_sum[...] += jnp.sum((normed_grad * unit).reshape(PIECE // 8, 8, model), axis=0)
        grad = normalized_back(normed_grad * gains_ref[1:2, :], unit, factor)
        grad = grad + upstream_ref[rows, :].astype(FULL)
        residual_grad[j] = grad
        attention_grad[rows, :] = grad.astype(LOW)
        attention_copy(j, half).start()

    loop(moe_back, 0, 3)
    router_copy().start()
    gain_two_copy().start()
    for fetch in fetches[3:]:
        fetch.wait()

    def image_back(image):
        rows = image_rows(image)
        mixed_grad = dot_last(attention_grad[rows, :], output_w_ref[...]).astype(LOW)
        queries, keys, values = query_ref[rows, :], key_ref[rows, :], value_ref[rows, :]
        query_parts, key_parts, value_parts = [], [], []
        for h in range(heads):
            cols = slice(h * HD, (h + 1) * HD)
            probs, _ = attention_probs(queries[:, cols], keys[:, cols])
            value_parts.append(dot_first(probs.astype(LOW), mixed_grad[:, cols]))
            probs_grad = dot_last(mixed_grad[:, cols], values[:, cols])
            level = jnp.sum(probs * probs_grad, axis=1, keepdims=True)
            score_grad = (probs * (probs_grad - level)).astype(LOW)
            query_parts.append(dot_plain(score_grad, keys[:, cols]) * HD**-0.5)
            key_parts.append(dot_first(score_grad, queries[:, cols]) * HD**-0.5)
        grads = [jnp.concatenate(p, axis=1).astype(LOW) for p in (query_parts, key_parts, value_parts)]
        query_grad[rows, :], key_grad[rows, :], value_grad[rows, :] = grads

    def answer_turn(k):
        answer_side_copy(k).wait_recv()
        rows = (answer_kept[k] + answer_far[k].astype(FULL)).astype(LOW)

        @pl.when(k == 0)
        def _():
            answer_rows(0, half)[...] = rows

        @pl.when(k > 0)
        def _():
            answer_final[k] = rows
            answer_copy(k).start()

    def grad_part(image):
        rows = image_rows(image)
        part = dot_plain(query_grad[rows, :], query_w_ref[...])
        part = part + dot_plain(key_grad[rows, :], key_w_ref[...])
        part = part + dot_plain(value_grad[rows, :], value_w_ref[...])
        unit, _ = normalized(tokens_ref[rows, :].astype(FULL))
        gain_one_sum[...] += jnp.sum((part * unit).reshape(PIECE // 8, 8, model), axis=0)
        return part

    def my_piece(source, k):
        at = partner(dp, k, n) * piece
        grain = math.gcd(piece, 8)
        span = -(-(piece + 8 - grain) // 8) * 8
        taken = source[pl.ds(pl.multiple_of(at // 8 * 8, 8), span), :]
        rows = taken[:piece]
        for shift in range(grain, 8, grain):
            rows = jnp.where(at % 8 == shift, taken[shift : shift + piece], rows)
        return rows.astype(LOW)

    def small_grads():
        router_copy().wait_recv()
        gain_two_copy().wait_recv()
        row = jnp.sum(gain_two_sum[...] + gain_two_in[...], axis=0, keepdims=True)
        column = jnp.concatenate(
            [row_to_column(row[:, i : i + 256]) for i in range(0, model, 256)], axis=0
        )
        totals_two[...] = jnp.concatenate(
            [
                dot_first(attention_grad[...], mixed_ref[...]),
                router_sum[...] + router_in[...],
                column,
            ],
            axis=1,
        )

        def send_small(i):
            k = in_turn((i + 1) % n, near)
            small_pieces[k] = my_piece(totals_two, k)

            @pl.when(k > 0)
            def _():
                small_copy(k).start()

        loop(send_small)

    for j in range(3):
        attention_copy(j, 1 - half).wait_recv()

    def attention_back(j):
        for owner in (1 - half, half):
            image_back(2 * j + owner)
        total.give(j, grad_part(2 * j + 1 - half))
        total.take(j, grad_part(2 * j + half))
        answer_turn((j + 1) % near)

        @pl.when(j == 1)
        def _():
            small_grads()

        @pl.when(j == 2)
        def _():
            answer_turn(0)

    loop(attention_back, 0, 3)

    gain_one_all[t] = jnp.sum(gain_one_sum[...], axis=0, keepdims=True)
    for d in (1, 2, 3):
        gain_copy(d, t).start()
    normed_one = normed_one_ref[...]
    totals[:, : 3 * query_grad.shape[1]] = jnp.concatenate(
        [
            dot_first(normed_one, query_grad[...]),
            dot_first(normed_one, key_grad[...]),
            dot_first(normed_one, value_grad[...]),
        ],
        axis=1,
    )

    def send_piece(i):
        k = in_turn((i + 1) % n, near)
        pieces[k] = my_piece(totals, k)

        @pl.when(k > 0)
        def _():
            piece_copy(k).start()

    loop(send_piece)


    def answers_here(i):
        k = in_turn(i, near)

        @pl.when((k > 0) & (k < near))
        def _():
            answer_copy(k).wait_recv()

        @pl.when(k >= near)
        def _():
            far_answer_copy(k).wait_recv()

        answer_pair_copy(k, half).start()

    loop(answers_here)
    loop(lambda k: answer_pair_copy(k, 1 - half).wait_recv())

    def block_rows(j):
        rows = image_rows(2 * j + half)
        residual = residual_ref[j]
        unit, _ = normalized(residual)
        gate_one, gate_two, _, _ = gates_of(rows, (unit * gains_ref[1:2, :]).astype(LOW))
        first, second = hots(rows)
        from_first = dot_plain(as_low(first), answers[...])
        from_second = dot_plain(as_low(second), answers[...])
        mine = jnp.where(side == 0, residual[:, :width], residual[:, width:])
        block_mine[j] = (mine + (gate_one * from_first + gate_two * from_second)).astype(LOW)
        block_copy(j).start()

    loop(block_rows, 0, 3)

    def tokens_back(j):
        rows = image_rows(2 * j + half)
        normed_grad = total.result(j)
        unit, factor = normalized(tokens_ref[rows, :].astype(FULL))
        grad = normalized_back(normed_grad * gains_ref[0:1, :], unit, factor)
        grad_tokens_ref[rows, :] = (residual_grad[j] + grad).astype(LOW)
        tokens_copy(j, half).start()

    loop(tokens_back, 0, 3)
    for d in (1, 2, 3):
        gain_copy(d, (t + 4 - d) % 4).wait_recv()
    gain_rows[0] = (gain_one_all[0] + gain_one_all[1]) + (gain_one_all[2] + gain_one_all[3])

    def send_gain(k):
        gain_row_copy(k).start()

    loop(send_gain, 1)

    def block_back(j):
        block_copy(j).wait_recv()
        block_ref[image_rows(2 * j + half), :] = both_sides(block_mine[j], block_other[j])
        block_pair_copy(j, half).start()

    for j in range(3):
        tokens_copy(j, 1 - half).wait_recv()
    unpad(grad_tokens_ref, tokens_out_ref)
    loop(block_back, 0, 3)
    for j in range(3):
        block_pair_copy(j, 1 - half).wait_recv()
    unpad(block_ref, block_out_ref)
    pieces_in[0] = pieces[0]
    small_in[0] = small_pieces[0]

    def arrive(k):
        piece_copy(k).wait_recv()
        small_copy(k).wait_recv()
        gain_row_copy(k).wait_recv()

    loop(arrive, 1)
    weights_ref[...] = jnp.sum(pieces_in[...].astype(FULL), axis=0)
    small_ref[...] = jnp.sum(small_in[...].astype(FULL), axis=0)
    gain_ref[...] = jnp.sum(gain_rows[...], axis=0)

    for j in range(3):
        moe_copy(j).wait_send()
        block_copy(j).wait_send()
        attention_copy(j, half).wait_send()
        total.sent(j)
        tokens_copy(j, half).wait_send()
        block_pair_copy(j, half).wait_send()
        gain_copy(j + 1, t).wait_send()
    router_copy().wait_send()
    gain_two_copy().wait_send()

    def left(k):
        @pl.when(k < near)
        def _():
            answer_side_copy(k).wait_send()

        @pl.when((k > 0) & (k < near))
        def _():
            answer_copy(k).wait_send()

        @pl.when(k >= near)
        def _():
            far_answer_copy(k).wait_send()

        answer_pair_copy(k, half).wait_send()

        @pl.when(k > 0)
        def _():
            piece_copy(k).wait_send()
            small_copy(k).wait_send()
            gain_row_copy(k).wait_send()

    loop(left)


def run_back(n, hp, row_count, first, later):
    upstream = later[1]
    rows, model = upstream.shape
    heads_width = later[8].shape[1]
    width = model // 2
    piece = model // n
    vmem = pl.BlockSpec(memory_space=VMEM)
    shape = jax.ShapeDtypeStruct
    slim = VMEM((3, PIECE, width), LOW)
    heads = VMEM((rows, heads_width), LOW)
    eight = VMEM((8, model), FULL)
    wide, narrow = 3 * heads_width, heads_width + n + 1
    quarter = VMEM((near_count(n), hp, width), LOW)
    three, many = dma(3), dma(n)
    return pl.pallas_call(
        functools.partial(back_kernel, n, hp),
        out_shape=(
            shape((row_count, model), LOW),
            shape((row_count, model), LOW),
            shape((piece, wide), FULL),
            shape((piece, narrow), FULL),
            shape((1, model), FULL),
        ),
        in_specs=[vmem] * (len(first) - 1) + [pl.BlockSpec(memory_space=pl.ANY)] * (1 + len(later)),
        out_specs=[vmem] * 5,
        scratch_shapes=[
            *[VMEM(a.shape, a.dtype) for a in later],
            slim, slim, slim, slim,
            VMEM((rows, model), LOW),
            VMEM((3, PIECE, model), FULL),
            heads, heads, heads,
            eight, eight, eight,
            VMEM((4, 1, model), FULL),
            VMEM((n, 1, model), FULL),
            VMEM((model, n), FULL),
            VMEM((model, n), FULL),
            VMEM((model, wide), FULL),
            VMEM((model, narrow), FULL),
            VMEM((n, piece, wide), LOW),
            VMEM((n, piece, wide), LOW),
            VMEM((n, piece, narrow), LOW),
            VMEM((n, piece, narrow), LOW),
            quarter, quarter,
            VMEM((n * 2 * hp, width), LOW),
            VMEM((rows, model), LOW),
            VMEM((rows, model), LOW),
            dma(len(later)),
            three, three, three, three, three, three, three, three, three, three,
            many, many, three, three, dma(2), dma(2),
            many, many, many, many, many, many, many, many, many, many,
            *Total.scratch(model),
        ],
        compiler_params=pltpu.CompilerParams(
            collective_id=2, has_side_effects=True, vmem_limit_bytes=VMEM_LIMIT
        ),
        name="back",
    )(*first, *later)


def results_kernel(
    threshold_ref,
    *refs,
):
    small_in, moved_in, moved_out, refs = refs[:6], refs[6:10], refs[10:14], refs[14:]
    (
        gain_one_ref,
        gain_two_ref,
        query_ref,
        key_ref,
        value_ref,
        output_ref,
        router_ref,
        clipped_query_ref,
        clipped_key_ref,
        head_max_ref,
        *held,
        sems,
    ) = refs
    held, own = held[:4], held[4:]
    weights_ref, small_ref, gain_row_ref, top_ref, query_w_ref, key_w_ref = own
    fetches, copies = [], []
    for i, (source, target) in enumerate(zip(moved_in, moved_out)):
        rows = source.shape[0]
        cut = rows // 16 * 8
        for part, at in enumerate((slice(0, cut), slice(cut, rows))):
            sem = sems.at[2 * i + part]
            fetches.append(pltpu.make_async_copy(source.at[at], held[i].at[at], sem))
            sem = sems.at[8 + 2 * i + part]
            copies.append(pltpu.make_async_copy(held[i].at[at], target.at[at], sem))
    small_fetches = [
        pltpu.make_async_copy(a, b, sems.at[16 + i]) for i, (a, b) in enumerate(zip(small_in, own))
    ]
    for fetch in fetches + small_fetches:
        fetch.start()
    for fetch, copy in zip(fetches, copies):
        fetch.wait()
        copy.start()
    for fetch in small_fetches:
        fetch.wait()
    piece, wide = query_ref.shape
    heads = head_max_ref.shape[0]
    query_ref[...] = weights_ref[:, :wide]
    key_ref[...] = weights_ref[:, wide : 2 * wide]
    value_ref[...] = weights_ref[:, 2 * wide :]
    small = small_ref[...]
    output_ref[...] = small[:, :wide].T
    n = router_ref.shape[0]
    router_ref[...] = small[:, wide : wide + n].T
    gain_two_ref[...] = column_to_row(small[:, wide + n :])[0]
    model = gain_row_ref.shape[1]
    lanes = lax.broadcasted_iota(jnp.int32, (piece, model), 1)
    mine = lax.broadcasted_iota(jnp.int32, (piece, model), 0) + lax.axis_index("dp") * piece
    column = jnp.sum(jnp.where(lanes == mine, gain_row_ref[...], 0.0), axis=1, keepdims=True)
    gain_one_ref[...] = column_to_row(column)[0]
    head_max_ref[...] = column_to_row(top_ref[:, 0:1])[0, :heads]
    for h in range(heads):
        rows = slice(h * HD, (h + 1) * HD)
        factor = jnp.sqrt(jnp.minimum(1.0, threshold_ref[h] / top_ref[h : h + 1, 0:1]))
        clipped_query_ref[rows, :] = query_w_ref[rows, :].astype(FULL) * factor
        clipped_key_ref[rows, :] = key_w_ref[rows, :].astype(FULL) * factor
    for copy in copies:
        copy.wait()


def run_results(n, threshold, weights, small, gain_row, top, query_w, key_w, moved):
    wide, model = query_w.shape
    piece = weights.shape[0]
    shape = jax.ShapeDtypeStruct
    vmem = pl.BlockSpec(memory_space=VMEM)
    hbm = pl.BlockSpec(memory_space=pl.ANY)
    grad, clipped = shape((piece, wide), FULL), shape((wide, model), FULL)
    return pl.pallas_call(
        results_kernel,
        out_shape=(
            *[shape(a.shape, a.dtype) for a in moved],
            shape((piece,), FULL),
            shape((piece,), FULL),
            grad,
            grad,
            grad,
            shape((wide, piece), FULL),
            shape((n, piece), FULL),
            clipped,
            clipped,
            shape(threshold.shape, FULL),
        ),
        in_specs=[pl.BlockSpec(memory_space=pltpu.SMEM)] + [hbm] * 10,
        out_specs=[hbm] * 4 + [vmem] * 10,
        scratch_shapes=[
            *[
                VMEM(a.shape, a.dtype)
                for a in (*moved, weights, small, gain_row, top, query_w, key_w)
            ],
            dma(22),
        ],
        compiler_params=pltpu.CompilerParams(vmem_limit_bytes=VMEM_LIMIT),
        name="results",
    )(threshold, weights, small, gain_row, top, query_w, key_w, *moved)


def body(
    tokens,
    gain_attn,
    w_query,
    w_key,
    w_value,
    w_output,
    gain_moe,
    w_router,
    expert_in,
    expert_out,
    routes,
    slot_ids,
    capacity,
    threshold,
    cotangent,
):
    n = lax.axis_size("dp")
    row_count, model = tokens.shape
    slot_count = 23 * TOK_DEV // (10 * n) + 1
    per_half = -(-slot_count // 2)
    hp = -(-per_half // 16) * 16
    gains = jnp.stack([gain_attn, gain_moe]).astype(FULL)
    across = (w_query.T, w_key.T, w_value.T)
    (
        place,
        index,
        peak,
        tokens_in,
        upstream,
        normed_one,
        query,
        key,
        value,
        mixed,
        residual,
        normed_two,
        spread,
    ) = run_front(
        n,
        hp,
        per_half,
        capacity,
        routes.T,
        slot_ids.T,
        tokens,
        cotangent,
        gains,
        (*across, w_output),
    )
    router = w_router.T
    back, gate_sums, top, answer_out, answer_kept, answer_ready, grad_first, grad_second = run_experts(
        n, hp, place, router, peak, normed_two, expert_in[0], expert_out[0], spread
    )
    block_out, grad_tokens, weight_grads, small, gain_rows = run_back(
        n,
        hp,
        row_count,
        (back.reshape(n * 2 * hp, -1), gate_sums, index, gains, w_output, router, answer_ready),
        (
            residual,
            upstream,
            answer_out,
            answer_kept,
            normed_one,
            query,
            key,
            value,
            mixed,
            tokens_in,
            *across,
        ),
    )
    (
        block_out,
        grad_tokens,
        grad_first,
        grad_second,
        gain_one,
        gain_two,
        grad_query,
        grad_key,
        grad_value,
        grad_output,
        grad_router,
        clipped_query,
        clipped_key,
        head_max,
    ) = run_results(
        n,
        threshold,
        weight_grads,
        small,
        gain_rows,
        top,
        *across[:2],
        (block_out, grad_tokens, grad_first, grad_second),
    )
    return (
        block_out,
        grad_tokens,
        gain_one,
        gain_two,
        grad_query,
        grad_key,
        grad_value,
        grad_output,
        grad_router.T,
        grad_first[None],
        grad_second[None],
        clipped_query.T,
        clipped_key.T,
        head_max,
    )


def solution(mesh):
    in_specs = (
        P("dp", None),
        P(),
        P(None, "tensor"),
        P(None, "tensor"),
        P(None, "tensor"),
        P("tensor", None),
        P(),
        P(),
        P("dp", None, "tensor"),
        P("dp", "tensor", None),
        P("dp", None),
        P("dp", None),
        P(),
        P("tensor"),
        P("dp", None),
    )
    out_specs = (
        P("dp", None),
        P("dp", None),
        P("dp"),
        P("dp"),
        P("dp", "tensor"),
        P("dp", "tensor"),
        P("dp", "tensor"),
        P("tensor", "dp"),
        P("dp", None),
        P("dp", None, "tensor"),
        P("dp", "tensor", None),
        P(None, "tensor"),
        P(None, "tensor"),
        P("tensor"),
    )
    return jax.shard_map(body, mesh=mesh, in_specs=in_specs, out_specs=out_specs, check_vma=False)
```

```python
import functools
import math

import jax
import jax.numpy as jnp
from jax import lax
from jax.experimental import pallas as pl
from jax.experimental.pallas import tpu as pltpu
from jax.sharding import PartitionSpec as P

HD = 64
SEQ = 197
PIECE = 208
SENT = slice(0, 200)
TOK_DEV = 1182
EPSILON = 1e-06
MESH = pl.DeviceIdType.MESH
VMEM_LIMIT = 60 * 2**20
SLOTS = 3
LAG = 4
VMEM = pltpu.VMEM
LOW, FULL = jnp.bfloat16, jnp.float32


def dot_plain(a, b):
    return jnp.dot(a, b, preferred_element_type=FULL)


def dot_last(a, b):
    return lax.dot_general(a, b, (((1,), (1,)), ((), ())), preferred_element_type=FULL)


def dot_first(a, b):
    return lax.dot_general(a, b, (((0,), (0,)), ((), ())), preferred_element_type=FULL)


def normalized(rows):
    centered = rows - jnp.mean(rows, axis=-1, keepdims=True)
    factor = lax.rsqrt(jnp.mean(centered * centered, axis=-1, keepdims=True) + EPSILON)
    return centered * factor, factor


def normalized_back(u, unit, factor):
    first = jnp.mean(u, axis=-1, keepdims=True)
    second = jnp.mean(u * unit, axis=-1, keepdims=True)
    return factor * (u - first - unit * second)


def same_index(size):
    rows = lax.broadcasted_iota(jnp.int32, (size, size), 0)
    return rows == lax.broadcasted_iota(jnp.int32, (size, size), 1)


def row_to_column(row):
    return jnp.sum(jnp.where(same_index(row.shape[1]), row, 0.0), axis=1, keepdims=True)


def column_to_row(column):
    return jnp.sum(jnp.where(same_index(column.shape[0]), column, 0.0), axis=0, keepdims=True)


def attention_probs(queries, keys):
    scores = dot_last(queries, keys) * HD**-0.5
    real = lax.broadcasted_iota(jnp.int32, scores.shape, 1) < SEQ
    scores = jnp.where(real, scores, -1e30)
    top = jnp.max(scores, axis=1, keepdims=True)
    powers = jnp.exp(scores - top)
    return powers * (1.0 / jnp.sum(powers, axis=1, keepdims=True)), top


def partner(dp, k, n):
    other, weight = 0, 1
    while weight < n:
        other = other + ((dp // weight + k // weight) % 2) * weight
        weight *= 2
    return other


def places():
    dp = lax.axis_index("dp")
    t = lax.axis_index("tensor")
    return dp, t, t % 2, t // 2, t + 1 - 2 * (t % 2), (t + 2) % 4


def remote(src, dst, sends, recvs, device):
    return pltpu.make_async_remote_copy(
        src_ref=src,
        dst_ref=dst,
        send_sem=sends,
        recv_sem=recvs,
        device_id=device,
        device_id_type=MESH,
    )


def signal(sem, device):
    pl.semaphore_signal(sem, inc=1, device_id=device, device_id_type=MESH)


def greet(n, dp, t, others):
    barrier = pltpu.get_barrier_semaphore()

    def one(k, carry):
        signal(barrier, (partner(dp, k, n), t))
        return carry

    lax.fori_loop(1, n, one, 0)
    for other in others:
        signal(barrier, (dp, other))


def await_greetings(n, others):
    pl.semaphore_wait(pltpu.get_barrier_semaphore(), n - 1 + len(others))


def image_rows(image):
    return pl.ds(pl.multiple_of(image * PIECE, PIECE), PIECE)


def dma(*shape):
    return pltpu.SemaphoreType.DMA(shape)


def near_count(n):
    return min(4, n)


class Spread:
    def __init__(self, n, hp, place, near_out, far_out, arrived, zs, zr, xs, xr, cs, cr, own):
        self.n, self.hp, self.near = n, hp, near_count(n)
        self.place, self.near_out, self.far_out, self.arrived = place, near_out, far_out, arrived
        self.zs, self.zr, self.xs, self.xr, self.cs, self.cr, self.own = zs, zr, xs, xr, cs, cr, own
        self.dp, self.t, self.half, self.side, self.mate, self.far = places()
        self.width = far_out.shape[2]

    def rows(self, owner):
        return pl.ds(pl.multiple_of(owner * self.hp, self.hp), self.hp)

    def columns(self, owner):
        return pl.ds(pl.multiple_of(owner * self.width, self.width), self.width)

    def peer(self, k):
        return (partner(self.dp, k, self.n), self.t)

    def own_copy(self):
        return pltpu.make_async_copy(
            self.near_out.at[0], self.arrived.at[0, self.rows(self.half)], self.own
        )

    def near_copy(self, k):
        return remote(
            self.near_out.at[k],
            self.arrived.at[k, self.rows(self.half)],
            self.zs.at[k],
            self.zr.at[k],
            self.peer(k),
        )

    def far_copy(self, k):
        return remote(
            self.far_out.at[k - self.near],
            self.arrived.at[k, self.rows(self.half), self.columns(self.side)],
            self.zs.at[k],
            self.zr.at[k],
            self.peer(k),
        )

    def side_copy(self, k, side):
        part = self.arrived.at[k, self.rows(self.half), self.columns(side)]
        return remote(part, part, self.xs.at[k], self.xr.at[k], (self.dp, self.far))

    def pair_copy(self, k, half):
        part = self.arrived.at[k, self.rows(half)]
        return remote(part, part, self.cs.at[k], self.cr.at[k], (self.dp, self.mate))

    def hot(self, k, row_count):
        slots = lax.broadcasted_iota(jnp.int32, (self.hp, row_count), 0) + k * self.hp
        is_first = self.place[0:1, :] == slots
        is_second = self.place[1:2, :] == slots
        return is_first, is_second

    def send(self, k, rows_ref):
        is_first, is_second = self.hot(k, rows_ref.shape[0])
        hot = jnp.where(is_first | is_second, 1.0, 0.0).astype(LOW)

        @pl.when(k < self.near)
        def _():
            self.near_out[k] = dot_plain(hot, rows_ref[...]).astype(LOW)

            @pl.when(k == 0)
            def _():
                self.own_copy().start()

            @pl.when(k > 0)
            def _():
                self.near_copy(k).start()

        @pl.when(k >= self.near)
        def _():
            mine = rows_ref[:, self.columns(self.side)]
            self.far_out[k - self.near] = dot_plain(hot, mine).astype(LOW)
            self.far_copy(k).start()

        return is_first, is_second

    def first_hop(self, k):
        @pl.when(k == 0)
        def _():
            self.own_copy().wait()

        @pl.when((k > 0) & (k < self.near))
        def _():
            self.near_copy(k).wait_recv()

        @pl.when(k >= self.near)
        def _():
            self.far_copy(k).wait_recv()
            self.side_copy(k, self.side).start()

    def second_hop(self, k):
        @pl.when(k >= self.near)
        def _():
            self.side_copy(k, 1 - self.side).wait_recv()

        self.pair_copy(k, self.half).start()

    def last_hop(self, k):
        self.pair_copy(k, 1 - self.half).wait_recv()

    def sent(self, k):
        @pl.when((k > 0) & (k < self.near))
        def _():
            self.near_copy(k).wait_send()

        @pl.when(k >= self.near)
        def _():
            self.far_copy(k).wait_send()
            self.side_copy(k, self.side).wait_send()

        self.pair_copy(k, self.half).wait_send()

    @staticmethod
    def scratch(n, hp, width):
        near = near_count(n)
        return [VMEM((near, hp, 2 * width), LOW), VMEM((n - near, hp, width), LOW)]

    @staticmethod
    def semaphores(n):
        return [dma(n), dma(n), dma(n), dma(n), dma(n), dma(n), pltpu.SemaphoreType.DMA]


def clear_unsent(rows_in):
    count, rows, width = rows_in.shape
    rows_in[:, SENT.stop :, :] = jnp.zeros((count, rows - SENT.stop, width), rows_in.dtype)


class Total:
    def __init__(self, part_out, pair_in, far_out, far_in, ps, pr, fs, fr):
        self.part_out, self.pair_in, self.far_out, self.far_in = part_out, pair_in, far_out, far_in
        self.ps, self.pr, self.fs, self.fr = ps, pr, fs, fr
        self.dp, _, _, _, self.mate, self.far = places()
        clear_unsent(far_in)

    def pair_copy(self, j):
        return remote(
            self.part_out.at[j], self.pair_in.at[j], self.ps.at[j], self.pr.at[j], (self.dp, self.mate)
        )

    def far_copy(self, j):
        return remote(
            self.far_out.at[j, SENT],
            self.far_in.at[j, SENT],
            self.fs.at[j],
            self.fr.at[j],
            (self.dp, self.far),
        )

    def give(self, j, rows):
        self.part_out[j] = rows
        self.pair_copy(j).start()

    def take(self, j, rows):
        self.pair_copy(j).wait_recv()
        self.far_out[j] = (rows + self.pair_in[j]).astype(LOW)
        self.far_copy(j).start()

    def result(self, j):
        self.far_copy(j).wait_recv()
        return self.far_out[j].astype(FULL) + self.far_in[j].astype(FULL)

    def sent(self, j):
        self.pair_copy(j).wait_send()
        self.far_copy(j).wait_send()

    @staticmethod
    def scratch(model):
        wide, slim = VMEM((3, PIECE, model), FULL), VMEM((3, PIECE, model), LOW)
        return [wide, wide, slim, slim, dma(3), dma(3), dma(3), dma(3)]


def padded_image(rows_ref, image):
    start = image * SEQ // 8 * 8
    length = min(PIECE, rows_ref.shape[0] - start)
    rows = lax.broadcasted_iota(jnp.int32, (PIECE, length), 0)
    columns = lax.broadcasted_iota(jnp.int32, (PIECE, length), 1)
    pick = (columns == rows + (image * SEQ - start)) & (rows < SEQ)
    return dot_plain(jnp.where(pick, 1.0, 0.0).astype(LOW), rows_ref[start : start + length, :])


def front_kernel(
    n,
    hp,
    per_half,
    capacity_ref,
    routes_ref,
    slot_ids_ref,
    tokens_ref,
    upstream_ref,
    gains_ref,
    query_w_ref,
    key_w_ref,
    value_w_ref,
    output_w_ref,
    place_ref,
    index_ref,
    peak_ref,
    *refs,
):
    outs, spread_hbm, scratch = refs[:9], refs[9], refs[10:]
    held, scratch = scratch[:9], scratch[9:]
    (
        tokens,
        upstream,
        normed_one,
        query,
        key,
        value,
        mixed_rows,
        residual_rows,
        normed_two,
    ) = held
    near_out, far_out, zs, zr, own, ns, nr, hs, xs, xr = scratch[:10]
    total = Total(*scratch[10:])
    dp, t, half, side, mate, far = places()
    heads = query_w_ref.shape[0] // HD
    near = near_count(n)
    width = far_out.shape[2]
    row_count = tokens.shape[0]
    greet(n, dp, t, (mate, far))
    peak_ref[...] = jnp.full(peak_ref.shape, -1e30, FULL)
    for image in range(row_count // PIECE):
        tokens[image * PIECE : (image + 1) * PIECE, :] = padded_image(tokens_ref, image).astype(LOW)

    def image_forward(image):
        rows = image_rows(image)
        unit, _ = normalized(tokens[rows, :].astype(FULL))
        normed = (unit * gains_ref[0:1, :]).astype(LOW)
        normed_one[rows, :] = normed
        queries = dot_last(normed, query_w_ref[...]).astype(LOW)
        keys = dot_last(normed, key_w_ref[...]).astype(LOW)
        values = dot_last(normed, value_w_ref[...]).astype(LOW)
        query[rows, :] = queries
        key[rows, :] = keys
        value[rows, :] = values
        mixed = []
        for h in range(heads):
            cols = slice(h * HD, (h + 1) * HD)
            probs, top = attention_probs(queries[:, cols], keys[:, cols])
            real = lax.broadcasted_iota(jnp.int32, top.shape, 0) < SEQ
            best = jnp.max(jnp.where(real, top, -1e30), axis=0, keepdims=True)
            peak_ref[h : h + 1, :] = jnp.maximum(peak_ref[h : h + 1, :], best)
            mixed.append(dot_plain(probs.astype(LOW), values[:, cols]))
        mixed = jnp.concatenate(mixed, axis=1).astype(LOW)
        mixed_rows[rows, :] = mixed
        return dot_plain(mixed, output_w_ref[...])

    def normed_copy(j, owner):
        rows = normed_two.at[image_rows(2 * j + owner)]
        return remote(rows, rows, ns.at[j], nr.at[j], (dp, mate))

    def keep(i):
        return pltpu.make_async_copy(held[i], outs[i], hs.at[i])

    def finish(j):
        rows = image_rows(2 * j + half)
        residual = tokens[rows, :].astype(FULL) + total.result(j)
        residual_rows[j] = residual
        unit, _ = normalized(residual)
        normed_two[rows, :] = (unit * gains_ref[1:2, :]).astype(LOW)
        normed_copy(j, half).start()

    def peer(k):
        return (partner(dp, k, n), t)

    def half_rows():
        return pl.ds(pl.multiple_of(half * hp, hp), hp)

    def side_columns():
        return pl.ds(pl.multiple_of(side * width, width), width)

    def own_copy():
        return pltpu.make_async_copy(near_out.at[0], spread_hbm.at[0, half_rows()], own)

    def near_copy(k):
        return remote(near_out.at[k], spread_hbm.at[k, half_rows()], zs.at[k], zr.at[k], peer(k))

    def far_copy(k):
        return remote(
            far_out.at[k - near],
            spread_hbm.at[k, half_rows(), side_columns()],
            zs.at[k],
            zr.at[k],
            peer(k),
        )

    def side_copy(k, owner):
        columns = pl.ds(pl.multiple_of(owner * width, width), width)
        part = spread_hbm.at[k, half_rows(), columns]
        return remote(part, part, xs.at[k], xr.at[k], (dp, far))

    def forward(k, carry):
        far_copy(k).wait_recv()
        side_copy(k, side).start()
        return carry

    def dispatch(k):
        slots = lax.broadcasted_iota(jnp.int32, (hp, row_count), 0) + k * hp
        hot = (place_ref[0:1, :] == slots) | (place_ref[1:2, :] == slots)
        hot = jnp.where(hot, 1.0, 0.0).astype(LOW)

        @pl.when(k < near)
        def _():
            near_out[k] = dot_plain(hot, upstream[...]).astype(LOW)

            @pl.when(k == 0)
            def _():
                own_copy().start()

            @pl.when(k > 0)
            def _():
                near_copy(k).start()

        @pl.when(k >= near)
        def _():
            far_out[k - near] = dot_plain(hot, upstream[:, side_columns()]).astype(LOW)
            far_copy(k).start()

    def places_of_pairs():
        routes, slot_ids = routes_ref[...], slot_ids_ref[...]
        limits = jnp.zeros_like(routes)
        for e in range(n):
            limits = jnp.where(routes == e, capacity_ref[e], limits)
        kept = slot_ids < limits
        step = jnp.zeros_like(routes)
        weight = 1
        while weight < n:
            step = step + (routes // weight + dp // weight) % 2 * weight
            weight *= 2
        upper = slot_ids >= per_half
        in_half = slot_ids - jnp.where(upper, per_half, 0)
        in_block = in_half + jnp.where(upper, hp, 0)
        mine = kept & (upper == (half == 1))
        place = jnp.where(mine, step * hp + in_half, -1)
        position = jnp.where(kept, step * (2 * hp) + in_block, -1)
        both = jnp.concatenate([place, position, routes, jnp.full_like(routes, -1)], axis=0)
        fill = jnp.full((8, PIECE - SEQ), -1, jnp.int32)
        spaced = []
        for image in range(row_count // PIECE):
            spaced += [both[:, image * SEQ : (image + 1) * SEQ], fill]
        return jnp.concatenate(spaced, axis=1)

    pairs = places_of_pairs()
    place_ref[...] = pairs
    index_ref[...] = pairs.T
    def step(j, carry):
        given = image_forward(2 * j + 1 - half)

        @pl.when(j == 0)
        def _():
            await_greetings(n, (mate, far))

        total.give(j, given)
        total.take(j, image_forward(2 * j + half))

        @pl.when(j == 0)
        def _():
            for image in range(row_count // PIECE):
                upstream[image * PIECE : (image + 1) * PIECE, :] = padded_image(
                    upstream_ref, image
                ).astype(LOW)

        def turn(k, inner):
            dispatch(k)
            return inner

        @pl.when(j == 0)
        def _():
            lax.fori_loop(near, n, turn, 0)

        @pl.when(j == 1)
        def _():
            lax.fori_loop(0, near, turn, 0)

        @pl.when(j >= 1)
        def _():
            finish(j - 1)

        return carry

    lax.fori_loop(0, 3, step, 0)
    for i in range(7):
        keep(i).start()
    early = n - (n - near) // 4
    lax.fori_loop(near, early, forward, 0)
    finish(2)
    lax.fori_loop(early, n, forward, 0)
    keep(7).start()
    own_copy().wait()

    def arrive(k, carry):
        near_copy(k).wait()
        return carry

    def far_arrive(k, carry):
        far_copy(k).wait_send()
        side_copy(k, side).wait_send()
        side_copy(k, 1 - side).wait_recv()
        return carry

    for j in range(3):
        normed_copy(j, 1 - half).wait_recv()
    keep(8).start()
    lax.fori_loop(1, near, arrive, 0)
    lax.fori_loop(near, n, far_arrive, 0)
    for j in range(3):
        total.sent(j)
        normed_copy(j, half).wait_send()
    for i in range(9):
        keep(i).wait()


def run_front(n, hp, per_half, capacity, routes, slot_ids, tokens, upstream, gains, weights):
    model = tokens.shape[1]
    rows = tokens.shape[0] // SEQ * PIECE
    heads_width = weights[0].shape[0]
    near = near_count(n)
    width = model // 2
    vmem = pl.BlockSpec(memory_space=VMEM)
    hbm = pl.BlockSpec(memory_space=pl.ANY)
    shape = jax.ShapeDtypeStruct
    slim, wide = shape((rows, heads_width), LOW), shape((rows, model), LOW)
    held = (wide, wide, wide, slim, slim, slim, slim, shape((3, PIECE, model), FULL), wide)
    return pl.pallas_call(
        functools.partial(front_kernel, n, hp, per_half),
        out_shape=(
            shape((8, rows), jnp.int32),
            shape((rows, 8), jnp.int32),
            shape((8, 128), FULL),
            *held,
            shape((n, 2 * hp, model), LOW),
        ),
        in_specs=[pl.BlockSpec(memory_space=pltpu.SMEM)] + [vmem] * 9,
        out_specs=[vmem] * 3 + [hbm] * 10,
        scratch_shapes=[
            *[VMEM(a.shape, a.dtype) for a in held],
            VMEM((near, hp, model), LOW),
            VMEM((n - near, hp, width), LOW),
            dma(n),
            dma(n),
            pltpu.SemaphoreType.DMA,
            dma(3),
            dma(3),
            dma(9),
            dma(n),
            dma(n),
            *Total.scratch(model),
        ],
        compiler_params=pltpu.CompilerParams(
            collective_id=0, has_side_effects=True, vmem_limit_bytes=VMEM_LIMIT
        ),
        name="front",
    )(capacity, routes, slot_ids, tokens, upstream, gains, *weights)


def in_turn(i, near):
    return jnp.where(i < 2 * near, i // 2 + (i % 2) * near, i)


def expert_kernel(
    n,
    hp,
    place_ref,
    router_ref,
    peak_ref,
    normed_hbm,
    first_hbm,
    second_hbm,
    upstream_hbm,
    back_ref,
    gate_sum_ref,
    top_ref,
    answer_out_hbm,
    answer_kept_hbm,
    answer_ready_hbm,
    grad_first_hbm,
    grad_second_hbm,
    *scratch,
):
    dp, t, half, side, mate, far = places()
    arrived = scratch[2]
    spread = Spread(n, hp, place_ref, *scratch[:10])
    (
        normed_ref,
        first_ref,
        second_ref,
        answer_out,
        answer_kept,
        grad_first_ref,
        grad_second_ref,
        os_,
        ws,
        cs,
        cr,
        answer_far,
        answer_ready,
        xs,
        xr,
    ) = scratch[44:]
    (
        upstream,
        hidden_all,
        pre_grad_all,
        parts,
        pair_in,
        kept,
        far_out,
        far_in,
        final,
        gate_out,
        gate_in,
        sum_out,
        sum_in,
        sums,
        peaks,
        us,
        ps,
        pr,
        fs,
        fr,
        rs,
        rr,
        ms,
        mr,
        gs,
        gr,
        hs,
        hr,
        ks,
        kr,
        qs,
        qr,
        ss,
        sr,
    ) = scratch[10:44]
    model = normed_ref.shape[1]
    width = model // 2
    near = spread.near
    greet(n, dp, t, [(t + d) % 4 for d in (1, 2, 3)])
    fetches = [
        pltpu.make_async_copy(a, b, ws.at[i])
        for i, (a, b) in enumerate(
            ((normed_hbm, normed_ref), (first_hbm, first_ref), (second_hbm, second_ref))
        )
    ]
    mine = (slice(0, n), spread.rows(half))
    fetches.append(pltpu.make_async_copy(upstream_hbm.at[mine], upstream.at[mine], us.at[0]))
    for fetch in fetches:
        fetch.start()

    def upstream_pair_copy(k, owner):
        part = upstream.at[k, spread.rows(owner)]
        return remote(part, part, cs.at[k], cr.at[k], (dp, mate))

    def answer_side_copy(k):
        return remote(
            answer_out.at[k], answer_far.at[k - near], xs.at[k], xr.at[k], (dp, far)
        )

    def keep(i):
        pairs = (
            (answer_out.at[slice(0, near)], answer_out_hbm),
            (answer_kept.at[slice(0, near)], answer_kept_hbm),
            (answer_ready, answer_ready_hbm),
        )
        return pltpu.make_async_copy(*pairs[i], os_.at[i])

    def gate_copy(k):
        return remote(gate_out.at[k], gate_in.at[k, half], gs.at[k], gr.at[k], spread.peer(k))

    def gate_pair_copy(k, owner):
        tile = gate_in.at[k, owner]
        return remote(tile, tile, hs.at[k], hr.at[k], (dp, mate))

    def part_copy(i, k):
        return remote(
            parts.at[i % 3, :, spread.rows(1 - half)],
            pair_in.at[k],
            ps.at[i % 3],
            pr.at[k],
            (dp, mate),
        )

    def far_copy(i, k):
        return remote(far_out.at[i % SLOTS], far_in.at[k], fs.at[i % SLOTS], fr.at[k], (dp, far))

    def return_copy(k):
        return remote(
            final.at[k], back_ref.at[k, spread.rows(half)], rs.at[k], rr.at[k], spread.peer(k)
        )

    def mate_copy(k, owner):
        rows = back_ref.at[k, spread.rows(owner)]
        return remote(rows, rows, ms.at[k], mr.at[k], (dp, mate))

    def sum_copy(k):
        return remote(sum_out.at[k], sum_in.at[k], ks.at[k], kr.at[k], spread.peer(k))

    def peak_copy(k):
        return remote(peak_ref, peaks.at[k], qs.at[k], qr.at[k], spread.peer(k))

    def share_copy(d, owner):
        return remote(
            sums.at[owner], sums.at[owner], ss.at[d - 1], sr.at[d - 1], (dp, (t + d) % 4)
        )

    def loop(body, first=0, last=n):
        def one(k, carry):
            body(k)
            return carry

        lax.fori_loop(first, last, one, 0)

    fetches[0].wait()
    logits = dot_last(router_ref[...], normed_ref[...])
    rows_of = lax.broadcasted_iota(jnp.int32, logits.shape, 0)
    one, two = (
        jnp.sum(jnp.where(rows_of == place_ref[r : r + 1, :], logits, 0.0), axis=0, keepdims=True)
        for r in (4, 5)
    )
    best = jnp.maximum(one, two)
    one, two = jnp.exp(one - best), jnp.exp(two - best)
    gate_one, gate_two = one / (one + two), two / (one + two)
    await_greetings(n, (1, 2, 3))

    def dispatch(i):
        k = in_turn((i + 1) % n, near)
        is_first, is_second = spread.send(k, normed_ref)
        gate = jnp.sum(
            jnp.where(is_first, gate_one, 0.0) + jnp.where(is_second, gate_two, 0.0),
            axis=1,
            keepdims=True,
        )
        tile = jnp.broadcast_to(column_to_row(gate), (8, hp))

        @pl.when(k == 0)
        def _():
            gate_in[0, half] = tile

        @pl.when(k > 0)
        def _():
            gate_out[k] = tile
            gate_copy(k).start()

    loop(dispatch)
    for fetch in fetches[1:]:
        fetch.wait()
    loop(lambda i: upstream_pair_copy(in_turn(i, near), half).start())

    def chunk(i, k):
        gate = jnp.concatenate(
            [row_to_column(gate_in[k, 0, 0:1, :]), row_to_column(gate_in[k, 1, 0:1, :])], axis=0
        )
        gradient = upstream[k].astype(FULL)
        answer_grad = (gradient * gate).astype(LOW)
        pre = dot_plain(arrived[k], first_ref[...])
        share = 0.5 * (1.0 + lax.erf(pre * math.sqrt(0.5)))
        slope = share + pre * (jnp.exp(-0.5 * pre * pre) * (1.0 / math.sqrt(2.0 * math.pi)))
        hidden = (pre * share).astype(LOW)
        hidden_all[k] = hidden
        answer = dot_plain(hidden, second_ref[...])
        parts[i % 3, 0] = answer.astype(LOW)
        gate_sum = jnp.sum(answer * gradient, axis=1, keepdims=True)
        upstream[k] = answer_grad
        pre_grad = (dot_last(answer_grad, second_ref[...]) * slope).astype(LOW)
        pre_grad_all[k] = pre_grad
        parts[i % 3, 1] = dot_last(pre_grad, first_ref[...]).astype(LOW)
        tile = jnp.broadcast_to(column_to_row(gate_sum), (8, 2 * hp))

        @pl.when(k == 0)
        def _():
            sum_in[0] = tile

        @pl.when(k > 0)
        def _():
            sum_out[k] = tile
            sum_copy(k).start()
            peak_copy(k).start()

    tile = 256
    tiles = model // tile

    def grad_copy(m, j):
        cols = pl.ds(pl.multiple_of(m * tile, tile), tile)
        ref, hbm = ((grad_first_ref, grad_first_hbm), (grad_second_ref, grad_second_hbm))[j]
        return pltpu.make_async_copy(ref.at[cols], hbm.at[cols], os_.at[3 + 2 * m + j])

    def grads(m):
        cols = pl.ds(pl.multiple_of(m * tile, tile), tile)
        rows_in = arrived[:, :, cols].reshape(n * 2 * hp, tile)
        grad_first_ref[cols, :] = dot_first(rows_in, pre_grad_all[...].reshape(n * 2 * hp, -1))
        grad_copy(m, 0).start()
        hidden = hidden_all[:, :, cols].reshape(n * 2 * hp, tile)
        grad_second_ref[cols, :] = dot_first(hidden, upstream[...].reshape(n * 2 * hp, model))
        grad_copy(m, 1).start()

    def step(i):
        @pl.when(i < n)
        def _():
            spread.first_hop(in_turn(i, near))

        @pl.when((i >= 1) & (i < n + 1))
        def _():
            k = in_turn(i - 1, near)
            spread.second_hop(k)

            @pl.when(k > 0)
            def _():
                gate_copy(k).wait_recv()

            gate_pair_copy(k, half).start()

        @pl.when((i >= 2) & (i < n + 2))
        def _():
            k = in_turn(i - 2, near)
            spread.last_hop(k)
            gate_pair_copy(k, 1 - half).wait_recv()
            upstream_pair_copy(k, 1 - half).wait_recv()
            upstream_pair_copy(k, half).wait_send()

            @pl.when(i >= 5)
            def _():
                part_copy(i - 5, in_turn(i - 5, near)).wait_send()

            chunk(i - 2, k)
            part_copy(i - 2, k).start()

        @pl.when((i >= 3) & (i < n + 3))
        def _():
            k = in_turn(i - 3, near)
            part_copy(i - 3, k).wait_recv()

            @pl.when(i >= 3 + SLOTS)
            def _():
                far_copy(i - 3 - SLOTS, in_turn(i - 3 - SLOTS, near)).wait_send()

            for j in (1, 0):
                whole = parts[(i - 3) % 3, j, spread.rows(half), :].astype(FULL) + pair_in[k, j].astype(FULL)
                low, high = whole[:, :width], whole[:, width:]
                stays = jnp.where(side == 0, low, high)
                goes = jnp.where(side == 0, high, low).astype(LOW)
                if j:
                    kept[(i - 3) % SLOTS] = stays
                    far_out[(i - 3) % SLOTS] = goes
                    far_copy(i - 3, k).start()
                else:
                    answer_kept[k] = stays
                    answer_out[k] = goes

        @pl.when((i >= LAG) & (i < n + LAG))
        def _():
            k = in_turn(i - LAG, near)
            far_copy(i - LAG, k).wait_recv()
            rows = (kept[(i - LAG) % SLOTS] + far_in[k].astype(FULL)).astype(LOW)

            @pl.when(k == 0)
            def _():
                back_ref[0, spread.rows(half), :] = rows

            @pl.when(k > 0)
            def _():
                final[k] = rows
                return_copy(k).start()

        @pl.when(i == n + 2)
        def _():
            loop(lambda k: answer_side_copy(k).start(), near)

        @pl.when((i >= n + 2) & (i < n + 2 + tiles))
        def _():
            grads(i - (n + 2))

    loop(step, 0, n + max(LAG, 2 + tiles))
    keep(0).start()
    keep(1).start()
    peaks[0] = peak_ref[...]

    def collect_sums(k):
        @pl.when(k > 0)
        def _():
            peak_copy(k).wait_recv()
            sum_copy(k).wait_recv()

        sums[t, pl.ds(k, 1), :] = sum_in[k, 0:1, :]

    loop(collect_sums)
    for d in (1, 2, 3):
        share_copy(d, t).start()
    top_ref[...] = jnp.max(peaks[...], axis=0)

    def collect(i):
        k = in_turn(i, near)

        @pl.when(k > 0)
        def _():
            return_copy(k).wait_recv()

        mate_copy(k, half).start()

    loop(collect)

    def answers_whole(k):
        answer_side_copy(k).wait_recv()
        answer_ready[k - near] = (answer_kept[k] + answer_far[k - near].astype(FULL)).astype(LOW)

    loop(answers_whole, near)
    keep(2).start()
    for d in (1, 2, 3):
        share_copy(d, (t + 4 - d) % 4).wait_recv()
    whole = (sums[0] + sums[1]) + (sums[2] + sums[3])
    whole = jnp.concatenate([whole[k : k + 1] for k in range(n)], axis=1)
    gate_sum_ref[...] = jnp.broadcast_to(whole, gate_sum_ref.shape)

    def finish(i):
        k = in_turn(i, near)
        mate_copy(k, 1 - half).wait_recv()
        mate_copy(k, half).wait_send()
        spread.sent(k)
        gate_pair_copy(k, half).wait_send()

        @pl.when(k > 0)
        def _():
            return_copy(k).wait_send()
            gate_copy(k).wait_send()
            sum_copy(k).wait_send()
            peak_copy(k).wait_send()

        @pl.when(i >= n - 3)
        def _():
            part_copy(i, k).wait_send()

        @pl.when(i >= n - SLOTS)
        def _():
            far_copy(i, k).wait_send()

    loop(finish)
    for d in (1, 2, 3):
        share_copy(d, t).wait_send()
    loop(lambda k: answer_side_copy(k).wait_send(), near)
    for i in range(3):
        keep(i).wait()
    for m in range(tiles):
        grad_copy(m, 0).wait()
        grad_copy(m, 1).wait()


def run_experts(n, hp, place, router, peak, normed, first, second, upstream):
    model = normed.shape[1]
    width = model // 2
    hidden = first.shape[1]
    near = near_count(n)
    vmem = pl.BlockSpec(memory_space=VMEM)
    hbm = pl.BlockSpec(memory_space=pl.ANY)
    shape = jax.ShapeDtypeStruct
    return pl.pallas_call(
        functools.partial(expert_kernel, n, hp),
        out_shape=(
            shape((n, 2 * hp, width), LOW),
            shape((8, n * 2 * hp), FULL),
            shape(peak.shape, FULL),
            shape((near, hp, width), LOW),
            shape((near, hp, width), FULL),
            shape((n - near, hp, width), LOW),
            shape((model, hidden), FULL),
            shape((hidden, model), FULL),
        ),
        in_specs=[vmem] * 3 + [hbm] * 4,
        out_specs=[vmem] * 3 + [hbm] * 5,
        scratch_shapes=[
            *Spread.scratch(n, hp, width),
            VMEM((n, 2 * hp, model), LOW),
            *Spread.semaphores(n),
            VMEM((n, 2 * hp, model), LOW),
            VMEM((n, 2 * hp, hidden), LOW),
            VMEM((n, 2 * hp, hidden), LOW),
            VMEM((3, 2, 2 * hp, model), LOW),
            VMEM((n, 2, hp, model), LOW),
            VMEM((SLOTS, hp, width), FULL),
            VMEM((SLOTS, hp, width), LOW),
            VMEM((n, hp, width), LOW),
            VMEM((n, hp, width), LOW),
            VMEM((n, 8, hp), FULL),
            VMEM((n, 2, 8, hp), FULL),
            VMEM((n, 8, 2 * hp), FULL),
            VMEM((n, 8, 2 * hp), FULL),
            VMEM((4, n, 2 * hp), FULL),
            VMEM((n, *peak.shape), FULL),
            dma(1),
            dma(3), dma(n), dma(SLOTS), dma(n), dma(n), dma(n), dma(n), dma(n),
            dma(n), dma(n), dma(n), dma(n), dma(n), dma(n), dma(n), dma(n), dma(3), dma(3),
            VMEM(normed.shape, LOW),
            VMEM(first.shape, LOW),
            VMEM(second.shape, LOW),
            VMEM((n, hp, width), LOW),
            VMEM((n, hp, width), FULL),
            VMEM((model, hidden), FULL),
            VMEM((hidden, model), FULL),
            dma(3 + 2 * (model // 256)),
            dma(3), dma(n), dma(n),
            VMEM((n - near, hp, width), LOW),
            VMEM((n - near, hp, width), LOW),
            dma(n), dma(n),
        ],
        compiler_params=pltpu.CompilerParams(
            collective_id=1, has_side_effects=True, vmem_limit_bytes=VMEM_LIMIT
        ),
        name="experts",
    )(place, router, peak, normed, first, second, upstream)


def unpad(rows_ref, out_ref):
    for image in range(rows_ref.shape[0] // PIECE):
        start = image * SEQ // 8 * 8
        length = min(PIECE, out_ref.shape[0] - start)
        shift = image * SEQ - start
        rows = lax.broadcasted_iota(jnp.int32, (length, PIECE), 0)
        columns = lax.broadcasted_iota(jnp.int32, (length, PIECE), 1)
        pick = (rows == columns + shift) & (columns < SEQ)
        image_part = rows_ref[image * PIECE : (image + 1) * PIECE, :]
        moved = dot_plain(jnp.where(pick, 1.0, 0.0).astype(LOW), image_part).astype(LOW)
        if shift:
            before = lax.broadcasted_iota(jnp.int32, (8, moved.shape[1]), 0) < shift
            first = jnp.where(before, out_ref[start : start + 8, :].astype(FULL), moved[:8].astype(FULL))
            out_ref[start : start + 8, :] = first.astype(LOW)
            out_ref[start + 8 : start + length, :] = moved[8:]
        else:
            out_ref[start : start + length, :] = moved


def back_kernel(
    n,
    hp,
    back_ref,
    gate_sum_ref,
    index_ref,
    gains_ref,
    output_w_ref,
    router_ref,
    answer_ready,
    *refs,
):
    later, outs, scratch = refs[:13], refs[13:18], refs[18:]
    block_out_ref, tokens_out_ref, weights_ref, small_ref, gain_ref = outs
    held, scratch = scratch[:13], scratch[13:]
    (
        residual_ref,
        upstream_ref,
        answer_out,
        answer_kept,
        normed_one_ref,
        query_ref,
        key_ref,
        value_ref,
        mixed_ref,
        tokens_ref,
        query_w_ref,
        key_w_ref,
        value_w_ref,
    ) = held
    dp, t, half, side, mate, far = places()
    (
        moe_mine,
        moe_other,
        block_mine,
        block_other,
        attention_grad,
        residual_grad,
        query_grad,
        key_grad,
        value_grad,
        gain_two_sum,
        gain_two_in,
        gain_one_sum,
        gain_one_all,
        gain_rows,
        router_sum,
        router_in,
        totals,
        totals_two,
        pieces,
        pieces_in,
        small_pieces,
        small_in,
        answer_far,
        answer_final,
        answers,
        block_ref,
        grad_tokens_ref,
        hs,
        as_,
        ar,
        bs,
        br,
        ts,
        tr,
        cs,
        cr,
        gs,
        gr,
        ws,
        wr,
        ls,
        lr,
        os_,
        or_,
        vs,
        vr,
        ds,
        dr,
        es,
        er,
        fs,
        fr,
        ks,
        kr,
    ) = scratch[:54]
    total = Total(*scratch[54:])
    heads = query_w_ref.shape[0] // HD
    model = upstream_ref.shape[1]
    width = model // 2
    slots = back_ref.shape[0]
    piece = pieces.shape[1]
    near = near_count(n)
    greet(n, dp, t, [(t + d) % 4 for d in (1, 2, 3)])
    fetches = [pltpu.make_async_copy(a, b, hs.at[i]) for i, (a, b) in enumerate(zip(later, held))]
    for fetch in fetches:
        fetch.start()

    def peer(k):
        return (partner(dp, k, n), t)

    def moe_copy(j):
        return remote(moe_mine.at[j, SENT], moe_other.at[j, SENT], as_.at[j], ar.at[j], (dp, far))

    def block_copy(j):
        return remote(block_mine.at[j, SENT], block_other.at[j, SENT], bs.at[j], br.at[j], (dp, far))

    def attention_copy(j, owner):
        rows = attention_grad.at[image_rows(2 * j + owner)]
        return remote(rows, rows, ts.at[j], tr.at[j], (dp, mate))

    def tokens_copy(j, owner):
        rows = grad_tokens_ref.at[image_rows(2 * j + owner)]
        return remote(rows, rows, cs.at[j], cr.at[j], (dp, mate))

    def block_pair_copy(j, owner):
        rows = block_ref.at[image_rows(2 * j + owner)]
        return remote(rows, rows, ls.at[j], lr.at[j], (dp, mate))

    def gain_copy(d, owner):
        return remote(
            gain_one_all.at[owner], gain_one_all.at[owner], gs.at[d - 1], gr.at[d - 1], (dp, (t + d) % 4)
        )

    def gain_row_copy(k):
        return remote(gain_rows.at[0], gain_rows.at[k], ks.at[k], kr.at[k], peer(k))

    def router_copy():
        return remote(router_sum, router_in, os_.at[0], or_.at[0], (dp, mate))

    def gain_two_copy():
        return remote(gain_two_sum, gain_two_in, os_.at[1], or_.at[1], (dp, mate))

    def piece_copy(k):
        return remote(pieces.at[k], pieces_in.at[k], ws.at[k], wr.at[k], peer(k))

    def small_copy(k):
        return remote(small_pieces.at[k], small_in.at[k], vs.at[k], vr.at[k], peer(k))

    def answer_rows(k, owner):
        return answers.at[pl.ds(pl.multiple_of((2 * k + owner) * hp, hp), hp)]

    def answer_side_copy(k):
        return remote(answer_out.at[k], answer_far.at[k], ds.at[k], dr.at[k], (dp, far))

    def answer_copy(k):
        return remote(answer_final.at[k], answer_rows(k, half), es.at[k], er.at[k], peer(k))

    def far_answer_copy(k):
        return remote(answer_ready.at[k - near], answer_rows(k, half), es.at[k], er.at[k], peer(k))

    def answer_pair_copy(k, owner):
        return remote(answer_rows(k, owner), answer_rows(k, owner), fs.at[k], fr.at[k], (dp, mate))

    def loop(body, first=0, last=n):
        def one(k, carry):
            body(k)
            return carry

        lax.fori_loop(first, last, one, 0)

    def both_sides(mine, other):
        low = jnp.where(side == 0, mine, other)
        high = jnp.where(side == 0, other, mine)
        return jnp.concatenate([low, high], axis=1)

    def hots(rows):
        columns = lax.broadcasted_iota(jnp.int32, (PIECE, slots), 1)
        return index_ref[rows, 2:3] == columns, index_ref[rows, 3:4] == columns

    def as_low(mask):
        return jnp.where(mask, 1.0, 0.0).astype(LOW)

    clear_unsent(moe_other)
    clear_unsent(block_other)
    gain_two_sum[...] = jnp.zeros_like(gain_two_sum)
    gain_one_sum[...] = jnp.zeros_like(gain_one_sum)
    router_sum[...] = jnp.zeros_like(router_sum)

    def combine(j):
        first, second = hots(image_rows(2 * j + half))
        moe_mine[j] = dot_plain(as_low(first | second), back_ref[...]).astype(LOW)

        @pl.when(j == 0)
        def _():
            await_greetings(n, (1, 2, 3))
            loop(lambda k: far_answer_copy(k).start(), near)

        moe_copy(j).start()

    loop(combine, 0, 3)
    for fetch in fetches[:3]:
        fetch.wait()
    loop(lambda k: answer_side_copy((k + 1) % near).start(), 0, near)

    def gates_of(rows, normed):
        logits = dot_last(normed, router_ref[...])
        lanes = lax.broadcasted_iota(jnp.int32, logits.shape, 1)
        hot_one = index_ref[rows, 4:5] == lanes
        hot_two = index_ref[rows, 5:6] == lanes
        one = jnp.sum(jnp.where(hot_one, logits, 0.0), axis=1, keepdims=True)
        two = jnp.sum(jnp.where(hot_two, logits, 0.0), axis=1, keepdims=True)
        top = jnp.maximum(one, two)
        one, two = jnp.exp(one - top), jnp.exp(two - top)
        return one / (one + two), two / (one + two), hot_one, hot_two

    def moe_back(j):
        rows = image_rows(2 * j + half)
        unit, factor = normalized(residual_ref[j])
        normed = (unit * gains_ref[1:2, :]).astype(LOW)
        gate_one, gate_two, hot_one, hot_two = gates_of(rows, normed)
        first, second = hots(rows)
        slot_sums = gate_sum_ref[0:1, :]
        grad_one = jnp.sum(jnp.where(first, slot_sums, 0.0), axis=1, keepdims=True)
        grad_two = jnp.sum(jnp.where(second, slot_sums, 0.0), axis=1, keepdims=True)
        mean = gate_one * grad_one + gate_two * grad_two
        logit_grad = jnp.where(hot_one, gate_one * (grad_one - mean), 0.0)
        logit_grad = logit_grad + jnp.where(hot_two, gate_two * (grad_two - mean), 0.0)
        logit_grad = logit_grad.astype(LOW)
        router_sum[...] += dot_first(normed, logit_grad)
        normed_grad = dot_plain(logit_grad, router_ref[...])
        moe_copy(j).wait_recv()
        normed_grad = normed_grad + both_sides(moe_mine[j].astype(FULL), moe_other[j].astype(FULL))
        gain_two_sum[...] += jnp.sum((normed_grad * unit).reshape(PIECE // 8, 8, model), axis=0)
        grad = normalized_back(normed_grad * gains_ref[1:2, :], unit, factor)
        grad = grad + upstream_ref[rows, :].astype(FULL)
        residual_grad[j] = grad
        attention_grad[rows, :] = grad.astype(LOW)
        attention_copy(j, half).start()

    loop(moe_back, 0, 3)
    router_copy().start()
    gain_two_copy().start()
    for fetch in fetches[3:]:
        fetch.wait()

    def image_back(image):
        rows = image_rows(image)
        mixed_grad = dot_last(attention_grad[rows, :], output_w_ref[...]).astype(LOW)
        queries, keys, values = query_ref[rows, :], key_ref[rows, :], value_ref[rows, :]
        query_parts, key_parts, value_parts = [], [], []
        for h in range(heads):
            cols = slice(h * HD, (h + 1) * HD)
            probs, _ = attention_probs(queries[:, cols], keys[:, cols])
            value_parts.append(dot_first(probs.astype(LOW), mixed_grad[:, cols]))
            probs_grad = dot_last(mixed_grad[:, cols], values[:, cols])
            level = jnp.sum(probs * probs_grad, axis=1, keepdims=True)
            score_grad = (probs * (probs_grad - level)).astype(LOW)
            query_parts.append(dot_plain(score_grad, keys[:, cols]) * HD**-0.5)
            key_parts.append(dot_first(score_grad, queries[:, cols]) * HD**-0.5)
        grads = [jnp.concatenate(p, axis=1).astype(LOW) for p in (query_parts, key_parts, value_parts)]
        query_grad[rows, :], key_grad[rows, :], value_grad[rows, :] = grads

    def answer_turn(k):
        answer_side_copy(k).wait_recv()
        rows = (answer_kept[k] + answer_far[k].astype(FULL)).astype(LOW)

        @pl.when(k == 0)
        def _():
            answer_rows(0, half)[...] = rows

        @pl.when(k > 0)
        def _():
            answer_final[k] = rows
            answer_copy(k).start()

    def grad_part(image):
        rows = image_rows(image)
        part = dot_plain(query_grad[rows, :], query_w_ref[...])
        part = part + dot_plain(key_grad[rows, :], key_w_ref[...])
        part = part + dot_plain(value_grad[rows, :], value_w_ref[...])
        unit, _ = normalized(tokens_ref[rows, :].astype(FULL))
        gain_one_sum[...] += jnp.sum((part * unit).reshape(PIECE // 8, 8, model), axis=0)
        return part

    def my_piece(source, k):
        at = partner(dp, k, n) * piece
        grain = math.gcd(piece, 8)
        span = -(-(piece + 8 - grain) // 8) * 8
        taken = source[pl.ds(pl.multiple_of(at // 8 * 8, 8), span), :]
        rows = taken[:piece]
        for shift in range(grain, 8, grain):
            rows = jnp.where(at % 8 == shift, taken[shift : shift + piece], rows)
        return rows.astype(LOW)

    def small_grads():
        router_copy().wait_recv()
        gain_two_copy().wait_recv()
        row = jnp.sum(gain_two_sum[...] + gain_two_in[...], axis=0, keepdims=True)
        column = jnp.concatenate(
            [row_to_column(row[:, i : i + 256]) for i in range(0, model, 256)], axis=0
        )
        totals_two[...] = jnp.concatenate(
            [
                dot_first(attention_grad[...], mixed_ref[...]),
                router_sum[...] + router_in[...],
                column,
            ],
            axis=1,
        )

        def send_small(i):
            k = in_turn((i + 1) % n, near)
            small_pieces[k] = my_piece(totals_two, k)

            @pl.when(k > 0)
            def _():
                small_copy(k).start()

        loop(send_small)

    for j in range(3):
        attention_copy(j, 1 - half).wait_recv()

    def attention_back(j):
        for owner in (1 - half, half):
            image_back(2 * j + owner)
        total.give(j, grad_part(2 * j + 1 - half))
        total.take(j, grad_part(2 * j + half))
        answer_turn((j + 1) % near)

        @pl.when(j == 0)
        def _():
            small_grads()

        @pl.when(j == 2)
        def _():
            answer_turn(0)

    loop(attention_back, 0, 3)

    gain_one_all[t] = jnp.sum(gain_one_sum[...], axis=0, keepdims=True)
    for d in (1, 2, 3):
        gain_copy(d, t).start()
    normed_one = normed_one_ref[...]
    totals[:, : 3 * query_grad.shape[1]] = jnp.concatenate(
        [
            dot_first(normed_one, query_grad[...]),
            dot_first(normed_one, key_grad[...]),
            dot_first(normed_one, value_grad[...]),
        ],
        axis=1,
    )

    def send_piece(i):
        k = in_turn((i + 1) % n, near)
        pieces[k] = my_piece(totals, k)

        @pl.when(k > 0)
        def _():
            piece_copy(k).start()

    loop(send_piece)


    def answers_here(i):
        k = in_turn(i, near)

        @pl.when((k > 0) & (k < near))
        def _():
            answer_copy(k).wait_recv()

        @pl.when(k >= near)
        def _():
            far_answer_copy(k).wait_recv()

        answer_pair_copy(k, half).start()

    loop(answers_here)
    loop(lambda k: answer_pair_copy(k, 1 - half).wait_recv())

    def block_rows(j):
        rows = image_rows(2 * j + half)
        residual = residual_ref[j]
        unit, _ = normalized(residual)
        gate_one, gate_two, _, _ = gates_of(rows, (unit * gains_ref[1:2, :]).astype(LOW))
        first, second = hots(rows)
        from_first = dot_plain(as_low(first), answers[...])
        from_second = dot_plain(as_low(second), answers[...])
        mine = jnp.where(side == 0, residual[:, :width], residual[:, width:])
        block_mine[j] = (mine + (gate_one * from_first + gate_two * from_second)).astype(LOW)
        block_copy(j).start()

    loop(block_rows, 0, 3)

    def tokens_back(j):
        rows = image_rows(2 * j + half)
        normed_grad = total.result(j)
        unit, factor = normalized(tokens_ref[rows, :].astype(FULL))
        grad = normalized_back(normed_grad * gains_ref[0:1, :], unit, factor)
        grad_tokens_ref[rows, :] = (residual_grad[j] + grad).astype(LOW)
        tokens_copy(j, half).start()

    loop(tokens_back, 0, 3)
    for d in (1, 2, 3):
        gain_copy(d, (t + 4 - d) % 4).wait_recv()
    gain_rows[0] = (gain_one_all[0] + gain_one_all[1]) + (gain_one_all[2] + gain_one_all[3])

    def send_gain(k):
        gain_row_copy(k).start()

    loop(send_gain, 1)

    def block_back(j):
        block_copy(j).wait_recv()
        block_ref[image_rows(2 * j + half), :] = both_sides(block_mine[j], block_other[j])
        block_pair_copy(j, half).start()

    for j in range(3):
        tokens_copy(j, 1 - half).wait_recv()
    unpad(grad_tokens_ref, tokens_out_ref)
    loop(block_back, 0, 3)
    for j in range(3):
        block_pair_copy(j, 1 - half).wait_recv()
    unpad(block_ref, block_out_ref)
    pieces_in[0] = pieces[0]
    small_in[0] = small_pieces[0]

    def arrive(k):
        piece_copy(k).wait_recv()
        small_copy(k).wait_recv()
        gain_row_copy(k).wait_recv()

    loop(arrive, 1)
    weights_ref[...] = jnp.sum(pieces_in[...].astype(FULL), axis=0)
    small_ref[...] = jnp.sum(small_in[...].astype(FULL), axis=0)
    gain_ref[...] = jnp.sum(gain_rows[...], axis=0)

    for j in range(3):
        moe_copy(j).wait_send()
        block_copy(j).wait_send()
        attention_copy(j, half).wait_send()
        total.sent(j)
        tokens_copy(j, half).wait_send()
        block_pair_copy(j, half).wait_send()
        gain_copy(j + 1, t).wait_send()
    router_copy().wait_send()
    gain_two_copy().wait_send()

    def left(k):
        @pl.when(k < near)
        def _():
            answer_side_copy(k).wait_send()

        @pl.when((k > 0) & (k < near))
        def _():
            answer_copy(k).wait_send()

        @pl.when(k >= near)
        def _():
            far_answer_copy(k).wait_send()

        answer_pair_copy(k, half).wait_send()

        @pl.when(k > 0)
        def _():
            piece_copy(k).wait_send()
            small_copy(k).wait_send()
            gain_row_copy(k).wait_send()

    loop(left)


def run_back(n, hp, row_count, first, later):
    upstream = later[1]
    rows, model = upstream.shape
    heads_width = later[8].shape[1]
    width = model // 2
    piece = model // n
    vmem = pl.BlockSpec(memory_space=VMEM)
    shape = jax.ShapeDtypeStruct
    slim = VMEM((3, PIECE, width), LOW)
    heads = VMEM((rows, heads_width), LOW)
    eight = VMEM((8, model), FULL)
    wide, narrow = 3 * heads_width, heads_width + n + 1
    quarter = VMEM((near_count(n), hp, width), LOW)
    three, many = dma(3), dma(n)
    return pl.pallas_call(
        functools.partial(back_kernel, n, hp),
        out_shape=(
            shape((row_count, model), LOW),
            shape((row_count, model), LOW),
            shape((piece, wide), FULL),
            shape((piece, narrow), FULL),
            shape((1, model), FULL),
        ),
        in_specs=[vmem] * (len(first) - 1) + [pl.BlockSpec(memory_space=pl.ANY)] * (1 + len(later)),
        out_specs=[vmem] * 5,
        scratch_shapes=[
            *[VMEM(a.shape, a.dtype) for a in later],
            slim, slim, slim, slim,
            VMEM((rows, model), LOW),
            VMEM((3, PIECE, model), FULL),
            heads, heads, heads,
            eight, eight, eight,
            VMEM((4, 1, model), FULL),
            VMEM((n, 1, model), FULL),
            VMEM((model, n), FULL),
            VMEM((model, n), FULL),
            VMEM((model, wide), FULL),
            VMEM((model, narrow), FULL),
            VMEM((n, piece, wide), LOW),
            VMEM((n, piece, wide), LOW),
            VMEM((n, piece, narrow), LOW),
            VMEM((n, piece, narrow), LOW),
            quarter, quarter,
            VMEM((n * 2 * hp, width), LOW),
            VMEM((rows, model), LOW),
            VMEM((rows, model), LOW),
            dma(len(later)),
            three, three, three, three, three, three, three, three, three, three,
            many, many, three, three, dma(2), dma(2),
            many, many, many, many, many, many, many, many, many, many,
            *Total.scratch(model),
        ],
        compiler_params=pltpu.CompilerParams(
            collective_id=2, has_side_effects=True, vmem_limit_bytes=VMEM_LIMIT
        ),
        name="back",
    )(*first, *later)


def results_kernel(
    threshold_ref,
    *refs,
):
    small_in, moved_in, moved_out, refs = refs[:6], refs[6:10], refs[10:14], refs[14:]
    (
        gain_one_ref,
        gain_two_ref,
        query_ref,
        key_ref,
        value_ref,
        output_ref,
        router_ref,
        clipped_query_ref,
        clipped_key_ref,
        head_max_ref,
        *held,
        sems,
    ) = refs
    held, own = held[:4], held[4:]
    weights_ref, small_ref, gain_row_ref, top_ref, query_w_ref, key_w_ref = own
    fetches, copies = [], []
    for i, (source, target) in enumerate(zip(moved_in, moved_out)):
        rows = source.shape[0]
        cut = rows // 16 * 8
        for part, at in enumerate((slice(0, cut), slice(cut, rows))):
            sem = sems.at[2 * i + part]
            fetches.append(pltpu.make_async_copy(source.at[at], held[i].at[at], sem))
            sem = sems.at[8 + 2 * i + part]
            copies.append(pltpu.make_async_copy(held[i].at[at], target.at[at], sem))
    small_fetches = [
        pltpu.make_async_copy(a, b, sems.at[16 + i]) for i, (a, b) in enumerate(zip(small_in, own))
    ]
    for fetch in fetches + small_fetches:
        fetch.start()
    for fetch, copy in zip(fetches, copies):
        fetch.wait()
        copy.start()
    for fetch in small_fetches:
        fetch.wait()
    piece, wide = query_ref.shape
    heads = head_max_ref.shape[0]
    query_ref[...] = weights_ref[:, :wide]
    key_ref[...] = weights_ref[:, wide : 2 * wide]
    value_ref[...] = weights_ref[:, 2 * wide :]
    small = small_ref[...]
    output_ref[...] = small[:, :wide].T
    n = router_ref.shape[0]
    router_ref[...] = small[:, wide : wide + n].T
    gain_two_ref[...] = column_to_row(small[:, wide + n :])[0]
    model = gain_row_ref.shape[1]
    lanes = lax.broadcasted_iota(jnp.int32, (piece, model), 1)
    mine = lax.broadcasted_iota(jnp.int32, (piece, model), 0) + lax.axis_index("dp") * piece
    column = jnp.sum(jnp.where(lanes == mine, gain_row_ref[...], 0.0), axis=1, keepdims=True)
    gain_one_ref[...] = column_to_row(column)[0]
    head_max_ref[...] = column_to_row(top_ref[:, 0:1])[0, :heads]
    for h in range(heads):
        rows = slice(h * HD, (h + 1) * HD)
        factor = jnp.sqrt(jnp.minimum(1.0, threshold_ref[h] / top_ref[h : h + 1, 0:1]))
        clipped_query_ref[rows, :] = query_w_ref[rows, :].astype(FULL) * factor
        clipped_key_ref[rows, :] = key_w_ref[rows, :].astype(FULL) * factor
    for copy in copies:
        copy.wait()


def run_results(n, threshold, weights, small, gain_row, top, query_w, key_w, moved):
    wide, model = query_w.shape
    piece = weights.shape[0]
    shape = jax.ShapeDtypeStruct
    vmem = pl.BlockSpec(memory_space=VMEM)
    hbm = pl.BlockSpec(memory_space=pl.ANY)
    grad, clipped = shape((piece, wide), FULL), shape((wide, model), FULL)
    return pl.pallas_call(
        results_kernel,
        out_shape=(
            *[shape(a.shape, a.dtype) for a in moved],
            shape((piece,), FULL),
            shape((piece,), FULL),
            grad,
            grad,
            grad,
            shape((wide, piece), FULL),
            shape((n, piece), FULL),
            clipped,
            clipped,
            shape(threshold.shape, FULL),
        ),
        in_specs=[pl.BlockSpec(memory_space=pltpu.SMEM)] + [hbm] * 10,
        out_specs=[hbm] * 4 + [vmem] * 10,
        scratch_shapes=[
            *[
                VMEM(a.shape, a.dtype)
                for a in (*moved, weights, small, gain_row, top, query_w, key_w)
            ],
            dma(22),
        ],
        compiler_params=pltpu.CompilerParams(vmem_limit_bytes=VMEM_LIMIT),
        name="results",
    )(threshold, weights, small, gain_row, top, query_w, key_w, *moved)


def body(
    tokens,
    gain_attn,
    w_query,
    w_key,
    w_value,
    w_output,
    gain_moe,
    w_router,
    expert_in,
    expert_out,
    routes,
    slot_ids,
    capacity,
    threshold,
    cotangent,
):
    n = lax.axis_size("dp")
    row_count, model = tokens.shape
    slot_count = 23 * TOK_DEV // (10 * n) + 1
    per_half = -(-slot_count // 2)
    hp = -(-per_half // 16) * 16
    gains = jnp.concatenate([gain_attn, gain_moe]).astype(FULL).reshape(2, -1)
    across = (w_query.T, w_key.T, w_value.T)
    (
        place,
        index,
        peak,
        tokens_in,
        upstream,
        normed_one,
        query,
        key,
        value,
        mixed,
        residual,
        normed_two,
        spread,
    ) = run_front(
        n,
        hp,
        per_half,
        capacity,
        routes.T,
        slot_ids.T,
        tokens,
        cotangent,
        gains,
        (*across, w_output),
    )
    router = w_router.T
    back, gate_sums, top, answer_out, answer_kept, answer_ready, grad_first, grad_second = run_experts(
        n, hp, place, router, peak, normed_two, expert_in[0], expert_out[0], spread
    )
    block_out, grad_tokens, weight_grads, small, gain_rows = run_back(
        n,
        hp,
        row_count,
        (back.reshape(n * 2 * hp, -1), gate_sums, index, gains, w_output, router, answer_ready),
        (
            residual,
            upstream,
            answer_out,
            answer_kept,
            normed_one,
            query,
            key,
            value,
            mixed,
            tokens_in,
            *across,
        ),
    )
    (
        block_out,
        grad_tokens,
        grad_first,
        grad_second,
        gain_one,
        gain_two,
        grad_query,
        grad_key,
        grad_value,
        grad_output,
        grad_router,
        clipped_query,
        clipped_key,
        head_max,
    ) = run_results(
        n,
        threshold,
        weight_grads,
        small,
        gain_rows,
        top,
        *across[:2],
        (block_out, grad_tokens, grad_first, grad_second),
    )
    return (
        block_out,
        grad_tokens,
        gain_one,
        gain_two,
        grad_query,
        grad_key,
        grad_value,
        grad_output,
        grad_router.T,
        grad_first[None],
        grad_second[None],
        clipped_query.T,
        clipped_key.T,
        head_max,
    )


def solution(mesh):
    in_specs = (
        P("dp", None),
        P(),
        P(None, "tensor"),
        P(None, "tensor"),
        P(None, "tensor"),
        P("tensor", None),
        P(),
        P(),
        P("dp", None, "tensor"),
        P("dp", "tensor", None),
        P("dp", None),
        P("dp", None),
        P(),
        P("tensor"),
        P("dp", None),
    )
    out_specs = (
        P("dp", None),
        P("dp", None),
        P("dp"),
        P("dp"),
        P("dp", "tensor"),
        P("dp", "tensor"),
        P("dp", "tensor"),
        P("tensor", "dp"),
        P("dp", None),
        P("dp", None, "tensor"),
        P("dp", "tensor", None),
        P(None, "tensor"),
        P(None, "tensor"),
        P("tensor"),
    )
    return jax.shard_map(body, mesh=mesh, in_specs=in_specs, out_specs=out_specs, check_vma=False)
```

```python
import functools
import math

import jax
import jax.numpy as jnp
from jax import lax
from jax.experimental import pallas as pl
from jax.experimental.pallas import tpu as pltpu
from jax.sharding import PartitionSpec as P

HD = 64
SEQ = 197
PIECE = 208
SENT = slice(0, 200)
TOK_DEV = 1182
EPSILON = 1e-06
MESH = pl.DeviceIdType.MESH
VMEM_LIMIT = 60 * 2**20
SLOTS = 3
LAG = 4
VMEM = pltpu.VMEM
LOW, FULL = jnp.bfloat16, jnp.float32


def dot_plain(a, b):
    return jnp.dot(a, b, preferred_element_type=FULL)


def dot_last(a, b):
    return lax.dot_general(a, b, (((1,), (1,)), ((), ())), preferred_element_type=FULL)


def dot_first(a, b):
    return lax.dot_general(a, b, (((0,), (0,)), ((), ())), preferred_element_type=FULL)


def normalized(rows):
    centered = rows - jnp.mean(rows, axis=-1, keepdims=True)
    factor = lax.rsqrt(jnp.mean(centered * centered, axis=-1, keepdims=True) + EPSILON)
    return centered * factor, factor


def normalized_back(u, unit, factor):
    first = jnp.mean(u, axis=-1, keepdims=True)
    second = jnp.mean(u * unit, axis=-1, keepdims=True)
    return factor * (u - first - unit * second)


def same_index(size):
    rows = lax.broadcasted_iota(jnp.int32, (size, size), 0)
    return rows == lax.broadcasted_iota(jnp.int32, (size, size), 1)


def row_to_column(row):
    return jnp.sum(jnp.where(same_index(row.shape[1]), row, 0.0), axis=1, keepdims=True)


def column_to_row(column):
    return jnp.sum(jnp.where(same_index(column.shape[0]), column, 0.0), axis=0, keepdims=True)


def attention_probs(queries, keys):
    scores = dot_last(queries, keys) * HD**-0.5
    real = lax.broadcasted_iota(jnp.int32, scores.shape, 1) < SEQ
    scores = jnp.where(real, scores, -1e30)
    top = jnp.max(scores, axis=1, keepdims=True)
    powers = jnp.exp(scores - top)
    return powers * (1.0 / jnp.sum(powers, axis=1, keepdims=True)), top


def partner(dp, k, n):
    other, weight = 0, 1
    while weight < n:
        other = other + ((dp // weight + k // weight) % 2) * weight
        weight *= 2
    return other


def places():
    dp = lax.axis_index("dp")
    t = lax.axis_index("tensor")
    return dp, t, t % 2, t // 2, t + 1 - 2 * (t % 2), (t + 2) % 4


def remote(src, dst, sends, recvs, device):
    return pltpu.make_async_remote_copy(
        src_ref=src,
        dst_ref=dst,
        send_sem=sends,
        recv_sem=recvs,
        device_id=device,
        device_id_type=MESH,
    )


def signal(sem, device):
    pl.semaphore_signal(sem, inc=1, device_id=device, device_id_type=MESH)


def greet(n, dp, t, others):
    barrier = pltpu.get_barrier_semaphore()

    def one(k, carry):
        signal(barrier, (partner(dp, k, n), t))
        return carry

    lax.fori_loop(1, n, one, 0)
    for other in others:
        signal(barrier, (dp, other))


def await_greetings(n, others):
    pl.semaphore_wait(pltpu.get_barrier_semaphore(), n - 1 + len(others))


def image_rows(image):
    return pl.ds(pl.multiple_of(image * PIECE, PIECE), PIECE)


def dma(*shape):
    return pltpu.SemaphoreType.DMA(shape)


def near_count(n):
    return min(4, n)


class Spread:
    def __init__(self, n, hp, place, near_out, far_out, arrived, zs, zr, xs, xr, cs, cr, own):
        self.n, self.hp, self.near = n, hp, near_count(n)
        self.place, self.near_out, self.far_out, self.arrived = place, near_out, far_out, arrived
        self.zs, self.zr, self.xs, self.xr, self.cs, self.cr, self.own = zs, zr, xs, xr, cs, cr, own
        self.dp, self.t, self.half, self.side, self.mate, self.far = places()
        self.width = far_out.shape[2]

    def rows(self, owner):
        return pl.ds(pl.multiple_of(owner * self.hp, self.hp), self.hp)

    def columns(self, owner):
        return pl.ds(pl.multiple_of(owner * self.width, self.width), self.width)

    def peer(self, k):
        return (partner(self.dp, k, self.n), self.t)

    def own_copy(self):
        return pltpu.make_async_copy(
            self.near_out.at[0], self.arrived.at[0, self.rows(self.half)], self.own
        )

    def near_copy(self, k):
        return remote(
            self.near_out.at[k],
            self.arrived.at[k, self.rows(self.half)],
            self.zs.at[k],
            self.zr.at[k],
            self.peer(k),
        )

    def far_copy(self, k):
        return remote(
            self.far_out.at[k - self.near],
            self.arrived.at[k, self.rows(self.half), self.columns(self.side)],
            self.zs.at[k],
            self.zr.at[k],
            self.peer(k),
        )

    def side_copy(self, k, side):
        part = self.arrived.at[k, self.rows(self.half), self.columns(side)]
        return remote(part, part, self.xs.at[k], self.xr.at[k], (self.dp, self.far))

    def pair_copy(self, k, half):
        part = self.arrived.at[k, self.rows(half)]
        return remote(part, part, self.cs.at[k], self.cr.at[k], (self.dp, self.mate))

    def hot(self, k, row_count):
        slots = lax.broadcasted_iota(jnp.int32, (self.hp, row_count), 0) + k * self.hp
        is_first = self.place[0:1, :] == slots
        is_second = self.place[1:2, :] == slots
        return is_first, is_second

    def send(self, k, rows_ref):
        is_first, is_second = self.hot(k, rows_ref.shape[0])
        hot = jnp.where(is_first | is_second, 1.0, 0.0).astype(LOW)

        @pl.when(k < self.near)
        def _():
            self.near_out[k] = dot_plain(hot, rows_ref[...]).astype(LOW)

            @pl.when(k == 0)
            def _():
                self.own_copy().start()

            @pl.when(k > 0)
            def _():
                self.near_copy(k).start()

        @pl.when(k >= self.near)
        def _():
            mine = rows_ref[:, self.columns(self.side)]
            self.far_out[k - self.near] = dot_plain(hot, mine).astype(LOW)
            self.far_copy(k).start()

        return is_first, is_second

    def first_hop(self, k):
        @pl.when(k == 0)
        def _():
            self.own_copy().wait()

        @pl.when((k > 0) & (k < self.near))
        def _():
            self.near_copy(k).wait_recv()

        @pl.when(k >= self.near)
        def _():
            self.far_copy(k).wait_recv()
            self.side_copy(k, self.side).start()

    def second_hop(self, k):
        @pl.when(k >= self.near)
        def _():
            self.side_copy(k, 1 - self.side).wait_recv()

        self.pair_copy(k, self.half).start()

    def last_hop(self, k):
        self.pair_copy(k, 1 - self.half).wait_recv()

    def sent(self, k):
        @pl.when((k > 0) & (k < self.near))
        def _():
            self.near_copy(k).wait_send()

        @pl.when(k >= self.near)
        def _():
            self.far_copy(k).wait_send()
            self.side_copy(k, self.side).wait_send()

        self.pair_copy(k, self.half).wait_send()

    @staticmethod
    def scratch(n, hp, width):
        near = near_count(n)
        return [VMEM((near, hp, 2 * width), LOW), VMEM((n - near, hp, width), LOW)]

    @staticmethod
    def semaphores(n):
        return [dma(n), dma(n), dma(n), dma(n), dma(n), dma(n), pltpu.SemaphoreType.DMA]


def clear_unsent(rows_in):
    count, rows, width = rows_in.shape
    rows_in[:, SENT.stop :, :] = jnp.zeros((count, rows - SENT.stop, width), rows_in.dtype)


class Total:
    def __init__(self, part_out, pair_in, far_out, far_in, ps, pr, fs, fr):
        self.part_out, self.pair_in, self.far_out, self.far_in = part_out, pair_in, far_out, far_in
        self.ps, self.pr, self.fs, self.fr = ps, pr, fs, fr
        self.dp, _, _, _, self.mate, self.far = places()
        clear_unsent(far_in)

    def pair_copy(self, j):
        return remote(
            self.part_out.at[j], self.pair_in.at[j], self.ps.at[j], self.pr.at[j], (self.dp, self.mate)
        )

    def far_copy(self, j):
        return remote(
            self.far_out.at[j, SENT],
            self.far_in.at[j, SENT],
            self.fs.at[j],
            self.fr.at[j],
            (self.dp, self.far),
        )

    def give(self, j, rows):
        self.part_out[j] = rows
        self.pair_copy(j).start()

    def take(self, j, rows):
        self.pair_copy(j).wait_recv()
        self.far_out[j] = (rows + self.pair_in[j]).astype(LOW)
        self.far_copy(j).start()

    def result(self, j):
        self.far_copy(j).wait_recv()
        return self.far_out[j].astype(FULL) + self.far_in[j].astype(FULL)

    def sent(self, j):
        self.pair_copy(j).wait_send()
        self.far_copy(j).wait_send()

    @staticmethod
    def scratch(model):
        wide, slim = VMEM((3, PIECE, model), FULL), VMEM((3, PIECE, model), LOW)
        return [wide, wide, slim, slim, dma(3), dma(3), dma(3), dma(3)]


def padded_image(rows_ref, image):
    start = image * SEQ // 8 * 8
    length = min(PIECE, rows_ref.shape[0] - start)
    rows = lax.broadcasted_iota(jnp.int32, (PIECE, length), 0)
    columns = lax.broadcasted_iota(jnp.int32, (PIECE, length), 1)
    pick = (columns == rows + (image * SEQ - start)) & (rows < SEQ)
    return dot_plain(jnp.where(pick, 1.0, 0.0).astype(LOW), rows_ref[start : start + length, :])


def front_kernel(
    n,
    hp,
    per_half,
    capacity_ref,
    routes_ref,
    slot_ids_ref,
    tokens_ref,
    upstream_ref,
    gains_ref,
    query_w_ref,
    key_w_ref,
    value_w_ref,
    output_w_ref,
    place_ref,
    index_ref,
    peak_ref,
    *refs,
):
    outs, spread_hbm, scratch = refs[:9], refs[9], refs[10:]
    held, scratch = scratch[:9], scratch[9:]
    (
        tokens,
        upstream,
        normed_one,
        query,
        key,
        value,
        mixed_rows,
        residual_rows,
        normed_two,
    ) = held
    near_out, far_out, zs, zr, own, ns, nr, hs, xs, xr = scratch[:10]
    total = Total(*scratch[10:])
    dp, t, half, side, mate, far = places()
    heads = query_w_ref.shape[0] // HD
    near = near_count(n)
    width = far_out.shape[2]
    row_count = tokens.shape[0]
    greet(n, dp, t, (mate, far))
    peak_ref[...] = jnp.full(peak_ref.shape, -1e30, FULL)
    for image in range(row_count // PIECE):
        tokens[image * PIECE : (image + 1) * PIECE, :] = padded_image(tokens_ref, image).astype(LOW)

    def image_forward(image):
        rows = image_rows(image)
        unit, _ = normalized(tokens[rows, :].astype(FULL))
        normed = (unit * gains_ref[0:1, :]).astype(LOW)
        normed_one[rows, :] = normed
        queries = dot_last(normed, query_w_ref[...]).astype(LOW)
        keys = dot_last(normed, key_w_ref[...]).astype(LOW)
        values = dot_last(normed, value_w_ref[...]).astype(LOW)
        query[rows, :] = queries
        key[rows, :] = keys
        value[rows, :] = values
        mixed = []
        for h in range(heads):
            cols = slice(h * HD, (h + 1) * HD)
            probs, top = attention_probs(queries[:, cols], keys[:, cols])
            real = lax.broadcasted_iota(jnp.int32, top.shape, 0) < SEQ
            best = jnp.max(jnp.where(real, top, -1e30), axis=0, keepdims=True)
            peak_ref[h : h + 1, :] = jnp.maximum(peak_ref[h : h + 1, :], best)
            mixed.append(dot_plain(probs.astype(LOW), values[:, cols]))
        mixed = jnp.concatenate(mixed, axis=1).astype(LOW)
        mixed_rows[rows, :] = mixed
        return dot_plain(mixed, output_w_ref[...])

    def normed_copy(j, owner):
        rows = normed_two.at[image_rows(2 * j + owner)]
        return remote(rows, rows, ns.at[j], nr.at[j], (dp, mate))

    def keep(i):
        return pltpu.make_async_copy(held[i], outs[i], hs.at[i])

    def finish(j):
        rows = image_rows(2 * j + half)
        residual = tokens[rows, :].astype(FULL) + total.result(j)
        residual_rows[j] = residual
        unit, _ = normalized(residual)
        normed_two[rows, :] = (unit * gains_ref[1:2, :]).astype(LOW)
        normed_copy(j, half).start()

    def peer(k):
        return (partner(dp, k, n), t)

    def half_rows():
        return pl.ds(pl.multiple_of(half * hp, hp), hp)

    def side_columns():
        return pl.ds(pl.multiple_of(side * width, width), width)

    def own_copy():
        return pltpu.make_async_copy(near_out.at[0], spread_hbm.at[0, half_rows()], own)

    def near_copy(k):
        return remote(near_out.at[k], spread_hbm.at[k, half_rows()], zs.at[k], zr.at[k], peer(k))

    def far_copy(k):
        return remote(
            far_out.at[k - near],
            spread_hbm.at[k, half_rows(), side_columns()],
            zs.at[k],
            zr.at[k],
            peer(k),
        )

    def side_copy(k, owner):
        columns = pl.ds(pl.multiple_of(owner * width, width), width)
        part = spread_hbm.at[k, half_rows(), columns]
        return remote(part, part, xs.at[k], xr.at[k], (dp, far))

    def forward(k, carry):
        far_copy(k).wait_recv()
        side_copy(k, side).start()
        return carry

    def dispatch(k):
        slots = lax.broadcasted_iota(jnp.int32, (hp, row_count), 0) + k * hp
        hot = (place_ref[0:1, :] == slots) | (place_ref[1:2, :] == slots)
        hot = jnp.where(hot, 1.0, 0.0).astype(LOW)

        @pl.when(k < near)
        def _():
            near_out[k] = dot_plain(hot, upstream[...]).astype(LOW)

            @pl.when(k == 0)
            def _():
                own_copy().start()

            @pl.when(k > 0)
            def _():
                near_copy(k).start()

        @pl.when(k >= near)
        def _():
            far_out[k - near] = dot_plain(hot, upstream[:, side_columns()]).astype(LOW)
            far_copy(k).start()

    def places_of_pairs():
        routes, slot_ids = routes_ref[...], slot_ids_ref[...]
        limits = jnp.zeros_like(routes)
        for e in range(n):
            limits = jnp.where(routes == e, capacity_ref[e], limits)
        kept = slot_ids < limits
        step = jnp.zeros_like(routes)
        weight = 1
        while weight < n:
            step = step + (routes // weight + dp // weight) % 2 * weight
            weight *= 2
        upper = slot_ids >= per_half
        in_half = slot_ids - jnp.where(upper, per_half, 0)
        in_block = in_half + jnp.where(upper, hp, 0)
        mine = kept & (upper == (half == 1))
        place = jnp.where(mine, step * hp + in_half, -1)
        position = jnp.where(kept, step * (2 * hp) + in_block, -1)
        both = jnp.concatenate([place, position, routes, jnp.full_like(routes, -1)], axis=0)
        fill = jnp.full((8, PIECE - SEQ), -1, jnp.int32)
        spaced = []
        for image in range(row_count // PIECE):
            spaced += [both[:, image * SEQ : (image + 1) * SEQ], fill]
        return jnp.concatenate(spaced, axis=1)

    pairs = places_of_pairs()
    place_ref[...] = pairs
    index_ref[...] = pairs.T
    def step(j, carry):
        given = image_forward(2 * j + 1 - half)

        @pl.when(j == 0)
        def _():
            await_greetings(n, (mate, far))

        total.give(j, given)
        total.take(j, image_forward(2 * j + half))

        @pl.when(j == 0)
        def _():
            for image in range(row_count // PIECE):
                upstream[image * PIECE : (image + 1) * PIECE, :] = padded_image(
                    upstream_ref, image
                ).astype(LOW)

        def turn(k, inner):
            dispatch(k)
            return inner

        @pl.when(j == 0)
        def _():
            lax.fori_loop(near, n, turn, 0)

        @pl.when(j == 1)
        def _():
            lax.fori_loop(0, near, turn, 0)

        @pl.when(j >= 1)
        def _():
            finish(j - 1)

        return carry

    lax.fori_loop(0, 3, step, 0)
    for i in range(7):
        keep(i).start()
    early = n - (n - near) // 4
    lax.fori_loop(near, early, forward, 0)
    finish(2)
    lax.fori_loop(early, n, forward, 0)
    keep(7).start()
    own_copy().wait()

    def arrive(k, carry):
        near_copy(k).wait()
        return carry

    def far_arrive(k, carry):
        far_copy(k).wait_send()
        side_copy(k, side).wait_send()
        side_copy(k, 1 - side).wait_recv()
        return carry

    for j in range(3):
        normed_copy(j, 1 - half).wait_recv()
    keep(8).start()
    lax.fori_loop(1, near, arrive, 0)
    lax.fori_loop(near, n, far_arrive, 0)
    for j in range(3):
        total.sent(j)
        normed_copy(j, half).wait_send()
    for i in range(9):
        keep(i).wait()


def run_front(n, hp, per_half, capacity, routes, slot_ids, tokens, upstream, gains, weights):
    model = tokens.shape[1]
    rows = tokens.shape[0] // SEQ * PIECE
    heads_width = weights[0].shape[0]
    near = near_count(n)
    width = model // 2
    vmem = pl.BlockSpec(memory_space=VMEM)
    hbm = pl.BlockSpec(memory_space=pl.ANY)
    shape = jax.ShapeDtypeStruct
    slim, wide = shape((rows, heads_width), LOW), shape((rows, model), LOW)
    held = (wide, wide, wide, slim, slim, slim, slim, shape((3, PIECE, model), FULL), wide)
    return pl.pallas_call(
        functools.partial(front_kernel, n, hp, per_half),
        out_shape=(
            shape((8, rows), jnp.int32),
            shape((rows, 8), jnp.int32),
            shape((8, 128), FULL),
            *held,
            shape((n, 2 * hp, model), LOW),
        ),
        in_specs=[pl.BlockSpec(memory_space=pltpu.SMEM)] + [vmem] * 9,
        out_specs=[vmem] * 3 + [hbm] * 10,
        scratch_shapes=[
            *[VMEM(a.shape, a.dtype) for a in held],
            VMEM((near, hp, model), LOW),
            VMEM((n - near, hp, width), LOW),
            dma(n),
            dma(n),
            pltpu.SemaphoreType.DMA,
            dma(3),
            dma(3),
            dma(9),
            dma(n),
            dma(n),
            *Total.scratch(model),
        ],
        compiler_params=pltpu.CompilerParams(
            collective_id=0, has_side_effects=True, vmem_limit_bytes=VMEM_LIMIT
        ),
        name="front",
    )(capacity, routes, slot_ids, tokens, upstream, gains, *weights)


def in_turn(i, near):
    return jnp.where(i < 2 * near, i // 2 + (i % 2) * near, i)


def expert_kernel(
    n,
    hp,
    place_ref,
    router_ref,
    peak_ref,
    normed_hbm,
    first_hbm,
    second_hbm,
    upstream_hbm,
    back_ref,
    gate_sum_ref,
    top_ref,
    answer_out_hbm,
    answer_kept_hbm,
    answer_ready_hbm,
    grad_first_hbm,
    grad_second_hbm,
    *scratch,
):
    dp, t, half, side, mate, far = places()
    arrived = scratch[2]
    spread = Spread(n, hp, place_ref, *scratch[:10])
    (
        normed_ref,
        first_ref,
        second_ref,
        answer_out,
        answer_kept,
        grad_first_ref,
        grad_second_ref,
        os_,
        ws,
        cs,
        cr,
        answer_far,
        answer_ready,
        xs,
        xr,
    ) = scratch[44:]
    (
        upstream,
        hidden_all,
        pre_grad_all,
        parts,
        pair_in,
        kept,
        far_out,
        far_in,
        final,
        gate_out,
        gate_in,
        sum_out,
        sum_in,
        sums,
        peaks,
        us,
        ps,
        pr,
        fs,
        fr,
        rs,
        rr,
        ms,
        mr,
        gs,
        gr,
        hs,
        hr,
        ks,
        kr,
        qs,
        qr,
        ss,
        sr,
    ) = scratch[10:44]
    model = normed_ref.shape[1]
    width = model // 2
    near = spread.near
    greet(n, dp, t, [(t + d) % 4 for d in (1, 2, 3)])
    fetches = [
        pltpu.make_async_copy(a, b, ws.at[i])
        for i, (a, b) in enumerate(
            ((normed_hbm, normed_ref), (first_hbm, first_ref), (second_hbm, second_ref))
        )
    ]
    mine = (slice(0, n), spread.rows(half))
    fetches.append(pltpu.make_async_copy(upstream_hbm.at[mine], upstream.at[mine], us.at[0]))
    for fetch in fetches:
        fetch.start()

    def upstream_pair_copy(k, owner):
        part = upstream.at[k, spread.rows(owner)]
        return remote(part, part, cs.at[k], cr.at[k], (dp, mate))

    def answer_side_copy(k):
        return remote(
            answer_out.at[k], answer_far.at[k - near], xs.at[k], xr.at[k], (dp, far)
        )

    def keep(i):
        pairs = (
            (answer_out.at[slice(0, near)], answer_out_hbm),
            (answer_kept.at[slice(0, near)], answer_kept_hbm),
            (answer_ready, answer_ready_hbm),
        )
        return pltpu.make_async_copy(*pairs[i], os_.at[i])

    def gate_copy(k):
        return remote(gate_out.at[k], gate_in.at[k, half], gs.at[k], gr.at[k], spread.peer(k))

    def gate_pair_copy(k, owner):
        tile = gate_in.at[k, owner]
        return remote(tile, tile, hs.at[k], hr.at[k], (dp, mate))

    def part_copy(i, k):
        return remote(
            parts.at[i % 3, :, spread.rows(1 - half)],
            pair_in.at[k],
            ps.at[i % 3],
            pr.at[k],
            (dp, mate),
        )

    def far_copy(i, k):
        return remote(far_out.at[i % SLOTS], far_in.at[k], fs.at[i % SLOTS], fr.at[k], (dp, far))

    def return_copy(k):
        return remote(
            final.at[k], back_ref.at[k, spread.rows(half)], rs.at[k], rr.at[k], spread.peer(k)
        )

    def mate_copy(k, owner):
        rows = back_ref.at[k, spread.rows(owner)]
        return remote(rows, rows, ms.at[k], mr.at[k], (dp, mate))

    def sum_copy(k):
        return remote(sum_out.at[k], sum_in.at[k], ks.at[k], kr.at[k], spread.peer(k))

    def peak_copy(k):
        return remote(peak_ref, peaks.at[k], qs.at[k], qr.at[k], spread.peer(k))

    def share_copy(d, owner):
        return remote(
            sums.at[owner], sums.at[owner], ss.at[d - 1], sr.at[d - 1], (dp, (t + d) % 4)
        )

    def loop(body, first=0, last=n):
        def one(k, carry):
            body(k)
            return carry

        lax.fori_loop(first, last, one, 0)

    fetches[0].wait()
    logits = dot_last(router_ref[...], normed_ref[...])
    rows_of = lax.broadcasted_iota(jnp.int32, logits.shape, 0)
    one, two = (
        jnp.sum(jnp.where(rows_of == place_ref[r : r + 1, :], logits, 0.0), axis=0, keepdims=True)
        for r in (4, 5)
    )
    best = jnp.maximum(one, two)
    one, two = jnp.exp(one - best), jnp.exp(two - best)
    gate_one, gate_two = one / (one + two), two / (one + two)
    await_greetings(n, (1, 2, 3))

    def dispatch(i):
        k = in_turn((i + 1) % n, near)
        is_first, is_second = spread.send(k, normed_ref)
        gate = jnp.sum(
            jnp.where(is_first, gate_one, 0.0) + jnp.where(is_second, gate_two, 0.0),
            axis=1,
            keepdims=True,
        )
        tile = jnp.broadcast_to(column_to_row(gate), (8, hp))

        @pl.when(k == 0)
        def _():
            gate_in[0, half] = tile

        @pl.when(k > 0)
        def _():
            gate_out[k] = tile
            gate_copy(k).start()

    loop(dispatch)
    for fetch in fetches[1:]:
        fetch.wait()
    loop(lambda i: upstream_pair_copy(in_turn(i, near), half).start())

    def chunk(i, k):
        gate = jnp.concatenate(
            [row_to_column(gate_in[k, 0, 0:1, :]), row_to_column(gate_in[k, 1, 0:1, :])], axis=0
        )
        gradient = upstream[k].astype(FULL)
        answer_grad = (gradient * gate).astype(LOW)
        pre = dot_plain(arrived[k], first_ref[...])
        share = 0.5 * (1.0 + lax.erf(pre * math.sqrt(0.5)))
        slope = share + pre * (jnp.exp(-0.5 * pre * pre) * (1.0 / math.sqrt(2.0 * math.pi)))
        hidden = (pre * share).astype(LOW)
        hidden_all[k] = hidden
        answer = dot_plain(hidden, second_ref[...])
        parts[i % 3, 0] = answer.astype(LOW)
        gate_sum = jnp.sum(answer * gradient, axis=1, keepdims=True)
        upstream[k] = answer_grad
        pre_grad = (dot_last(answer_grad, second_ref[...]) * slope).astype(LOW)
        pre_grad_all[k] = pre_grad
        parts[i % 3, 1] = dot_last(pre_grad, first_ref[...]).astype(LOW)
        tile = jnp.broadcast_to(column_to_row(gate_sum), (8, 2 * hp))

        @pl.when(k == 0)
        def _():
            sum_in[0] = tile

        @pl.when(k > 0)
        def _():
            sum_out[k] = tile
            sum_copy(k).start()
            peak_copy(k).start()

    tile = 256
    tiles = model // tile

    def grad_copy(m, j):
        cols = pl.ds(pl.multiple_of(m * tile, tile), tile)
        ref, hbm = ((grad_first_ref, grad_first_hbm), (grad_second_ref, grad_second_hbm))[j]
        return pltpu.make_async_copy(ref.at[cols], hbm.at[cols], os_.at[3 + 2 * m + j])

    def grads(m):
        cols = pl.ds(pl.multiple_of(m * tile, tile), tile)
        rows_in = arrived[:, :, cols].reshape(n * 2 * hp, tile)
        grad_first_ref[cols, :] = dot_first(rows_in, pre_grad_all[...].reshape(n * 2 * hp, -1))
        grad_copy(m, 0).start()
        hidden = hidden_all[:, :, cols].reshape(n * 2 * hp, tile)
        grad_second_ref[cols, :] = dot_first(hidden, upstream[...].reshape(n * 2 * hp, model))
        grad_copy(m, 1).start()

    def step(i):
        @pl.when(i < n)
        def _():
            spread.first_hop(in_turn(i, near))

        @pl.when((i >= 1) & (i < n + 1))
        def _():
            k = in_turn(i - 1, near)
            spread.second_hop(k)

            @pl.when(k > 0)
            def _():
                gate_copy(k).wait_recv()

            gate_pair_copy(k, half).start()

        @pl.when((i >= 2) & (i < n + 2))
        def _():
            k = in_turn(i - 2, near)
            spread.last_hop(k)
            gate_pair_copy(k, 1 - half).wait_recv()
            upstream_pair_copy(k, 1 - half).wait_recv()
            upstream_pair_copy(k, half).wait_send()

            @pl.when(i >= 5)
            def _():
                part_copy(i - 5, in_turn(i - 5, near)).wait_send()

            chunk(i - 2, k)
            part_copy(i - 2, k).start()

        @pl.when((i >= 3) & (i < n + 3))
        def _():
            k = in_turn(i - 3, near)
            part_copy(i - 3, k).wait_recv()

            @pl.when(i >= 3 + SLOTS)
            def _():
                far_copy(i - 3 - SLOTS, in_turn(i - 3 - SLOTS, near)).wait_send()

            for j in (1, 0):
                whole = parts[(i - 3) % 3, j, spread.rows(half), :].astype(FULL) + pair_in[k, j].astype(FULL)
                low, high = whole[:, :width], whole[:, width:]
                stays = jnp.where(side == 0, low, high)
                goes = jnp.where(side == 0, high, low).astype(LOW)
                if j:
                    kept[(i - 3) % SLOTS] = stays
                    far_out[(i - 3) % SLOTS] = goes
                    far_copy(i - 3, k).start()
                else:
                    answer_kept[k] = stays
                    answer_out[k] = goes

        @pl.when((i >= LAG) & (i < n + LAG))
        def _():
            k = in_turn(i - LAG, near)
            far_copy(i - LAG, k).wait_recv()
            rows = (kept[(i - LAG) % SLOTS] + far_in[k].astype(FULL)).astype(LOW)

            @pl.when(k == 0)
            def _():
                back_ref[0, spread.rows(half), :] = rows

            @pl.when(k > 0)
            def _():
                final[k] = rows
                return_copy(k).start()

        @pl.when(i == n + 2)
        def _():
            loop(lambda k: answer_side_copy(k).start(), near)

        @pl.when((i >= n + 2) & (i < n + 2 + tiles))
        def _():
            grads(i - (n + 2))

    loop(step, 0, n + max(LAG, 2 + tiles))
    keep(0).start()
    keep(1).start()
    peaks[0] = peak_ref[...]

    def collect_sums(k):
        @pl.when(k > 0)
        def _():
            peak_copy(k).wait_recv()
            sum_copy(k).wait_recv()

        sums[t, pl.ds(k, 1), :] = sum_in[k, 0:1, :]

    loop(collect_sums)
    for d in (1, 2, 3):
        share_copy(d, t).start()
    top_ref[...] = jnp.max(peaks[...], axis=0)

    def collect(i):
        k = in_turn(i, near)

        @pl.when(k > 0)
        def _():
            return_copy(k).wait_recv()

        mate_copy(k, half).start()

    loop(collect)

    def answers_whole(k):
        answer_side_copy(k).wait_recv()
        answer_ready[k - near] = (answer_kept[k] + answer_far[k - near].astype(FULL)).astype(LOW)

    loop(answers_whole, near)
    keep(2).start()
    for d in (1, 2, 3):
        share_copy(d, (t + 4 - d) % 4).wait_recv()
    whole = (sums[0] + sums[1]) + (sums[2] + sums[3])
    whole = jnp.concatenate([whole[k : k + 1] for k in range(n)], axis=1)
    gate_sum_ref[...] = jnp.broadcast_to(whole, gate_sum_ref.shape)

    def finish(i):
        k = in_turn(i, near)
        mate_copy(k, 1 - half).wait_recv()
        mate_copy(k, half).wait_send()
        spread.sent(k)
        gate_pair_copy(k, half).wait_send()

        @pl.when(k > 0)
        def _():
            return_copy(k).wait_send()
            gate_copy(k).wait_send()
            sum_copy(k).wait_send()
            peak_copy(k).wait_send()

        @pl.when(i >= n - 3)
        def _():
            part_copy(i, k).wait_send()

        @pl.when(i >= n - SLOTS)
        def _():
            far_copy(i, k).wait_send()

    loop(finish)
    for d in (1, 2, 3):
        share_copy(d, t).wait_send()
    loop(lambda k: answer_side_copy(k).wait_send(), near)
    for i in range(3):
        keep(i).wait()
    for m in range(tiles):
        grad_copy(m, 0).wait()
        grad_copy(m, 1).wait()


def run_experts(n, hp, place, router, peak, normed, first, second, upstream):
    model = normed.shape[1]
    width = model // 2
    hidden = first.shape[1]
    near = near_count(n)
    vmem = pl.BlockSpec(memory_space=VMEM)
    hbm = pl.BlockSpec(memory_space=pl.ANY)
    shape = jax.ShapeDtypeStruct
    return pl.pallas_call(
        functools.partial(expert_kernel, n, hp),
        out_shape=(
            shape((n, 2 * hp, width), LOW),
            shape((8, n * 2 * hp), FULL),
            shape(peak.shape, FULL),
            shape((near, hp, width), LOW),
            shape((near, hp, width), FULL),
            shape((n - near, hp, width), LOW),
            shape((model, hidden), FULL),
            shape((hidden, model), FULL),
        ),
        in_specs=[vmem] * 3 + [hbm] * 4,
        out_specs=[vmem] * 3 + [hbm] * 5,
        scratch_shapes=[
            *Spread.scratch(n, hp, width),
            VMEM((n, 2 * hp, model), LOW),
            *Spread.semaphores(n),
            VMEM((n, 2 * hp, model), LOW),
            VMEM((n, 2 * hp, hidden), LOW),
            VMEM((n, 2 * hp, hidden), LOW),
            VMEM((3, 2, 2 * hp, model), LOW),
            VMEM((n, 2, hp, model), LOW),
            VMEM((SLOTS, hp, width), FULL),
            VMEM((SLOTS, hp, width), LOW),
            VMEM((n, hp, width), LOW),
            VMEM((n, hp, width), LOW),
            VMEM((n, 8, hp), FULL),
            VMEM((n, 2, 8, hp), FULL),
            VMEM((n, 8, 2 * hp), FULL),
            VMEM((n, 8, 2 * hp), FULL),
            VMEM((4, n, 2 * hp), FULL),
            VMEM((n, *peak.shape), FULL),
            dma(1),
            dma(3), dma(n), dma(SLOTS), dma(n), dma(n), dma(n), dma(n), dma(n),
            dma(n), dma(n), dma(n), dma(n), dma(n), dma(n), dma(n), dma(n), dma(3), dma(3),
            VMEM(normed.shape, LOW),
            VMEM(first.shape, LOW),
            VMEM(second.shape, LOW),
            VMEM((n, hp, width), LOW),
            VMEM((n, hp, width), FULL),
            VMEM((model, hidden), FULL),
            VMEM((hidden, model), FULL),
            dma(3 + 2 * (model // 256)),
            dma(3), dma(n), dma(n),
            VMEM((n - near, hp, width), LOW),
            VMEM((n - near, hp, width), LOW),
            dma(n), dma(n),
        ],
        compiler_params=pltpu.CompilerParams(
            collective_id=1, has_side_effects=True, vmem_limit_bytes=VMEM_LIMIT
        ),
        name="experts",
    )(place, router, peak, normed, first, second, upstream)


def unpad(rows_ref, out_ref):
    for image in range(rows_ref.shape[0] // PIECE):
        start = image * SEQ // 8 * 8
        length = min(PIECE, out_ref.shape[0] - start)
        shift = image * SEQ - start
        rows = lax.broadcasted_iota(jnp.int32, (length, PIECE), 0)
        columns = lax.broadcasted_iota(jnp.int32, (length, PIECE), 1)
        pick = (rows == columns + shift) & (columns < SEQ)
        image_part = rows_ref[image * PIECE : (image + 1) * PIECE, :]
        moved = dot_plain(jnp.where(pick, 1.0, 0.0).astype(LOW), image_part).astype(LOW)
        if shift:
            before = lax.broadcasted_iota(jnp.int32, (8, moved.shape[1]), 0) < shift
            first = jnp.where(before, out_ref[start : start + 8, :].astype(FULL), moved[:8].astype(FULL))
            out_ref[start : start + 8, :] = first.astype(LOW)
            out_ref[start + 8 : start + length, :] = moved[8:]
        else:
            out_ref[start : start + length, :] = moved


def back_kernel(
    n,
    hp,
    gate_sum_ref,
    index_ref,
    gains_ref,
    output_w_ref,
    router_ref,
    answer_ready,
    *refs,
):
    later, outs, scratch = refs[:14], refs[14:19], refs[19:]
    block_out_ref, tokens_out_ref, weights_ref, small_ref, gain_ref = outs
    held, scratch = scratch[:14], scratch[14:]
    (
        back_ref,
        residual_ref,
        upstream_ref,
        answer_out,
        answer_kept,
        normed_one_ref,
        query_ref,
        key_ref,
        value_ref,
        mixed_ref,
        tokens_ref,
        query_w_ref,
        key_w_ref,
        value_w_ref,
    ) = held
    dp, t, half, side, mate, far = places()
    (
        moe_mine,
        moe_other,
        block_mine,
        block_other,
        attention_grad,
        residual_grad,
        query_grad,
        key_grad,
        value_grad,
        gain_two_sum,
        gain_two_in,
        gain_one_sum,
        gain_one_all,
        gain_rows,
        router_sum,
        router_in,
        totals,
        totals_two,
        pieces,
        pieces_in,
        small_pieces,
        small_in,
        answer_far,
        answer_final,
        answers,
        block_ref,
        grad_tokens_ref,
        hs,
        as_,
        ar,
        bs,
        br,
        ts,
        tr,
        cs,
        cr,
        gs,
        gr,
        ws,
        wr,
        ls,
        lr,
        os_,
        or_,
        vs,
        vr,
        ds,
        dr,
        es,
        er,
        fs,
        fr,
        ks,
        kr,
    ) = scratch[:54]
    total = Total(*scratch[54:])
    heads = query_w_ref.shape[0] // HD
    model = upstream_ref.shape[1]
    width = model // 2
    slots = back_ref.shape[0]
    piece = pieces.shape[1]
    near = near_count(n)
    greet(n, dp, t, [(t + d) % 4 for d in (1, 2, 3)])
    fetches = [pltpu.make_async_copy(a, b, hs.at[i]) for i, (a, b) in enumerate(zip(later, held))]
    for fetch in fetches:
        fetch.start()

    def peer(k):
        return (partner(dp, k, n), t)

    def moe_copy(j):
        return remote(moe_mine.at[j, SENT], moe_other.at[j, SENT], as_.at[j], ar.at[j], (dp, far))

    def block_copy(j):
        return remote(block_mine.at[j, SENT], block_other.at[j, SENT], bs.at[j], br.at[j], (dp, far))

    def attention_copy(j, owner):
        rows = attention_grad.at[image_rows(2 * j + owner)]
        return remote(rows, rows, ts.at[j], tr.at[j], (dp, mate))

    def tokens_copy(j, owner):
        rows = grad_tokens_ref.at[image_rows(2 * j + owner)]
        return remote(rows, rows, cs.at[j], cr.at[j], (dp, mate))

    def block_pair_copy(j, owner):
        rows = block_ref.at[image_rows(2 * j + owner)]
        return remote(rows, rows, ls.at[j], lr.at[j], (dp, mate))

    def gain_copy(d, owner):
        return remote(
            gain_one_all.at[owner], gain_one_all.at[owner], gs.at[d - 1], gr.at[d - 1], (dp, (t + d) % 4)
        )

    def gain_row_copy(k):
        return remote(gain_rows.at[0], gain_rows.at[k], ks.at[k], kr.at[k], peer(k))

    def router_copy():
        return remote(router_sum, router_in, os_.at[0], or_.at[0], (dp, mate))

    def gain_two_copy():
        return remote(gain_two_sum, gain_two_in, os_.at[1], or_.at[1], (dp, mate))

    def piece_copy(k):
        return remote(pieces.at[k], pieces_in.at[k], ws.at[k], wr.at[k], peer(k))

    def small_copy(k):
        return remote(small_pieces.at[k], small_in.at[k], vs.at[k], vr.at[k], peer(k))

    def answer_rows(k, owner):
        return answers.at[pl.ds(pl.multiple_of((2 * k + owner) * hp, hp), hp)]

    def answer_side_copy(k):
        return remote(answer_out.at[k], answer_far.at[k], ds.at[k], dr.at[k], (dp, far))

    def answer_copy(k):
        return remote(answer_final.at[k], answer_rows(k, half), es.at[k], er.at[k], peer(k))

    def far_answer_copy(k):
        return remote(answer_ready.at[k - near], answer_rows(k, half), es.at[k], er.at[k], peer(k))

    def answer_pair_copy(k, owner):
        return remote(answer_rows(k, owner), answer_rows(k, owner), fs.at[k], fr.at[k], (dp, mate))

    def loop(body, first=0, last=n):
        def one(k, carry):
            body(k)
            return carry

        lax.fori_loop(first, last, one, 0)

    def both_sides(mine, other):
        low = jnp.where(side == 0, mine, other)
        high = jnp.where(side == 0, other, mine)
        return jnp.concatenate([low, high], axis=1)

    def hots(rows):
        columns = lax.broadcasted_iota(jnp.int32, (PIECE, slots), 1)
        return index_ref[rows, 2:3] == columns, index_ref[rows, 3:4] == columns

    def as_low(mask):
        return jnp.where(mask, 1.0, 0.0).astype(LOW)

    clear_unsent(moe_other)
    clear_unsent(block_other)
    gain_two_sum[...] = jnp.zeros_like(gain_two_sum)
    gain_one_sum[...] = jnp.zeros_like(gain_one_sum)
    router_sum[...] = jnp.zeros_like(router_sum)

    def combine(j):
        first, second = hots(image_rows(2 * j + half))
        moe_mine[j] = dot_plain(as_low(first | second), back_ref[...]).astype(LOW)

        @pl.when(j == 0)
        def _():
            await_greetings(n, (1, 2, 3))
            loop(lambda k: far_answer_copy(k).start(), near)

        moe_copy(j).start()

    fetches[0].wait()
    loop(combine, 0, 3)
    for fetch in fetches[1:4]:
        fetch.wait()
    loop(lambda k: answer_side_copy((k + 1) % near).start(), 0, near)

    def gates_of(rows, normed):
        logits = dot_last(normed, router_ref[...])
        lanes = lax.broadcasted_iota(jnp.int32, logits.shape, 1)
        hot_one = index_ref[rows, 4:5] == lanes
        hot_two = index_ref[rows, 5:6] == lanes
        one = jnp.sum(jnp.where(hot_one, logits, 0.0), axis=1, keepdims=True)
        two = jnp.sum(jnp.where(hot_two, logits, 0.0), axis=1, keepdims=True)
        top = jnp.maximum(one, two)
        one, two = jnp.exp(one - top), jnp.exp(two - top)
        return one / (one + two), two / (one + two), hot_one, hot_two

    def moe_back(j):
        rows = image_rows(2 * j + half)
        unit, factor = normalized(residual_ref[j])
        normed = (unit * gains_ref[1:2, :]).astype(LOW)
        gate_one, gate_two, hot_one, hot_two = gates_of(rows, normed)
        first, second = hots(rows)
        slot_sums = gate_sum_ref[0:1, :]
        grad_one = jnp.sum(jnp.where(first, slot_sums, 0.0), axis=1, keepdims=True)
        grad_two = jnp.sum(jnp.where(second, slot_sums, 0.0), axis=1, keepdims=True)
        mean = gate_one * grad_one + gate_two * grad_two
        logit_grad = jnp.where(hot_one, gate_one * (grad_one - mean), 0.0)
        logit_grad = logit_grad + jnp.where(hot_two, gate_two * (grad_two - mean), 0.0)
        logit_grad = logit_grad.astype(LOW)
        router_sum[...] += dot_first(normed, logit_grad)
        normed_grad = dot_plain(logit_grad, router_ref[...])
        moe_copy(j).wait_recv()
        normed_grad = normed_grad + both_sides(moe_mine[j].astype(FULL), moe_other[j].astype(FULL))
        gain_two_sum[...] += jnp.sum((normed_grad * unit).reshape(PIECE // 8, 8, model), axis=0)
        grad = normalized_back(normed_grad * gains_ref[1:2, :], unit, factor)
        grad = grad + upstream_ref[rows, :].astype(FULL)
        residual_grad[j] = grad
        attention_grad[rows, :] = grad.astype(LOW)
        attention_copy(j, half).start()

    loop(moe_back, 0, 3)
    router_copy().start()
    gain_two_copy().start()
    for fetch in fetches[4:]:
        fetch.wait()

    def image_back(image):
        rows = image_rows(image)
        mixed_grad = dot_last(attention_grad[rows, :], output_w_ref[...]).astype(LOW)
        queries, keys, values = query_ref[rows, :], key_ref[rows, :], value_ref[rows, :]
        query_parts, key_parts, value_parts = [], [], []
        for h in range(heads):
            cols = slice(h * HD, (h + 1) * HD)
            probs, _ = attention_probs(queries[:, cols], keys[:, cols])
            value_parts.append(dot_first(probs.astype(LOW), mixed_grad[:, cols]))
            probs_grad = dot_last(mixed_grad[:, cols], values[:, cols])
            level = jnp.sum(probs * probs_grad, axis=1, keepdims=True)
            score_grad = (probs * (probs_grad - level)).astype(LOW)
            query_parts.append(dot_plain(score_grad, keys[:, cols]) * HD**-0.5)
            key_parts.append(dot_first(score_grad, queries[:, cols]) * HD**-0.5)
        grads = [jnp.concatenate(p, axis=1).astype(LOW) for p in (query_parts, key_parts, value_parts)]
        query_grad[rows, :], key_grad[rows, :], value_grad[rows, :] = grads

    def answer_turn(k):
        answer_side_copy(k).wait_recv()
        rows = (answer_kept[k] + answer_far[k].astype(FULL)).astype(LOW)

        @pl.when(k == 0)
        def _():
            answer_rows(0, half)[...] = rows

        @pl.when(k > 0)
        def _():
            answer_final[k] = rows
            answer_copy(k).start()

    def grad_part(image):
        rows = image_rows(image)
        part = dot_plain(query_grad[rows, :], query_w_ref[...])
        part = part + dot_plain(key_grad[rows, :], key_w_ref[...])
        part = part + dot_plain(value_grad[rows, :], value_w_ref[...])
        unit, _ = normalized(tokens_ref[rows, :].astype(FULL))
        gain_one_sum[...] += jnp.sum((part * unit).reshape(PIECE // 8, 8, model), axis=0)
        return part

    def my_piece(source, k):
        at = partner(dp, k, n) * piece
        grain = math.gcd(piece, 8)
        span = -(-(piece + 8 - grain) // 8) * 8
        taken = source[pl.ds(pl.multiple_of(at // 8 * 8, 8), span), :]
        rows = taken[:piece]
        for shift in range(grain, 8, grain):
            rows = jnp.where(at % 8 == shift, taken[shift : shift + piece], rows)
        return rows.astype(LOW)

    def small_grads():
        router_copy().wait_recv()
        gain_two_copy().wait_recv()
        row = jnp.sum(gain_two_sum[...] + gain_two_in[...], axis=0, keepdims=True)
        column = jnp.concatenate(
            [row_to_column(row[:, i : i + 256]) for i in range(0, model, 256)], axis=0
        )
        totals_two[...] = jnp.concatenate(
            [
                dot_first(attention_grad[...], mixed_ref[...]),
                router_sum[...] + router_in[...],
                column,
            ],
            axis=1,
        )

        def send_small(i):
            k = in_turn((i + 1) % n, near)
            small_pieces[k] = my_piece(totals_two, k)

            @pl.when(k > 0)
            def _():
                small_copy(k).start()

        loop(send_small)

    for j in range(3):
        attention_copy(j, 1 - half).wait_recv()

    def attention_back(j):
        for owner in (1 - half, half):
            image_back(2 * j + owner)
        total.give(j, grad_part(2 * j + 1 - half))
        total.take(j, grad_part(2 * j + half))
        answer_turn((j + 1) % near)

        @pl.when(j == 0)
        def _():
            small_grads()

        @pl.when(j == 2)
        def _():
            answer_turn(0)

    loop(attention_back, 0, 3)

    gain_one_all[t] = jnp.sum(gain_one_sum[...], axis=0, keepdims=True)
    for d in (1, 2, 3):
        gain_copy(d, t).start()
    normed_one = normed_one_ref[...]
    totals[:, : 3 * query_grad.shape[1]] = jnp.concatenate(
        [
            dot_first(normed_one, query_grad[...]),
            dot_first(normed_one, key_grad[...]),
            dot_first(normed_one, value_grad[...]),
        ],
        axis=1,
    )

    def send_piece(i):
        k = in_turn((i + 1) % n, near)
        pieces[k] = my_piece(totals, k)

        @pl.when(k > 0)
        def _():
            piece_copy(k).start()

    loop(send_piece)


    def answers_here(i):
        k = in_turn(i, near)

        @pl.when((k > 0) & (k < near))
        def _():
            answer_copy(k).wait_recv()

        @pl.when(k >= near)
        def _():
            far_answer_copy(k).wait_recv()

        answer_pair_copy(k, half).start()

    loop(answers_here)
    loop(lambda k: answer_pair_copy(k, 1 - half).wait_recv())

    def block_rows(j):
        rows = image_rows(2 * j + half)
        residual = residual_ref[j]
        unit, _ = normalized(residual)
        gate_one, gate_two, _, _ = gates_of(rows, (unit * gains_ref[1:2, :]).astype(LOW))
        first, second = hots(rows)
        from_first = dot_plain(as_low(first), answers[...])
        from_second = dot_plain(as_low(second), answers[...])
        mine = jnp.where(side == 0, residual[:, :width], residual[:, width:])
        block_mine[j] = (mine + (gate_one * from_first + gate_two * from_second)).astype(LOW)
        block_copy(j).start()

    loop(block_rows, 0, 3)

    def tokens_back(j):
        rows = image_rows(2 * j + half)
        normed_grad = total.result(j)
        unit, factor = normalized(tokens_ref[rows, :].astype(FULL))
        grad = normalized_back(normed_grad * gains_ref[0:1, :], unit, factor)
        grad_tokens_ref[rows, :] = (residual_grad[j] + grad).astype(LOW)
        tokens_copy(j, half).start()

    loop(tokens_back, 0, 3)
    for d in (1, 2, 3):
        gain_copy(d, (t + 4 - d) % 4).wait_recv()
    gain_rows[0] = (gain_one_all[0] + gain_one_all[1]) + (gain_one_all[2] + gain_one_all[3])

    def send_gain(k):
        gain_row_copy(k).start()

    loop(send_gain, 1)

    def block_back(j):
        block_copy(j).wait_recv()
        block_ref[image_rows(2 * j + half), :] = both_sides(block_mine[j], block_other[j])
        block_pair_copy(j, half).start()

    for j in range(3):
        tokens_copy(j, 1 - half).wait_recv()
    unpad(grad_tokens_ref, tokens_out_ref)
    loop(block_back, 0, 3)
    for j in range(3):
        block_pair_copy(j, 1 - half).wait_recv()
    unpad(block_ref, block_out_ref)
    pieces_in[0] = pieces[0]
    small_in[0] = small_pieces[0]

    def arrive(k):
        piece_copy(k).wait_recv()
        small_copy(k).wait_recv()
        gain_row_copy(k).wait_recv()

    loop(arrive, 1)
    weights_ref[...] = jnp.sum(pieces_in[...].astype(FULL), axis=0)
    small_ref[...] = jnp.sum(small_in[...].astype(FULL), axis=0)
    gain_ref[...] = jnp.sum(gain_rows[...], axis=0)

    for j in range(3):
        moe_copy(j).wait_send()
        block_copy(j).wait_send()
        attention_copy(j, half).wait_send()
        total.sent(j)
        tokens_copy(j, half).wait_send()
        block_pair_copy(j, half).wait_send()
        gain_copy(j + 1, t).wait_send()
    router_copy().wait_send()
    gain_two_copy().wait_send()

    def left(k):
        @pl.when(k < near)
        def _():
            answer_side_copy(k).wait_send()

        @pl.when((k > 0) & (k < near))
        def _():
            answer_copy(k).wait_send()

        @pl.when(k >= near)
        def _():
            far_answer_copy(k).wait_send()

        answer_pair_copy(k, half).wait_send()

        @pl.when(k > 0)
        def _():
            piece_copy(k).wait_send()
            small_copy(k).wait_send()
            gain_row_copy(k).wait_send()

    loop(left)


def run_back(n, hp, row_count, first, later):
    upstream = later[2]
    rows, model = upstream.shape
    heads_width = later[9].shape[1]
    width = model // 2
    piece = model // n
    vmem = pl.BlockSpec(memory_space=VMEM)
    shape = jax.ShapeDtypeStruct
    slim = VMEM((3, PIECE, width), LOW)
    heads = VMEM((rows, heads_width), LOW)
    eight = VMEM((8, model), FULL)
    wide, narrow = 3 * heads_width, heads_width + n + 1
    quarter = VMEM((near_count(n), hp, width), LOW)
    three, many = dma(3), dma(n)
    return pl.pallas_call(
        functools.partial(back_kernel, n, hp),
        out_shape=(
            shape((row_count, model), LOW),
            shape((row_count, model), LOW),
            shape((piece, wide), FULL),
            shape((piece, narrow), FULL),
            shape((1, model), FULL),
        ),
        in_specs=[vmem] * (len(first) - 1) + [pl.BlockSpec(memory_space=pl.ANY)] * (1 + len(later)),
        out_specs=[vmem] * 5,
        scratch_shapes=[
            *[VMEM(a.shape, a.dtype) for a in later],
            slim, slim, slim, slim,
            VMEM((rows, model), LOW),
            VMEM((3, PIECE, model), FULL),
            heads, heads, heads,
            eight, eight, eight,
            VMEM((4, 1, model), FULL),
            VMEM((n, 1, model), FULL),
            VMEM((model, n), FULL),
            VMEM((model, n), FULL),
            VMEM((model, wide), FULL),
            VMEM((model, narrow), FULL),
            VMEM((n, piece, wide), LOW),
            VMEM((n, piece, wide), LOW),
            VMEM((n, piece, narrow), LOW),
            VMEM((n, piece, narrow), LOW),
            quarter, quarter,
            VMEM((n * 2 * hp, width), LOW),
            VMEM((rows, model), LOW),
            VMEM((rows, model), LOW),
            dma(len(later)),
            three, three, three, three, three, three, three, three, three, three,
            many, many, three, three, dma(2), dma(2),
            many, many, many, many, many, many, many, many, many, many,
            *Total.scratch(model),
        ],
        compiler_params=pltpu.CompilerParams(
            collective_id=2, has_side_effects=True, vmem_limit_bytes=VMEM_LIMIT
        ),
        name="back",
    )(*first, *later)


def results_kernel(
    threshold_ref,
    *refs,
):
    small_in, moved_in, moved_out, refs = refs[:6], refs[6:10], refs[10:14], refs[14:]
    (
        gain_one_ref,
        gain_two_ref,
        query_ref,
        key_ref,
        value_ref,
        output_ref,
        router_ref,
        clipped_query_ref,
        clipped_key_ref,
        head_max_ref,
        *held,
        sems,
    ) = refs
    held, own = held[:4], held[4:]
    weights_ref, small_ref, gain_row_ref, top_ref, query_w_ref, key_w_ref = own
    fetches, copies = [], []
    for i, (source, target) in enumerate(zip(moved_in, moved_out)):
        rows = source.shape[0]
        cut = rows // 16 * 8
        for part, at in enumerate((slice(0, cut), slice(cut, rows))):
            sem = sems.at[2 * i + part]
            fetches.append(pltpu.make_async_copy(source.at[at], held[i].at[at], sem))
            sem = sems.at[8 + 2 * i + part]
            copies.append(pltpu.make_async_copy(held[i].at[at], target.at[at], sem))
    small_fetches = [
        pltpu.make_async_copy(a, b, sems.at[16 + i]) for i, (a, b) in enumerate(zip(small_in, own))
    ]
    for fetch in fetches + small_fetches:
        fetch.start()
    for fetch, copy in zip(fetches, copies):
        fetch.wait()
        copy.start()
    for fetch in small_fetches:
        fetch.wait()
    piece, wide = query_ref.shape
    heads = head_max_ref.shape[0]
    query_ref[...] = weights_ref[:, :wide]
    key_ref[...] = weights_ref[:, wide : 2 * wide]
    value_ref[...] = weights_ref[:, 2 * wide :]
    small = small_ref[...]
    output_ref[...] = small[:, :wide].T
    n = router_ref.shape[0]
    router_ref[...] = small[:, wide : wide + n].T
    gain_two_ref[...] = column_to_row(small[:, wide + n :])[0]
    model = gain_row_ref.shape[1]
    lanes = lax.broadcasted_iota(jnp.int32, (piece, model), 1)
    mine = lax.broadcasted_iota(jnp.int32, (piece, model), 0) + lax.axis_index("dp") * piece
    column = jnp.sum(jnp.where(lanes == mine, gain_row_ref[...], 0.0), axis=1, keepdims=True)
    gain_one_ref[...] = column_to_row(column)[0]
    head_max_ref[...] = column_to_row(top_ref[:, 0:1])[0, :heads]
    for h in range(heads):
        rows = slice(h * HD, (h + 1) * HD)
        factor = jnp.sqrt(jnp.minimum(1.0, threshold_ref[h] / top_ref[h : h + 1, 0:1]))
        clipped_query_ref[rows, :] = query_w_ref[rows, :].astype(FULL) * factor
        clipped_key_ref[rows, :] = key_w_ref[rows, :].astype(FULL) * factor
    for copy in copies:
        copy.wait()


def run_results(n, threshold, weights, small, gain_row, top, query_w, key_w, moved):
    wide, model = query_w.shape
    piece = weights.shape[0]
    shape = jax.ShapeDtypeStruct
    vmem = pl.BlockSpec(memory_space=VMEM)
    hbm = pl.BlockSpec(memory_space=pl.ANY)
    grad, clipped = shape((piece, wide), FULL), shape((wide, model), FULL)
    return pl.pallas_call(
        results_kernel,
        out_shape=(
            *[shape(a.shape, a.dtype) for a in moved],
            shape((piece,), FULL),
            shape((piece,), FULL),
            grad,
            grad,
            grad,
            shape((wide, piece), FULL),
            shape((n, piece), FULL),
            clipped,
            clipped,
            shape(threshold.shape, FULL),
        ),
        in_specs=[pl.BlockSpec(memory_space=pltpu.SMEM)] + [hbm] * 10,
        out_specs=[hbm] * 4 + [vmem] * 10,
        scratch_shapes=[
            *[
                VMEM(a.shape, a.dtype)
                for a in (*moved, weights, small, gain_row, top, query_w, key_w)
            ],
            dma(22),
        ],
        compiler_params=pltpu.CompilerParams(vmem_limit_bytes=VMEM_LIMIT),
        name="results",
    )(threshold, weights, small, gain_row, top, query_w, key_w, *moved)


def body(
    tokens,
    gain_attn,
    w_query,
    w_key,
    w_value,
    w_output,
    gain_moe,
    w_router,
    expert_in,
    expert_out,
    routes,
    slot_ids,
    capacity,
    threshold,
    cotangent,
):
    n = lax.axis_size("dp")
    row_count, model = tokens.shape
    slot_count = 23 * TOK_DEV // (10 * n) + 1
    per_half = -(-slot_count // 2)
    hp = -(-per_half // 16) * 16
    gains = jnp.concatenate([gain_attn, gain_moe]).astype(FULL).reshape(2, -1)
    across = (w_query.T, w_key.T, w_value.T)
    (
        place,
        index,
        peak,
        tokens_in,
        upstream,
        normed_one,
        query,
        key,
        value,
        mixed,
        residual,
        normed_two,
        spread,
    ) = run_front(
        n,
        hp,
        per_half,
        capacity,
        routes.T,
        slot_ids.T,
        tokens,
        cotangent,
        gains,
        (*across, w_output),
    )
    router = w_router.T
    back, gate_sums, top, answer_out, answer_kept, answer_ready, grad_first, grad_second = run_experts(
        n, hp, place, router, peak, normed_two, expert_in[0], expert_out[0], spread
    )
    block_out, grad_tokens, weight_grads, small, gain_rows = run_back(
        n,
        hp,
        row_count,
        (gate_sums, index, gains, w_output, router, answer_ready),
        (
            back.reshape(n * 2 * hp, -1),
            residual,
            upstream,
            answer_out,
            answer_kept,
            normed_one,
            query,
            key,
            value,
            mixed,
            tokens_in,
            *across,
        ),
    )
    (
        block_out,
        grad_tokens,
        grad_first,
        grad_second,
        gain_one,
        gain_two,
        grad_query,
        grad_key,
        grad_value,
        grad_output,
        grad_router,
        clipped_query,
        clipped_key,
        head_max,
    ) = run_results(
        n,
        threshold,
        weight_grads,
        small,
        gain_rows,
        top,
        *across[:2],
        (block_out, grad_tokens, grad_first, grad_second),
    )
    return (
        block_out,
        grad_tokens,
        gain_one,
        gain_two,
        grad_query,
        grad_key,
        grad_value,
        grad_output,
        grad_router.T,
        grad_first[None],
        grad_second[None],
        clipped_query.T,
        clipped_key.T,
        head_max,
    )


def solution(mesh):
    in_specs = (
        P("dp", None),
        P(),
        P(None, "tensor"),
        P(None, "tensor"),
        P(None, "tensor"),
        P("tensor", None),
        P(),
        P(),
        P("dp", None, "tensor"),
        P("dp", "tensor", None),
        P("dp", None),
        P("dp", None),
        P(),
        P("tensor"),
        P("dp", None),
    )
    out_specs = (
        P("dp", None),
        P("dp", None),
        P("dp"),
        P("dp"),
        P("dp", "tensor"),
        P("dp", "tensor"),
        P("dp", "tensor"),
        P("tensor", "dp"),
        P("dp", None),
        P("dp", None, "tensor"),
        P("dp", "tensor", None),
        P(None, "tensor"),
        P(None, "tensor"),
        P("tensor"),
    )
    return jax.shard_map(body, mesh=mesh, in_specs=in_specs, out_specs=out_specs, check_vma=False)
```
